32 devices in a mesh: dp: 8 (over z, x), tensor: 4 (over y, core).
Axes of the slice: x: 2, y: 2, z: 4, core: 2. Of those that a mesh axis runs over, the one named last changes fastest.
Arguments:
- patches: bfloat16 [24, 2048, 1024], P('dp', 'tensor'), may hold values from -6 to 6
- cotangent: bfloat16 [24, 2048, 1024], P('dp', 'tensor'), may hold values from -6 to 6
- empty_slots: int32 [8], replicated, may hold values from 0 to 2
- dataset_id: int32 [24], replicated, may hold values from 0 to 5
- dataset_weight: int32 [6], replicated, may hold values from 1 to 8
- query_key_value_weight: bfloat16 [3, 1024, 1024], P(None, None, 'tensor'), may hold values from -0.25 to 0.25
- qv_bias: float32 [2, 1024], P(None, 'tensor'), may hold values from -3 to 3
- output_projection_weight: bfloat16 [1024, 1024], P('tensor'), may hold values from -0.75 to 0.75
- out_bias: float32 [1024], replicated, may hold values from -2 to 2
- up_projection_weight: bfloat16 [1024, 4096], P(None, 'tensor'), may hold values from -0.1875 to 0.1875
- up_bias: float32 [4096], P('tensor'), may hold values from -2 to 2
- down_projection_weight: bfloat16 [4096, 1024], P('tensor'), may hold values from -0.09375 to 0.09375
- down_bias: float32 [1024], replicated, may hold values from -2 to 2
- attn_gain: float32 [1024], replicated, may hold values from 0.5 to 1.5
- attn_shift: float32 [1024], replicated, may hold values from -1.5 to 1.5
- mlp_gain: float32 [1024], replicated, may hold values from 0.5 to 1.5
- mlp_shift: float32 [1024], replicated, may hold values from -1.5 to 1.5
Outputs:
- block_out: bfloat16 [24, 2048, 1024], P('dp', 'tensor')
- grad_patches: bfloat16 [24, 2048, 1024], P('dp', 'tensor')
- grad_qkv_weight: float32 [3, 1024, 1024], P(None, None, 'tensor')
- grad_qv_bias: float32 [2, 1024], P(None, 'tensor')
- grad_out_weight: float32 [1024, 1024], P('tensor')
- grad_out_bias: float32 [1024], replicated
- grad_up_weight: float32 [1024, 4096], P(None, 'tensor')
- grad_up_bias: float32 [4096], P('tensor')
- grad_down_weight: float32 [4096, 1024], P('tensor')
- grad_down_bias: float32 [1024], replicated
- grad_attn_gain: float32 [1024], replicated
- grad_attn_shift: float32 [1024], replicated
- sensitivity_feedforward_scale: float32 [1024], replicated
- grad_mlp_shift: float32 [1024], replicated
The draws below stay inside these ranges and needn't reach their ends.
All inputs are finite; a program needn't handle non-finite values.
Results may differ from the reference program's by a relative error of at most 0.02.
Values may be sent and summed in bfloat16 or wider, within the bound.
No kernel may reach another device: no remote copies, remote signals or barrier semaphores. Data moves between devices by JAX's collectives and lax.ppermute only.
A program may use at most 256 MiB of HBM per device.

```python
import math
import jax
import jax.numpy as jnp
import numpy as np
from jax import lax

D = 1024
H = 16
HD = 64
FF = 4096
LEN = 2048
SLOTS = 3
GROUPS = 6
ITEMS = 24
N_DP = 8


def place_ends(values, own_key, least, largest):
    longest = values.shape.index(max(values.shape))
    spots = []
    for shift in (0, 1):
        where = [jax.random.randint(jax.random.fold_in(own_key, axis), (), 0, length) for axis, length in enumerate(values.shape)]
        where[longest] = (where[longest] + shift) % values.shape[longest]
        spots.append(tuple(where))
    return values.at[spots[0]].set(least).at[spots[1]].set(largest)


def steps_of(own_key, extent, split, low, top_value):
    loudness = 1.0
    for position, shards_of in split:
        steps = jax.random.uniform(jax.random.fold_in(jax.random.fold_in(own_key, 6), position), (shards_of,), jnp.float32, low / len(split), top_value / len(split))
        loudness = loudness * jnp.repeat(jnp.exp(steps), extent[position] // shards_of).reshape((-1,) + (1,) * (len(extent) - 1 - position))
    return loudness


def cumulative_ranks(number_of, skew):
    portions = [(1 << 20) // math.isqrt(rank ** skew) + 1 for rank in range(1, number_of + 1)]
    deviation = 1 + sum(portions) // (1 << 30)
    return np.cumsum(np.array([max(1, weight // deviation) for weight in portions]))


def ranked_ids(stream_key, dims, number_of, lean):
    grid = cumulative_ranks(number_of, lean)
    pick = jax.random.randint(jax.random.fold_in(stream_key, 1), dims, 0, int(grid[number_of - 1]))
    grade = jnp.searchsorted(jnp.asarray(grid, jnp.int32), pick, side="right")
    return jax.random.permutation(jax.random.fold_in(stream_key, 2), number_of)[grade].astype(jnp.int32)


def scatter_about(key, shape, deviation, limit, pieces=(), held_as=jnp.bfloat16):
    level = steps_of(key, shape, pieces, -0.22, 0.18) if pieces else 1.0
    values = jax.random.normal(key, shape, jnp.float32) * deviation * level
    return jnp.minimum(jnp.maximum(values, -limit), limit).astype(held_as)


def setup_inputs(seed: int = 0) -> dict:
    splits = jax.random.split(jax.random.key(seed), 18)
    return {
        "patches": scatter_about(splits[0], (ITEMS, LEN, D), 1.0, 6.0, ((0, 8), (1, 4))),
        "cotangent": scatter_about(splits[1], (ITEMS, LEN, D), 1.0, 6.0, ((0, 8), (1, 4))),
        "empty_slots": place_ends(ranked_ids(splits[2], (N_DP,), SLOTS, 2), jax.random.fold_in(splits[2], 3), 0, SLOTS - 1).astype(jnp.int32),
        "dataset_id": place_ends(ranked_ids(splits[3], (ITEMS,), GROUPS, 2), jax.random.fold_in(splits[3], 3), 0, GROUPS - 1).astype(jnp.int32),
        "dataset_weight": place_ends(jax.random.randint(splits[4], (GROUPS,), 1, 9), jax.random.fold_in(splits[4], 1), 1, 8).astype(jnp.int32),
        "query_key_value_weight": scatter_about(splits[5], (3, D, D), (D // 2) ** -0.5, 0.25, ((2, 4),)),
        "qv_bias": scatter_about(splits[6], (2, D), 0.5, 3.0, ((1, 4),), jnp.float32),
        "output_projection_weight": scatter_about(splits[7], (D, D), (D // 16) ** -0.5, 0.75, ((0, 4),)),
        "out_bias": scatter_about(splits[8], (D,), 0.3, 2.0, (), jnp.float32),
        "up_projection_weight": scatter_about(splits[9], (D, FF), D ** -0.5, 0.1875, ((1, 4),)),
        "up_bias": scatter_about(splits[10], (FF,), 0.3, 2.0, ((0, 4),), jnp.float32),
        "down_projection_weight": scatter_about(splits[11], (FF, D), FF ** -0.5, 0.09375, ((0, 4),)),
        "down_bias": scatter_about(splits[12], (D,), 0.3, 2.0, (), jnp.float32),
        "attn_gain": jnp.clip(1.0 + 0.1 * jax.random.normal(splits[13], (D,), jnp.float32), 0.5, 1.5),
        "attn_shift": scatter_about(splits[14], (D,), 0.2, 1.5, (), jnp.float32),
        "mlp_gain": jnp.clip(1.0 + 0.1 * jax.random.normal(splits[15], (D,), jnp.float32), 0.5, 1.5),
        "mlp_shift": scatter_about(splits[16], (D,), 0.2, 1.5, (), jnp.float32),
    }


@jax.custom_vjp
def low(v):
    return lax.optimization_barrier(v.astype(jnp.bfloat16)).astype(jnp.float32)

@jax.custom_vjp
def low_back(v):
    return v

def low_keep(v):
    return (low(v), None)

def low_pass(kept, grad):
    return (grad,)

def back_keep(v):
    return (v, None)

def back_low(kept, grad):
    return (low(grad),)
low.defvjp(low_keep, low_pass)
low_back.defvjp(back_keep, back_low)
HIGHEST_PREC = lax.Precision.HIGHEST

def norm_rows(source, norm_gain, norm_shift):
    row_mean = lax.optimization_barrier(jnp.mean(source, axis=-1, keepdims=True))
    centred = source - row_mean
    spread = lax.optimization_barrier(jnp.mean(centred * centred, axis=-1, keepdims=True))
    return centred * lax.rsqrt(spread + 1e-05) * norm_gain + norm_shift

def attend(queries, key_rows, values):
    qblock = min(512, LEN)
    score_scale = HD ** (-0.5)
    blocks = queries.reshape(LEN // qblock, qblock, H, HD)

    def one_block(query_block):
        scores = low_back(jnp.einsum('qhd,khd->hqk', query_block, key_rows, precision=HIGHEST_PREC) * score_scale)
        attn_weights = jax.nn.softmax(scores, axis=-1)
        return jnp.einsum('hqk,khd->qhd', low(attn_weights), values, precision=HIGHEST_PREC)
    attended = lax.map(jax.checkpoint(one_block), blocks)
    return attended.reshape(LEN, D)

def layer(item_rows, params):
    query_key_value_weight, qv_bias, output_projection_weight, out_bias, up_projection_weight, up_bias, down_projection_weight, down_bias, attn_gain, attn_shift, mlp_gain, mlp_shift = params
    normed = low(norm_rows(item_rows, attn_gain, attn_shift))
    queries = low_back(low(jnp.dot(normed, query_key_value_weight[0], precision=HIGHEST_PREC) + qv_bias[0]))
    key_rows = low_back(low(jnp.dot(normed, query_key_value_weight[1], precision=HIGHEST_PREC)))
    values = low_back(low(jnp.dot(normed, query_key_value_weight[2], precision=HIGHEST_PREC) + qv_bias[1]))
    attended = attend(queries.reshape(LEN, H, HD), key_rows.reshape(LEN, H, HD), values.reshape(LEN, H, HD))
    attended = low_back(low(attended))
    residual = item_rows + low_back(jnp.dot(attended, output_projection_weight, precision=HIGHEST_PREC)) + out_bias
    normed_mlp = low(norm_rows(residual, mlp_gain, mlp_shift))
    hidden_pre = low_back(jnp.dot(normed_mlp, up_projection_weight, precision=HIGHEST_PREC) + up_bias)
    latent_activations = low(jax.nn.gelu(hidden_pre, approximate=False))
    return residual + low_back(jnp.dot(latent_activations, down_projection_weight, precision=HIGHEST_PREC)) + down_bias

def reference(patches, cotangent, empty_slots, dataset_id, dataset_weight, query_key_value_weight, qv_bias, output_projection_weight, out_bias, up_projection_weight, up_bias, down_projection_weight, down_bias, attn_gain, attn_shift, mlp_gain, mlp_shift):
    slot_index = jnp.arange(N_DP * SLOTS, dtype=jnp.int32) % SLOTS
    filled = jnp.repeat(SLOTS - empty_slots, SLOTS)
    valid_item = (slot_index < filled).astype(jnp.float32)
    numerator = dataset_weight[dataset_id].astype(jnp.float32)
    total_items = jnp.sum(valid_item)
    total_weight = jnp.sum(valid_item * numerator)
    sample_multiplier = valid_item * numerator * total_items / total_weight
    params = tuple((array.astype(jnp.float32) for array in (query_key_value_weight, qv_bias, output_projection_weight, out_bias, up_projection_weight, up_bias, down_projection_weight, down_bias, attn_gain, attn_shift, mlp_gain, mlp_shift)))

    def forward(inputs, weights_all):

        def scan_step(state_carry, item_rows):
            return (state_carry, jax.checkpoint(layer)(item_rows, weights_all))
        unused_carry, outputs = lax.scan(scan_step, jnp.zeros((), jnp.float32), inputs)
        return outputs * valid_item[:, None, None]
    result, pullback = jax.vjp(forward, patches.astype(jnp.float32), params)
    grad_inputs, grad_params = pullback(cotangent.astype(jnp.float32) * sample_multiplier[:, None, None])
    gradient = tuple((entry / total_items for entry in grad_params))
    return (result.astype(jnp.bfloat16), grad_inputs.astype(jnp.bfloat16), gradient[0], gradient[1], gradient[2], gradient[3], gradient[4], gradient[5], gradient[6], gradient[7], gradient[8], gradient[9], gradient[10], gradient[11])
```

```python
import jax
import jax.numpy as jnp
from jax import lax
from jax.experimental import pallas as pl
from jax.experimental.pallas import tpu as pltpu
from jax.sharding import PartitionSpec as P

HD = 64
SCORE_SCALE = HD ** (-0.5)
LOG2E = 1.4426950408889634
SQRT_HALF = 0.7071067811865476
INV_SQRT_2PI = 0.3989422804014327
epsilon = 1e-05
f32 = jnp.float32
bf16 = jnp.bfloat16
VMEM_LIMIT = 60 << 20
COST_SCALE = 64


def nn(a, b):
    return lax.dot_general(a, b, (((1,), (0,)), ((), ())), preferred_element_type=f32)


def nt(a, b):
    return lax.dot_general(a, b, (((1,), (1,)), ((), ())), preferred_element_type=f32)


def tn(a, b):
    return lax.dot_general(a, b, (((0,), (0,)), ((), ())), preferred_element_type=f32)


def tie(first, second):
    return lax.optimization_barrier((first, second))


def largest_block(extent, limit):
    block = min(extent, limit)
    while extent % block:
        block //= 2
    return block


def norm_rows(source, norm_gain, norm_shift):
    row_mean = jnp.mean(source, axis=-1, keepdims=True)
    centred = source - row_mean
    spread = jnp.mean(centred * centred, axis=-1, keepdims=True)
    return centred * lax.rsqrt(spread + epsilon) * norm_gain + norm_shift


def attend(qkv):
    _, length, width = qkv.shape
    lanes = min(128, width)
    heads = lanes // HD
    qblock = largest_block(length, 1024)
    to_log2 = SCORE_SCALE * LOG2E

    def body(q_ref, k_ref, v_ref, out_ref, lse_ref):
        queries = q_ref[...]
        keys = k_ref[...]
        values_t = v_ref[...].T
        lane = lax.broadcasted_iota(jnp.int32, (1, lanes), 1)
        outs = []
        for h in range(heads):
            own = queries
            if heads > 1:
                own = jnp.where(lane // HD == h, queries, jnp.zeros_like(queries))
            scores = nt(keys, own)
            top = jnp.max(scores, axis=0, keepdims=True)
            exp_scores = jnp.exp2((scores - top) * to_log2)
            total = jnp.sum(exp_scores, axis=0, keepdims=True)
            outs.append(nn(values_t[h * HD : (h + 1) * HD, :], exp_scores.astype(bf16)) / total)
            lse_ref[h : h + 1, :] = top * to_log2 + jnp.log2(total)
        out_ref[...] = jnp.concatenate(outs, axis=0).T.astype(bf16)

    pairs = width // lanes
    return pl.pallas_call(
        body,
        grid=(pairs, length // qblock),
        in_specs=[
            pl.BlockSpec((None, qblock, lanes), lambda h, j: (0, j, h)),
            pl.BlockSpec((None, length, lanes), lambda h, j: (1, 0, h)),
            pl.BlockSpec((None, length, lanes), lambda h, j: (2, 0, h)),
        ],
        out_specs=[
            pl.BlockSpec((qblock, lanes), lambda h, j: (j, h)),
            pl.BlockSpec((None, heads, qblock), lambda h, j: (h, 0, j)),
        ],
        out_shape=[
            jax.ShapeDtypeStruct((length, width), bf16),
            jax.ShapeDtypeStruct((pairs, heads, length), f32),
        ],
        compiler_params=pltpu.CompilerParams(vmem_limit_bytes=VMEM_LIMIT),
        cost_estimate=pl.CostEstimate(
            flops=8 * length * length * width // COST_SCALE,
            transcendentals=0,
            bytes_accessed=length * width,
        ),
        name="attend",
    )(qkv, qkv, qkv)


def attend_back(qkv, attended, grad_attended, lse):
    _, length, width = qkv.shape
    lanes = min(128, width)
    heads = lanes // HD
    kblock = largest_block(length, 512)
    kblocks = length // kblock
    to_log2 = SCORE_SCALE * LOG2E

    def body(q_ref, k_ref, v_ref, out_ref, grad_ref, lse_ref, dqkv_ref, dq_acc, row_dot):
        kb = pl.program_id(1)
        queries = q_ref[...]
        grads = grad_ref[...]
        keys = k_ref[...]
        values = v_ref[...]
        keys_t = keys.T
        lane = lax.broadcasted_iota(jnp.int32, (1, lanes), 1)

        @pl.when(kb == 0)
        def _():
            product = out_ref[...].astype(f32) * grads.astype(f32)
            high = product.astype(bf16)
            rest = (product - high.astype(f32)).astype(bf16)
            pick = lax.broadcasted_iota(jnp.int32, (8, lanes), 0)
            mask = (lax.broadcasted_iota(jnp.int32, (8, lanes), 1) // HD == pick).astype(f32).astype(bf16)
            row_dot[...] = nt(mask, high) + nt(mask, rest)

        dk = None
        dv = None
        dqs = []
        for h in range(heads):
            own_q = queries
            own_g = grads
            if heads > 1:
                mine = lane // HD == h
                own_q = jnp.where(mine, queries, jnp.zeros_like(queries))
                own_g = jnp.where(mine, grads, jnp.zeros_like(grads))
            scores = nt(keys, own_q)
            weights = jnp.exp2(scores * to_log2 - lse_ref[h : h + 1, :])
            grad_weights = nt(values, own_g)
            grad_scores = (weights * (grad_weights - row_dot[h : h + 1, :])).astype(bf16)
            dv_h = nn(weights.astype(bf16), own_g)
            dk_h = nn(grad_scores, own_q)
            dv = dv_h if dv is None else dv + dv_h
            dk = dk_h if dk is None else dk + dk_h
            dqs.append(nn(keys_t[h * HD : (h + 1) * HD, :], grad_scores))
        rows = pl.ds(pl.multiple_of(kb * kblock, kblock), kblock)
        dqkv_ref[1, rows, :] = (dk * SCORE_SCALE).astype(bf16)
        dqkv_ref[2, rows, :] = dv.astype(bf16)
        dq = jnp.concatenate(dqs, axis=0)
        if kblocks == 1:
            dqkv_ref[0] = (dq * SCORE_SCALE).T.astype(bf16)
            return

        @pl.when(kb == 0)
        def _():
            dq_acc[...] = dq

        @pl.when((kb > 0) & (kb < kblocks - 1))
        def _():
            dq_acc[...] += dq

        @pl.when(kb == kblocks - 1)
        def _():
            dqkv_ref[0] = ((dq_acc[...] + dq) * SCORE_SCALE).T.astype(bf16)

    pairs = width // lanes
    return pl.pallas_call(
        body,
        grid=(pairs, kblocks),
        in_specs=[
            pl.BlockSpec((None, length, lanes), lambda h, kb: (0, 0, h)),
            pl.BlockSpec((None, kblock, lanes), lambda h, kb: (1, kb, h)),
            pl.BlockSpec((None, kblock, lanes), lambda h, kb: (2, kb, h)),
            pl.BlockSpec((length, lanes), lambda h, kb: (0, h)),
            pl.BlockSpec((length, lanes), lambda h, kb: (0, h)),
            pl.BlockSpec((None, heads, length), lambda h, kb: (h, 0, 0)),
        ],
        out_specs=pl.BlockSpec((3, length, lanes), lambda h, kb: (0, 0, h)),
        out_shape=jax.ShapeDtypeStruct((3, length, width), bf16),
        scratch_shapes=[pltpu.VMEM((lanes, length), f32), pltpu.VMEM((8, length), f32)],
        compiler_params=pltpu.CompilerParams(vmem_limit_bytes=VMEM_LIMIT),
        cost_estimate=pl.CostEstimate(
            flops=20 * length * length * width // COST_SCALE,
            transcendentals=0,
            bytes_accessed=length * width,
        ),
        name="attend_back",
    )(qkv, qkv, qkv, attended, grad_attended, lse)


def mlp_forward(normed, up, up_bias, down, total):
    rows, model = normed.shape
    units = up.shape[1]
    block = largest_block(rows, 512)
    first = total is None

    def body(*refs):
        if first:
            x_ref, up_ref, bias_ref, down_ref, hidden_ref, slope_ref, sum_ref = refs
        else:
            x_ref, up_ref, bias_ref, down_ref, before_ref, hidden_ref, slope_ref, sum_ref = refs
        part = largest_block(units, 256)
        for j in range(units // part):
            cols = slice(j * part, (j + 1) * part)
            pre = nn(x_ref[...], up_ref[:, cols]) + bias_ref[:, cols]
            cdf = 0.5 + 0.5 * lax.erf(pre * SQRT_HALF)
            density = jnp.exp2(pre * pre * (-0.5 * LOG2E)) * INV_SQRT_2PI
            hidden_ref[:, cols] = (pre * cdf).astype(bf16)
            slope_ref[:, cols] = (cdf + pre * density).astype(bf16)
        out = nn(hidden_ref[...], down_ref[...])
        sum_ref[...] = out if first else before_ref[...] + out

    row_spec = pl.BlockSpec((block, model), lambda i: (i, 0))
    unit_spec = pl.BlockSpec((block, units), lambda i: (i, 0))
    in_specs = [
        row_spec,
        pl.BlockSpec((model, units), lambda i: (0, 0)),
        pl.BlockSpec((1, units), lambda i: (0, 0)),
        pl.BlockSpec((units, model), lambda i: (0, 0)),
    ]
    operands = [normed, up, up_bias, down]
    if not first:
        in_specs.append(row_spec)
        operands.append(total)
    return pl.pallas_call(
        body,
        grid=(rows // block,),
        in_specs=in_specs,
        out_specs=[unit_spec, unit_spec, row_spec],
        out_shape=[
            jax.ShapeDtypeStruct((rows, units), bf16),
            jax.ShapeDtypeStruct((rows, units), bf16),
            jax.ShapeDtypeStruct((rows, model), f32),
        ],
        input_output_aliases={} if first else {4: 2},
        compiler_params=pltpu.CompilerParams(vmem_limit_bytes=VMEM_LIMIT),
        cost_estimate=pl.CostEstimate(
            flops=4 * rows * model * units // COST_SCALE,
            transcendentals=0,
            bytes_accessed=rows * units,
        ),
        name="mlp_forward",
    )(*operands)


def mlp_backward(cot, down, slope, up, total):
    rows, model = cot.shape
    units = up.shape[1]
    block = largest_block(rows, 512)
    first = total is None

    def body(*refs):
        if first:
            cot_ref, down_ref, slope_ref, up_ref, grad_ref, bias_ref, sum_ref = refs
        else:
            cot_ref, down_ref, slope_ref, up_ref, before_ref, grad_ref, bias_ref, sum_ref = refs
        part = largest_block(units, 256)

        @pl.when(pl.program_id(0) == 0)
        def _():
            bias_ref[...] = jnp.zeros_like(bias_ref)

        for j in range(units // part):
            cols = slice(j * part, (j + 1) * part)
            grad = nt(cot_ref[...], down_ref[cols, :]) * slope_ref[:, cols].astype(f32)
            low = grad.astype(bf16)
            grad_ref[:, cols] = low
            bias_ref[:, cols] += jnp.sum(low.astype(f32), axis=0, keepdims=True)
        out = nt(grad_ref[...], up_ref[...])
        sum_ref[...] = out if first else before_ref[...] + out

    row_spec = pl.BlockSpec((block, model), lambda i: (i, 0))
    unit_spec = pl.BlockSpec((block, units), lambda i: (i, 0))
    in_specs = [
        row_spec,
        pl.BlockSpec((units, model), lambda i: (0, 0)),
        unit_spec,
        pl.BlockSpec((model, units), lambda i: (0, 0)),
    ]
    operands = [cot, down, slope, up]
    if not first:
        in_specs.append(row_spec)
        operands.append(total)
    return pl.pallas_call(
        body,
        grid=(rows // block,),
        in_specs=in_specs,
        out_specs=[unit_spec, pl.BlockSpec((1, units), lambda i: (0, 0)), row_spec],
        out_shape=[
            jax.ShapeDtypeStruct((rows, units), bf16),
            jax.ShapeDtypeStruct((1, units), f32),
            jax.ShapeDtypeStruct((rows, model), f32),
        ],
        input_output_aliases={} if first else {4: 2},
        compiler_params=pltpu.CompilerParams(vmem_limit_bytes=VMEM_LIMIT),
        cost_estimate=pl.CostEstimate(
            flops=4 * rows * model * units // COST_SCALE,
            transcendentals=0,
            bytes_accessed=rows * units,
        ),
        name="mlp_backward",
    )(*operands)


def project_back(normed, dqkv, weight, before, last):
    rows, model = normed.shape
    width = weight.shape[2]
    block = largest_block(rows, 512)
    steps = rows // block
    first = before is None

    def kernel(*refs):
        normed_ref, dqkv_ref, weight_ref = refs[:3]
        rest = refs[3:]
        if not first:
            wgrad_before, column_before = rest[:2]
            rest = rest[2:]
        row_ref, wgrad_ref, column_ref = rest[:3]
        step = pl.program_id(0)

        @pl.when(step == 0)
        def _():
            if first:
                wgrad_ref[...] = jnp.zeros_like(wgrad_ref)
                column_ref[...] = jnp.zeros_like(column_ref)
            else:
                wgrad_ref[...] = wgrad_before[...]
                column_ref[...] = column_before[...]

        row_grad = nt(dqkv_ref[0], weight_ref[0])
        for c in range(1, 3):
            row_grad = row_grad + nt(dqkv_ref[c], weight_ref[c])
        row_ref[...] = row_grad.astype(bf16)
        for c in range(3):
            wgrad_ref[c] += tn(normed_ref[...], dqkv_ref[c])
            column_ref[c : c + 1, :] += jnp.sum(dqkv_ref[c].astype(f32), axis=0, keepdims=True)
        if last:
            low_ref = rest[3]

            @pl.when(step == steps - 1)
            def _():
                low_ref[:, :model, :] = wgrad_ref[...].astype(bf16)
                for c in range(3):
                    row = jnp.broadcast_to(column_ref[c : c + 1, :], (16, width))
                    low_ref[c, model:, :] = row.astype(bf16)

    whole = pl.BlockSpec((3, model, width), lambda i: (0, 0, 0))
    columns = pl.BlockSpec((8, width), lambda i: (0, 0))
    row_spec = pl.BlockSpec((block, model), lambda i: (i, 0))
    operands = [normed, dqkv, weight]
    in_specs = [row_spec, pl.BlockSpec((3, block, width), lambda i: (0, i, 0)), whole]
    if not first:
        operands += list(before)
        in_specs += [whole, columns]
    out_specs = [row_spec, whole, columns]
    out_shape = [
        jax.ShapeDtypeStruct((rows, model), bf16),
        jax.ShapeDtypeStruct((3, model, width), f32),
        jax.ShapeDtypeStruct((8, width), f32),
    ]
    if last:
        out_specs.append(pl.BlockSpec((3, model + 16, width), lambda i: (0, 0, 0)))
        out_shape.append(jax.ShapeDtypeStruct((3, model + 16, width), bf16))
    return pl.pallas_call(
        kernel,
        grid=(steps,),
        in_specs=in_specs,
        out_specs=out_specs,
        out_shape=out_shape,
        input_output_aliases={} if first else {3: 1, 4: 2},
        compiler_params=pltpu.CompilerParams(vmem_limit_bytes=VMEM_LIMIT),
        cost_estimate=pl.CostEstimate(
            flops=12 * rows * model * width // COST_SCALE,
            transcendentals=0,
            bytes_accessed=rows * width,
        ),
        name="project_back",
    )(*operands)


def make_shards(tensor_size, group_size):
    square = tensor_size == 4

    def swap(value, bits):
        return lax.ppermute(value, "tensor", [(i, i ^ bits) for i in range(tensor_size)])

    def gather_far(own):
        return swap(own, 2) if square else lax.all_gather(own, "tensor")

    def gather_near(own, far):
        if not square:
            return [far[i] for i in range(tensor_size)]
        return [own, swap(own, 1), far, swap(far, 1)]

    def exchange_blocks(blocks):
        if not square:
            moved = lax.all_to_all(jnp.stack(blocks), "tensor", 0, 0)
            return [moved[i] for i in range(tensor_size)]
        return [blocks[0], swap(blocks[1], 1), swap(blocks[2], 2), swap(blocks[3], 3)]

    def sum_near(blocks, anchor):
        if not square:
            return (jnp.stack(blocks), None), anchor
        anchor, (near_own, near_far) = tie(anchor, (swap(blocks[1], 1), swap(blocks[3], 1)))
        far = (blocks[2].astype(f32) + near_far.astype(f32)).astype(blocks[2].dtype)
        return (blocks[0].astype(f32) + near_own.astype(f32), far), anchor

    def sum_far(stage, anchor):
        own, far = stage
        if not square:
            own = lax.psum_scatter(own, "tensor", scatter_dimension=0, tiled=False).astype(f32)
            anchor, own = tie(anchor, own)
            return own, anchor
        anchor, received = tie(anchor, swap(far, 2))
        return own + received.astype(f32), anchor

    steps = []
    for axis, size in (("tensor", tensor_size), ("dp", group_size)):
        bit = 1
        while bit < size:
            steps.append((axis, [(i, i ^ bit) for i in range(size)]))
            bit *= 2
    tensor_steps = [step for step in steps if step[0] == "tensor"]

    def sum_step(value, step, anchor):
        anchor, received = tie(anchor, lax.ppermute(value, step[0], step[1]))
        return value + received, anchor

    def in_order(stacked):
        if not square:
            return stacked
        own = lax.axis_index("tensor")
        return jnp.concatenate(
            [lax.dynamic_slice_in_dim(stacked, own ^ i, 1, axis=0) for i in range(tensor_size)], axis=0
        )

    def shards(
        patches,
        cotangent,
        empty_slots,
        dataset_id,
        dataset_weight,
        query_key_value_weight,
        qv_bias,
        output_projection_weight,
        out_bias,
        up_projection_weight,
        up_bias,
        down_projection_weight,
        down_bias,
        attn_gain,
        attn_shift,
        mlp_gain,
        mlp_shift,
    ):
        slot_count, own_rows, model = patches.shape
        width = query_key_value_weight.shape[2]
        group_slots = empty_slots.shape[0]
        slot_index = jnp.arange(group_slots * slot_count, dtype=jnp.int32) % slot_count
        filled = jnp.repeat(slot_count - empty_slots, slot_count)
        valid_all = (slot_index < filled).astype(f32)
        table_hits = dataset_id[:, None] == jnp.arange(dataset_weight.shape[0], dtype=jnp.int32)[None, :]
        numerator = jnp.sum(jnp.where(table_hits, dataset_weight[None, :], 0), axis=1).astype(f32)
        total_items = jnp.sum(valid_all)
        total_weight = jnp.sum(valid_all * numerator)
        multiplier_whole = valid_all * numerator * total_items / total_weight
        own_start = lax.axis_index("dp") * slot_count
        own_scale = lax.dynamic_slice_in_dim(multiplier_whole, own_start, slot_count)
        own_valid = lax.dynamic_slice_in_dim(valid_all, own_start, slot_count)
        row_scale = jnp.repeat(own_scale, own_rows)[:, None]
        row_valid = jnp.repeat(own_valid, own_rows)[:, None]
        all_rows = slot_count * own_rows

        inputs = patches.astype(f32)
        normed = norm_rows(inputs, attn_gain, attn_shift).astype(bf16)
        proj_bias = jnp.stack([qv_bias[0], jnp.zeros_like(qv_bias[0]), qv_bias[1]])[:, None, :]

        bias_row = up_bias[None, :]
        bias_far = gather_far(bias_row)
        normed = [normed[i] for i in range(slot_count)]
        normed_far = [gather_far(normed[0])]
        qkvs, attended, lses, attended_rows, normed_every = [], [], [], [], []
        for i in range(slot_count):
            if i + 1 < slot_count:
                if i == 0:
                    normed_far[0], normed[1] = tie(normed_far[0], normed[1])
                normed_far.append(gather_far(normed[i + 1]))
            every = jnp.concatenate(gather_near(normed[i], normed_far[i]), axis=0)
            if i == slot_count - 1:
                every, (up_far, out_far) = tie(every, (up_far, out_far))
            else:
                every = lax.optimization_barrier(every)
            qkv = (
                jnp.einsum("wz,gzh->gwh", every, query_key_value_weight, preferred_element_type=f32) + proj_bias
            ).astype(bf16)
            if i == 0:
                qkv, (out_own, up_own, ahead) = tie(
                    qkv, (output_projection_weight, up_projection_weight, normed[min(2, slot_count - 1)])
                )
                if slot_count > 2:
                    normed[2] = ahead
                out_far = gather_far(out_own)
                up_far = gather_far(up_own)
            if i == 0:
                qkv, bias_far = tie(qkv, bias_far)
            out, lse = attend(qkv)
            if i == 0:
                out, down_own = tie(out, down_projection_weight)
                down_far = gather_far(down_own)
            if i == slot_count - 1:
                out, down_far = tie(out, down_far)
            moved = exchange_blocks([out[b * own_rows : (b + 1) * own_rows] for b in range(tensor_size)])
            normed_every.append(every)
            qkvs.append(qkv)
            attended.append(out)
            lses.append(lse)
            attended_rows.append(jnp.concatenate(moved, axis=1))
        attended_rows = jnp.concatenate(attended_rows, axis=0)
        out_weight = jnp.concatenate(gather_near(out_own, out_far), axis=0)
        attended_rows, out_weight = tie(attended_rows, out_weight)
        bias_blocks = gather_near(bias_row, bias_far)
        up_blocks = gather_near(up_own, up_far)
        down_blocks = gather_near(down_own, down_far)

        flat_inputs = inputs.reshape(all_rows, model)
        residual = flat_inputs + nn(attended_rows, out_weight) + out_bias
        normed_mlp = norm_rows(residual, mlp_gain, mlp_shift).astype(bf16)
        cot_scaled = cotangent.astype(f32).reshape(all_rows, model) * row_scale
        cot_low = cot_scaled.astype(bf16)

        total = None
        hiddens, slopes = [], []
        for b in range(tensor_size):
            hidden, slope, total = mlp_forward(normed_mlp, up_blocks[b], bias_blocks[b], down_blocks[b], total)
            hiddens.append(hidden)
            slopes.append(slope)
        output = ((residual + total + down_bias) * row_valid).astype(bf16)

        down_grads = [tn(hidden, cot_low).astype(bf16) for hidden in hiddens]
        cot_back, down_grads = tie(cot_low, down_grads)

        total = None
        pre_grads, bias_grads = [], []
        for b in range(tensor_size):
            pre_grad, bias_grad, total = mlp_backward(cot_back, down_blocks[b], slopes[b], up_blocks[b], total)
            if b == 0:
                down_stage, total = sum_near(down_grads, total)
            pre_grads.append(pre_grad)
            bias_grads.append(bias_grad)
        down_sum, total = sum_far(down_stage, total)
        down_all = lax.psum(down_sum.astype(bf16), "dp")
        mlp_norm_back = jax.vjp(norm_rows, residual, mlp_gain, mlp_shift)[1]
        grad_resid_norm, grad_mlp_gain, grad_mlp_shift = mlp_norm_back(total)
        grad_residual = cot_scaled + grad_resid_norm
        grad_out_bias = jnp.sum(grad_residual, axis=0)
        grad_down_bias = jnp.sum(cot_scaled, axis=0)
        grad_res_low = grad_residual.astype(bf16)
        grad_attended_rows = nt(grad_res_low, out_weight).astype(bf16)
        grad_attended_rows, (pre_grads, grad_res_wide) = tie(grad_attended_rows, (pre_grads, grad_res_low))

        grad_attended = []
        for i in range(slot_count):
            rows = grad_attended_rows[i * own_rows : (i + 1) * own_rows]
            moved = exchange_blocks([rows[:, b * width : (b + 1) * width] for b in range(tensor_size)])
            grad_attended.append(jnp.concatenate(moved, axis=0))

        up_grads = [tn(normed_mlp, pre_grad).astype(bf16) for pre_grad in pre_grads]
        out_grads = tn(attended_rows, grad_res_wide).astype(bf16)
        out_grads = [out_grads[b * width : (b + 1) * width] for b in range(tensor_size)]

        up_stage, grad_attended[0] = sum_near(up_grads, grad_attended[0])
        out_stage, grad_attended[0] = sum_near(out_grads, grad_attended[0])
        small_rows = jnp.stack([grad_mlp_gain, grad_mlp_shift, grad_out_bias, grad_down_bias])
        bias_rows = in_order(jnp.concatenate(bias_grads, axis=0))
        smalls = jnp.concatenate([small_rows.reshape(-1), bias_rows.reshape(-1)]).reshape(-1, 128)
        waiting = list(steps)

        weights_wide = query_key_value_weight.astype(f32)
        sums = None
        grad_normed = []
        for i in range(slot_count):
            last = i == slot_count - 1
            dqkv = attend_back(qkvs[i], attended[i], grad_attended[i], lses[i])
            if i == 0:
                up_sum, dqkv = sum_far(up_stage, dqkv)
                out_sum, dqkv = sum_far(out_stage, dqkv)
                dqkv, down_all = tie(dqkv, down_all)
                up_sum, down_all = tie(up_sum, down_all)
                up_all = lax.psum((up_sum.astype(bf16), out_sum.astype(bf16)), "dp")
            if last:
                dqkv, up_all = tie(dqkv, up_all)
            if waiting:
                smalls, dqkv = sum_step(smalls, waiting.pop(0), dqkv)
            results = project_back(normed_every[i], dqkv, query_key_value_weight, sums, last)
            partial, sums = results[0], results[1:3]
            while waiting and (last or len(waiting) % 2):
                smalls, partial = sum_step(smalls, waiting.pop(0), partial)
            if last:
                qkv_all = lax.psum(results[3], "dp")
            grad_normed.append([partial[b * own_rows : (b + 1) * own_rows] for b in range(tensor_size)])
        for i in range(slot_count):
            anchor = inputs[i]
            stage, anchor = sum_near(grad_normed[i], anchor)
            grad_normed[i] = sum_far(stage, anchor)[0]
        grad_normed, qkv_all = tie(jnp.stack(grad_normed), qkv_all)
        attn_norm_back = jax.vjp(lambda v: norm_rows(v, attn_gain, attn_shift), inputs)[1]
        grad_inputs = (
            grad_residual.reshape(slot_count, own_rows, model) + attn_norm_back(grad_normed)[0]
        ).astype(bf16)
        weight_grad = qkv_all[:, :model].astype(f32)
        columns = qkv_all[:, model].astype(f32)
        raw = jnp.stack(
            [
                jnp.sum(weight_grad * weights_wide, axis=(0, 2)),
                jnp.sum(columns[:, None, :] * weights_wide, axis=(0, 2)),
            ]
        )
        for step in tensor_steps:
            raw = raw + lax.ppermute(raw, step[0], step[1])
        up_all, out_all = [value.astype(f32) for value in up_all]
        down_all = down_all.astype(f32)
        inverse = 1.0 / total_items
        smalls = smalls.reshape(-1) * inverse
        small_rows = smalls[: 4 * model].reshape(4, model)
        units = up_bias.shape[0]
        bias_all = lax.dynamic_slice_in_dim(smalls[4 * model :], lax.axis_index("tensor") * units, units)
        shift_all = raw[1] * inverse
        gain_all = (raw[0] * inverse - attn_shift * shift_all) / attn_gain
        columns = columns * inverse
        return (
            output.reshape(patches.shape),
            grad_inputs,
            weight_grad * inverse,
            jnp.stack([columns[0], columns[2]]),
            out_all * inverse,
            small_rows[2],
            up_all * inverse,
            bias_all,
            down_all * inverse,
            small_rows[3],
            gain_all,
            shift_all,
            small_rows[0],
            small_rows[1],
        )

    return shards


def solution(mesh):
    items = P("dp", "tensor", None)
    return jax.shard_map(
        make_shards(mesh.shape["tensor"], mesh.shape["dp"]),
        mesh=mesh,
        in_specs=(
            items,
            items,
            P(),
            P(),
            P(),
            P(None, None, "tensor"),
            P(None, "tensor"),
            P("tensor", None),
            P(),
            P(None, "tensor"),
            P("tensor"),
            P("tensor", None),
            P(),
            P(),
            P(),
            P(),
            P(),
        ),
        out_specs=(
            items,
            items,
            P(None, None, "tensor"),
            P(None, "tensor"),
            P("tensor", None),
            P(),
            P(None, "tensor"),
            P("tensor"),
            P("tensor", None),
            P(),
            P(),
            P(),
            P(),
            P(),
        ),
        check_vma=False,
    )
```

```python
import jax
import jax.numpy as jnp
from jax import lax
from jax.experimental import pallas as pl
from jax.experimental.pallas import tpu as pltpu
from jax.sharding import PartitionSpec as P

HD = 64
SCORE_SCALE = HD ** (-0.5)
LOG2E = 1.4426950408889634
SQRT_HALF = 0.7071067811865476
INV_SQRT_2PI = 0.3989422804014327
epsilon = 1e-05
f32 = jnp.float32
bf16 = jnp.bfloat16
VMEM_LIMIT = 60 << 20
COST_SCALE = 64


def nn(a, b):
    return lax.dot_general(a, b, (((1,), (0,)), ((), ())), preferred_element_type=f32)


def nt(a, b):
    return lax.dot_general(a, b, (((1,), (1,)), ((), ())), preferred_element_type=f32)


def tn(a, b):
    return lax.dot_general(a, b, (((0,), (0,)), ((), ())), preferred_element_type=f32)


def tie(first, second):
    return lax.optimization_barrier((first, second))


def largest_block(extent, limit):
    block = min(extent, limit)
    while extent % block:
        block //= 2
    return block


def norm_rows(source, norm_gain, norm_shift):
    row_mean = jnp.mean(source, axis=-1, keepdims=True)
    centred = source - row_mean
    spread = jnp.mean(centred * centred, axis=-1, keepdims=True)
    return centred * lax.rsqrt(spread + epsilon) * norm_gain + norm_shift


def attend(qkv):
    _, length, width = qkv.shape
    lanes = min(128, width)
    heads = lanes // HD
    qblock = largest_block(length, 1024)
    to_log2 = SCORE_SCALE * LOG2E

    def body(q_ref, k_ref, v_ref, out_ref, lse_ref):
        queries = q_ref[...]
        keys = k_ref[...]
        values_t = v_ref[...].T
        lane = lax.broadcasted_iota(jnp.int32, (1, lanes), 1)
        outs = []
        for h in range(heads):
            own = queries
            if heads > 1:
                own = jnp.where(lane // HD == h, queries, jnp.zeros_like(queries))
            scores = nt(keys, own)
            top = jnp.max(scores, axis=0, keepdims=True)
            exp_scores = jnp.exp2((scores - top) * to_log2)
            total = jnp.sum(exp_scores, axis=0, keepdims=True)
            outs.append(nn(values_t[h * HD : (h + 1) * HD, :], exp_scores.astype(bf16)) / total)
            lse_ref[h : h + 1, :] = top * to_log2 + jnp.log2(total)
        out_ref[...] = jnp.concatenate(outs, axis=0).T.astype(bf16)

    pairs = width // lanes
    return pl.pallas_call(
        body,
        grid=(pairs, length // qblock),
        in_specs=[
            pl.BlockSpec((None, qblock, lanes), lambda h, j: (0, j, h)),
            pl.BlockSpec((None, length, lanes), lambda h, j: (1, 0, h)),
            pl.BlockSpec((None, length, lanes), lambda h, j: (2, 0, h)),
        ],
        out_specs=[
            pl.BlockSpec((qblock, lanes), lambda h, j: (j, h)),
            pl.BlockSpec((None, heads, qblock), lambda h, j: (h, 0, j)),
        ],
        out_shape=[
            jax.ShapeDtypeStruct((length, width), bf16),
            jax.ShapeDtypeStruct((pairs, heads, length), f32),
        ],
        compiler_params=pltpu.CompilerParams(vmem_limit_bytes=VMEM_LIMIT),
        cost_estimate=pl.CostEstimate(
            flops=8 * length * length * width // COST_SCALE,
            transcendentals=0,
            bytes_accessed=length * width,
        ),
        name="attend",
    )(qkv, qkv, qkv)


def attend_back(qkv, attended, grad_attended, lse):
    _, length, width = qkv.shape
    lanes = min(128, width)
    heads = lanes // HD
    kblock = largest_block(length, 512)
    kblocks = length // kblock
    to_log2 = SCORE_SCALE * LOG2E

    def body(q_ref, k_ref, v_ref, out_ref, grad_ref, lse_ref, dqkv_ref, dq_acc, row_dot):
        kb = pl.program_id(1)
        queries = q_ref[...]
        grads = grad_ref[...]
        keys = k_ref[...]
        values = v_ref[...]
        keys_t = keys.T
        lane = lax.broadcasted_iota(jnp.int32, (1, lanes), 1)

        @pl.when(kb == 0)
        def _():
            product = out_ref[...].astype(f32) * grads.astype(f32)
            high = product.astype(bf16)
            rest = (product - high.astype(f32)).astype(bf16)
            pick = lax.broadcasted_iota(jnp.int32, (8, lanes), 0)
            mask = (lax.broadcasted_iota(jnp.int32, (8, lanes), 1) // HD == pick).astype(f32).astype(bf16)
            row_dot[...] = nt(mask, high) + nt(mask, rest)

        dk = None
        dv = None
        dqs = []
        for h in range(heads):
            own_q = queries
            own_g = grads
            if heads > 1:
                mine = lane // HD == h
                own_q = jnp.where(mine, queries, jnp.zeros_like(queries))
                own_g = jnp.where(mine, grads, jnp.zeros_like(grads))
            scores = nt(keys, own_q)
            weights = jnp.exp2(scores * to_log2 - lse_ref[h : h + 1, :])
            grad_weights = nt(values, own_g)
            grad_scores = (weights * (grad_weights - row_dot[h : h + 1, :])).astype(bf16)
            dv_h = nn(weights.astype(bf16), own_g)
            dk_h = nn(grad_scores, own_q)
            dv = dv_h if dv is None else dv + dv_h
            dk = dk_h if dk is None else dk + dk_h
            dqs.append(nn(keys_t[h * HD : (h + 1) * HD, :], grad_scores))
        rows = pl.ds(pl.multiple_of(kb * kblock, kblock), kblock)
        dqkv_ref[1, rows, :] = (dk * SCORE_SCALE).astype(bf16)
        dqkv_ref[2, rows, :] = dv.astype(bf16)
        dq = jnp.concatenate(dqs, axis=0)
        if kblocks == 1:
            dqkv_ref[0] = (dq * SCORE_SCALE).T.astype(bf16)
            return

        @pl.when(kb == 0)
        def _():
            dq_acc[...] = dq

        @pl.when((kb > 0) & (kb < kblocks - 1))
        def _():
            dq_acc[...] += dq

        @pl.when(kb == kblocks - 1)
        def _():
            dqkv_ref[0] = ((dq_acc[...] + dq) * SCORE_SCALE).T.astype(bf16)

    pairs = width // lanes
    return pl.pallas_call(
        body,
        grid=(pairs, kblocks),
        in_specs=[
            pl.BlockSpec((None, length, lanes), lambda h, kb: (0, 0, h)),
            pl.BlockSpec((None, kblock, lanes), lambda h, kb: (1, kb, h)),
            pl.BlockSpec((None, kblock, lanes), lambda h, kb: (2, kb, h)),
            pl.BlockSpec((length, lanes), lambda h, kb: (0, h)),
            pl.BlockSpec((length, lanes), lambda h, kb: (0, h)),
            pl.BlockSpec((None, heads, length), lambda h, kb: (h, 0, 0)),
        ],
        out_specs=pl.BlockSpec((3, length, lanes), lambda h, kb: (0, 0, h)),
        out_shape=jax.ShapeDtypeStruct((3, length, width), bf16),
        scratch_shapes=[pltpu.VMEM((lanes, length), f32), pltpu.VMEM((8, length), f32)],
        compiler_params=pltpu.CompilerParams(vmem_limit_bytes=VMEM_LIMIT),
        cost_estimate=pl.CostEstimate(
            flops=20 * length * length * width // COST_SCALE,
            transcendentals=0,
            bytes_accessed=length * width,
        ),
        name="attend_back",
    )(qkv, qkv, qkv, attended, grad_attended, lse)


def hint(flops, size):
    return pl.CostEstimate(flops=flops // COST_SCALE, transcendentals=0, bytes_accessed=size)


def params():
    return pltpu.CompilerParams(vmem_limit_bytes=VMEM_LIMIT)


def norm_item(patches, item, norm_gain, norm_shift):
    _, rows, model = patches.shape
    block = largest_block(rows, 256)

    def body(x_ref, gain_ref, shift_ref, out_ref):
        out_ref[...] = norm_rows(x_ref[...].astype(f32), gain_ref[...], shift_ref[...]).astype(bf16)

    vector = pl.BlockSpec((1, model), lambda i: (0, 0))
    return pl.pallas_call(
        body,
        grid=(rows // block,),
        in_specs=[pl.BlockSpec((None, block, model), lambda i: (item, i, 0)), vector, vector],
        out_specs=pl.BlockSpec((block, model), lambda i: (i, 0)),
        out_shape=jax.ShapeDtypeStruct((rows, model), bf16),
        compiler_params=params(),
        cost_estimate=hint(0, rows * model),
        name="norm_item",
    )(patches, norm_gain, norm_shift)


def out_project(patches, item, heads, weight, out_bias, norm_gain, norm_shift, before):
    slots, rows, model = patches.shape
    block = largest_block(rows, 256)
    steps = rows // block
    count = len(heads)

    def body(*refs):
        x_ref, weight_ref, bias_ref, gain_ref, shift_ref = refs[:5]
        head_refs = refs[5 : 5 + count]
        attended_ref, residual_ref, normed_ref = refs[-3:]
        attended = [ref[...] for ref in head_refs]
        attended = attended[0] if count == 1 else jnp.concatenate(attended, axis=1)
        attended_ref[...] = attended
        residual = x_ref[...].astype(f32) + nn(attended, weight_ref[...]) + bias_ref[...]
        residual_ref[...] = residual
        normed_ref[...] = norm_rows(residual, gain_ref[...], shift_ref[...]).astype(bf16)

    vector = pl.BlockSpec((1, model), lambda i: (0, 0))
    placed = pl.BlockSpec((block, model), lambda i: (item * steps + i, 0))
    operands = [patches, weight, out_bias, norm_gain, norm_shift, *heads]
    in_specs = [
        pl.BlockSpec((None, block, model), lambda i: (item, i, 0)),
        pl.BlockSpec((model, model), lambda i: (0, 0)),
        vector,
        vector,
        vector,
    ] + [pl.BlockSpec((block, head.shape[1]), lambda i: (i, 0)) for head in heads]
    aliases = {}
    if before is not None:
        aliases = {len(operands) + k: k for k in range(3)}
        operands += before
        in_specs += [pl.BlockSpec(memory_space=pl.ANY)] * 3
    return pl.pallas_call(
        body,
        grid=(steps,),
        in_specs=in_specs,
        out_specs=[placed] * 3,
        out_shape=[jax.ShapeDtypeStruct((slots * rows, model), t) for t in (bf16, f32, bf16)],
        input_output_aliases=aliases,
        compiler_params=params(),
        cost_estimate=hint(2 * rows * model * model, rows * model),
        name="out_project",
    )(*operands)


def residual_back(total, residual, cotangent, scale, item, weight, norm_gain, low_before, pieces):
    slots, rows, model = cotangent.shape
    block = largest_block(rows, 256)
    steps = rows // block
    piece = model // pieces

    def body(*refs):
        total_ref, residual_ref, cot_ref, scale_ref, weight_ref, gain_ref = refs[:6]
        outs = refs[6:] if low_before is None else refs[7:]
        grad_ref, low_ref, sum_ref = outs[:3]
        attended_refs = outs[3:]
        residual = residual_ref[...]
        centred = residual - jnp.mean(residual, axis=-1, keepdims=True)
        rate = lax.rsqrt(jnp.mean(centred * centred, axis=-1, keepdims=True) + epsilon)
        xhat = centred * rate
        grad_normed = total_ref[...]
        scaled = grad_normed * gain_ref[...]
        inner = jnp.mean(scaled, axis=-1, keepdims=True)
        outer = jnp.mean(scaled * xhat, axis=-1, keepdims=True)
        cot = cot_ref[...].astype(f32) * scale_ref[item]
        grad = cot + rate * (scaled - inner - xhat * outer)
        grad_ref[...] = grad
        low = grad.astype(bf16)
        low_ref[...] = low

        @pl.when(pl.program_id(0) == 0)
        def _():
            sum_ref[...] = jnp.zeros_like(sum_ref)

        for k, value in enumerate((grad_normed * xhat, grad_normed, grad, cot)):
            sum_ref[k : k + 1, :] += jnp.sum(value, axis=0, keepdims=True)
        attended = nt(low, weight_ref[...]).astype(bf16)
        for k in range(pieces):
            attended_refs[k][...] = attended[:, k * piece : (k + 1) * piece]

    row_spec = pl.BlockSpec((block, model), lambda i: (i, 0))
    placed = pl.BlockSpec((block, model), lambda i: (item * steps + i, 0))
    operands = [total, residual, cotangent, scale, weight, norm_gain]
    in_specs = [
        placed,
        placed,
        pl.BlockSpec((None, block, model), lambda i: (item, i, 0)),
        pl.BlockSpec(memory_space=pltpu.SMEM),
        pl.BlockSpec((model, model), lambda i: (0, 0)),
        pl.BlockSpec((1, model), lambda i: (0, 0)),
    ]
    aliases = {}
    if low_before is not None:
        aliases = {6: 1}
        operands.append(low_before)
        in_specs.append(pl.BlockSpec(memory_space=pl.ANY))
    return pl.pallas_call(
        body,
        grid=(steps,),
        in_specs=in_specs,
        out_specs=[row_spec, placed, pl.BlockSpec((8, model), lambda i: (0, 0))]
        + [pl.BlockSpec((block, piece), lambda i: (i, 0))] * pieces,
        out_shape=[
            jax.ShapeDtypeStruct((rows, model), f32),
            jax.ShapeDtypeStruct((slots * rows, model), bf16),
            jax.ShapeDtypeStruct((8, model), f32),
        ]
        + [jax.ShapeDtypeStruct((rows, piece), bf16)] * pieces,
        input_output_aliases=aliases,
        compiler_params=params(),
        cost_estimate=hint(2 * rows * model * model, rows * model),
        name="residual_back",
    )(*operands)


def input_back(terms, patches, item, grad_residual, norm_gain, before):
    slots, rows, model = patches.shape
    block = largest_block(rows, 256)
    count = len(terms)

    def body(*refs):
        x_ref, grad_ref, gain_ref = refs[:3]
        out_ref = refs[-1]
        grad_normed = refs[3][...].astype(f32)
        for k in range(1, count):
            grad_normed = grad_normed + refs[3 + k][...].astype(f32)
        source = x_ref[...].astype(f32)
        centred = source - jnp.mean(source, axis=-1, keepdims=True)
        rate = lax.rsqrt(jnp.mean(centred * centred, axis=-1, keepdims=True) + epsilon)
        xhat = centred * rate
        scaled = grad_normed * gain_ref[...]
        inner = jnp.mean(scaled, axis=-1, keepdims=True)
        outer = jnp.mean(scaled * xhat, axis=-1, keepdims=True)
        out_ref[...] = (grad_ref[...] + rate * (scaled - inner - xhat * outer)).astype(bf16)

    row_spec = pl.BlockSpec((block, model), lambda i: (i, 0))
    placed = pl.BlockSpec((None, block, model), lambda i: (item, i, 0))
    operands = [patches, grad_residual, norm_gain, *terms]
    in_specs = [placed, row_spec, pl.BlockSpec((1, model), lambda i: (0, 0))] + [row_spec] * count
    aliases = {}
    if before is not None:
        aliases = {len(operands): 0}
        operands.append(before)
        in_specs.append(pl.BlockSpec(memory_space=pl.ANY))
    return pl.pallas_call(
        body,
        grid=(rows // block,),
        in_specs=in_specs,
        out_specs=placed,
        out_shape=jax.ShapeDtypeStruct((slots, rows, model), bf16),
        input_output_aliases=aliases,
        compiler_params=params(),
        cost_estimate=hint(0, rows * model),
        name="input_back",
    )(*operands)


def mlp_forward(normed, cot, ups, biases, downs, total):
    rows, model = normed.shape
    count = len(ups)
    units = ups[0].shape[1]
    block = largest_block(rows, 512)
    steps = rows // block
    first = total is None

    def body(*refs):
        x_ref, cot_ref = refs[:2]
        up_refs, bias_refs, down_refs = (refs[2 + k * count : 2 + (k + 1) * count] for k in range(3))
        rest = refs[2 + 3 * count :]
        if not first:
            before_ref = rest[0]
            rest = rest[1:]
        slope_ref, sum_ref = rest[:2]
        grad_refs = rest[2 : 2 + count]
        hidden_ref, acc_ref = rest[2 + count :]
        step = pl.program_id(0)
        part = largest_block(units, 256)
        for k in range(count):
            for j in range(units // part):
                cols = slice(j * part, (j + 1) * part)
                wide = slice(k * units + j * part, k * units + (j + 1) * part)
                pre = nn(x_ref[...], up_refs[k][:, cols]) + bias_refs[k][:, cols]
                cdf = 0.5 + 0.5 * lax.erf(pre * SQRT_HALF)
                density = jnp.exp2(pre * pre * (-0.5 * LOG2E)) * INV_SQRT_2PI
                hidden_ref[:, wide] = (pre * cdf).astype(bf16)
                slope_ref[:, wide] = (cdf + pre * density).astype(bf16)
        out = None if first else before_ref[...]
        for k in range(count):
            hidden = hidden_ref[:, k * units : (k + 1) * units]
            product = nn(hidden, down_refs[k][...])
            out = product if out is None else out + product
            grad = tn(hidden, cot_ref[...])

            @pl.when(step == 0)
            def _():
                acc_ref[k] = grad

            @pl.when(step > 0)
            def _():
                acc_ref[k] += grad

        sum_ref[...] = out

        @pl.when(step == steps - 1)
        def _():
            for k in range(count):
                grad_refs[k][...] = acc_ref[k].astype(bf16)

    row_spec = pl.BlockSpec((block, model), lambda i: (i, 0))
    slope_spec = pl.BlockSpec((block, count * units), lambda i: (i, 0))
    up_spec = pl.BlockSpec((model, units), lambda i: (0, 0), pipeline_mode=pl.Buffered(1))
    down_spec = pl.BlockSpec((units, model), lambda i: (0, 0), pipeline_mode=pl.Buffered(1))
    grad_spec = pl.BlockSpec((units, model), lambda i: (0, 0))
    operands = [normed, cot, *ups, *biases, *downs]
    in_specs = [row_spec, row_spec] + [up_spec] * count
    in_specs += [pl.BlockSpec((1, units), lambda i: (0, 0))] * count + [down_spec] * count
    aliases = {}
    if not first:
        aliases = {len(operands): 1}
        operands.append(total)
        in_specs.append(row_spec)
    return pl.pallas_call(
        body,
        grid=(steps,),
        in_specs=in_specs,
        out_specs=[slope_spec, row_spec] + [grad_spec] * count,
        out_shape=[
            jax.ShapeDtypeStruct((rows, count * units), bf16),
            jax.ShapeDtypeStruct((rows, model), f32),
        ]
        + [jax.ShapeDtypeStruct((units, model), bf16)] * count,
        scratch_shapes=[pltpu.VMEM((block, count * units), bf16), pltpu.VMEM((count, units, model), f32)],
        input_output_aliases=aliases,
        compiler_params=params(),
        cost_estimate=hint(6 * rows * model * units * count, rows * units),
        name="mlp_forward",
    )(*operands)


def mlp_backward(cot, slope, ups, downs, before, index, calls):
    rows, model = cot.shape
    count = len(ups)
    units = ups[0].shape[1]
    block = largest_block(rows, 512)
    first = before is None

    def body(*refs):
        cot_ref, slope_ref = refs[:2]
        up_refs, down_refs = refs[2 : 2 + count], refs[2 + count : 2 + 2 * count]
        grad_ref, sum_ref, bias_ref = refs[-3:]

        @pl.when(pl.program_id(0) == 0)
        def _():
            bias_ref[...] = jnp.zeros_like(bias_ref)

        out = None if first else refs[3 + 2 * count][...]
        part = largest_block(units, 512)
        for k in range(count):
            for j in range(units // part):
                rows_of = slice(j * part, (j + 1) * part)
                wide = slice(k * units + j * part, k * units + (j + 1) * part)
                low = (nt(cot_ref[...], down_refs[k][rows_of, :]) * slope_ref[:, wide].astype(f32)).astype(bf16)
                grad_ref[:, wide] = low
                bias_ref[:, wide] += jnp.sum(low.astype(f32), axis=0, keepdims=True)
            product = nt(grad_ref[:, k * units : (k + 1) * units], up_refs[k][...])
            out = product if out is None else out + product
        sum_ref[...] = out

    row_spec = pl.BlockSpec((block, model), lambda i: (i, 0))
    slope_spec = pl.BlockSpec((block, count * units), lambda i: (i, 0))
    up_spec = pl.BlockSpec((model, units), lambda i: (0, 0), pipeline_mode=pl.Buffered(1))
    down_spec = pl.BlockSpec((units, model), lambda i: (0, 0), pipeline_mode=pl.Buffered(1))
    operands = [cot, slope, *ups, *downs]
    in_specs = [row_spec, slope_spec] + [up_spec] * count + [down_spec] * count
    aliases = {}
    if not first:
        aliases = {len(operands): 0, len(operands) + 1: 1}
        operands += before
        in_specs += [pl.BlockSpec(memory_space=pl.ANY), row_spec]
    return pl.pallas_call(
        body,
        grid=(rows // block,),
        in_specs=in_specs,
        out_specs=[
            pl.BlockSpec((block, count * units), lambda i: (i, index)),
            row_spec,
            pl.BlockSpec((1, count * units), lambda i: (0, 0)),
        ],
        out_shape=[
            jax.ShapeDtypeStruct((rows, calls * count * units), bf16),
            jax.ShapeDtypeStruct((rows, model), f32),
            jax.ShapeDtypeStruct((1, count * units), f32),
        ],
        input_output_aliases=aliases,
        compiler_params=params(),
        cost_estimate=hint(4 * rows * model * units * count, rows * units),
        name="mlp_backward",
    )(*operands)


def weight_back(normed, pre_grad, attended, grad_low, pieces):
    rows, model = normed.shape
    every = pre_grad.shape[1]
    units = every // pieces
    piece = model // pieces
    block = largest_block(rows, 512)
    steps = rows // block

    def body(x_ref, pre_ref, attended_ref, grad_ref, *refs):
        up_refs, out_refs = refs[:pieces], refs[pieces : 2 * pieces]
        up_acc, out_acc = refs[2 * pieces :]
        step = pl.program_id(0)

        @pl.when(step == 0)
        def _():
            up_acc[...] = jnp.zeros_like(up_acc)
            out_acc[...] = jnp.zeros_like(out_acc)

        part = largest_block(every, 512)
        for j in range(every // part):
            cols = slice(j * part, (j + 1) * part)
            up_acc[:, cols] += tn(x_ref[...], pre_ref[:, cols])
        part = largest_block(model, 512)
        for j in range(model // part):
            cols = slice(j * part, (j + 1) * part)
            out_acc[:, cols] += tn(attended_ref[...], grad_ref[:, cols])

        @pl.when(step == steps - 1)
        def _():
            for k in range(pieces):
                up_refs[k][...] = up_acc[:, k * units : (k + 1) * units].astype(bf16)
                out_refs[k][...] = out_acc[k * piece : (k + 1) * piece, :].astype(bf16)

    row_spec = pl.BlockSpec((block, model), lambda i: (i, 0))
    return pl.pallas_call(
        body,
        grid=(steps,),
        in_specs=[row_spec, pl.BlockSpec((block, every), lambda i: (i, 0)), row_spec, row_spec],
        out_specs=[pl.BlockSpec((model, units), lambda i: (0, 0))] * pieces
        + [pl.BlockSpec((piece, model), lambda i: (0, 0))] * pieces,
        out_shape=[jax.ShapeDtypeStruct((model, units), bf16)] * pieces
        + [jax.ShapeDtypeStruct((piece, model), bf16)] * pieces,
        scratch_shapes=[pltpu.VMEM((model, every), f32), pltpu.VMEM((model, model), f32)],
        compiler_params=params(),
        cost_estimate=hint(2 * rows * model * (every + model), rows * model),
        name="weight_back",
    )(normed, pre_grad, attended, grad_low)


def project_back(normed, dqkv, weight, before, last, pieces):
    rows, model = normed.shape
    width = weight.shape[2]
    block = rows // pieces
    steps = pieces
    first = before is None

    def kernel(*refs):
        normed_ref, dqkv_ref, weight_ref = refs[:3]
        rest = refs[3:]
        if not first:
            wgrad_before, column_before = rest[:2]
            rest = rest[2:]
        row_refs, rest = rest[:pieces], rest[pieces:]
        wgrad_ref, column_ref = rest[:2]
        step = pl.program_id(0)

        @pl.when(step == 0)
        def _():
            if first:
                wgrad_ref[...] = jnp.zeros_like(wgrad_ref)
                column_ref[...] = jnp.zeros_like(column_ref)
            else:
                wgrad_ref[...] = wgrad_before[...]
                column_ref[...] = column_before[...]

        row_grad = nt(dqkv_ref[0], weight_ref[0])
        for c in range(1, 3):
            row_grad = row_grad + nt(dqkv_ref[c], weight_ref[c])
        row_grad = row_grad.astype(bf16)
        for k in range(pieces):

            @pl.when(step == k)
            def _():
                row_refs[k][...] = row_grad

        for c in range(3):
            wgrad_ref[c] += tn(normed_ref[...], dqkv_ref[c])
            column_ref[c : c + 1, :] += jnp.sum(dqkv_ref[c].astype(f32), axis=0, keepdims=True)
        if last:
            low_ref = rest[2]

            @pl.when(step == steps - 1)
            def _():
                low_ref[:, :model, :] = wgrad_ref[...].astype(bf16)
                for c in range(3):
                    row = jnp.broadcast_to(column_ref[c : c + 1, :], (16, width))
                    low_ref[c, model:, :] = row.astype(bf16)

    whole = pl.BlockSpec((3, model, width), lambda i: (0, 0, 0))
    columns = pl.BlockSpec((8, width), lambda i: (0, 0))
    row_spec = pl.BlockSpec((block, model), lambda i: (i, 0))
    operands = [normed, dqkv, weight]
    in_specs = [row_spec, pl.BlockSpec((3, block, width), lambda i: (0, i, 0)), whole]
    if not first:
        operands += list(before)
        in_specs += [whole, columns]
    out_specs = [pl.BlockSpec((block, model), lambda i: (0, 0))] * pieces + [whole, columns]
    out_shape = [jax.ShapeDtypeStruct((block, model), bf16)] * pieces + [
        jax.ShapeDtypeStruct((3, model, width), f32),
        jax.ShapeDtypeStruct((8, width), f32),
    ]
    if last:
        out_specs.append(pl.BlockSpec((3, model + 16, width), lambda i: (0, 0, 0)))
        out_shape.append(jax.ShapeDtypeStruct((3, model + 16, width), bf16))
    return pl.pallas_call(
        kernel,
        grid=(steps,),
        in_specs=in_specs,
        out_specs=out_specs,
        out_shape=out_shape,
        input_output_aliases={} if first else {3: pieces, 4: pieces + 1},
        compiler_params=pltpu.CompilerParams(vmem_limit_bytes=VMEM_LIMIT),
        cost_estimate=pl.CostEstimate(
            flops=12 * rows * model * width // COST_SCALE,
            transcendentals=0,
            bytes_accessed=rows * width,
        ),
        name="project_back",
    )(*operands)


def make_shards(tensor_size, group_size):
    square = tensor_size == 4

    def swap(value, bits):
        return lax.ppermute(value, "tensor", [(i, i ^ bits) for i in range(tensor_size)])

    def gather_far(own):
        return swap(own, 2) if square else lax.all_gather(own, "tensor")

    def gather_near(own, far):
        if not square:
            return [far[i] for i in range(tensor_size)]
        return [own, swap(own, 1), far, swap(far, 1)]

    def exchange_blocks(blocks):
        if not square:
            moved = lax.all_to_all(jnp.stack(blocks), "tensor", 0, 0)
            return [moved[i] for i in range(tensor_size)]
        return [blocks[0], swap(blocks[1], 1), swap(blocks[2], 2), swap(blocks[3], 3)]

    def sum_near(blocks, anchor):
        if not square:
            return (jnp.stack(blocks),), anchor
        anchor, (near_own, near_far) = tie(anchor, (swap(blocks[1], 1), swap(blocks[3], 1)))
        far = (blocks[2].astype(f32) + near_far.astype(f32)).astype(blocks[2].dtype)
        return (blocks[0], near_own, far), anchor

    def sums_near(lists, anchor):
        if not square:
            return [sum_near(blocks, anchor)[0] for blocks in lists], anchor
        moved = [(swap(blocks[1], 1), swap(blocks[3], 1)) for blocks in lists]
        anchor, moved = tie(anchor, moved)
        return [
            (blocks[0], own, (blocks[2].astype(f32) + far.astype(f32)).astype(blocks[2].dtype))
            for blocks, (own, far) in zip(lists, moved, strict=True)
        ], anchor

    def terms_far(stage, anchor):
        if not square:
            own = lax.psum_scatter(stage[0], "tensor", scatter_dimension=0, tiled=False)
            anchor, own = tie(anchor, own)
            return [own], anchor
        own, near, far = stage
        anchor, received = tie(anchor, swap(far, 2))
        return [own, near, received], anchor

    def sum_far(stage, anchor):
        terms, anchor = terms_far(stage, anchor)
        total = terms[0].astype(f32)
        for term in terms[1:]:
            total = total + term.astype(f32)
        return total.astype(terms[0].dtype), anchor

    steps = []
    for axis, size in (("tensor", tensor_size), ("dp", group_size)):
        bit = 1
        while bit < size:
            steps.append((axis, [(i, i ^ bit) for i in range(size)]))
            bit *= 2
    tensor_steps = [step for step in steps if step[0] == "tensor"]

    def sum_step(value, step, anchor):
        anchor, received = tie(anchor, lax.ppermute(value, step[0], step[1]))
        return value + received, anchor

    def ring_plan():
        bits = [1 << k for k in range(group_size.bit_length() - 1)]
        return [(bit, True) for bit in bits] + [(bit, False) for bit in reversed(bits)]

    def ring_step(value, step, anchor):
        bit, reducing = step
        side = (lax.axis_index("dp") // bit) % 2
        pairs = [(i, i ^ bit) for i in range(group_size)]
        if reducing:
            half = value.shape[0] // 2
            sent = lax.dynamic_slice_in_dim(value, (1 - side) * half, half, axis=0)
            anchor, received = tie(anchor, lax.ppermute(sent, "dp", pairs))
            kept = lax.dynamic_slice_in_dim(value, side * half, half, axis=0)
            return (kept.astype(f32) + received.astype(f32)).astype(value.dtype), anchor
        anchor, received = tie(anchor, lax.ppermute(value, "dp", pairs))
        return in_halves(value, received, side), anchor

    def in_halves(own, other, side):
        rows = own.shape[0]
        whole = jnp.zeros((2 * rows,) + own.shape[1:], own.dtype)
        whole = lax.dynamic_update_slice_in_dim(whole, own, side * rows, axis=0)
        return lax.dynamic_update_slice_in_dim(whole, other, (1 - side) * rows, axis=0)

    def fetch_half(own):
        half = own.shape[0] // 2
        side = lax.axis_index("dp") % 2
        return swap(lax.dynamic_slice_in_dim(own, side * half, half, axis=0), 2)

    def fetch_rest(half):
        return lax.ppermute(half, "dp", [(i, i ^ 1) for i in range(group_size)])

    def in_order(stacked):
        if not square:
            return stacked
        own = lax.axis_index("tensor")
        return jnp.concatenate(
            [lax.dynamic_slice_in_dim(stacked, own ^ i, 1, axis=0) for i in range(tensor_size)], axis=0
        )

    def shards(
        patches,
        cotangent,
        empty_slots,
        dataset_id,
        dataset_weight,
        query_key_value_weight,
        qv_bias,
        output_projection_weight,
        out_bias,
        up_projection_weight,
        up_bias,
        down_projection_weight,
        down_bias,
        attn_gain,
        attn_shift,
        mlp_gain,
        mlp_shift,
    ):
        slot_count, own_rows, model = patches.shape
        width = query_key_value_weight.shape[2]
        group_slots = empty_slots.shape[0]
        slot_index = jnp.arange(group_slots * slot_count, dtype=jnp.int32) % slot_count
        filled = jnp.repeat(slot_count - empty_slots, slot_count)
        valid_all = (slot_index < filled).astype(f32)
        table_hits = dataset_id[:, None] == jnp.arange(dataset_weight.shape[0], dtype=jnp.int32)[None, :]
        numerator = jnp.sum(jnp.where(table_hits, dataset_weight[None, :], 0), axis=1).astype(f32)
        total_items = jnp.sum(valid_all)
        total_weight = jnp.sum(valid_all * numerator)
        multiplier_whole = valid_all * numerator * total_items / total_weight
        own_start = lax.axis_index("dp") * slot_count
        own_scale = lax.dynamic_slice_in_dim(multiplier_whole, own_start, slot_count)
        own_valid = lax.dynamic_slice_in_dim(valid_all, own_start, slot_count)
        all_rows = slot_count * own_rows
        row_scale = jnp.repeat(own_scale, own_rows)[:, None]
        row_valid = jnp.repeat(own_valid, own_rows)[:, None]
        gain_row, shift_row, mlp_gain_row, mlp_shift_row, out_bias_row = (
            value[None, :] for value in (attn_gain, attn_shift, mlp_gain, mlp_shift, out_bias)
        )
        proj_bias = jnp.stack([qv_bias[0], jnp.zeros_like(qv_bias[0]), qv_bias[1]])[:, None, :]
        bias_row = up_bias[None, :]

        dp_side = lax.axis_index("dp") % 2
        fetch = fetch_half if square else gather_far
        weights_near = ()
        if square:
            weights_near = tuple(
                swap(value, 1) for value in (output_projection_weight, up_projection_weight, down_projection_weight)
            )

        normed = [norm_item(patches, 0, gain_row, shift_row)]
        normed_far = [gather_far(normed[0])]
        bias_far = gather_far(bias_row)
        qkvs, attended, lses, heads_own, normed_every = [], [], [], [], []
        for i in range(slot_count):
            if i + 1 < slot_count:
                if i == 0:
                    normed += [norm_item(patches, k, gain_row, shift_row) for k in range(1, slot_count)]
                    normed_far[0], normed[1] = tie(normed_far[0], normed[1])
                normed_far.append(gather_far(normed[i + 1]))
            every = jnp.concatenate(gather_near(normed[i], normed_far[i]), axis=0)
            every = lax.optimization_barrier(every)
            qkv = (
                jnp.einsum("wz,gzh->gwh", every, query_key_value_weight, preferred_element_type=f32) + proj_bias
            ).astype(bf16)
            if i == 0:
                qkv, (up_own, weights_near, bias_far) = tie(qkv, (up_projection_weight, weights_near, bias_far))
                up_far = fetch(up_own)
            out, lse = attend(qkv)
            if i + 1 < slot_count:
                out, (normed[i + 1], normed_far[i + 1]) = tie(out, (normed[i + 1], normed_far[i + 1]))
            if i == 0:
                out, (down_own, out_own, up_far) = tie(out, (down_projection_weight, output_projection_weight, up_far))
                down_far = fetch(down_own)
                out_far = gather_far(out_own)
                if square:
                    up_rest = fetch_rest(up_far)
            if i == min(1, slot_count - 1) and square:
                out, (down_far, up_rest) = tie(out, (down_far, up_rest))
                up_far = in_halves(up_far, up_rest, dp_side)
                up_diag = swap(up_far, 1)
                down_rest = fetch_rest(down_far)
            if i == slot_count - 1:
                out, out_far = tie(out, out_far)
                if square:
                    out, (down_rest, up_diag) = tie(out, (down_rest, up_diag))
                    down_far = in_halves(down_far, down_rest, dp_side)
                    down_diag = swap(down_far, 1)
            heads_own.append(exchange_blocks([out[b * own_rows : (b + 1) * own_rows] for b in range(tensor_size)]))
            normed_every.append(every)
            qkvs.append(qkv)
            attended.append(out)
            lses.append(lse)
        if square:
            out_weight = jnp.concatenate([out_own, weights_near[0], out_far, swap(out_far, 1)], axis=0)
        else:
            out_weight = jnp.concatenate(gather_near(out_own, out_far), axis=0)
        rows_done = None
        for i in range(slot_count):
            heads = heads_own[i] if square else [jnp.concatenate(heads_own[i], axis=1)]
            rows_done = out_project(
                patches, i, heads, out_weight, out_bias_row, mlp_gain_row, mlp_shift_row, rows_done
            )
        attended_rows, residual, normed_mlp = rows_done
        cot_low = (cotangent.astype(f32).reshape(all_rows, model) * row_scale).astype(bf16)

        bias_blocks = gather_near(bias_row, bias_far)
        if square:
            up_blocks = [up_own, weights_near[1], up_far, up_diag]
            down_blocks = [down_own, weights_near[2], down_far, down_diag]
        else:
            up_blocks = gather_near(up_own, up_far)
            down_blocks = gather_near(down_own, down_far)
        calls = tensor_size // 2
        total = None
        slopes, down_grads = [], []
        for c in range(calls):
            pair = slice(2 * c, 2 * c + 2)
            slope, total, *grads = mlp_forward(
                normed_mlp, cot_low, up_blocks[pair], bias_blocks[pair], down_blocks[pair], total
            )
            slopes.append(slope)
            down_grads += grads
        output = ((residual + total + down_bias) * row_valid).astype(bf16)

        cot_back, down_grads = tie(cot_low, down_grads)
        before = None
        bias_grads = []
        for c in range(calls):
            pair = slice(2 * c, 2 * c + 2)
            *before, bias_grad = mlp_backward(
                cot_back, slopes[c], up_blocks[pair], down_blocks[pair], before, c, calls
            )
            bias_grads.append(bias_grad)
            if c == 0:
                down_stage, before = sum_near(down_grads, before)
        down_sum, before = sum_far(down_stage, before)
        ring = ring_plan()
        pre_grad, total = before

        grad_low = None
        grad_residuals, grad_attended, sums = [], [], []
        for i in range(slot_count):
            grad_residual, grad_low, item_sums, *pieces = residual_back(
                total, residual, cotangent, own_scale, i, out_weight, mlp_gain_row, grad_low, tensor_size
            )
            grad_residuals.append(grad_residual)
            sums.append(item_sums[:4])
            grad_attended.append(exchange_blocks(pieces))
        weight_grads = weight_back(normed_mlp, pre_grad, attended_rows, grad_low, tensor_size)
        weight_grads, grad_attended[0] = tie(weight_grads, grad_attended[0])
        down_sum, weight_grads = ring_step(down_sum, ring.pop(0), weight_grads)
        up_grads, out_grads = weight_grads[:tensor_size], weight_grads[tensor_size:]

        (up_stage, out_stage), grad_attended[0] = sums_near([up_grads, out_grads], grad_attended[0])
        small_rows = sum(sums[1:], sums[0])
        bias_rows = in_order(jnp.concatenate(bias_grads, axis=1).reshape(tensor_size, -1))
        smalls = jnp.concatenate([small_rows.reshape(-1), bias_rows.reshape(-1)]).reshape(-1, 128)
        waiting = list(steps)

        weights_wide = query_key_value_weight.astype(f32)
        sums = None
        grad_normed = []
        for i in range(slot_count):
            last = i == slot_count - 1
            dqkv = attend_back(qkvs[i], attended[i], jnp.concatenate(grad_attended[i], axis=0), lses[i])
            if not last:
                dqkv, grad_attended[i + 1] = tie(dqkv, grad_attended[i + 1])
            if i >= 2:
                grad_normed[i - 2], dqkv = terms_far(grad_normed[i - 2], dqkv)
            if i >= 1:
                grad_normed[i - 1], dqkv = sum_near(grad_normed[i - 1], dqkv)
            if i == 0:
                up_sum, dqkv = sum_far(up_stage, dqkv)
                out_sum, dqkv = sum_far(out_stage, dqkv)
                up_all = lax.psum((up_sum, out_sum), "dp")
            if last:
                dqkv, up_all = tie(dqkv, up_all)
            if waiting:
                smalls, dqkv = sum_step(smalls, waiting.pop(0), dqkv)
            if ring:
                down_sum, dqkv = ring_step(down_sum, ring.pop(0), dqkv)
            results = project_back(normed_every[i], dqkv, query_key_value_weight, sums, last, tensor_size)
            partial, sums = results[:tensor_size], results[tensor_size : tensor_size + 2]
            while ring and (last or len(ring) % 2 == 0):
                down_sum, partial = ring_step(down_sum, ring.pop(0), partial)
            while waiting and (last or len(waiting) % 2):
                smalls, partial = sum_step(smalls, waiting.pop(0), partial)
            if last:
                qkv_all = lax.psum(results[-1], "dp")
            grad_normed.append(partial)
        grad_inputs = None
        for i in range(slot_count):
            grad_residual = grad_residuals[i]
            if i == slot_count - 1:
                grad_normed[i], grad_residual = sum_near(grad_normed[i], grad_residual)
            terms = grad_normed[i]
            if i >= slot_count - 2:
                terms, grad_residual = terms_far(terms, grad_residual)
            if i == slot_count - 1:
                grad_residual, qkv_all = tie(grad_residual, qkv_all)
            grad_inputs = input_back(terms, patches, i, grad_residual, gain_row, grad_inputs)
        weight_grad = qkv_all[:, :model].astype(f32)
        columns = qkv_all[:, model].astype(f32)
        raw = jnp.stack(
            [
                jnp.sum(weight_grad * weights_wide, axis=(0, 2)),
                jnp.sum(columns[:, None, :] * weights_wide, axis=(0, 2)),
            ]
        )
        for step in tensor_steps:
            raw = raw + lax.ppermute(raw, step[0], step[1])
        up_all, out_all = [value.astype(f32) for value in up_all]
        down_all = down_sum.astype(f32)
        inverse = 1.0 / total_items
        smalls = smalls.reshape(-1) * inverse
        small_rows = smalls[: 4 * model].reshape(4, model)
        units = up_bias.shape[0]
        bias_all = lax.dynamic_slice_in_dim(smalls[4 * model :], lax.axis_index("tensor") * units, units)
        shift_all = raw[1] * inverse
        gain_all = (raw[0] * inverse - attn_shift * shift_all) / attn_gain
        columns = columns * inverse
        return (
            output.reshape(patches.shape),
            grad_inputs,
            weight_grad * inverse,
            jnp.stack([columns[0], columns[2]]),
            out_all * inverse,
            small_rows[2],
            up_all * inverse,
            bias_all,
            down_all * inverse,
            small_rows[3],
            gain_all,
            shift_all,
            small_rows[0],
            small_rows[1],
        )

    return shards


def solution(mesh):
    items = P("dp", "tensor", None)
    return jax.shard_map(
        make_shards(mesh.shape["tensor"], mesh.shape["dp"]),
        mesh=mesh,
        in_specs=(
            items,
            items,
            P(),
            P(),
            P(),
            P(None, None, "tensor"),
            P(None, "tensor"),
            P("tensor", None),
            P(),
            P(None, "tensor"),
            P("tensor"),
            P("tensor", None),
            P(),
            P(),
            P(),
            P(),
            P(),
        ),
        out_specs=(
            items,
            items,
            P(None, None, "tensor"),
            P(None, "tensor"),
            P("tensor", None),
            P(),
            P(None, "tensor"),
            P("tensor"),
            P("tensor", None),
            P(),
            P(),
            P(),
            P(),
            P(),
        ),
        check_vma=False,
    )
```

```python
import jax
import jax.numpy as jnp
from jax import lax
from jax.experimental import pallas as pl
from jax.experimental.pallas import tpu as pltpu
from jax.sharding import PartitionSpec as P

HD = 64
SCORE_SCALE = HD ** (-0.5)
LOG2E = 1.4426950408889634
SQRT_HALF = 0.7071067811865476
INV_SQRT_2PI = 0.3989422804014327
epsilon = 1e-05
f32 = jnp.float32
bf16 = jnp.bfloat16
VMEM_LIMIT = 60 << 20
COST_SCALE = 64


def nn(a, b):
    return lax.dot_general(a, b, (((1,), (0,)), ((), ())), preferred_element_type=f32)


def nt(a, b):
    return lax.dot_general(a, b, (((1,), (1,)), ((), ())), preferred_element_type=f32)


def tn(a, b):
    return lax.dot_general(a, b, (((0,), (0,)), ((), ())), preferred_element_type=f32)


def tie(first, second):
    return lax.optimization_barrier((first, second))


def largest_block(extent, limit):
    block = min(extent, limit)
    while extent % block:
        block //= 2
    return block


def norm_rows(source, norm_gain, norm_shift):
    row_mean = jnp.mean(source, axis=-1, keepdims=True)
    centred = source - row_mean
    spread = jnp.mean(centred * centred, axis=-1, keepdims=True)
    return centred * lax.rsqrt(spread + epsilon) * norm_gain + norm_shift


def attend(qkv):
    _, length, width = qkv.shape
    lanes = min(128, width)
    heads = lanes // HD
    qblock = largest_block(length, 1024)
    to_log2 = SCORE_SCALE * LOG2E

    def body(q_ref, k_ref, v_ref, out_ref, lse_ref):
        queries = q_ref[...]
        keys = k_ref[...]
        values_t = v_ref[...].T
        lane = lax.broadcasted_iota(jnp.int32, (1, lanes), 1)
        outs = []
        for h in range(heads):
            own = queries
            if heads > 1:
                own = jnp.where(lane // HD == h, queries, jnp.zeros_like(queries))
            scores = nt(keys, own)
            top = jnp.max(scores, axis=0, keepdims=True)
            exp_scores = jnp.exp2((scores - top) * to_log2)
            total = jnp.sum(exp_scores, axis=0, keepdims=True)
            outs.append(nn(values_t[h * HD : (h + 1) * HD, :], exp_scores.astype(bf16)) / total)
            lse_ref[h : h + 1, :] = top * to_log2 + jnp.log2(total)
        out_ref[...] = jnp.concatenate(outs, axis=0).T.astype(bf16)

    pairs = width // lanes
    return pl.pallas_call(
        body,
        grid=(pairs, length // qblock),
        in_specs=[
            pl.BlockSpec((None, qblock, lanes), lambda h, j: (0, j, h)),
            pl.BlockSpec((None, length, lanes), lambda h, j: (1, 0, h)),
            pl.BlockSpec((None, length, lanes), lambda h, j: (2, 0, h)),
        ],
        out_specs=[
            pl.BlockSpec((qblock, lanes), lambda h, j: (j, h)),
            pl.BlockSpec((None, heads, qblock), lambda h, j: (h, 0, j)),
        ],
        out_shape=[
            jax.ShapeDtypeStruct((length, width), bf16),
            jax.ShapeDtypeStruct((pairs, heads, length), f32),
        ],
        compiler_params=pltpu.CompilerParams(vmem_limit_bytes=VMEM_LIMIT),
        cost_estimate=pl.CostEstimate(
            flops=8 * length * length * width // COST_SCALE,
            transcendentals=0,
            bytes_accessed=length * width,
        ),
        name="attend",
    )(qkv, qkv, qkv)


def attend_back(qkv, attended, grad_attended, lse):
    _, length, width = qkv.shape
    lanes = min(128, width)
    heads = lanes // HD
    kblock = largest_block(length, 512)
    kblocks = length // kblock
    to_log2 = SCORE_SCALE * LOG2E

    def body(q_ref, k_ref, v_ref, out_ref, grad_ref, lse_ref, dqkv_ref, dq_acc, row_dot):
        kb = pl.program_id(1)
        queries = q_ref[...]
        grads = grad_ref[...]
        keys = k_ref[...]
        values = v_ref[...]
        keys_t = keys.T
        lane = lax.broadcasted_iota(jnp.int32, (1, lanes), 1)

        @pl.when(kb == 0)
        def _():
            product = out_ref[...].astype(f32) * grads.astype(f32)
            high = product.astype(bf16)
            rest = (product - high.astype(f32)).astype(bf16)
            pick = lax.broadcasted_iota(jnp.int32, (8, lanes), 0)
            mask = (lax.broadcasted_iota(jnp.int32, (8, lanes), 1) // HD == pick).astype(f32).astype(bf16)
            row_dot[...] = nt(mask, high) + nt(mask, rest)

        dk = None
        dv = None
        dqs = []
        for h in range(heads):
            own_q = queries
            own_g = grads
            if heads > 1:
                mine = lane // HD == h
                own_q = jnp.where(mine, queries, jnp.zeros_like(queries))
                own_g = jnp.where(mine, grads, jnp.zeros_like(grads))
            scores = nt(keys, own_q)
            weights = jnp.exp2(scores * to_log2 - lse_ref[h : h + 1, :])
            grad_weights = nt(values, own_g)
            grad_scores = (weights * (grad_weights - row_dot[h : h + 1, :])).astype(bf16)
            dv_h = nn(weights.astype(bf16), own_g)
            dk_h = nn(grad_scores, own_q)
            dv = dv_h if dv is None else dv + dv_h
            dk = dk_h if dk is None else dk + dk_h
            dqs.append(nn(keys_t[h * HD : (h + 1) * HD, :], grad_scores))
        rows = pl.ds(pl.multiple_of(kb * kblock, kblock), kblock)
        dqkv_ref[1, rows, :] = (dk * SCORE_SCALE).astype(bf16)
        dqkv_ref[2, rows, :] = dv.astype(bf16)
        dq = jnp.concatenate(dqs, axis=0)
        if kblocks == 1:
            dqkv_ref[0] = (dq * SCORE_SCALE).T.astype(bf16)
            return

        @pl.when(kb == 0)
        def _():
            dq_acc[...] = dq

        @pl.when((kb > 0) & (kb < kblocks - 1))
        def _():
            dq_acc[...] += dq

        @pl.when(kb == kblocks - 1)
        def _():
            dqkv_ref[0] = ((dq_acc[...] + dq) * SCORE_SCALE).T.astype(bf16)

    pairs = width // lanes
    return pl.pallas_call(
        body,
        grid=(pairs, kblocks),
        in_specs=[
            pl.BlockSpec((None, length, lanes), lambda h, kb: (0, 0, h)),
            pl.BlockSpec((None, kblock, lanes), lambda h, kb: (1, kb, h)),
            pl.BlockSpec((None, kblock, lanes), lambda h, kb: (2, kb, h)),
            pl.BlockSpec((length, lanes), lambda h, kb: (0, h)),
            pl.BlockSpec((length, lanes), lambda h, kb: (0, h)),
            pl.BlockSpec((None, heads, length), lambda h, kb: (h, 0, 0)),
        ],
        out_specs=pl.BlockSpec((3, length, lanes), lambda h, kb: (0, 0, h)),
        out_shape=jax.ShapeDtypeStruct((3, length, width), bf16),
        scratch_shapes=[pltpu.VMEM((lanes, length), f32), pltpu.VMEM((8, length), f32)],
        compiler_params=pltpu.CompilerParams(vmem_limit_bytes=VMEM_LIMIT),
        cost_estimate=pl.CostEstimate(
            flops=20 * length * length * width // COST_SCALE,
            transcendentals=0,
            bytes_accessed=length * width,
        ),
        name="attend_back",
    )(qkv, qkv, qkv, attended, grad_attended, lse)


def hint(flops, size):
    return pl.CostEstimate(flops=flops // COST_SCALE, transcendentals=0, bytes_accessed=size)


def params():
    return pltpu.CompilerParams(vmem_limit_bytes=VMEM_LIMIT)


def norm_item(patches, item, norm_gain, norm_shift):
    _, rows, model = patches.shape
    block = largest_block(rows, 256)

    def body(x_ref, gain_ref, shift_ref, out_ref):
        out_ref[...] = norm_rows(x_ref[...].astype(f32), gain_ref[...], shift_ref[...]).astype(bf16)

    vector = pl.BlockSpec((1, model), lambda i: (0, 0))
    return pl.pallas_call(
        body,
        grid=(rows // block,),
        in_specs=[pl.BlockSpec((None, block, model), lambda i: (item, i, 0)), vector, vector],
        out_specs=pl.BlockSpec((block, model), lambda i: (i, 0)),
        out_shape=jax.ShapeDtypeStruct((rows, model), bf16),
        compiler_params=params(),
        cost_estimate=hint(0, rows * model),
        name="norm_item",
    )(patches, norm_gain, norm_shift)


def out_project(patches, item, place, heads, weight, out_bias, norm_gain, norm_shift, before):
    slots, rows, model = patches.shape
    block = largest_block(rows, 256)
    steps = rows // block
    count, _, width = heads.shape

    def body(*refs):
        place_ref, x_ref, weight_ref, bias_ref, gain_ref, shift_ref, head_ref = refs[:7]
        attended_ref, residual_ref, normed_ref = refs[-3:]
        for k in range(count):
            attended_ref[:, k * width : (k + 1) * width] = head_ref[place_ref[0] ^ k]
        attended = attended_ref[...]
        residual = x_ref[...].astype(f32) + nn(attended, weight_ref[...]) + bias_ref[...]
        residual_ref[...] = residual
        normed_ref[...] = norm_rows(residual, gain_ref[...], shift_ref[...]).astype(bf16)

    vector = pl.BlockSpec((1, model), lambda i: (0, 0))
    placed = pl.BlockSpec((block, model), lambda i: (item * steps + i, 0))
    operands = [place, patches, weight, out_bias, norm_gain, norm_shift, heads]
    in_specs = [
        pl.BlockSpec(memory_space=pltpu.SMEM),
        pl.BlockSpec((None, block, model), lambda i: (item, i, 0)),
        pl.BlockSpec((model, model), lambda i: (0, 0)),
        vector,
        vector,
        vector,
        pl.BlockSpec((count, block, width), lambda i: (0, i, 0)),
    ]
    aliases = {}
    if before is not None:
        aliases = {len(operands) + k: k for k in range(3)}
        operands += before
        in_specs += [pl.BlockSpec(memory_space=pl.ANY)] * 3
    return pl.pallas_call(
        body,
        grid=(steps,),
        in_specs=in_specs,
        out_specs=[placed] * 3,
        out_shape=[jax.ShapeDtypeStruct((slots * rows, model), t) for t in (bf16, f32, bf16)],
        input_output_aliases=aliases,
        compiler_params=params(),
        cost_estimate=hint(2 * rows * model * model, rows * model),
        name="out_project",
    )(*operands)


def residual_back(total, residual, cotangent, scale, item, place, weight, norm_gain, low_before, pieces):
    slots, rows, model = cotangent.shape
    block = largest_block(rows, 256)
    steps = rows // block
    piece = model // pieces

    def body(*refs):
        place_ref, total_ref, residual_ref, cot_ref, scale_ref, weight_ref, gain_ref = refs[:7]
        grad_ref, low_ref, sum_ref, attended_ref = refs[-4:]
        residual = residual_ref[...]
        centred = residual - jnp.mean(residual, axis=-1, keepdims=True)
        rate = lax.rsqrt(jnp.mean(centred * centred, axis=-1, keepdims=True) + epsilon)
        xhat = centred * rate
        grad_normed = total_ref[...]
        scaled = grad_normed * gain_ref[...]
        inner = jnp.mean(scaled, axis=-1, keepdims=True)
        outer = jnp.mean(scaled * xhat, axis=-1, keepdims=True)
        cot = cot_ref[...].astype(f32) * scale_ref[item]
        grad = cot + rate * (scaled - inner - xhat * outer)
        grad_ref[...] = grad
        low = grad.astype(bf16)
        low_ref[...] = low

        @pl.when(pl.program_id(0) == 0)
        def _():
            sum_ref[...] = jnp.zeros_like(sum_ref)

        for k, value in enumerate((grad_normed * xhat, grad_normed, grad, cot)):
            sum_ref[k : k + 1, :] += jnp.sum(value, axis=0, keepdims=True)
        attended = nt(low, weight_ref[...]).astype(bf16)
        for k in range(pieces):
            attended_ref[place_ref[0] ^ k] = attended[:, k * piece : (k + 1) * piece]

    row_spec = pl.BlockSpec((block, model), lambda i: (i, 0))
    placed = pl.BlockSpec((block, model), lambda i: (item * steps + i, 0))
    operands = [place, total, residual, cotangent, scale, weight, norm_gain]
    in_specs = [
        pl.BlockSpec(memory_space=pltpu.SMEM),
        placed,
        placed,
        pl.BlockSpec((None, block, model), lambda i: (item, i, 0)),
        pl.BlockSpec(memory_space=pltpu.SMEM),
        pl.BlockSpec((model, model), lambda i: (0, 0)),
        pl.BlockSpec((1, model), lambda i: (0, 0)),
    ]
    aliases = {}
    if low_before is not None:
        aliases = {7: 1}
        operands.append(low_before)
        in_specs.append(pl.BlockSpec(memory_space=pl.ANY))
    return pl.pallas_call(
        body,
        grid=(steps,),
        in_specs=in_specs,
        out_specs=[
            row_spec,
            placed,
            pl.BlockSpec((8, model), lambda i: (0, 0)),
            pl.BlockSpec((pieces, block, piece), lambda i: (0, i, 0)),
        ],
        out_shape=[
            jax.ShapeDtypeStruct((rows, model), f32),
            jax.ShapeDtypeStruct((slots * rows, model), bf16),
            jax.ShapeDtypeStruct((8, model), f32),
            jax.ShapeDtypeStruct((pieces, rows, piece), bf16),
        ],
        input_output_aliases=aliases,
        compiler_params=params(),
        cost_estimate=hint(2 * rows * model * model, rows * model),
        name="residual_back",
    )(*operands)


def input_back(terms, patches, item, grad_residual, norm_gain, before):
    slots, rows, model = patches.shape
    block = largest_block(rows, 256)
    count = len(terms)

    def body(*refs):
        x_ref, grad_ref, gain_ref = refs[:3]
        out_ref = refs[-1]
        grad_normed = refs[3][...].astype(f32)
        for k in range(1, count):
            grad_normed = grad_normed + refs[3 + k][...].astype(f32)
        source = x_ref[...].astype(f32)
        centred = source - jnp.mean(source, axis=-1, keepdims=True)
        rate = lax.rsqrt(jnp.mean(centred * centred, axis=-1, keepdims=True) + epsilon)
        xhat = centred * rate
        scaled = grad_normed * gain_ref[...]
        inner = jnp.mean(scaled, axis=-1, keepdims=True)
        outer = jnp.mean(scaled * xhat, axis=-1, keepdims=True)
        out_ref[...] = (grad_ref[...] + rate * (scaled - inner - xhat * outer)).astype(bf16)

    row_spec = pl.BlockSpec((block, model), lambda i: (i, 0))
    placed = pl.BlockSpec((None, block, model), lambda i: (item, i, 0))
    operands = [patches, grad_residual, norm_gain, *terms]
    in_specs = [placed, row_spec, pl.BlockSpec((1, model), lambda i: (0, 0))] + [row_spec] * count
    aliases = {}
    if before is not None:
        aliases = {len(operands): 0}
        operands.append(before)
        in_specs.append(pl.BlockSpec(memory_space=pl.ANY))
    return pl.pallas_call(
        body,
        grid=(rows // block,),
        in_specs=in_specs,
        out_specs=placed,
        out_shape=jax.ShapeDtypeStruct((slots, rows, model), bf16),
        input_output_aliases=aliases,
        compiler_params=params(),
        cost_estimate=hint(0, rows * model),
        name="input_back",
    )(*operands)


def mlp_forward(normed, cot, ups, biases, downs, total):
    rows, model = normed.shape
    count = len(ups)
    units = ups[0].shape[1]
    block = largest_block(rows, 512)
    steps = rows // block
    first = total is None

    def body(*refs):
        x_ref, cot_ref = refs[:2]
        up_refs, bias_refs, down_refs = (refs[2 + k * count : 2 + (k + 1) * count] for k in range(3))
        rest = refs[2 + 3 * count :]
        if not first:
            before_ref = rest[0]
            rest = rest[1:]
        slope_ref, sum_ref = rest[:2]
        grad_refs = rest[2 : 2 + count]
        hidden_ref, acc_ref = rest[2 + count :]
        step = pl.program_id(0)
        part = largest_block(units, 256)
        for k in range(count):
            for j in range(units // part):
                cols = slice(j * part, (j + 1) * part)
                wide = slice(k * units + j * part, k * units + (j + 1) * part)
                pre = nn(x_ref[...], up_refs[k][:, cols]) + bias_refs[k][:, cols]
                cdf = 0.5 + 0.5 * lax.erf(pre * SQRT_HALF)
                density = jnp.exp2(pre * pre * (-0.5 * LOG2E)) * INV_SQRT_2PI
                hidden_ref[:, wide] = (pre * cdf).astype(bf16)
                slope_ref[:, wide] = (cdf + pre * density).astype(bf16)
        out = None if first else before_ref[...]
        for k in range(count):
            hidden = hidden_ref[:, k * units : (k + 1) * units]
            product = nn(hidden, down_refs[k][...])
            out = product if out is None else out + product
            grad = tn(hidden, cot_ref[...])

            @pl.when(step == 0)
            def _():
                acc_ref[k] = grad

            @pl.when(step > 0)
            def _():
                acc_ref[k] += grad

        sum_ref[...] = out

        @pl.when(step == steps - 1)
        def _():
            for k in range(count):
                grad_refs[k][...] = acc_ref[k].astype(bf16)

    row_spec = pl.BlockSpec((block, model), lambda i: (i, 0))
    slope_spec = pl.BlockSpec((block, count * units), lambda i: (i, 0))
    up_spec = pl.BlockSpec((model, units), lambda i: (0, 0), pipeline_mode=pl.Buffered(1))
    down_spec = pl.BlockSpec((units, model), lambda i: (0, 0), pipeline_mode=pl.Buffered(1))
    grad_spec = pl.BlockSpec((units, model), lambda i: (0, 0))
    operands = [normed, cot, *ups, *biases, *downs]
    in_specs = [row_spec, row_spec] + [up_spec] * count
    in_specs += [pl.BlockSpec((1, units), lambda i: (0, 0))] * count + [down_spec] * count
    aliases = {}
    if not first:
        aliases = {len(operands): 1}
        operands.append(total)
        in_specs.append(row_spec)
    return pl.pallas_call(
        body,
        grid=(steps,),
        in_specs=in_specs,
        out_specs=[slope_spec, row_spec] + [grad_spec] * count,
        out_shape=[
            jax.ShapeDtypeStruct((rows, count * units), bf16),
            jax.ShapeDtypeStruct((rows, model), f32),
        ]
        + [jax.ShapeDtypeStruct((units, model), bf16)] * count,
        scratch_shapes=[pltpu.VMEM((block, count * units), bf16), pltpu.VMEM((count, units, model), f32)],
        input_output_aliases=aliases,
        compiler_params=params(),
        cost_estimate=hint(6 * rows * model * units * count, rows * units),
        name="mlp_forward",
    )(*operands)


def mlp_backward(cot, slope, ups, downs, before, index, calls):
    rows, model = cot.shape
    count = len(ups)
    units = ups[0].shape[1]
    block = largest_block(rows, 512)
    first = before is None

    def body(*refs):
        cot_ref, slope_ref = refs[:2]
        up_refs, down_refs = refs[2 : 2 + count], refs[2 + count : 2 + 2 * count]
        grad_ref, sum_ref, bias_ref = refs[-3:]

        @pl.when(pl.program_id(0) == 0)
        def _():
            bias_ref[...] = jnp.zeros_like(bias_ref)

        out = None if first else refs[3 + 2 * count][...]
        part = largest_block(units, 512)
        for k in range(count):
            for j in range(units // part):
                rows_of = slice(j * part, (j + 1) * part)
                wide = slice(k * units + j * part, k * units + (j + 1) * part)
                low = (nt(cot_ref[...], down_refs[k][rows_of, :]) * slope_ref[:, wide].astype(f32)).astype(bf16)
                grad_ref[:, wide] = low
                bias_ref[:, wide] += jnp.sum(low.astype(f32), axis=0, keepdims=True)
            product = nt(grad_ref[:, k * units : (k + 1) * units], up_refs[k][...])
            out = product if out is None else out + product
        sum_ref[...] = out

    row_spec = pl.BlockSpec((block, model), lambda i: (i, 0))
    slope_spec = pl.BlockSpec((block, count * units), lambda i: (i, 0))
    up_spec = pl.BlockSpec((model, units), lambda i: (0, 0), pipeline_mode=pl.Buffered(1))
    down_spec = pl.BlockSpec((units, model), lambda i: (0, 0), pipeline_mode=pl.Buffered(1))
    operands = [cot, slope, *ups, *downs]
    in_specs = [row_spec, slope_spec] + [up_spec] * count + [down_spec] * count
    aliases = {}
    if not first:
        aliases = {len(operands): 0, len(operands) + 1: 1}
        operands += before
        in_specs += [pl.BlockSpec(memory_space=pl.ANY), row_spec]
    return pl.pallas_call(
        body,
        grid=(rows // block,),
        in_specs=in_specs,
        out_specs=[
            pl.BlockSpec((block, count * units), lambda i: (i, index)),
            row_spec,
            pl.BlockSpec((1, count * units), lambda i: (0, 0)),
        ],
        out_shape=[
            jax.ShapeDtypeStruct((rows, calls * count * units), bf16),
            jax.ShapeDtypeStruct((rows, model), f32),
            jax.ShapeDtypeStruct((1, count * units), f32),
        ],
        input_output_aliases=aliases,
        compiler_params=params(),
        cost_estimate=hint(4 * rows * model * units * count, rows * units),
        name="mlp_backward",
    )(*operands)


def weight_back(normed, pre_grad, attended, grad_low, pieces):
    rows, model = normed.shape
    every = pre_grad.shape[1]
    units = every // pieces
    piece = model // pieces
    block = largest_block(rows, 512)
    steps = rows // block

    def body(x_ref, pre_ref, attended_ref, grad_ref, *refs):
        up_refs, out_refs = refs[:pieces], refs[pieces : 2 * pieces]
        up_acc, out_acc = refs[2 * pieces :]
        step = pl.program_id(0)

        @pl.when(step == 0)
        def _():
            up_acc[...] = jnp.zeros_like(up_acc)
            out_acc[...] = jnp.zeros_like(out_acc)

        part = largest_block(every, 512)
        for j in range(every // part):
            cols = slice(j * part, (j + 1) * part)
            up_acc[:, cols] += tn(x_ref[...], pre_ref[:, cols])
        part = largest_block(model, 512)
        for j in range(model // part):
            cols = slice(j * part, (j + 1) * part)
            out_acc[:, cols] += tn(attended_ref[...], grad_ref[:, cols])

        @pl.when(step == steps - 1)
        def _():
            for k in range(pieces):
                up_refs[k][...] = up_acc[:, k * units : (k + 1) * units].astype(bf16)
                out_refs[k][...] = out_acc[k * piece : (k + 1) * piece, :].astype(bf16)

    row_spec = pl.BlockSpec((block, model), lambda i: (i, 0))
    return pl.pallas_call(
        body,
        grid=(steps,),
        in_specs=[row_spec, pl.BlockSpec((block, every), lambda i: (i, 0)), row_spec, row_spec],
        out_specs=[pl.BlockSpec((model, units), lambda i: (0, 0))] * pieces
        + [pl.BlockSpec((piece, model), lambda i: (0, 0))] * pieces,
        out_shape=[jax.ShapeDtypeStruct((model, units), bf16)] * pieces
        + [jax.ShapeDtypeStruct((piece, model), bf16)] * pieces,
        scratch_shapes=[pltpu.VMEM((model, every), f32), pltpu.VMEM((model, model), f32)],
        compiler_params=params(),
        cost_estimate=hint(2 * rows * model * (every + model), rows * model),
        name="weight_back",
    )(normed, pre_grad, attended, grad_low)


def project_back(place, normed, dqkv, weight, before, last, pieces):
    rows, model = normed.shape
    width = weight.shape[2]
    block = rows // pieces
    steps = pieces
    first = before is None

    def kernel(*refs):
        place_ref, normed_ref, dqkv_ref, weight_ref = refs[:4]
        rest = refs[4:]
        if not first:
            wgrad_before, column_before = rest[:2]
            rest = rest[2:]
        row_refs, rest = rest[:pieces], rest[pieces:]
        wgrad_ref, column_ref = rest[:2]
        step = pl.program_id(0)

        @pl.when(step == 0)
        def _():
            if first:
                wgrad_ref[...] = jnp.zeros_like(wgrad_ref)
                column_ref[...] = jnp.zeros_like(column_ref)
            else:
                wgrad_ref[...] = wgrad_before[...]
                column_ref[...] = column_before[...]

        row_grad = nt(dqkv_ref[0], weight_ref[0])
        for c in range(1, 3):
            row_grad = row_grad + nt(dqkv_ref[c], weight_ref[c])
        row_grad = row_grad.astype(bf16)
        for k in range(pieces):

            @pl.when(step == place_ref[0] ^ k)
            def _():
                row_refs[k][...] = row_grad

        for c in range(3):
            wgrad_ref[c] += tn(normed_ref[...], dqkv_ref[c])
            column_ref[c : c + 1, :] += jnp.sum(dqkv_ref[c].astype(f32), axis=0, keepdims=True)
        if last:
            low_ref = rest[2]

            @pl.when(step == steps - 1)
            def _():
                low_ref[:, :model, :] = wgrad_ref[...].astype(bf16)
                for c in range(3):
                    row = jnp.broadcast_to(column_ref[c : c + 1, :], (16, width))
                    low_ref[c, model:, :] = row.astype(bf16)

    whole = pl.BlockSpec((3, model, width), lambda i: (0, 0, 0))
    columns = pl.BlockSpec((8, width), lambda i: (0, 0))
    row_spec = pl.BlockSpec((block, model), lambda i: (i, 0))
    operands = [place, normed, dqkv, weight]
    in_specs = [pl.BlockSpec(memory_space=pltpu.SMEM), row_spec, pl.BlockSpec((3, block, width), lambda i: (0, i, 0)), whole]
    if not first:
        operands += list(before)
        in_specs += [whole, columns]
    out_specs = [pl.BlockSpec((block, model), lambda i: (0, 0))] * pieces + [whole, columns]
    out_shape = [jax.ShapeDtypeStruct((block, model), bf16)] * pieces + [
        jax.ShapeDtypeStruct((3, model, width), f32),
        jax.ShapeDtypeStruct((8, width), f32),
    ]
    if last:
        out_specs.append(pl.BlockSpec((3, model + 16, width), lambda i: (0, 0, 0)))
        out_shape.append(jax.ShapeDtypeStruct((3, model + 16, width), bf16))
    return pl.pallas_call(
        kernel,
        grid=(steps,),
        in_specs=in_specs,
        out_specs=out_specs,
        out_shape=out_shape,
        input_output_aliases={} if first else {4: pieces, 5: pieces + 1},
        compiler_params=pltpu.CompilerParams(vmem_limit_bytes=VMEM_LIMIT),
        cost_estimate=pl.CostEstimate(
            flops=12 * rows * model * width // COST_SCALE,
            transcendentals=0,
            bytes_accessed=rows * width,
        ),
        name="project_back",
    )(*operands)


def make_shards(tensor_size, group_size):
    square = tensor_size == 4

    def swap(value, bits):
        return lax.ppermute(value, "tensor", [(i, i ^ bits) for i in range(tensor_size)])

    def gather_far(own):
        return swap(own, 2) if square else lax.all_gather(own, "tensor")

    def gather_near(own, far):
        if not square:
            return [far[i] for i in range(tensor_size)]
        return [own, swap(own, 1), far, swap(far, 1)]

    def exchange(stacked):
        return lax.all_to_all(stacked, "tensor", 0, 0)

    def sum_near(blocks, anchor):
        if not square:
            return (jnp.stack(blocks),), anchor
        anchor, (near_own, near_far) = tie(anchor, (swap(blocks[1], 1), swap(blocks[3], 1)))
        far = (blocks[2].astype(f32) + near_far.astype(f32)).astype(blocks[2].dtype)
        return (blocks[0], near_own, far), anchor

    def sums_near(lists, anchor):
        if not square:
            return [sum_near(blocks, anchor)[0] for blocks in lists], anchor
        moved = [(swap(blocks[1], 1), swap(blocks[3], 1)) for blocks in lists]
        anchor, moved = tie(anchor, moved)
        return [
            (blocks[0], own, (blocks[2].astype(f32) + far.astype(f32)).astype(blocks[2].dtype))
            for blocks, (own, far) in zip(lists, moved, strict=True)
        ], anchor

    def terms_far(stage, anchor):
        if not square:
            own = lax.psum_scatter(stage[0], "tensor", scatter_dimension=0, tiled=False)
            anchor, own = tie(anchor, own)
            return [own], anchor
        own, near, far = stage
        anchor, received = tie(anchor, swap(far, 2))
        return [own, near, received], anchor

    def sum_far(stage, anchor):
        terms, anchor = terms_far(stage, anchor)
        total = terms[0].astype(f32)
        for term in terms[1:]:
            total = total + term.astype(f32)
        return total.astype(terms[0].dtype), anchor

    steps = []
    for axis, size in (("tensor", tensor_size), ("dp", group_size)):
        bit = 1
        while bit < size:
            steps.append((axis, [(i, i ^ bit) for i in range(size)]))
            bit *= 2
    tensor_steps = [step for step in steps if step[0] == "tensor"]

    def sum_step(value, step, anchor):
        anchor, received = tie(anchor, lax.ppermute(value, step[0], step[1]))
        return value + received, anchor

    def ring_plan():
        bits = [1 << k for k in range(group_size.bit_length() - 1)]
        return [(bit, True) for bit in bits] + [(bit, False) for bit in reversed(bits)]

    def ring_step(value, step, anchor):
        bit, reducing = step
        side = (lax.axis_index("dp") // bit) % 2
        pairs = [(i, i ^ bit) for i in range(group_size)]
        if reducing:
            half = value.shape[0] // 2
            sent = lax.dynamic_slice_in_dim(value, (1 - side) * half, half, axis=0)
            anchor, received = tie(anchor, lax.ppermute(sent, "dp", pairs))
            kept = lax.dynamic_slice_in_dim(value, side * half, half, axis=0)
            return (kept.astype(f32) + received.astype(f32)).astype(value.dtype), anchor
        anchor, received = tie(anchor, lax.ppermute(value, "dp", pairs))
        return in_halves(value, received, side), anchor

    def in_halves(own, other, side):
        rows = own.shape[0]
        whole = jnp.zeros((2 * rows,) + own.shape[1:], own.dtype)
        whole = lax.dynamic_update_slice_in_dim(whole, own, side * rows, axis=0)
        return lax.dynamic_update_slice_in_dim(whole, other, (1 - side) * rows, axis=0)

    def fetch_half(own):
        half = own.shape[0] // 2
        side = lax.axis_index("dp") % 2
        return swap(lax.dynamic_slice_in_dim(own, side * half, half, axis=0), 2)

    def fetch_rest(half):
        return lax.ppermute(half, "dp", [(i, i ^ 1) for i in range(group_size)])

    def in_order(stacked):
        if not square:
            return stacked
        own = lax.axis_index("tensor")
        return jnp.concatenate(
            [lax.dynamic_slice_in_dim(stacked, own ^ i, 1, axis=0) for i in range(tensor_size)], axis=0
        )

    def shards(
        patches,
        cotangent,
        empty_slots,
        dataset_id,
        dataset_weight,
        query_key_value_weight,
        qv_bias,
        output_projection_weight,
        out_bias,
        up_projection_weight,
        up_bias,
        down_projection_weight,
        down_bias,
        attn_gain,
        attn_shift,
        mlp_gain,
        mlp_shift,
    ):
        slot_count, own_rows, model = patches.shape
        width = query_key_value_weight.shape[2]
        group_slots = empty_slots.shape[0]
        slot_index = jnp.arange(group_slots * slot_count, dtype=jnp.int32) % slot_count
        filled = jnp.repeat(slot_count - empty_slots, slot_count)
        valid_all = (slot_index < filled).astype(f32)
        table_hits = dataset_id[:, None] == jnp.arange(dataset_weight.shape[0], dtype=jnp.int32)[None, :]
        numerator = jnp.sum(jnp.where(table_hits, dataset_weight[None, :], 0), axis=1).astype(f32)
        total_items = jnp.sum(valid_all)
        total_weight = jnp.sum(valid_all * numerator)
        multiplier_whole = valid_all * numerator * total_items / total_weight
        own_start = lax.axis_index("dp") * slot_count
        own_scale = lax.dynamic_slice_in_dim(multiplier_whole, own_start, slot_count)
        own_valid = lax.dynamic_slice_in_dim(valid_all, own_start, slot_count)
        all_rows = slot_count * own_rows
        row_scale = jnp.repeat(own_scale, own_rows)[:, None]
        row_valid = jnp.repeat(own_valid, own_rows)[:, None]
        gain_row, shift_row, mlp_gain_row, mlp_shift_row, out_bias_row = (
            value[None, :] for value in (attn_gain, attn_shift, mlp_gain, mlp_shift, out_bias)
        )
        proj_bias = jnp.stack([qv_bias[0], jnp.zeros_like(qv_bias[0]), qv_bias[1]])[:, None, :]
        bias_row = up_bias[None, :]

        dp_side = lax.axis_index("dp") % 2
        place = jnp.zeros((1,), jnp.int32)
        if square:
            place = place + lax.axis_index("tensor")
        fetch = fetch_half if square else gather_far
        weights_near = ()
        if square:
            weights_near = tuple(
                swap(value, 1) for value in (output_projection_weight, up_projection_weight, down_projection_weight)
            )

        def gather_rows(own):
            return lax.all_gather(own, "tensor", axis=0, tiled=True)

        normed = [norm_item(patches, i, gain_row, shift_row) for i in range(slot_count)]
        every = gather_rows(normed[0])
        bias_far = gather_far(bias_row)
        qkvs, attended, lses, heads_own, normed_every = [], [], [], [], []
        for i in range(slot_count):
            last = i == slot_count - 1
            normed_every.append(every)
            following = None
            if not last:
                every, following = tie(every, normed[i + 1])
                following = gather_rows(following)
            qkv = (
                jnp.einsum("wz,gzh->gwh", every, query_key_value_weight, preferred_element_type=f32) + proj_bias
            ).astype(bf16)
            if i == 0:
                qkv, (up_own, weights_near, bias_far) = tie(qkv, (up_projection_weight, weights_near, bias_far))
                up_far = fetch(up_own)
            out, lse = attend(qkv)
            if i == 0:
                out, (following, down_own, out_own, up_far) = tie(
                    out, (following, down_projection_weight, output_projection_weight, up_far)
                )
                down_far = fetch(down_own)
                out_far = gather_far(out_own)
                if square:
                    up_rest = fetch_rest(up_far)
            elif not last:
                out, (following, heads_own[-1], out_far, down_far) = tie(
                    out, (following, heads_own[-1], out_far, down_far)
                )
                if square:
                    out, up_rest = tie(out, up_rest)
                    up_far = in_halves(up_far, up_rest, dp_side)
                    up_diag = swap(up_far, 1)
                    down_rest = fetch_rest(down_far)
                    out_diag = swap(out_far, 1)
            if last:
                out, heads_own[-1] = tie(out, heads_own[-1])
                if square:
                    out, (down_rest, up_diag, out_diag) = tie(out, (down_rest, up_diag, out_diag))
                    down_far = in_halves(down_far, down_rest, dp_side)
                    down_diag = swap(down_far, 1)
            heads_own.append(exchange(out.reshape(tensor_size, own_rows, width)))
            qkvs.append(qkv)
            attended.append(out)
            lses.append(lse)
            every = following
        if square:
            out_weight = jnp.concatenate([out_own, weights_near[0], out_far, out_diag], axis=0)
        else:
            out_weight = jnp.concatenate(gather_near(out_own, out_far), axis=0)
        rows_done = None
        for i in range(slot_count):
            if i == slot_count - 1:
                rows_done, heads_own[i] = tie(rows_done, heads_own[i])
            rows_done = out_project(
                patches, i, place, heads_own[i], out_weight, out_bias_row, mlp_gain_row, mlp_shift_row, rows_done
            )
        attended_rows, residual, normed_mlp = rows_done
        cot_low = (cotangent.astype(f32).reshape(all_rows, model) * row_scale).astype(bf16)

        bias_blocks = gather_near(bias_row, bias_far)
        if square:
            up_blocks = [up_own, weights_near[1], up_far, up_diag]
            down_blocks = [down_own, weights_near[2], down_far, down_diag]
        else:
            up_blocks = gather_near(up_own, up_far)
            down_blocks = gather_near(down_own, down_far)
        calls = tensor_size // 2
        total = None
        slopes, down_grads = [], []
        for c in range(calls):
            pair = slice(2 * c, 2 * c + 2)
            slope, total, *grads = mlp_forward(
                normed_mlp, cot_low, up_blocks[pair], bias_blocks[pair], down_blocks[pair], total
            )
            slopes.append(slope)
            down_grads += grads
        output = ((residual + total + down_bias) * row_valid).astype(bf16)

        cot_back, down_grads = tie(cot_low, down_grads)
        before = None
        bias_grads = []
        for c in range(calls):
            pair = slice(2 * c, 2 * c + 2)
            *before, bias_grad = mlp_backward(
                cot_back, slopes[c], up_blocks[pair], down_blocks[pair], before, c, calls
            )
            bias_grads.append(bias_grad)
            if c == 0:
                down_stage, before = sum_near(down_grads, before)
        ring = ring_plan()
        pre_grad, total = before

        grad_low = None
        grad_residuals, grad_attended, sums = [], [], []
        for i in range(slot_count):
            grad_residual, grad_low, item_sums, pieces = residual_back(
                total, residual, cotangent, own_scale, i, place, out_weight, mlp_gain_row, grad_low, tensor_size
            )
            grad_residuals.append(grad_residual)
            sums.append(item_sums[:4])
            grad_attended.append(exchange(pieces))
        weight_grads = weight_back(normed_mlp, pre_grad, attended_rows, grad_low, tensor_size)
        weight_grads, grad_attended[:2] = tie(weight_grads, grad_attended[:2])
        down_sum, weight_grads = sum_far(down_stage, weight_grads)
        up_grads, out_grads = weight_grads[:tensor_size], weight_grads[tensor_size:]

        (up_stage, out_stage), grad_attended[0] = sums_near([up_grads, out_grads], grad_attended[0])
        small_rows = sum(sums[1:], sums[0])
        bias_rows = in_order(jnp.concatenate(bias_grads, axis=1).reshape(tensor_size, -1))
        smalls = jnp.concatenate([small_rows.reshape(-1), bias_rows.reshape(-1)]).reshape(-1, 128)
        waiting = list(steps)

        weights_wide = query_key_value_weight.astype(f32)
        sums = None
        grad_normed = []
        for i in range(slot_count):
            last = i == slot_count - 1
            dqkv = attend_back(qkvs[i], attended[i], grad_attended[i].reshape(-1, width), lses[i])
            if 1 <= i < slot_count - 1:
                dqkv, grad_attended[i + 1] = tie(dqkv, grad_attended[i + 1])
            if i >= 2:
                grad_normed[i - 2], dqkv = terms_far(grad_normed[i - 2], dqkv)
            if i >= 1:
                grad_normed[i - 1], dqkv = sum_near(grad_normed[i - 1], dqkv)
            if i == 0:
                up_sum, dqkv = sum_far(up_stage, dqkv)
                out_sum, dqkv = sum_far(out_stage, dqkv)
                up_all = lax.psum((up_sum, out_sum), "dp")
            if last:
                dqkv, up_all = tie(dqkv, up_all)
            if waiting and i > 0:
                smalls, dqkv = sum_step(smalls, waiting.pop(0), dqkv)
            if ring:
                down_sum, dqkv = ring_step(down_sum, ring.pop(0), dqkv)
            results = project_back(place, normed_every[i], dqkv, query_key_value_weight, sums, last, tensor_size)
            partial, sums = results[:tensor_size], results[tensor_size : tensor_size + 2]
            if waiting:
                smalls, partial = sum_step(smalls, waiting.pop(0), partial)
            if ring and not last:
                down_sum, partial = ring_step(down_sum, ring.pop(0), partial)
            if last:
                qkv_all = lax.psum(results[-1], "dp")
            grad_normed.append(partial)
        grad_inputs = None
        for i in range(slot_count):
            grad_residual = grad_residuals[i]
            if i == slot_count - 1:
                grad_normed[i], grad_residual = sum_near(grad_normed[i], grad_residual)
            terms = grad_normed[i]
            if i >= slot_count - 2:
                terms, grad_residual = terms_far(terms, grad_residual)
            if i == slot_count - 1:
                grad_residual, qkv_all = tie(grad_residual, qkv_all)
            grad_inputs = input_back(terms, patches, i, grad_residual, gain_row, grad_inputs)
        for step in ring:
            down_sum = ring_step(down_sum, step, place)[0]
        for step in waiting:
            smalls = sum_step(smalls, step, place)[0]
        weight_grad = qkv_all[:, :model].astype(f32)
        columns = qkv_all[:, model].astype(f32)
        raw = jnp.stack(
            [
                jnp.sum(weight_grad * weights_wide, axis=(0, 2)),
                jnp.sum(columns[:, None, :] * weights_wide, axis=(0, 2)),
            ]
        )
        for step in tensor_steps:
            raw = raw + lax.ppermute(raw, step[0], step[1])
        up_all, out_all = [value.astype(f32) for value in up_all]
        down_all = down_sum.astype(f32)
        inverse = 1.0 / total_items
        smalls = smalls.reshape(-1) * inverse
        small_rows = smalls[: 4 * model].reshape(4, model)
        units = up_bias.shape[0]
        bias_all = lax.dynamic_slice_in_dim(smalls[4 * model :], lax.axis_index("tensor") * units, units)
        shift_all = raw[1] * inverse
        gain_all = (raw[0] * inverse - attn_shift * shift_all) / attn_gain
        columns = columns * inverse
        return (
            output.reshape(patches.shape),
            grad_inputs,
            weight_grad * inverse,
            jnp.stack([columns[0], columns[2]]),
            out_all * inverse,
            small_rows[2],
            up_all * inverse,
            bias_all,
            down_all * inverse,
            small_rows[3],
            gain_all,
            shift_all,
            small_rows[0],
            small_rows[1],
        )

    return shards


def solution(mesh):
    items = P("dp", "tensor", None)
    return jax.shard_map(
        make_shards(mesh.shape["tensor"], mesh.shape["dp"]),
        mesh=mesh,
        in_specs=(
            items,
            items,
            P(),
            P(),
            P(),
            P(None, None, "tensor"),
            P(None, "tensor"),
            P("tensor", None),
            P(),
            P(None, "tensor"),
            P("tensor"),
            P("tensor", None),
            P(),
            P(),
            P(),
            P(),
            P(),
        ),
        out_specs=(
            items,
            items,
            P(None, None, "tensor"),
            P(None, "tensor"),
            P("tensor", None),
            P(),
            P(None, "tensor"),
            P("tensor"),
            P("tensor", None),
            P(),
            P(),
            P(),
            P(),
            P(),
        ),
        check_vma=False,
    )
```

```python
import jax
import jax.numpy as jnp
from jax import lax
from jax.experimental import pallas as pl
from jax.experimental.pallas import tpu as pltpu
from jax.sharding import PartitionSpec as P

HD = 64
SCORE_SCALE = HD ** (-0.5)
LOG2E = 1.4426950408889634
SQRT_HALF = 0.7071067811865476
INV_SQRT_2PI = 0.3989422804014327
epsilon = 1e-05
f32 = jnp.float32
bf16 = jnp.bfloat16
VMEM_LIMIT = 60 << 20
COST_SCALE = 64


def nn(a, b):
    return lax.dot_general(a, b, (((1,), (0,)), ((), ())), preferred_element_type=f32)


def nt(a, b):
    return lax.dot_general(a, b, (((1,), (1,)), ((), ())), preferred_element_type=f32)


def tn(a, b):
    return lax.dot_general(a, b, (((0,), (0,)), ((), ())), preferred_element_type=f32)


def tie(first, second):
    return lax.optimization_barrier((first, second))


def largest_block(extent, limit):
    block = min(extent, limit)
    while extent % block:
        block //= 2
    return block


def norm_rows(source, norm_gain, norm_shift):
    row_mean = jnp.mean(source, axis=-1, keepdims=True)
    centred = source - row_mean
    spread = jnp.mean(centred * centred, axis=-1, keepdims=True)
    return centred * lax.rsqrt(spread + epsilon) * norm_gain + norm_shift


def attend(qkv):
    _, length, width = qkv.shape
    lanes = min(128, width)
    heads = lanes // HD
    qblock = largest_block(length, 1024)
    to_log2 = SCORE_SCALE * LOG2E

    def body(q_ref, k_ref, v_ref, out_ref, lse_ref):
        queries = q_ref[...]
        keys = k_ref[...]
        values_t = v_ref[...].T
        lane = lax.broadcasted_iota(jnp.int32, (1, lanes), 1)
        outs = []
        for h in range(heads):
            own = queries
            if heads > 1:
                own = jnp.where(lane // HD == h, queries, jnp.zeros_like(queries))
            scores = nt(keys, own)
            top = jnp.max(scores, axis=0, keepdims=True)
            exp_scores = jnp.exp2((scores - top) * to_log2)
            total = jnp.sum(exp_scores, axis=0, keepdims=True)
            outs.append(nn(values_t[h * HD : (h + 1) * HD, :], exp_scores.astype(bf16)) / total)
            lse_ref[h : h + 1, :] = top * to_log2 + jnp.log2(total)
        out_ref[...] = jnp.concatenate(outs, axis=0).T.astype(bf16)

    pairs = width // lanes
    return pl.pallas_call(
        body,
        grid=(pairs, length // qblock),
        in_specs=[
            pl.BlockSpec((None, qblock, lanes), lambda h, j: (0, j, h)),
            pl.BlockSpec((None, length, lanes), lambda h, j: (1, 0, h)),
            pl.BlockSpec((None, length, lanes), lambda h, j: (2, 0, h)),
        ],
        out_specs=[
            pl.BlockSpec((qblock, lanes), lambda h, j: (j, h)),
            pl.BlockSpec((None, heads, qblock), lambda h, j: (h, 0, j)),
        ],
        out_shape=[
            jax.ShapeDtypeStruct((length, width), bf16),
            jax.ShapeDtypeStruct((pairs, heads, length), f32),
        ],
        compiler_params=pltpu.CompilerParams(vmem_limit_bytes=VMEM_LIMIT),
        cost_estimate=pl.CostEstimate(
            flops=8 * length * length * width // COST_SCALE,
            transcendentals=0,
            bytes_accessed=length * width,
        ),
        name="attend",
    )(qkv, qkv, qkv)


def attend_back(qkv, attended, grad_attended, item, lse):
    _, length, width = qkv.shape
    lanes = min(128, width)
    shards_of = grad_attended.shape[0]
    heads = lanes // HD
    kblock = largest_block(length, 512)
    kblocks = length // kblock
    to_log2 = SCORE_SCALE * LOG2E

    def body(q_ref, k_ref, v_ref, out_ref, grad_ref, lse_ref, dqkv_ref, dq_acc, row_dot):
        kb = pl.program_id(1)
        queries = q_ref[...]
        grads = grad_ref[...].reshape(length, lanes)
        keys = k_ref[...]
        values = v_ref[...]
        keys_t = keys.T
        lane = lax.broadcasted_iota(jnp.int32, (1, lanes), 1)

        @pl.when(kb == 0)
        def _():
            product = out_ref[...].astype(f32) * grads.astype(f32)
            high = product.astype(bf16)
            rest = (product - high.astype(f32)).astype(bf16)
            pick = lax.broadcasted_iota(jnp.int32, (8, lanes), 0)
            mask = (lax.broadcasted_iota(jnp.int32, (8, lanes), 1) // HD == pick).astype(f32).astype(bf16)
            row_dot[...] = nt(mask, high) + nt(mask, rest)

        dk = None
        dv = None
        dqs = []
        for h in range(heads):
            own_q = queries
            own_g = grads
            if heads > 1:
                mine = lane // HD == h
                own_q = jnp.where(mine, queries, jnp.zeros_like(queries))
                own_g = jnp.where(mine, grads, jnp.zeros_like(grads))
            scores = nt(keys, own_q)
            weights = jnp.exp2(scores * to_log2 - lse_ref[h : h + 1, :])
            grad_weights = nt(values, own_g)
            grad_scores = (weights * (grad_weights - row_dot[h : h + 1, :])).astype(bf16)
            dv_h = nn(weights.astype(bf16), own_g)
            dk_h = nn(grad_scores, own_q)
            dv = dv_h if dv is None else dv + dv_h
            dk = dk_h if dk is None else dk + dk_h
            dqs.append(nn(keys_t[h * HD : (h + 1) * HD, :], grad_scores))
        rows = pl.ds(pl.multiple_of(kb * kblock, kblock), kblock)
        dqkv_ref[1, rows, :] = (dk * SCORE_SCALE).astype(bf16)
        dqkv_ref[2, rows, :] = dv.astype(bf16)
        dq = jnp.concatenate(dqs, axis=0)
        if kblocks == 1:
            dqkv_ref[0] = (dq * SCORE_SCALE).T.astype(bf16)
            return

        @pl.when(kb == 0)
        def _():
            dq_acc[...] = dq

        @pl.when((kb > 0) & (kb < kblocks - 1))
        def _():
            dq_acc[...] += dq

        @pl.when(kb == kblocks - 1)
        def _():
            dqkv_ref[0] = ((dq_acc[...] + dq) * SCORE_SCALE).T.astype(bf16)

    pairs = width // lanes
    return pl.pallas_call(
        body,
        grid=(pairs, kblocks),
        in_specs=[
            pl.BlockSpec((None, length, lanes), lambda h, kb: (0, 0, h)),
            pl.BlockSpec((None, kblock, lanes), lambda h, kb: (1, kb, h)),
            pl.BlockSpec((None, kblock, lanes), lambda h, kb: (2, kb, h)),
            pl.BlockSpec((length, lanes), lambda h, kb: (0, h)),
            pl.BlockSpec((shards_of, length // shards_of, lanes), lambda h, kb: (0, item, h)),
            pl.BlockSpec((None, heads, length), lambda h, kb: (h, 0, 0)),
        ],
        out_specs=pl.BlockSpec((3, length, lanes), lambda h, kb: (0, 0, h)),
        out_shape=jax.ShapeDtypeStruct((3, length, width), bf16),
        scratch_shapes=[pltpu.VMEM((lanes, length), f32), pltpu.VMEM((8, length), f32)],
        compiler_params=pltpu.CompilerParams(vmem_limit_bytes=VMEM_LIMIT),
        cost_estimate=pl.CostEstimate(
            flops=20 * length * length * width // COST_SCALE,
            transcendentals=0,
            bytes_accessed=length * width,
        ),
        name="attend_back",
    )(qkv, qkv, qkv, attended, grad_attended, lse)


def hint(flops, size):
    return pl.CostEstimate(flops=flops // COST_SCALE, transcendentals=0, bytes_accessed=size)


def params():
    return pltpu.CompilerParams(vmem_limit_bytes=VMEM_LIMIT)


def norm_item(patches, item, norm_gain, norm_shift):
    _, rows, model = patches.shape
    block = largest_block(rows, 256)

    def body(x_ref, gain_ref, shift_ref, out_ref):
        out_ref[...] = norm_rows(x_ref[...].astype(f32), gain_ref[...], shift_ref[...]).astype(bf16)

    vector = pl.BlockSpec((1, model), lambda i: (0, 0))
    return pl.pallas_call(
        body,
        grid=(rows // block,),
        in_specs=[pl.BlockSpec((None, block, model), lambda i: (item, i, 0)), vector, vector],
        out_specs=pl.BlockSpec((block, model), lambda i: (i, 0)),
        out_shape=jax.ShapeDtypeStruct((rows, model), bf16),
        compiler_params=params(),
        cost_estimate=hint(0, rows * model),
        name="norm_item",
    )(patches, norm_gain, norm_shift)


def out_project(patches, item, place, heads, weight, out_bias, norm_gain, norm_shift, before):
    slots, rows, model = patches.shape
    block = largest_block(rows, 256)
    steps = rows // block
    count, _, width = heads.shape

    def body(*refs):
        place_ref, x_ref, weight_ref, bias_ref, gain_ref, shift_ref, head_ref = refs[:7]
        attended_ref, residual_ref, normed_ref = refs[-3:]
        for k in range(count):
            attended_ref[:, k * width : (k + 1) * width] = head_ref[place_ref[0] ^ k]
        attended = attended_ref[...]
        residual = x_ref[...].astype(f32) + nn(attended, weight_ref[...]) + bias_ref[...]
        residual_ref[...] = residual
        normed_ref[...] = norm_rows(residual, gain_ref[...], shift_ref[...]).astype(bf16)

    vector = pl.BlockSpec((1, model), lambda i: (0, 0))
    placed = pl.BlockSpec((block, model), lambda i: (item * steps + i, 0))
    operands = [place, patches, weight, out_bias, norm_gain, norm_shift, heads]
    in_specs = [
        pl.BlockSpec(memory_space=pltpu.SMEM),
        pl.BlockSpec((None, block, model), lambda i: (item, i, 0)),
        pl.BlockSpec((model, model), lambda i: (0, 0)),
        vector,
        vector,
        vector,
        pl.BlockSpec((count, block, width), lambda i: (0, i, 0)),
    ]
    aliases = {}
    if before is not None:
        aliases = {len(operands) + k: k for k in range(3)}
        operands += before
        in_specs += [pl.BlockSpec(memory_space=pl.ANY)] * 3
    return pl.pallas_call(
        body,
        grid=(steps,),
        in_specs=in_specs,
        out_specs=[placed] * 3,
        out_shape=[jax.ShapeDtypeStruct((slots * rows, model), t) for t in (bf16, f32, bf16)],
        input_output_aliases=aliases,
        compiler_params=params(),
        cost_estimate=hint(2 * rows * model * model, rows * model),
        name="out_project",
    )(*operands)


def residual_back(total, residual, cotangent, scale, place, weight, norm_gain, pieces):
    slots, rows, model = cotangent.shape
    block = largest_block(rows, 256)
    steps = rows // block
    piece = model // pieces

    def body(*refs):
        place_ref, total_ref, residual_ref, cot_ref, scale_ref, weight_ref, gain_ref = refs[:7]
        grad_ref, low_ref, sum_ref, attended_ref = refs[-4:]
        residual = residual_ref[...]
        centred = residual - jnp.mean(residual, axis=-1, keepdims=True)
        rate = lax.rsqrt(jnp.mean(centred * centred, axis=-1, keepdims=True) + epsilon)
        xhat = centred * rate
        grad_normed = total_ref[...]
        scaled = grad_normed * gain_ref[...]
        inner = jnp.mean(scaled, axis=-1, keepdims=True)
        outer = jnp.mean(scaled * xhat, axis=-1, keepdims=True)
        cot = cot_ref[...].astype(f32) * scale_ref[pl.program_id(0) // steps]
        grad = cot + rate * (scaled - inner - xhat * outer)
        grad_ref[...] = grad
        low = grad.astype(bf16)
        low_ref[...] = low

        @pl.when(pl.program_id(0) == 0)
        def _():
            sum_ref[...] = jnp.zeros_like(sum_ref)

        for k, value in enumerate((grad_normed * xhat, grad_normed, grad, cot)):
            sum_ref[k : k + 1, :] += jnp.sum(value, axis=0, keepdims=True)
        attended = nt(low, weight_ref[...]).astype(bf16)
        for k in range(pieces):
            attended_ref[place_ref[0] ^ k] = attended[:, k * piece : (k + 1) * piece]

    row_spec = pl.BlockSpec((block, model), lambda i: (i, 0))
    return pl.pallas_call(
        body,
        grid=(slots * steps,),
        in_specs=[
            pl.BlockSpec(memory_space=pltpu.SMEM),
            row_spec,
            row_spec,
            pl.BlockSpec((None, block, model), lambda i: (i // steps, i % steps, 0)),
            pl.BlockSpec(memory_space=pltpu.SMEM),
            pl.BlockSpec((model, model), lambda i: (0, 0)),
            pl.BlockSpec((1, model), lambda i: (0, 0)),
        ],
        out_specs=[
            row_spec,
            row_spec,
            pl.BlockSpec((8, model), lambda i: (0, 0)),
            pl.BlockSpec((pieces, block, piece), lambda i: (0, i, 0)),
        ],
        out_shape=[
            jax.ShapeDtypeStruct((slots * rows, model), f32),
            jax.ShapeDtypeStruct((slots * rows, model), bf16),
            jax.ShapeDtypeStruct((8, model), f32),
            jax.ShapeDtypeStruct((pieces, slots * rows, piece), bf16),
        ],
        compiler_params=params(),
        cost_estimate=hint(2 * slots * rows * model * model, rows * model),
        name="residual_back",
    )(place, total, residual, cotangent, scale, weight, norm_gain)


def input_back(terms, patches, item, grad_residual, norm_gain, before):
    slots, rows, model = patches.shape
    block = largest_block(rows, 256)
    count = len(terms)

    def body(*refs):
        x_ref, grad_ref, gain_ref = refs[:3]
        out_ref = refs[-1]
        grad_normed = refs[3][...].astype(f32)
        for k in range(1, count):
            grad_normed = grad_normed + refs[3 + k][...].astype(f32)
        source = x_ref[...].astype(f32)
        centred = source - jnp.mean(source, axis=-1, keepdims=True)
        rate = lax.rsqrt(jnp.mean(centred * centred, axis=-1, keepdims=True) + epsilon)
        xhat = centred * rate
        scaled = grad_normed * gain_ref[...]
        inner = jnp.mean(scaled, axis=-1, keepdims=True)
        outer = jnp.mean(scaled * xhat, axis=-1, keepdims=True)
        out_ref[...] = (grad_ref[...] + rate * (scaled - inner - xhat * outer)).astype(bf16)

    row_spec = pl.BlockSpec((block, model), lambda i: (i, 0))
    placed = pl.BlockSpec((None, block, model), lambda i: (item, i, 0))
    operands = [patches, grad_residual, norm_gain, *terms]
    steps = rows // block
    grad_spec = pl.BlockSpec((block, model), lambda i: (item * steps + i, 0))
    in_specs = [placed, grad_spec, pl.BlockSpec((1, model), lambda i: (0, 0))] + [row_spec] * count
    aliases = {}
    if before is not None:
        aliases = {len(operands): 0}
        operands.append(before)
        in_specs.append(pl.BlockSpec(memory_space=pl.ANY))
    return pl.pallas_call(
        body,
        grid=(rows // block,),
        in_specs=in_specs,
        out_specs=placed,
        out_shape=jax.ShapeDtypeStruct((slots, rows, model), bf16),
        input_output_aliases=aliases,
        compiler_params=params(),
        cost_estimate=hint(0, rows * model),
        name="input_back",
    )(*operands)


def mlp_forward(normed, cot, ups, biases, downs, total):
    rows, model = normed.shape
    count = len(ups)
    units = ups[0].shape[1]
    block = largest_block(rows, 512)
    steps = rows // block
    first = total is None

    def body(*refs):
        x_ref, cot_ref = refs[:2]
        up_refs, bias_refs, down_refs = (refs[2 + k * count : 2 + (k + 1) * count] for k in range(3))
        rest = refs[2 + 3 * count :]
        if not first:
            before_ref = rest[0]
            rest = rest[1:]
        slope_ref, sum_ref = rest[:2]
        grad_refs = rest[2 : 2 + count]
        hidden_ref, acc_ref = rest[2 + count :]
        step = pl.program_id(0)
        part = largest_block(units, 256)
        for k in range(count):
            for j in range(units // part):
                cols = slice(j * part, (j + 1) * part)
                wide = slice(k * units + j * part, k * units + (j + 1) * part)
                pre = nn(x_ref[...], up_refs[k][:, cols]) + bias_refs[k][:, cols]
                cdf = 0.5 + 0.5 * lax.erf(pre * SQRT_HALF)
                density = jnp.exp2(pre * pre * (-0.5 * LOG2E)) * INV_SQRT_2PI
                hidden_ref[:, wide] = (pre * cdf).astype(bf16)
                slope_ref[:, wide] = (cdf + pre * density).astype(bf16)
        out = None if first else before_ref[...]
        for k in range(count):
            hidden = hidden_ref[:, k * units : (k + 1) * units]
            product = nn(hidden, down_refs[k][...])
            out = product if out is None else out + product
            grad = tn(hidden, cot_ref[...])

            @pl.when(step == 0)
            def _():
                acc_ref[k] = grad

            @pl.when(step > 0)
            def _():
                acc_ref[k] += grad

        sum_ref[...] = out

        @pl.when(step == steps - 1)
        def _():
            for k in range(count):
                grad_refs[k][...] = acc_ref[k].astype(bf16)

    row_spec = pl.BlockSpec((block, model), lambda i: (i, 0))
    slope_spec = pl.BlockSpec((block, count * units), lambda i: (i, 0))
    up_spec = pl.BlockSpec((model, units), lambda i: (0, 0), pipeline_mode=pl.Buffered(1))
    down_spec = pl.BlockSpec((units, model), lambda i: (0, 0), pipeline_mode=pl.Buffered(1))
    grad_spec = pl.BlockSpec((units, model), lambda i: (0, 0))
    operands = [normed, cot, *ups, *biases, *downs]
    in_specs = [row_spec, row_spec] + [up_spec] * count
    in_specs += [pl.BlockSpec((1, units), lambda i: (0, 0))] * count + [down_spec] * count
    aliases = {}
    if not first:
        aliases = {len(operands): 1}
        operands.append(total)
        in_specs.append(row_spec)
    return pl.pallas_call(
        body,
        grid=(steps,),
        in_specs=in_specs,
        out_specs=[slope_spec, row_spec] + [grad_spec] * count,
        out_shape=[
            jax.ShapeDtypeStruct((rows, count * units), bf16),
            jax.ShapeDtypeStruct((rows, model), f32),
        ]
        + [jax.ShapeDtypeStruct((units, model), bf16)] * count,
        scratch_shapes=[pltpu.VMEM((block, count * units), bf16), pltpu.VMEM((count, units, model), f32)],
        input_output_aliases=aliases,
        compiler_params=params(),
        cost_estimate=hint(6 * rows * model * units * count, rows * units),
        name="mlp_forward",
    )(*operands)


def cot_back(cot, downs):
    rows, model = cot.shape
    count = len(downs)
    units = downs[0].shape[0]
    block = largest_block(rows, 512)

    def body(cot_ref, *refs):
        for k in range(count):
            refs[count][:, k * units : (k + 1) * units] = nt(cot_ref[...], refs[k][...]).astype(bf16)

    return pl.pallas_call(
        body,
        grid=(rows // block,),
        in_specs=[pl.BlockSpec((block, model), lambda i: (i, 0))]
        + [pl.BlockSpec((units, model), lambda i: (0, 0))] * count,
        out_specs=pl.BlockSpec((block, count * units), lambda i: (i, 0)),
        out_shape=jax.ShapeDtypeStruct((rows, count * units), bf16),
        compiler_params=params(),
        cost_estimate=hint(2 * rows * model * units * count, rows * units),
        name="cot_back",
    )(cot, *downs)


def mlp_backward(cot, slope, ups, downs, before, index, calls):
    rows, _ = cot.shape
    model = ups[0].shape[0]
    count = len(ups)
    units = ups[0].shape[1]
    block = largest_block(rows, 512)
    first = before is None

    def body(*refs):
        cot_ref, slope_ref = refs[:2]
        up_refs, down_refs = refs[2 : 2 + count], refs[2 + count : 2 + count + len(downs)]
        grad_ref, sum_ref, bias_ref = refs[-3:]

        @pl.when(pl.program_id(0) == 0)
        def _():
            bias_ref[...] = jnp.zeros_like(bias_ref)

        out = None if first else refs[3 + count + len(downs)][...]
        part = largest_block(units, 512)
        for k in range(count):
            for j in range(units // part):
                rows_of = slice(j * part, (j + 1) * part)
                wide = slice(k * units + j * part, k * units + (j + 1) * part)
                if downs:
                    product = nt(cot_ref[...], down_refs[k][rows_of, :])
                else:
                    product = cot_ref[:, wide].astype(f32)
                low = (product * slope_ref[:, wide].astype(f32)).astype(bf16)
                grad_ref[:, wide] = low
                bias_ref[:, wide] += jnp.sum(low.astype(f32), axis=0, keepdims=True)
            product = nt(grad_ref[:, k * units : (k + 1) * units], up_refs[k][...])
            out = product if out is None else out + product
        sum_ref[...] = out

    row_spec = pl.BlockSpec((block, model), lambda i: (i, 0))
    slope_spec = pl.BlockSpec((block, count * units), lambda i: (i, 0))
    up_spec = pl.BlockSpec((model, units), lambda i: (0, 0), pipeline_mode=pl.Buffered(1))
    down_spec = pl.BlockSpec((units, model), lambda i: (0, 0), pipeline_mode=pl.Buffered(1))
    operands = [cot, slope, *ups, *downs]
    in_specs = [row_spec if downs else slope_spec, slope_spec] + [up_spec] * count + [down_spec] * len(downs)
    aliases = {}
    if not first:
        aliases = {len(operands): 0, len(operands) + 1: 1}
        operands += before
        in_specs += [pl.BlockSpec(memory_space=pl.ANY), row_spec]
    return pl.pallas_call(
        body,
        grid=(rows // block,),
        in_specs=in_specs,
        out_specs=[
            pl.BlockSpec((block, count * units), lambda i: (i, index)),
            row_spec,
            pl.BlockSpec((1, count * units), lambda i: (0, 0)),
        ],
        out_shape=[
            jax.ShapeDtypeStruct((rows, calls * count * units), bf16),
            jax.ShapeDtypeStruct((rows, model), f32),
            jax.ShapeDtypeStruct((1, count * units), f32),
        ],
        input_output_aliases=aliases,
        compiler_params=params(),
        cost_estimate=hint(4 * rows * model * units * count, rows * units),
        name="mlp_backward",
    )(*operands)


def weight_back(normed, pre_grad, attended, grad_low, pieces):
    rows, model = normed.shape
    every = pre_grad.shape[1]
    units = every // pieces
    piece = model // pieces
    block = largest_block(rows, 512)
    steps = rows // block

    def body(x_ref, pre_ref, attended_ref, grad_ref, *refs):
        up_refs, out_refs = refs[:pieces], refs[pieces : 2 * pieces]
        up_acc, out_acc = refs[2 * pieces :]
        step = pl.program_id(0)

        @pl.when(step == 0)
        def _():
            up_acc[...] = jnp.zeros_like(up_acc)
            out_acc[...] = jnp.zeros_like(out_acc)

        part = largest_block(every, 512)
        for j in range(every // part):
            cols = slice(j * part, (j + 1) * part)
            up_acc[:, cols] += tn(x_ref[...], pre_ref[:, cols])
        part = largest_block(model, 512)
        for j in range(model // part):
            cols = slice(j * part, (j + 1) * part)
            out_acc[:, cols] += tn(attended_ref[...], grad_ref[:, cols])

        @pl.when(step == steps - 1)
        def _():
            for k in range(pieces):
                up_refs[k][...] = up_acc[:, k * units : (k + 1) * units].astype(bf16)
                out_refs[k][...] = out_acc[k * piece : (k + 1) * piece, :].astype(bf16)

    row_spec = pl.BlockSpec((block, model), lambda i: (i, 0))
    return pl.pallas_call(
        body,
        grid=(steps,),
        in_specs=[row_spec, pl.BlockSpec((block, every), lambda i: (i, 0)), row_spec, row_spec],
        out_specs=[pl.BlockSpec((model, units), lambda i: (0, 0))] * pieces
        + [pl.BlockSpec((piece, model), lambda i: (0, 0))] * pieces,
        out_shape=[jax.ShapeDtypeStruct((model, units), bf16)] * pieces
        + [jax.ShapeDtypeStruct((piece, model), bf16)] * pieces,
        scratch_shapes=[pltpu.VMEM((model, every), f32), pltpu.VMEM((model, model), f32)],
        compiler_params=params(),
        cost_estimate=hint(2 * rows * model * (every + model), rows * model),
        name="weight_back",
    )(normed, pre_grad, attended, grad_low)


def project_back(place, normed, dqkv, weight, before, last, pieces):
    rows, model = normed.shape
    width = weight.shape[2]
    block = rows // pieces
    steps = pieces
    first = before is None

    def kernel(*refs):
        place_ref, normed_ref, dqkv_ref, weight_ref = refs[:4]
        rest = refs[4:]
        if not first:
            wgrad_before, column_before = rest[:2]
            rest = rest[2:]
        row_refs, rest = rest[:pieces], rest[pieces:]
        wgrad_ref, column_ref = rest[:2]
        step = pl.program_id(0)

        @pl.when(step == 0)
        def _():
            if first:
                wgrad_ref[...] = jnp.zeros_like(wgrad_ref)
                column_ref[...] = jnp.zeros_like(column_ref)
            else:
                wgrad_ref[...] = wgrad_before[...]
                column_ref[...] = column_before[...]

        row_grad = nt(dqkv_ref[0], weight_ref[0])
        for c in range(1, 3):
            row_grad = row_grad + nt(dqkv_ref[c], weight_ref[c])
        row_grad = row_grad.astype(bf16)
        for k in range(pieces):

            @pl.when(step == place_ref[0] ^ k)
            def _():
                row_refs[k][...] = row_grad

        for c in range(3):
            wgrad_ref[c] += tn(normed_ref[...], dqkv_ref[c])
            column_ref[c : c + 1, :] += jnp.sum(dqkv_ref[c].astype(f32), axis=0, keepdims=True)
        if last:
            low_ref = rest[2]

            @pl.when(step == steps - 1)
            def _():
                low_ref[:, :model, :] = wgrad_ref[...].astype(bf16)
                for c in range(3):
                    row = jnp.broadcast_to(column_ref[c : c + 1, :], (16, width))
                    low_ref[c, model:, :] = row.astype(bf16)

    whole = pl.BlockSpec((3, model, width), lambda i: (0, 0, 0))
    columns = pl.BlockSpec((8, width), lambda i: (0, 0))
    row_spec = pl.BlockSpec((block, model), lambda i: (i, 0))
    operands = [place, normed, dqkv, weight]
    in_specs = [pl.BlockSpec(memory_space=pltpu.SMEM), row_spec, pl.BlockSpec((3, block, width), lambda i: (0, i, 0)), whole]
    if not first:
        operands += list(before)
        in_specs += [whole, columns]
    out_specs = [pl.BlockSpec((block, model), lambda i: (0, 0))] * pieces + [whole, columns]
    out_shape = [jax.ShapeDtypeStruct((block, model), bf16)] * pieces + [
        jax.ShapeDtypeStruct((3, model, width), f32),
        jax.ShapeDtypeStruct((8, width), f32),
    ]
    if last:
        out_specs.append(pl.BlockSpec((3, model + 16, width), lambda i: (0, 0, 0)))
        out_shape.append(jax.ShapeDtypeStruct((3, model + 16, width), bf16))
    return pl.pallas_call(
        kernel,
        grid=(steps,),
        in_specs=in_specs,
        out_specs=out_specs,
        out_shape=out_shape,
        input_output_aliases={} if first else {4: pieces, 5: pieces + 1},
        compiler_params=pltpu.CompilerParams(vmem_limit_bytes=VMEM_LIMIT),
        cost_estimate=pl.CostEstimate(
            flops=12 * rows * model * width // COST_SCALE,
            transcendentals=0,
            bytes_accessed=rows * width,
        ),
        name="project_back",
    )(*operands)


def make_shards(tensor_size, group_size):
    square = tensor_size == 4

    def swap(value, bits):
        return lax.ppermute(value, "tensor", [(i, i ^ bits) for i in range(tensor_size)])

    def gather_far(own):
        return swap(own, 2) if square else lax.all_gather(own, "tensor")

    def gather_near(own, far):
        if not square:
            return [far[i] for i in range(tensor_size)]
        return [own, swap(own, 1), far, swap(far, 1)]

    def exchange(stacked):
        return lax.all_to_all(stacked, "tensor", 0, 0)

    def sum_near(blocks, anchor):
        if not square:
            return (jnp.stack(blocks),), anchor
        anchor, (near_own, near_far) = tie(anchor, (swap(blocks[1], 1), swap(blocks[3], 1)))
        far = (blocks[2].astype(f32) + near_far.astype(f32)).astype(blocks[2].dtype)
        return (blocks[0], near_own, far), anchor

    def sums_near(lists, anchor):
        if not square:
            return [sum_near(blocks, anchor)[0] for blocks in lists], anchor
        moved = [(swap(blocks[1], 1), swap(blocks[3], 1)) for blocks in lists]
        anchor, moved = tie(anchor, moved)
        return [
            (blocks[0], own, (blocks[2].astype(f32) + far.astype(f32)).astype(blocks[2].dtype))
            for blocks, (own, far) in zip(lists, moved, strict=True)
        ], anchor

    def terms_far(stage, anchor):
        if not square:
            own = lax.psum_scatter(stage[0], "tensor", scatter_dimension=0, tiled=False)
            anchor, own = tie(anchor, own)
            return [own], anchor
        own, near, far = stage
        anchor, received = tie(anchor, swap(far, 2))
        return [own, near, received], anchor

    def sum_far(stage, anchor):
        terms, anchor = terms_far(stage, anchor)
        total = terms[0].astype(f32)
        for term in terms[1:]:
            total = total + term.astype(f32)
        return total.astype(terms[0].dtype), anchor

    steps = []
    for axis, size in (("tensor", tensor_size), ("dp", group_size)):
        bit = 1
        while bit < size:
            steps.append((axis, [(i, i ^ bit) for i in range(size)]))
            bit *= 2

    def sum_step(value, step, anchor):
        anchor, received = tie(anchor, lax.ppermute(value, step[0], step[1]))
        return value + received, anchor

    def ring_plan():
        bits = [1 << k for k in range(group_size.bit_length() - 1)]
        return [(bit, True) for bit in bits] + [(bit, False) for bit in reversed(bits)]

    def ring_step(value, step, anchor):
        bit, reducing = step
        side = (lax.axis_index("dp") // bit) % 2
        pairs = [(i, i ^ bit) for i in range(group_size)]
        if reducing:
            half = value.shape[0] // 2
            sent = lax.dynamic_slice_in_dim(value, (1 - side) * half, half, axis=0)
            anchor, received = tie(anchor, lax.ppermute(sent, "dp", pairs))
            kept = lax.dynamic_slice_in_dim(value, side * half, half, axis=0)
            return (kept.astype(f32) + received.astype(f32)).astype(value.dtype), anchor
        anchor, received = tie(anchor, lax.ppermute(value, "dp", pairs))
        return in_halves(value, received, side), anchor

    def in_halves(own, other, side):
        rows = own.shape[0]
        whole = jnp.zeros((2 * rows,) + own.shape[1:], own.dtype)
        whole = lax.dynamic_update_slice_in_dim(whole, own, side * rows, axis=0)
        return lax.dynamic_update_slice_in_dim(whole, other, (1 - side) * rows, axis=0)

    def fetch_half(own):
        half = own.shape[0] // 2
        side = lax.axis_index("dp") % 2
        return swap(lax.dynamic_slice_in_dim(own, side * half, half, axis=0), 2)

    def fetch_rest(half):
        return lax.ppermute(half, "dp", [(i, i ^ 1) for i in range(group_size)])

    def in_order(stacked):
        if not square:
            return stacked
        own = lax.axis_index("tensor")
        return jnp.concatenate(
            [lax.dynamic_slice_in_dim(stacked, own ^ i, 1, axis=0) for i in range(tensor_size)], axis=0
        )

    def shards(
        patches,
        cotangent,
        empty_slots,
        dataset_id,
        dataset_weight,
        query_key_value_weight,
        qv_bias,
        output_projection_weight,
        out_bias,
        up_projection_weight,
        up_bias,
        down_projection_weight,
        down_bias,
        attn_gain,
        attn_shift,
        mlp_gain,
        mlp_shift,
    ):
        slot_count, own_rows, model = patches.shape
        width = query_key_value_weight.shape[2]
        group_slots = empty_slots.shape[0]
        slot_index = jnp.arange(group_slots * slot_count, dtype=jnp.int32) % slot_count
        filled = jnp.repeat(slot_count - empty_slots, slot_count)
        valid_all = (slot_index < filled).astype(f32)
        table_hits = dataset_id[:, None] == jnp.arange(dataset_weight.shape[0], dtype=jnp.int32)[None, :]
        numerator = jnp.sum(jnp.where(table_hits, dataset_weight[None, :], 0), axis=1).astype(f32)
        total_items = jnp.sum(valid_all)
        total_weight = jnp.sum(valid_all * numerator)
        multiplier_whole = valid_all * numerator * total_items / total_weight
        own_start = lax.axis_index("dp") * slot_count
        own_scale = lax.dynamic_slice_in_dim(multiplier_whole, own_start, slot_count)
        own_valid = lax.dynamic_slice_in_dim(valid_all, own_start, slot_count)
        all_rows = slot_count * own_rows
        row_scale = jnp.repeat(own_scale, own_rows)[:, None]
        row_valid = jnp.repeat(own_valid, own_rows)[:, None]
        gain_row, shift_row, mlp_gain_row, mlp_shift_row, out_bias_row = (
            value[None, :] for value in (attn_gain, attn_shift, mlp_gain, mlp_shift, out_bias)
        )
        proj_bias = jnp.stack([qv_bias[0], jnp.zeros_like(qv_bias[0]), qv_bias[1]])[:, None, :]
        bias_row = up_bias[None, :]

        dp_side = lax.axis_index("dp") % 2
        place = jnp.zeros((1,), jnp.int32)
        if square:
            place = place + lax.axis_index("tensor")
        fetch = fetch_half if square else gather_far
        weights_near = ()
        if square:
            weights_near = tuple(
                swap(value, 1) for value in (output_projection_weight, up_projection_weight, down_projection_weight)
            )

        def gather_rows(own):
            return lax.all_gather(own, "tensor", axis=0, tiled=True)

        normed = [norm_item(patches, i, gain_row, shift_row) for i in range(slot_count)]
        every = gather_rows(normed[0])
        bias_far = gather_far(bias_row)
        cot_low = (cotangent.astype(f32).reshape(all_rows, model) * row_scale).astype(bf16)
        early = None
        if square:
            early = cot_back(cot_low, [down_projection_weight, weights_near[2]])
            every, early = tie(every, early)
        qkvs, attended, lses, heads_own, normed_every = [], [], [], [], []
        for i in range(slot_count):
            last = i == slot_count - 1
            normed_every.append(every)
            following = None
            if not last:
                every, following = tie(every, normed[i + 1])
                following = gather_rows(following)
            qkv = (
                jnp.einsum("wz,gzh->gwh", every, query_key_value_weight, preferred_element_type=f32) + proj_bias
            ).astype(bf16)
            if i == 0:
                qkv, (weights_near, bias_far) = tie(qkv, (weights_near, bias_far))
            out, lse = attend(qkv)
            if not last:
                out, following = tie(out, following)
            if i == 0:
                out, (up_own, down_own, out_own) = tie(
                    out, (up_projection_weight, down_projection_weight, output_projection_weight)
                )
                out_far = gather_far(out_own)
                up_far = fetch(up_own)
                down_far = fetch(down_own)
            else:
                out, heads_own[-1] = tie(out, heads_own[-1])
            if last:
                out, (out_far, up_far, down_far) = tie(out, (out_far, up_far, down_far))
            heads_own.append(exchange(out.reshape(tensor_size, own_rows, width)))
            qkvs.append(qkv)
            attended.append(out)
            lses.append(lse)
            every = following
        if square:
            up_rest = fetch_rest(up_far)
            down_rest = fetch_rest(down_far)
            out_weight = jnp.concatenate([out_own, weights_near[0], out_far, swap(out_far, 1)], axis=0)
        else:
            out_weight = jnp.concatenate(gather_near(out_own, out_far), axis=0)
        rows_done = None
        for i in range(slot_count):
            if i == slot_count - 1:
                rows_done, heads_own[i] = tie(rows_done, heads_own[i])
            rows_done = out_project(
                patches, i, place, heads_own[i], out_weight, out_bias_row, mlp_gain_row, mlp_shift_row, rows_done
            )
        if square:
            rows_done, (up_rest, down_rest) = tie(rows_done, (up_rest, down_rest))
            up_far = in_halves(up_far, up_rest, dp_side)
            down_far = in_halves(down_far, down_rest, dp_side)
            up_diag = swap(up_far, 1)
            down_diag = swap(down_far, 1)
        attended_rows, residual, normed_mlp = rows_done

        bias_blocks = gather_near(bias_row, bias_far)
        if square:
            up_blocks = [up_own, weights_near[1]]
            down_blocks = [down_own, weights_near[2]]
        else:
            up_blocks = gather_near(up_own, up_far)
            down_blocks = gather_near(down_own, down_far)
        calls = tensor_size // 2
        total = None
        slopes, down_grads = [], []
        for c in range(calls):
            pair = slice(2 * c, 2 * c + 2)
            if c == 1 and square:
                total, moved = tie(total, (up_far, up_diag, down_far, down_diag))
                up_blocks += moved[:2]
                down_blocks += moved[2:]
            slope, total, *grads = mlp_forward(
                normed_mlp, cot_low, up_blocks[pair], bias_blocks[pair], down_blocks[pair], total
            )
            slopes.append(slope)
            down_grads += grads
        output = ((residual + total + down_bias) * row_valid).astype(bf16)

        cot_late, down_grads = tie(cot_low, down_grads)
        before = None
        bias_grads = []
        for c in range(calls):
            pair = slice(2 * c, 2 * c + 2)
            if c == 0 and square:
                *before, bias_grad = mlp_backward(early, slopes[c], up_blocks[pair], [], before, c, calls)
            else:
                *before, bias_grad = mlp_backward(
                    cot_late, slopes[c], up_blocks[pair], down_blocks[pair], before, c, calls
                )
            bias_grads.append(bias_grad)
            if c == 0:
                down_stage, before = sum_near(down_grads, before)
        ring = ring_plan()
        pre_grad, total = before

        grad_residual, grad_low, small_rows, pieces = residual_back(
            total, residual, cotangent, own_scale, place, out_weight, mlp_gain_row, tensor_size
        )
        down_sum, pieces = sum_far(down_stage, pieces)
        grad_attended = exchange(pieces)
        weight_grads = weight_back(normed_mlp, pre_grad, attended_rows, grad_low, tensor_size)
        weight_grads, grad_attended = tie(weight_grads, grad_attended)
        up_grads, out_grads = weight_grads[:tensor_size], weight_grads[tensor_size:]

        (up_stage, out_stage), grad_attended = sums_near([up_grads, out_grads], grad_attended)
        bias_rows = in_order(jnp.concatenate(bias_grads, axis=1).reshape(tensor_size, -1))
        smalls = jnp.concatenate([small_rows[:4].reshape(-1), bias_rows.reshape(-1)]).reshape(-1, 128)
        waiting = list(steps)

        weights_wide = query_key_value_weight.astype(f32)
        sums = None
        grad_normed = []
        for i in range(slot_count):
            last = i == slot_count - 1
            dqkv = attend_back(qkvs[i], attended[i], grad_attended, i, lses[i])
            if i >= 2:
                grad_normed[i - 2], dqkv = terms_far(grad_normed[i - 2], dqkv)
            if i >= 1:
                grad_normed[i - 1], dqkv = sum_near(grad_normed[i - 1], dqkv)
            if i == 0:
                up_sum, dqkv = sum_far(up_stage, dqkv)
                out_sum, dqkv = sum_far(out_stage, dqkv)
                up_all = lax.psum((up_sum, out_sum), "dp")
            if last:
                dqkv, up_all = tie(dqkv, up_all)
            if waiting and i > 0:
                smalls, dqkv = sum_step(smalls, waiting.pop(0), dqkv)
            if ring:
                down_sum, dqkv = ring_step(down_sum, ring.pop(0), dqkv)
            results = project_back(place, normed_every[i], dqkv, query_key_value_weight, sums, last, tensor_size)
            partial, sums = results[:tensor_size], results[tensor_size : tensor_size + 2]
            if waiting:
                smalls, partial = sum_step(smalls, waiting.pop(0), partial)
            if ring and not last:
                down_sum, partial = ring_step(down_sum, ring.pop(0), partial)
            if last:
                grad_residual, qkv_low = tie(grad_residual, results[-1])
                qkv_all = lax.psum(qkv_low, "dp")
                raw = jnp.stack(
                    [
                        jnp.sum(sums[0] * weights_wide, axis=(0, 2)),
                        jnp.sum(sums[1][:3, None, :] * weights_wide, axis=(0, 2)),
                    ]
                )
                for step in steps:
                    raw = raw + lax.ppermute(raw, step[0], step[1])
            grad_normed.append(partial)
        grad_inputs = None
        for i in range(slot_count):
            if i == slot_count - 1:
                grad_normed[i], grad_residual = sum_near(grad_normed[i], grad_residual)
            terms = grad_normed[i]
            if i >= slot_count - 2:
                terms, grad_residual = terms_far(terms, grad_residual)
            if i == slot_count - 1:
                grad_residual, qkv_all = tie(grad_residual, qkv_all)
            grad_inputs = input_back(terms, patches, i, grad_residual, gain_row, grad_inputs)
        for step in ring:
            down_sum = ring_step(down_sum, step, place)[0]
        for step in waiting:
            smalls = sum_step(smalls, step, place)[0]
        weight_grad = qkv_all[:, :model].astype(f32)
        columns = qkv_all[:, model].astype(f32)
        up_all, out_all = [value.astype(f32) for value in up_all]
        down_all = down_sum.astype(f32)
        inverse = 1.0 / total_items
        smalls = smalls.reshape(-1) * inverse
        small_rows = smalls[: 4 * model].reshape(4, model)
        units = up_bias.shape[0]
        bias_all = lax.dynamic_slice_in_dim(smalls[4 * model :], lax.axis_index("tensor") * units, units)
        shift_all = raw[1] * inverse
        gain_all = (raw[0] * inverse - attn_shift * shift_all) / attn_gain
        columns = columns * inverse
        return (
            output.reshape(patches.shape),
            grad_inputs,
            weight_grad * inverse,
            jnp.stack([columns[0], columns[2]]),
            out_all * inverse,
            small_rows[2],
            up_all * inverse,
            bias_all,
            down_all * inverse,
            small_rows[3],
            gain_all,
            shift_all,
            small_rows[0],
            small_rows[1],
        )

    return shards


def solution(mesh):
    items = P("dp", "tensor", None)
    return jax.shard_map(
        make_shards(mesh.shape["tensor"], mesh.shape["dp"]),
        mesh=mesh,
        in_specs=(
            items,
            items,
            P(),
            P(),
            P(),
            P(None, None, "tensor"),
            P(None, "tensor"),
            P("tensor", None),
            P(),
            P(None, "tensor"),
            P("tensor"),
            P("tensor", None),
            P(),
            P(),
            P(),
            P(),
            P(),
        ),
        out_specs=(
            items,
            items,
            P(None, None, "tensor"),
            P(None, "tensor"),
            P("tensor", None),
            P(),
            P(None, "tensor"),
            P("tensor"),
            P("tensor", None),
            P(),
            P(),
            P(),
            P(),
            P(),
        ),
        check_vma=False,
    )
```

```python
import jax
import jax.numpy as jnp
from jax import lax
from jax.experimental import pallas as pl
from jax.experimental.pallas import tpu as pltpu
from jax.sharding import PartitionSpec as P

HD = 64
SCORE_SCALE = HD ** (-0.5)
LOG2E = 1.4426950408889634
SQRT_HALF = 0.7071067811865476
INV_SQRT_2PI = 0.3989422804014327
epsilon = 1e-05
f32 = jnp.float32
bf16 = jnp.bfloat16
VMEM_LIMIT = 60 << 20
COST_SCALE = 64


def nn(a, b):
    return lax.dot_general(a, b, (((1,), (0,)), ((), ())), preferred_element_type=f32)


def nt(a, b):
    return lax.dot_general(a, b, (((1,), (1,)), ((), ())), preferred_element_type=f32)


def tn(a, b):
    return lax.dot_general(a, b, (((0,), (0,)), ((), ())), preferred_element_type=f32)


def tie(first, second):
    return lax.optimization_barrier((first, second))


def largest_block(extent, limit):
    block = min(extent, limit)
    while extent % block:
        block //= 2
    return block


def norm_rows(source, norm_gain, norm_shift):
    row_mean = jnp.mean(source, axis=-1, keepdims=True)
    centred = source - row_mean
    spread = jnp.mean(centred * centred, axis=-1, keepdims=True)
    return centred * lax.rsqrt(spread + epsilon) * norm_gain + norm_shift


def attend(qkv):
    _, length, width = qkv.shape
    lanes = min(128, width)
    heads = lanes // HD
    qblock = largest_block(length, 2048)
    to_log2 = SCORE_SCALE * LOG2E

    def body(q_ref, k_ref, v_ref, out_ref, lse_ref):
        queries = q_ref[...]
        keys = k_ref[...]
        values_t = v_ref[...].T
        lane = lax.broadcasted_iota(jnp.int32, (1, lanes), 1)
        outs = []
        for h in range(heads):
            own = queries
            if heads > 1:
                own = jnp.where(lane // HD == h, queries, jnp.zeros_like(queries))
            scores = nt(keys, own)
            top = jnp.max(scores, axis=0, keepdims=True)
            exp_scores = jnp.exp2((scores - top) * to_log2)
            total = jnp.sum(exp_scores, axis=0, keepdims=True)
            outs.append(nn(values_t[h * HD : (h + 1) * HD, :], exp_scores.astype(bf16)) / total)
            lse_ref[h : h + 1, :] = top * to_log2 + jnp.log2(total)
        out_ref[...] = jnp.concatenate(outs, axis=0).T.astype(bf16)

    pairs = width // lanes
    return pl.pallas_call(
        body,
        grid=(pairs, length // qblock),
        in_specs=[
            pl.BlockSpec((None, qblock, lanes), lambda h, j: (0, j, h)),
            pl.BlockSpec((None, length, lanes), lambda h, j: (1, 0, h)),
            pl.BlockSpec((None, length, lanes), lambda h, j: (2, 0, h)),
        ],
        out_specs=[
            pl.BlockSpec((qblock, lanes), lambda h, j: (j, h)),
            pl.BlockSpec((None, heads, qblock), lambda h, j: (h, 0, j)),
        ],
        out_shape=[
            jax.ShapeDtypeStruct((length, width), bf16),
            jax.ShapeDtypeStruct((pairs, heads, length), f32),
        ],
        compiler_params=pltpu.CompilerParams(vmem_limit_bytes=VMEM_LIMIT),
        cost_estimate=pl.CostEstimate(
            flops=8 * length * length * width // COST_SCALE,
            transcendentals=0,
            bytes_accessed=length * width,
        ),
        name="attend",
    )(qkv, qkv, qkv)


def attend_back(qkv, attended, grad_attended, item, lse):
    _, length, width = qkv.shape
    lanes = min(128, width)
    shards_of = grad_attended.shape[0]
    heads = lanes // HD
    kblock = largest_block(length, 1024)
    kblocks = length // kblock
    to_log2 = SCORE_SCALE * LOG2E

    def body(q_ref, k_ref, v_ref, out_ref, grad_ref, lse_ref, dqkv_ref, dq_acc, row_dot):
        kb = pl.program_id(1)
        queries = q_ref[...]
        grads = grad_ref[...].reshape(length, lanes)
        keys = k_ref[...]
        values = v_ref[...]
        keys_t = keys.T
        lane = lax.broadcasted_iota(jnp.int32, (1, lanes), 1)

        @pl.when(kb == 0)
        def _():
            product = out_ref[...].astype(f32) * grads.astype(f32)
            high = product.astype(bf16)
            rest = (product - high.astype(f32)).astype(bf16)
            pick = lax.broadcasted_iota(jnp.int32, (8, lanes), 0)
            mask = (lax.broadcasted_iota(jnp.int32, (8, lanes), 1) // HD == pick).astype(f32).astype(bf16)
            row_dot[...] = nt(mask, high) + nt(mask, rest)

        dk = None
        dv = None
        dqs = []
        for h in range(heads):
            own_q = queries
            own_g = grads
            if heads > 1:
                mine = lane // HD == h
                own_q = jnp.where(mine, queries, jnp.zeros_like(queries))
                own_g = jnp.where(mine, grads, jnp.zeros_like(grads))
            scores = nt(keys, own_q)
            weights = jnp.exp2(scores * to_log2 - lse_ref[h : h + 1, :])
            grad_weights = nt(values, own_g)
            grad_scores = (weights * (grad_weights - row_dot[h : h + 1, :])).astype(bf16)
            dv_h = nn(weights.astype(bf16), own_g)
            dk_h = nn(grad_scores, own_q)
            dv = dv_h if dv is None else dv + dv_h
            dk = dk_h if dk is None else dk + dk_h
            dqs.append(nn(keys_t[h * HD : (h + 1) * HD, :], grad_scores))
        rows = pl.ds(pl.multiple_of(kb * kblock, kblock), kblock)
        dqkv_ref[1, rows, :] = (dk * SCORE_SCALE).astype(bf16)
        dqkv_ref[2, rows, :] = dv.astype(bf16)
        dq = jnp.concatenate(dqs, axis=0)
        if kblocks == 1:
            dqkv_ref[0] = (dq * SCORE_SCALE).T.astype(bf16)
            return

        @pl.when(kb == 0)
        def _():
            dq_acc[...] = dq

        @pl.when((kb > 0) & (kb < kblocks - 1))
        def _():
            dq_acc[...] += dq

        @pl.when(kb == kblocks - 1)
        def _():
            dqkv_ref[0] = ((dq_acc[...] + dq) * SCORE_SCALE).T.astype(bf16)

    pairs = width // lanes
    return pl.pallas_call(
        body,
        grid=(pairs, kblocks),
        in_specs=[
            pl.BlockSpec((None, length, lanes), lambda h, kb: (0, 0, h)),
            pl.BlockSpec((None, kblock, lanes), lambda h, kb: (1, kb, h)),
            pl.BlockSpec((None, kblock, lanes), lambda h, kb: (2, kb, h)),
            pl.BlockSpec((length, lanes), lambda h, kb: (0, h)),
            pl.BlockSpec((shards_of, length // shards_of, lanes), lambda h, kb: (0, item, h)),
            pl.BlockSpec((None, heads, length), lambda h, kb: (h, 0, 0)),
        ],
        out_specs=pl.BlockSpec((3, length, lanes), lambda h, kb: (0, 0, h)),
        out_shape=jax.ShapeDtypeStruct((3, length, width), bf16),
        scratch_shapes=[pltpu.VMEM((lanes, length), f32), pltpu.VMEM((8, length), f32)],
        compiler_params=pltpu.CompilerParams(vmem_limit_bytes=VMEM_LIMIT),
        cost_estimate=pl.CostEstimate(
            flops=20 * length * length * width // COST_SCALE,
            transcendentals=0,
            bytes_accessed=length * width,
        ),
        name="attend_back",
    )(qkv, qkv, qkv, attended, grad_attended, lse)


def hint(flops, size):
    return pl.CostEstimate(flops=flops // COST_SCALE, transcendentals=0, bytes_accessed=size)


def params():
    return pltpu.CompilerParams(vmem_limit_bytes=VMEM_LIMIT)


def norm_item(patches, item, norm_gain, norm_shift):
    _, rows, model = patches.shape
    block = largest_block(rows, 256)

    def body(x_ref, gain_ref, shift_ref, out_ref):
        out_ref[...] = norm_rows(x_ref[...].astype(f32), gain_ref[...], shift_ref[...]).astype(bf16)

    vector = pl.BlockSpec((1, model), lambda i: (0, 0))
    return pl.pallas_call(
        body,
        grid=(rows // block,),
        in_specs=[pl.BlockSpec((None, block, model), lambda i: (item, i, 0)), vector, vector],
        out_specs=pl.BlockSpec((block, model), lambda i: (i, 0)),
        out_shape=jax.ShapeDtypeStruct((rows, model), bf16),
        compiler_params=params(),
        cost_estimate=hint(0, rows * model),
        name="norm_item",
    )(patches, norm_gain, norm_shift)


def out_project(patches, item, place, heads, weight, out_bias, norm_gain, norm_shift, before):
    slots, rows, model = patches.shape
    block = largest_block(rows, 256)
    steps = rows // block
    count, _, width = heads.shape

    def body(*refs):
        place_ref, x_ref, weight_ref, bias_ref, gain_ref, shift_ref, head_ref = refs[:7]
        attended_ref, residual_ref, normed_ref = refs[-3:]
        for k in range(count):
            attended_ref[:, k * width : (k + 1) * width] = head_ref[place_ref[0] ^ k]
        attended = attended_ref[...]
        residual = x_ref[...].astype(f32) + nn(attended, weight_ref[...]) + bias_ref[...]
        residual_ref[...] = residual
        normed_ref[...] = norm_rows(residual, gain_ref[...], shift_ref[...]).astype(bf16)

    vector = pl.BlockSpec((1, model), lambda i: (0, 0))
    placed = pl.BlockSpec((block, model), lambda i: (item * steps + i, 0))
    operands = [place, patches, weight, out_bias, norm_gain, norm_shift, heads]
    in_specs = [
        pl.BlockSpec(memory_space=pltpu.SMEM),
        pl.BlockSpec((None, block, model), lambda i: (item, i, 0)),
        pl.BlockSpec((model, model), lambda i: (0, 0)),
        vector,
        vector,
        vector,
        pl.BlockSpec((count, block, width), lambda i: (0, i, 0)),
    ]
    aliases = {}
    if before is not None:
        aliases = {len(operands) + k: k for k in range(3)}
        operands += before
        in_specs += [pl.BlockSpec(memory_space=pl.ANY)] * 3
    return pl.pallas_call(
        body,
        grid=(steps,),
        in_specs=in_specs,
        out_specs=[placed] * 3,
        out_shape=[jax.ShapeDtypeStruct((slots * rows, model), t) for t in (bf16, f32, bf16)],
        input_output_aliases=aliases,
        compiler_params=params(),
        cost_estimate=hint(2 * rows * model * model, rows * model),
        name="out_project",
    )(*operands)


def residual_back(total, residual, cotangent, scale, place, weight, norm_gain, pieces):
    slots, rows, model = cotangent.shape
    block = largest_block(rows, 256)
    steps = rows // block
    piece = model // pieces

    def body(*refs):
        place_ref, total_ref, residual_ref, cot_ref, scale_ref, weight_ref, gain_ref = refs[:7]
        grad_ref, low_ref, sum_ref, attended_ref = refs[-4:]
        residual = residual_ref[...]
        centred = residual - jnp.mean(residual, axis=-1, keepdims=True)
        rate = lax.rsqrt(jnp.mean(centred * centred, axis=-1, keepdims=True) + epsilon)
        xhat = centred * rate
        grad_normed = total_ref[...]
        scaled = grad_normed * gain_ref[...]
        inner = jnp.mean(scaled, axis=-1, keepdims=True)
        outer = jnp.mean(scaled * xhat, axis=-1, keepdims=True)
        cot = cot_ref[...].astype(f32) * scale_ref[pl.program_id(0) // steps]
        grad = cot + rate * (scaled - inner - xhat * outer)
        grad_ref[...] = grad
        low = grad.astype(bf16)
        low_ref[...] = low

        @pl.when(pl.program_id(0) == 0)
        def _():
            sum_ref[...] = jnp.zeros_like(sum_ref)

        for k, value in enumerate((grad_normed * xhat, grad_normed, grad, cot)):
            sum_ref[k : k + 1, :] += jnp.sum(value, axis=0, keepdims=True)
        attended = nt(low, weight_ref[...]).astype(bf16)
        for k in range(pieces):
            attended_ref[place_ref[0] ^ k] = attended[:, k * piece : (k + 1) * piece]

    row_spec = pl.BlockSpec((block, model), lambda i: (i, 0))
    return pl.pallas_call(
        body,
        grid=(slots * steps,),
        in_specs=[
            pl.BlockSpec(memory_space=pltpu.SMEM),
            row_spec,
            row_spec,
            pl.BlockSpec((None, block, model), lambda i: (i // steps, i % steps, 0)),
            pl.BlockSpec(memory_space=pltpu.SMEM),
            pl.BlockSpec((model, model), lambda i: (0, 0)),
            pl.BlockSpec((1, model), lambda i: (0, 0)),
        ],
        out_specs=[
            row_spec,
            row_spec,
            pl.BlockSpec((8, model), lambda i: (0, 0)),
            pl.BlockSpec((pieces, block, piece), lambda i: (0, i, 0)),
        ],
        out_shape=[
            jax.ShapeDtypeStruct((slots * rows, model), f32),
            jax.ShapeDtypeStruct((slots * rows, model), bf16),
            jax.ShapeDtypeStruct((8, model), f32),
            jax.ShapeDtypeStruct((pieces, slots * rows, piece), bf16),
        ],
        compiler_params=params(),
        cost_estimate=hint(2 * slots * rows * model * model, rows * model),
        name="residual_back",
    )(place, total, residual, cotangent, scale, weight, norm_gain)


def input_back(terms, patches, item, grad_residual, norm_gain, before):
    slots, rows, model = patches.shape
    block = largest_block(rows, 256)
    count = len(terms)

    def body(*refs):
        x_ref, grad_ref, gain_ref = refs[:3]
        out_ref = refs[-1]
        grad_normed = refs[3][...].astype(f32)
        for k in range(1, count):
            grad_normed = grad_normed + refs[3 + k][...].astype(f32)
        source = x_ref[...].astype(f32)
        centred = source - jnp.mean(source, axis=-1, keepdims=True)
        rate = lax.rsqrt(jnp.mean(centred * centred, axis=-1, keepdims=True) + epsilon)
        xhat = centred * rate
        scaled = grad_normed * gain_ref[...]
        inner = jnp.mean(scaled, axis=-1, keepdims=True)
        outer = jnp.mean(scaled * xhat, axis=-1, keepdims=True)
        out_ref[...] = (grad_ref[...] + rate * (scaled - inner - xhat * outer)).astype(bf16)

    row_spec = pl.BlockSpec((block, model), lambda i: (i, 0))
    placed = pl.BlockSpec((None, block, model), lambda i: (item, i, 0))
    operands = [patches, grad_residual, norm_gain, *terms]
    steps = rows // block
    grad_spec = pl.BlockSpec((block, model), lambda i: (item * steps + i, 0))
    in_specs = [placed, grad_spec, pl.BlockSpec((1, model), lambda i: (0, 0))] + [row_spec] * count
    aliases = {}
    if before is not None:
        aliases = {len(operands): 0}
        operands.append(before)
        in_specs.append(pl.BlockSpec(memory_space=pl.ANY))
    return pl.pallas_call(
        body,
        grid=(rows // block,),
        in_specs=in_specs,
        out_specs=placed,
        out_shape=jax.ShapeDtypeStruct((slots, rows, model), bf16),
        input_output_aliases=aliases,
        compiler_params=params(),
        cost_estimate=hint(0, rows * model),
        name="input_back",
    )(*operands)


def mlp_forward(normed, cot, ups, biases, downs, total):
    rows, model = normed.shape
    count = len(ups)
    units = ups[0].shape[1]
    block = largest_block(rows, 512)
    steps = rows // block
    first = total is None

    def body(*refs):
        x_ref, cot_ref = refs[:2]
        up_refs, bias_refs, down_refs = (refs[2 + k * count : 2 + (k + 1) * count] for k in range(3))
        rest = refs[2 + 3 * count :]
        if not first:
            before_ref = rest[0]
            rest = rest[1:]
        slope_ref, sum_ref = rest[:2]
        grad_refs = rest[2 : 2 + count]
        hidden_ref, acc_ref = rest[2 + count :]
        step = pl.program_id(0)
        part = largest_block(units, 256)
        for k in range(count):
            for j in range(units // part):
                cols = slice(j * part, (j + 1) * part)
                wide = slice(k * units + j * part, k * units + (j + 1) * part)
                pre = nn(x_ref[...], up_refs[k][:, cols]) + bias_refs[k][:, cols]
                cdf = 0.5 + 0.5 * lax.erf(pre * SQRT_HALF)
                density = jnp.exp2(pre * pre * (-0.5 * LOG2E)) * INV_SQRT_2PI
                hidden_ref[:, wide] = (pre * cdf).astype(bf16)
                slope_ref[:, wide] = (cdf + pre * density).astype(bf16)
        out = None if first else before_ref[...]
        for k in range(count):
            hidden = hidden_ref[:, k * units : (k + 1) * units]
            product = nn(hidden, down_refs[k][...])
            out = product if out is None else out + product
            grad = tn(hidden, cot_ref[...])

            @pl.when(step == 0)
            def _():
                acc_ref[k] = grad

            @pl.when(step > 0)
            def _():
                acc_ref[k] += grad

        sum_ref[...] = out

        @pl.when(step == steps - 1)
        def _():
            for k in range(count):
                grad_refs[k][...] = acc_ref[k].astype(bf16)

    row_spec = pl.BlockSpec((block, model), lambda i: (i, 0))
    slope_spec = pl.BlockSpec((block, count * units), lambda i: (i, 0))
    up_spec = pl.BlockSpec((model, units), lambda i: (0, 0), pipeline_mode=pl.Buffered(1))
    down_spec = pl.BlockSpec((units, model), lambda i: (0, 0), pipeline_mode=pl.Buffered(1))
    grad_spec = pl.BlockSpec((units, model), lambda i: (0, 0))
    operands = [normed, cot, *ups, *biases, *downs]
    in_specs = [row_spec, row_spec] + [up_spec] * count
    in_specs += [pl.BlockSpec((1, units), lambda i: (0, 0))] * count + [down_spec] * count
    aliases = {}
    if not first:
        aliases = {len(operands): 1}
        operands.append(total)
        in_specs.append(row_spec)
    return pl.pallas_call(
        body,
        grid=(steps,),
        in_specs=in_specs,
        out_specs=[slope_spec, row_spec] + [grad_spec] * count,
        out_shape=[
            jax.ShapeDtypeStruct((rows, count * units), bf16),
            jax.ShapeDtypeStruct((rows, model), f32),
        ]
        + [jax.ShapeDtypeStruct((units, model), bf16)] * count,
        scratch_shapes=[pltpu.VMEM((block, count * units), bf16), pltpu.VMEM((count, units, model), f32)],
        input_output_aliases=aliases,
        compiler_params=params(),
        cost_estimate=hint(6 * rows * model * units * count, rows * units),
        name="mlp_forward",
    )(*operands)


def cot_back(cot, downs):
    rows, model = cot.shape
    count = len(downs)
    units = downs[0].shape[0]
    block = largest_block(rows, 512)

    def body(cot_ref, *refs):
        for k in range(count):
            refs[count][:, k * units : (k + 1) * units] = nt(cot_ref[...], refs[k][...]).astype(bf16)

    return pl.pallas_call(
        body,
        grid=(rows // block,),
        in_specs=[pl.BlockSpec((block, model), lambda i: (i, 0))]
        + [pl.BlockSpec((units, model), lambda i: (0, 0))] * count,
        out_specs=pl.BlockSpec((block, count * units), lambda i: (i, 0)),
        out_shape=jax.ShapeDtypeStruct((rows, count * units), bf16),
        compiler_params=params(),
        cost_estimate=hint(2 * rows * model * units * count, rows * units),
        name="cot_back",
    )(cot, *downs)


def mlp_backward(cot, slope, ups, downs, before, index, calls):
    rows, _ = cot.shape
    model = ups[0].shape[0]
    count = len(ups)
    units = ups[0].shape[1]
    block = largest_block(rows, 512)
    first = before is None

    def body(*refs):
        cot_ref, slope_ref = refs[:2]
        up_refs, down_refs = refs[2 : 2 + count], refs[2 + count : 2 + count + len(downs)]
        grad_ref, sum_ref, bias_ref = refs[-3:]

        @pl.when(pl.program_id(0) == 0)
        def _():
            bias_ref[...] = jnp.zeros_like(bias_ref)

        out = None if first else refs[3 + count + len(downs)][...]
        part = largest_block(units, 512)
        for k in range(count):
            for j in range(units // part):
                rows_of = slice(j * part, (j + 1) * part)
                wide = slice(k * units + j * part, k * units + (j + 1) * part)
                if downs:
                    product = nt(cot_ref[...], down_refs[k][rows_of, :])
                else:
                    product = cot_ref[:, wide].astype(f32)
                low = (product * slope_ref[:, wide].astype(f32)).astype(bf16)
                grad_ref[:, wide] = low
                bias_ref[:, wide] += jnp.sum(low.astype(f32), axis=0, keepdims=True)
            product = nt(grad_ref[:, k * units : (k + 1) * units], up_refs[k][...])
            out = product if out is None else out + product
        sum_ref[...] = out

    row_spec = pl.BlockSpec((block, model), lambda i: (i, 0))
    slope_spec = pl.BlockSpec((block, count * units), lambda i: (i, 0))
    up_spec = pl.BlockSpec((model, units), lambda i: (0, 0), pipeline_mode=pl.Buffered(1))
    down_spec = pl.BlockSpec((units, model), lambda i: (0, 0), pipeline_mode=pl.Buffered(1))
    operands = [cot, slope, *ups, *downs]
    in_specs = [row_spec if downs else slope_spec, slope_spec] + [up_spec] * count + [down_spec] * len(downs)
    aliases = {}
    if not first:
        aliases = {len(operands): 0, len(operands) + 1: 1}
        operands += before
        in_specs += [pl.BlockSpec(memory_space=pl.ANY), row_spec]
    return pl.pallas_call(
        body,
        grid=(rows // block,),
        in_specs=in_specs,
        out_specs=[
            pl.BlockSpec((block, count * units), lambda i: (i, index)),
            row_spec,
            pl.BlockSpec((1, count * units), lambda i: (0, 0)),
        ],
        out_shape=[
            jax.ShapeDtypeStruct((rows, calls * count * units), bf16),
            jax.ShapeDtypeStruct((rows, model), f32),
            jax.ShapeDtypeStruct((1, count * units), f32),
        ],
        input_output_aliases=aliases,
        compiler_params=params(),
        cost_estimate=hint(4 * rows * model * units * count, rows * units),
        name="mlp_backward",
    )(*operands)


def weight_back(normed, pre_grad, attended, grad_low, pieces):
    rows, model = normed.shape
    every = pre_grad.shape[1]
    units = every // pieces
    piece = model // pieces
    block = largest_block(rows, 512)
    steps = rows // block

    def body(x_ref, pre_ref, attended_ref, grad_ref, *refs):
        up_refs, out_refs = refs[:pieces], refs[pieces : 2 * pieces]
        up_acc, out_acc = refs[2 * pieces :]
        step = pl.program_id(0)

        @pl.when(step == 0)
        def _():
            up_acc[...] = jnp.zeros_like(up_acc)
            out_acc[...] = jnp.zeros_like(out_acc)

        part = largest_block(every, 512)
        for j in range(every // part):
            cols = slice(j * part, (j + 1) * part)
            up_acc[:, cols] += tn(x_ref[...], pre_ref[:, cols])
        part = largest_block(model, 512)
        for j in range(model // part):
            cols = slice(j * part, (j + 1) * part)
            out_acc[:, cols] += tn(attended_ref[...], grad_ref[:, cols])

        @pl.when(step == steps - 1)
        def _():
            for k in range(pieces):
                up_refs[k][...] = up_acc[:, k * units : (k + 1) * units].astype(bf16)
                out_refs[k][...] = out_acc[k * piece : (k + 1) * piece, :].astype(bf16)

    row_spec = pl.BlockSpec((block, model), lambda i: (i, 0))
    return pl.pallas_call(
        body,
        grid=(steps,),
        in_specs=[row_spec, pl.BlockSpec((block, every), lambda i: (i, 0)), row_spec, row_spec],
        out_specs=[pl.BlockSpec((model, units), lambda i: (0, 0))] * pieces
        + [pl.BlockSpec((piece, model), lambda i: (0, 0))] * pieces,
        out_shape=[jax.ShapeDtypeStruct((model, units), bf16)] * pieces
        + [jax.ShapeDtypeStruct((piece, model), bf16)] * pieces,
        scratch_shapes=[pltpu.VMEM((model, every), f32), pltpu.VMEM((model, model), f32)],
        compiler_params=params(),
        cost_estimate=hint(2 * rows * model * (every + model), rows * model),
        name="weight_back",
    )(normed, pre_grad, attended, grad_low)


def project_back(place, normed, dqkv, weight, before, last, pieces):
    rows, model = normed.shape
    width = weight.shape[2]
    block = rows // pieces
    steps = pieces
    first = before is None
    given = 0 if last else pieces

    def kernel(*refs):
        place_ref, normed_ref, dqkv_ref, weight_ref = refs[:4]
        rest = refs[4:]
        if not first:
            wgrad_before, column_before = rest[:2]
            rest = rest[2:]
        row_refs, rest = rest[:given], rest[given:]
        wgrad_ref, column_ref = rest[:2]
        step = pl.program_id(0)

        @pl.when(step == 0)
        def _():
            if first:
                wgrad_ref[...] = jnp.zeros_like(wgrad_ref)
                column_ref[...] = jnp.zeros_like(column_ref)
            else:
                wgrad_ref[...] = wgrad_before[...]
                column_ref[...] = column_before[...]

        if not last:
            row_grad = nt(dqkv_ref[0], weight_ref[0])
            for c in range(1, 3):
                row_grad = row_grad + nt(dqkv_ref[c], weight_ref[c])
            row_grad = row_grad.astype(bf16)
            for k in range(pieces):

                @pl.when(step == place_ref[0] ^ k)
                def _():
                    row_refs[k][...] = row_grad

        for c in range(3):
            wgrad_ref[c] += tn(normed_ref[...], dqkv_ref[c])
            column_ref[c : c + 1, :] += jnp.sum(dqkv_ref[c].astype(f32), axis=0, keepdims=True)
        if last:
            low_ref = rest[2]

            @pl.when(step == steps - 1)
            def _():
                low_ref[:, :model, :] = wgrad_ref[...].astype(bf16)
                for c in range(3):
                    row = jnp.broadcast_to(column_ref[c : c + 1, :], (16, width))
                    low_ref[c, model:, :] = row.astype(bf16)

    whole = pl.BlockSpec((3, model, width), lambda i: (0, 0, 0))
    columns = pl.BlockSpec((8, width), lambda i: (0, 0))
    row_spec = pl.BlockSpec((block, model), lambda i: (i, 0))
    operands = [place, normed, dqkv, weight]
    in_specs = [pl.BlockSpec(memory_space=pltpu.SMEM), row_spec, pl.BlockSpec((3, block, width), lambda i: (0, i, 0)), whole]
    if not first:
        operands += list(before)
        in_specs += [whole, columns]
    out_specs = [pl.BlockSpec((block, model), lambda i: (0, 0))] * given + [whole, columns]
    out_shape = [jax.ShapeDtypeStruct((block, model), bf16)] * given + [
        jax.ShapeDtypeStruct((3, model, width), f32),
        jax.ShapeDtypeStruct((8, width), f32),
    ]
    if last:
        out_specs.append(pl.BlockSpec((3, model + 16, width), lambda i: (0, 0, 0)))
        out_shape.append(jax.ShapeDtypeStruct((3, model + 16, width), bf16))
    return pl.pallas_call(
        kernel,
        grid=(steps,),
        in_specs=in_specs,
        out_specs=out_specs,
        out_shape=out_shape,
        input_output_aliases={} if first else {4: given, 5: given + 1},
        compiler_params=pltpu.CompilerParams(vmem_limit_bytes=VMEM_LIMIT),
        cost_estimate=pl.CostEstimate(
            flops=12 * rows * model * width // COST_SCALE,
            transcendentals=0,
            bytes_accessed=rows * width,
        ),
        name="project_back",
    )(*operands)


def project_rows(place, dqkv, weight, pieces):
    _, rows, width = dqkv.shape
    model = weight.shape[1]
    block = rows // pieces

    def kernel(place_ref, dqkv_ref, weight_ref, *row_refs):
        row_grad = nt(dqkv_ref[0], weight_ref[0])
        for c in range(1, 3):
            row_grad = row_grad + nt(dqkv_ref[c], weight_ref[c])
        row_grad = row_grad.astype(bf16)
        for k in range(pieces):

            @pl.when(pl.program_id(0) == place_ref[0] ^ k)
            def _():
                row_refs[k][...] = row_grad

    return pl.pallas_call(
        kernel,
        grid=(pieces,),
        in_specs=[
            pl.BlockSpec(memory_space=pltpu.SMEM),
            pl.BlockSpec((3, block, width), lambda i: (0, i, 0)),
            pl.BlockSpec((3, model, width), lambda i: (0, 0, 0)),
        ],
        out_specs=[pl.BlockSpec((block, model), lambda i: (0, 0))] * pieces,
        out_shape=[jax.ShapeDtypeStruct((block, model), bf16)] * pieces,
        compiler_params=params(),
        cost_estimate=hint(6 * rows * model * width, rows * width),
        name="project_rows",
    )(place, dqkv, weight)


def make_shards(tensor_size, group_size):
    square = tensor_size == 4

    def swap(value, bits):
        return lax.ppermute(value, "tensor", [(i, i ^ bits) for i in range(tensor_size)])

    def gather_far(own):
        return swap(own, 2) if square else lax.all_gather(own, "tensor")

    def gather_near(own, far):
        if not square:
            return [far[i] for i in range(tensor_size)]
        return [own, swap(own, 1), far, swap(far, 1)]

    def exchange(stacked):
        return lax.all_to_all(stacked, "tensor", 0, 0)

    def sum_near(blocks, anchor):
        if not square:
            return (jnp.stack(blocks),), anchor
        anchor, (near_own, near_far) = tie(anchor, (swap(blocks[1], 1), swap(blocks[3], 1)))
        far = (blocks[2].astype(f32) + near_far.astype(f32)).astype(blocks[2].dtype)
        return (blocks[0], near_own, far), anchor

    def sums_near(lists, anchor):
        if not square:
            return [sum_near(blocks, anchor)[0] for blocks in lists], anchor
        moved = [(swap(blocks[1], 1), swap(blocks[3], 1)) for blocks in lists]
        anchor, moved = tie(anchor, moved)
        return [
            (blocks[0], own, (blocks[2].astype(f32) + far.astype(f32)).astype(blocks[2].dtype))
            for blocks, (own, far) in zip(lists, moved, strict=True)
        ], anchor

    def terms_far(stage, anchor):
        if not square:
            own = lax.psum_scatter(stage[0], "tensor", scatter_dimension=0, tiled=False)
            anchor, own = tie(anchor, own)
            return [own], anchor
        own, near, far = stage
        anchor, received = tie(anchor, swap(far, 2))
        return [own, near, received], anchor

    def sum_far(stage, anchor):
        terms, anchor = terms_far(stage, anchor)
        total = terms[0].astype(f32)
        for term in terms[1:]:
            total = total + term.astype(f32)
        return total.astype(terms[0].dtype), anchor

    steps = []
    for axis, size in (("tensor", tensor_size), ("dp", group_size)):
        bit = 1
        while bit < size:
            steps.append((axis, [(i, i ^ bit) for i in range(size)]))
            bit *= 2

    def sum_step(value, step, anchor):
        anchor, received = tie(anchor, lax.ppermute(value, step[0], step[1]))
        return value + received, anchor

    def ring_plan():
        bits = [1 << k for k in range(group_size.bit_length() - 1)]
        return [(bit, True) for bit in bits] + [(bit, False) for bit in reversed(bits)]

    def ring_step(value, step, anchor):
        bit, reducing = step
        side = (lax.axis_index("dp") // bit) % 2
        pairs = [(i, i ^ bit) for i in range(group_size)]
        if reducing:
            half = value.shape[0] // 2
            sent = lax.dynamic_slice_in_dim(value, (1 - side) * half, half, axis=0)
            anchor, received = tie(anchor, lax.ppermute(sent, "dp", pairs))
            kept = lax.dynamic_slice_in_dim(value, side * half, half, axis=0)
            return (kept.astype(f32) + received.astype(f32)).astype(value.dtype), anchor
        anchor, received = tie(anchor, lax.ppermute(value, "dp", pairs))
        return in_halves(value, received, side), anchor

    def in_halves(own, other, side):
        rows = own.shape[0]
        whole = jnp.zeros((2 * rows,) + own.shape[1:], own.dtype)
        whole = lax.dynamic_update_slice_in_dim(whole, own, side * rows, axis=0)
        return lax.dynamic_update_slice_in_dim(whole, other, (1 - side) * rows, axis=0)

    def fetch_half(own):
        half = own.shape[0] // 2
        side = lax.axis_index("dp") % 2
        return swap(lax.dynamic_slice_in_dim(own, side * half, half, axis=0), 2)

    def fetch_rest(half):
        return lax.ppermute(half, "dp", [(i, i ^ 1) for i in range(group_size)])

    def in_order(stacked):
        if not square:
            return stacked
        own = lax.axis_index("tensor")
        return jnp.concatenate(
            [lax.dynamic_slice_in_dim(stacked, own ^ i, 1, axis=0) for i in range(tensor_size)], axis=0
        )

    def shards(
        patches,
        cotangent,
        empty_slots,
        dataset_id,
        dataset_weight,
        query_key_value_weight,
        qv_bias,
        output_projection_weight,
        out_bias,
        up_projection_weight,
        up_bias,
        down_projection_weight,
        down_bias,
        attn_gain,
        attn_shift,
        mlp_gain,
        mlp_shift,
    ):
        slot_count, own_rows, model = patches.shape
        width = query_key_value_weight.shape[2]
        group_slots = empty_slots.shape[0]
        slot_index = jnp.arange(group_slots * slot_count, dtype=jnp.int32) % slot_count
        filled = jnp.repeat(slot_count - empty_slots, slot_count)
        valid_all = (slot_index < filled).astype(f32)
        table_hits = dataset_id[:, None] == jnp.arange(dataset_weight.shape[0], dtype=jnp.int32)[None, :]
        numerator = jnp.sum(jnp.where(table_hits, dataset_weight[None, :], 0), axis=1).astype(f32)
        total_items = jnp.sum(valid_all)
        total_weight = jnp.sum(valid_all * numerator)
        multiplier_whole = valid_all * numerator * total_items / total_weight
        own_start = lax.axis_index("dp") * slot_count
        own_scale = lax.dynamic_slice_in_dim(multiplier_whole, own_start, slot_count)
        own_valid = lax.dynamic_slice_in_dim(valid_all, own_start, slot_count)
        all_rows = slot_count * own_rows
        row_scale = jnp.repeat(own_scale, own_rows)[:, None]
        row_valid = jnp.repeat(own_valid, own_rows)[:, None]
        gain_row, shift_row, mlp_gain_row, mlp_shift_row, out_bias_row = (
            value[None, :] for value in (attn_gain, attn_shift, mlp_gain, mlp_shift, out_bias)
        )
        proj_bias = jnp.stack([qv_bias[0], jnp.zeros_like(qv_bias[0]), qv_bias[1]])[:, None, :]
        bias_row = up_bias[None, :]

        dp_side = lax.axis_index("dp") % 2
        place = jnp.zeros((1,), jnp.int32)
        if square:
            place = place + lax.axis_index("tensor")
        fetch = fetch_half if square else gather_far
        weights_near = ()
        if square:
            weights_near = tuple(
                swap(value, 1) for value in (output_projection_weight, up_projection_weight, down_projection_weight)
            )

        def gather_rows(own):
            return lax.all_gather(own, "tensor", axis=0, tiled=True)

        normed = [norm_item(patches, i, gain_row, shift_row) for i in range(slot_count)]
        every = gather_rows(normed[0])
        bias_far = gather_far(bias_row)
        cot_low = (cotangent.astype(f32).reshape(all_rows, model) * row_scale).astype(bf16)
        early = None
        if square:
            early = cot_back(cot_low, [down_projection_weight, weights_near[2]])
            every, early = tie(every, early)
        qkvs, attended, lses, heads_own, normed_every = [], [], [], [], []
        for i in range(slot_count):
            last = i == slot_count - 1
            normed_every.append(every)
            following = None
            if not last:
                every, following = tie(every, normed[i + 1])
                following = gather_rows(following)
            qkv = (
                jnp.einsum("wz,gzh->gwh", every, query_key_value_weight, preferred_element_type=f32) + proj_bias
            ).astype(bf16)
            if i == 0:
                qkv, (weights_near, bias_far) = tie(qkv, (weights_near, bias_far))
            out, lse = attend(qkv)
            if not last:
                out, following = tie(out, following)
            if i > 0:
                out, heads_own[-1] = tie(out, heads_own[-1])
            if i == min(1, slot_count - 1):
                out, (up_own, down_own, out_own) = tie(
                    out, (up_projection_weight, down_projection_weight, output_projection_weight)
                )
                out_far = gather_far(out_own)
                up_far = fetch(up_own)
                down_far = fetch(down_own)
            if last:
                out, (out_far, up_far) = tie(out, (out_far, up_far))
            heads_own.append(exchange(out.reshape(tensor_size, own_rows, width)))
            qkvs.append(qkv)
            attended.append(out)
            lses.append(lse)
            every = following
        if square:
            up_rest = fetch_rest(up_far)
            out_weight = jnp.concatenate([out_own, weights_near[0], out_far, swap(out_far, 1)], axis=0)
        else:
            out_weight = jnp.concatenate(gather_near(out_own, out_far), axis=0)
        rows_done = None
        for i in range(slot_count):
            if i == slot_count - 1:
                rows_done, (heads_own[i], down_far) = tie(rows_done, (heads_own[i], down_far))
            rows_done = out_project(
                patches, i, place, heads_own[i], out_weight, out_bias_row, mlp_gain_row, mlp_shift_row, rows_done
            )
        if square:
            down_rest = fetch_rest(down_far)
            rows_done, up_rest = tie(rows_done, up_rest)
            up_far = in_halves(up_far, up_rest, dp_side)
            up_diag = swap(up_far, 1)
        attended_rows, residual, normed_mlp = rows_done

        bias_blocks = gather_near(bias_row, bias_far)
        if square:
            up_blocks = [up_own, weights_near[1]]
            down_blocks = [down_own, weights_near[2]]
        else:
            up_blocks = gather_near(up_own, up_far)
            down_blocks = gather_near(down_own, down_far)
        calls = tensor_size // 2
        total = None
        slopes, down_grads = [], []
        for c in range(calls):
            pair = slice(2 * c, 2 * c + 2)
            if c == 1 and square:
                total, (up_diag, down_rest) = tie(total, (up_diag, down_rest))
                down_far = in_halves(down_far, down_rest, dp_side)
                up_blocks += [up_far, up_diag]
                down_blocks += [down_far, swap(down_far, 1)]
            slope, total, *grads = mlp_forward(
                normed_mlp, cot_low, up_blocks[pair], bias_blocks[pair], down_blocks[pair], total
            )
            slopes.append(slope)
            down_grads += grads
        output = ((residual + total + down_bias) * row_valid).astype(bf16)

        cot_late, down_grads = tie(cot_low, down_grads)
        before = None
        bias_grads = []
        for c in range(calls):
            pair = slice(2 * c, 2 * c + 2)
            if c == 0 and square:
                *before, bias_grad = mlp_backward(early, slopes[c], up_blocks[pair], [], before, c, calls)
            else:
                *before, bias_grad = mlp_backward(
                    cot_late, slopes[c], up_blocks[pair], down_blocks[pair], before, c, calls
                )
            bias_grads.append(bias_grad)
            if c == 0:
                down_stage, before = sum_near(down_grads, before)
        ring = ring_plan()
        pre_grad, total = before

        grad_residual, grad_low, small_rows, pieces = residual_back(
            total, residual, cotangent, own_scale, place, out_weight, mlp_gain_row, tensor_size
        )
        down_sum, pieces = sum_far(down_stage, pieces)
        grad_attended = exchange(pieces)
        weight_grads = weight_back(normed_mlp, pre_grad, attended_rows, grad_low, tensor_size)
        weight_grads, grad_attended = tie(weight_grads, grad_attended)
        up_grads, out_grads = weight_grads[:tensor_size], weight_grads[tensor_size:]

        (up_stage, out_stage), grad_attended = sums_near([up_grads, out_grads], grad_attended)
        bias_rows = in_order(jnp.concatenate(bias_grads, axis=1).reshape(tensor_size, -1))
        smalls = jnp.concatenate([small_rows[:4].reshape(-1), bias_rows.reshape(-1)]).reshape(-1, 128)
        waiting = list(steps)

        weights_wide = query_key_value_weight.astype(f32)
        sums = None
        grad_normed = []
        for i in range(slot_count):
            last = i == slot_count - 1
            dqkv = attend_back(qkvs[i], attended[i], grad_attended, i, lses[i])
            if i >= 2:
                grad_normed[i - 2], dqkv = terms_far(grad_normed[i - 2], dqkv)
            if i >= 1 and not last:
                grad_normed[i - 1], dqkv = sum_near(grad_normed[i - 1], dqkv)
            if i == 0:
                up_sum, dqkv = sum_far(up_stage, dqkv)
                out_sum, dqkv = sum_far(out_stage, dqkv)
                up_all = lax.psum((up_sum, out_sum), "dp")
            if last:
                dqkv, up_all = tie(dqkv, up_all)
            if waiting and i > 0:
                smalls, dqkv = sum_step(smalls, waiting.pop(0), dqkv)
            if ring:
                down_sum, dqkv = ring_step(down_sum, ring.pop(0), dqkv)
            results = project_back(place, normed_every[i], dqkv, query_key_value_weight, sums, last, tensor_size)
            if not last:
                partial, sums = results[:tensor_size], results[tensor_size:]
                if waiting:
                    smalls, partial = sum_step(smalls, waiting.pop(0), partial)
                if ring:
                    down_sum, partial = ring_step(down_sum, ring.pop(0), partial)
            else:
                *sums, qkv_low = results
                qkv_low, (dqkv, grad_residual) = tie(qkv_low, (dqkv, grad_residual))
                qkv_all = lax.psum(qkv_low, "dp")
                partial = project_rows(place, dqkv, query_key_value_weight, tensor_size)
                if i >= 1:
                    grad_normed[i - 1], partial = sum_near(grad_normed[i - 1], partial)
                raw = jnp.stack(
                    [
                        jnp.sum(sums[0] * weights_wide, axis=(0, 2)),
                        jnp.sum(sums[1][:3, None, :] * weights_wide, axis=(0, 2)),
                    ]
                )
                for step in steps:
                    raw = raw + lax.ppermute(raw, step[0], step[1])
            grad_normed.append(partial)
        grad_inputs = None
        for i in range(slot_count):
            if i == slot_count - 1:
                grad_normed[i], grad_residual = sum_near(grad_normed[i], grad_residual)
            terms = grad_normed[i]
            if i >= slot_count - 2:
                terms, grad_residual = terms_far(terms, grad_residual)
            grad_inputs = input_back(terms, patches, i, grad_residual, gain_row, grad_inputs)
        grad_inputs, qkv_all = tie(grad_inputs, qkv_all)
        for step in ring:
            down_sum = ring_step(down_sum, step, place)[0]
        for step in waiting:
            smalls = sum_step(smalls, step, place)[0]
        weight_grad = qkv_all[:, :model].astype(f32)
        columns = qkv_all[:, model].astype(f32)
        up_all, out_all = [value.astype(f32) for value in up_all]
        down_all = down_sum.astype(f32)
        inverse = 1.0 / total_items
        smalls = smalls.reshape(-1) * inverse
        small_rows = smalls[: 4 * model].reshape(4, model)
        units = up_bias.shape[0]
        bias_all = lax.dynamic_slice_in_dim(smalls[4 * model :], lax.axis_index("tensor") * units, units)
        shift_all = raw[1] * inverse
        gain_all = (raw[0] * inverse - attn_shift * shift_all) / attn_gain
        columns = columns * inverse
        return (
            output.reshape(patches.shape),
            grad_inputs,
            weight_grad * inverse,
            jnp.stack([columns[0], columns[2]]),
            out_all * inverse,
            small_rows[2],
            up_all * inverse,
            bias_all,
            down_all * inverse,
            small_rows[3],
            gain_all,
            shift_all,
            small_rows[0],
            small_rows[1],
        )

    return shards


def solution(mesh):
    items = P("dp", "tensor", None)
    return jax.shard_map(
        make_shards(mesh.shape["tensor"], mesh.shape["dp"]),
        mesh=mesh,
        in_specs=(
            items,
            items,
            P(),
            P(),
            P(),
            P(None, None, "tensor"),
            P(None, "tensor"),
            P("tensor", None),
            P(),
            P(None, "tensor"),
            P("tensor"),
            P("tensor", None),
            P(),
            P(),
            P(),
            P(),
            P(),
        ),
        out_specs=(
            items,
            items,
            P(None, None, "tensor"),
            P(None, "tensor"),
            P("tensor", None),
            P(),
            P(None, "tensor"),
            P("tensor"),
            P("tensor", None),
            P(),
            P(),
            P(),
            P(),
            P(),
        ),
        check_vma=False,
    )
```

```python
import jax
import jax.numpy as jnp
from jax import lax
from jax.experimental import pallas as pl
from jax.experimental.pallas import tpu as pltpu
from jax.sharding import PartitionSpec as P

HD = 64
SCORE_SCALE = HD ** (-0.5)
LOG2E = 1.4426950408889634
SQRT_HALF = 0.7071067811865476
INV_SQRT_2PI = 0.3989422804014327
epsilon = 1e-05
f32 = jnp.float32
bf16 = jnp.bfloat16
VMEM_LIMIT = 60 << 20
COST_SCALE = 64


def nn(a, b):
    return lax.dot_general(a, b, (((1,), (0,)), ((), ())), preferred_element_type=f32)


def nt(a, b):
    return lax.dot_general(a, b, (((1,), (1,)), ((), ())), preferred_element_type=f32)


def tn(a, b):
    return lax.dot_general(a, b, (((0,), (0,)), ((), ())), preferred_element_type=f32)


def tie(first, second):
    return lax.optimization_barrier((first, second))


def largest_block(extent, limit):
    block = min(extent, limit)
    while extent % block:
        block //= 2
    return block


def norm_rows(source, norm_gain, norm_shift):
    row_mean = jnp.mean(source, axis=-1, keepdims=True)
    centred = source - row_mean
    spread = jnp.mean(centred * centred, axis=-1, keepdims=True)
    return centred * lax.rsqrt(spread + epsilon) * norm_gain + norm_shift


def attend(qkv):
    _, length, width = qkv.shape
    lanes = min(128, width)
    heads = lanes // HD
    qblock = largest_block(length, 2048)
    to_log2 = SCORE_SCALE * LOG2E

    def body(q_ref, k_ref, v_ref, out_ref, lse_ref):
        queries = q_ref[...]
        keys = k_ref[...]
        values_t = v_ref[...].T
        lane = lax.broadcasted_iota(jnp.int32, (1, lanes), 1)
        outs = []
        for h in range(heads):
            own = queries
            if heads > 1:
                own = jnp.where(lane // HD == h, queries, jnp.zeros_like(queries))
            scores = nt(keys, own)
            top = jnp.max(scores, axis=0, keepdims=True)
            exp_scores = jnp.exp2((scores - top) * to_log2)
            total = jnp.sum(exp_scores, axis=0, keepdims=True)
            outs.append(nn(values_t[h * HD : (h + 1) * HD, :], exp_scores.astype(bf16)) / total)
            lse_ref[h : h + 1, :] = top * to_log2 + jnp.log2(total)
        out_ref[...] = jnp.concatenate(outs, axis=0).T.astype(bf16)

    pairs = width // lanes
    return pl.pallas_call(
        body,
        grid=(pairs, length // qblock),
        in_specs=[
            pl.BlockSpec((None, qblock, lanes), lambda h, j: (0, j, h)),
            pl.BlockSpec((None, length, lanes), lambda h, j: (1, 0, h)),
            pl.BlockSpec((None, length, lanes), lambda h, j: (2, 0, h)),
        ],
        out_specs=[
            pl.BlockSpec((qblock, lanes), lambda h, j: (j, h)),
            pl.BlockSpec((None, heads, qblock), lambda h, j: (h, 0, j)),
        ],
        out_shape=[
            jax.ShapeDtypeStruct((length, width), bf16),
            jax.ShapeDtypeStruct((pairs, heads, length), f32),
        ],
        compiler_params=pltpu.CompilerParams(vmem_limit_bytes=VMEM_LIMIT),
        cost_estimate=pl.CostEstimate(
            flops=8 * length * length * width // COST_SCALE,
            transcendentals=0,
            bytes_accessed=length * width,
        ),
        name="attend",
    )(qkv, qkv, qkv)


def attend_back(qkv, attended, grad_attended, item, lse):
    _, length, width = qkv.shape
    lanes = min(128, width)
    shards_of = grad_attended.shape[0]
    heads = lanes // HD
    kblock = largest_block(length, 1024)
    kblocks = length // kblock
    to_log2 = SCORE_SCALE * LOG2E

    def body(q_ref, k_ref, v_ref, out_ref, grad_ref, lse_ref, dqkv_ref, dq_acc, row_dot):
        kb = pl.program_id(1)
        queries = q_ref[...]
        grads = grad_ref[...].reshape(length, lanes)
        keys = k_ref[...]
        values = v_ref[...]
        keys_t = keys.T
        lane = lax.broadcasted_iota(jnp.int32, (1, lanes), 1)

        @pl.when(kb == 0)
        def _():
            product = out_ref[...].astype(f32) * grads.astype(f32)
            high = product.astype(bf16)
            rest = (product - high.astype(f32)).astype(bf16)
            pick = lax.broadcasted_iota(jnp.int32, (8, lanes), 0)
            mask = (lax.broadcasted_iota(jnp.int32, (8, lanes), 1) // HD == pick).astype(f32).astype(bf16)
            row_dot[...] = nt(mask, high) + nt(mask, rest)

        dk = None
        dv = None
        dqs = []
        for h in range(heads):
            own_q = queries
            own_g = grads
            if heads > 1:
                mine = lane // HD == h
                own_q = jnp.where(mine, queries, jnp.zeros_like(queries))
                own_g = jnp.where(mine, grads, jnp.zeros_like(grads))
            scores = nt(keys, own_q)
            weights = jnp.exp2(scores * to_log2 - lse_ref[h : h + 1, :])
            grad_weights = nt(values, own_g)
            grad_scores = (weights * (grad_weights - row_dot[h : h + 1, :])).astype(bf16)
            dv_h = nn(weights.astype(bf16), own_g)
            dk_h = nn(grad_scores, own_q)
            dv = dv_h if dv is None else dv + dv_h
            dk = dk_h if dk is None else dk + dk_h
            dqs.append(nn(keys_t[h * HD : (h + 1) * HD, :], grad_scores))
        rows = pl.ds(pl.multiple_of(kb * kblock, kblock), kblock)
        dqkv_ref[1, rows, :] = (dk * SCORE_SCALE).astype(bf16)
        dqkv_ref[2, rows, :] = dv.astype(bf16)
        dq = jnp.concatenate(dqs, axis=0)
        if kblocks == 1:
            dqkv_ref[0] = (dq * SCORE_SCALE).T.astype(bf16)
            return

        @pl.when(kb == 0)
        def _():
            dq_acc[...] = dq

        @pl.when((kb > 0) & (kb < kblocks - 1))
        def _():
            dq_acc[...] += dq

        @pl.when(kb == kblocks - 1)
        def _():
            dqkv_ref[0] = ((dq_acc[...] + dq) * SCORE_SCALE).T.astype(bf16)

    pairs = width // lanes
    return pl.pallas_call(
        body,
        grid=(pairs, kblocks),
        in_specs=[
            pl.BlockSpec((None, length, lanes), lambda h, kb: (0, 0, h)),
            pl.BlockSpec((None, kblock, lanes), lambda h, kb: (1, kb, h)),
            pl.BlockSpec((None, kblock, lanes), lambda h, kb: (2, kb, h)),
            pl.BlockSpec((length, lanes), lambda h, kb: (0, h)),
            pl.BlockSpec((shards_of, length // shards_of, lanes), lambda h, kb: (0, item, h)),
            pl.BlockSpec((None, heads, length), lambda h, kb: (h, 0, 0)),
        ],
        out_specs=pl.BlockSpec((3, length, lanes), lambda h, kb: (0, 0, h)),
        out_shape=jax.ShapeDtypeStruct((3, length, width), bf16),
        scratch_shapes=[pltpu.VMEM((lanes, length), f32), pltpu.VMEM((8, length), f32)],
        compiler_params=pltpu.CompilerParams(vmem_limit_bytes=VMEM_LIMIT),
        cost_estimate=pl.CostEstimate(
            flops=20 * length * length * width // COST_SCALE,
            transcendentals=0,
            bytes_accessed=length * width,
        ),
        name="attend_back",
    )(qkv, qkv, qkv, attended, grad_attended, lse)


def hint(flops, size):
    return pl.CostEstimate(flops=flops // COST_SCALE, transcendentals=0, bytes_accessed=size)


def params():
    return pltpu.CompilerParams(vmem_limit_bytes=VMEM_LIMIT)


def norm_item(patches, item, norm_gain, norm_shift):
    _, rows, model = patches.shape
    block = largest_block(rows, 256)

    def body(x_ref, gain_ref, shift_ref, out_ref):
        out_ref[...] = norm_rows(x_ref[...].astype(f32), gain_ref[...], shift_ref[...]).astype(bf16)

    vector = pl.BlockSpec((1, model), lambda i: (0, 0))
    return pl.pallas_call(
        body,
        grid=(rows // block,),
        in_specs=[pl.BlockSpec((None, block, model), lambda i: (item, i, 0)), vector, vector],
        out_specs=pl.BlockSpec((block, model), lambda i: (i, 0)),
        out_shape=jax.ShapeDtypeStruct((rows, model), bf16),
        compiler_params=params(),
        cost_estimate=hint(0, rows * model),
        name="norm_item",
    )(patches, norm_gain, norm_shift)


def out_project(patches, item, place, heads, weight, out_bias, norm_gain, norm_shift, before):
    slots, rows, model = patches.shape
    block = largest_block(rows, 256)
    steps = rows // block
    count, _, width = heads.shape

    def body(*refs):
        place_ref, x_ref, weight_ref, bias_ref, gain_ref, shift_ref, head_ref = refs[:7]
        attended_ref, residual_ref, normed_ref = refs[-3:]
        for k in range(count):
            attended_ref[:, k * width : (k + 1) * width] = head_ref[place_ref[0] ^ k]
        attended = attended_ref[...]
        residual = x_ref[...].astype(f32) + nn(attended, weight_ref[...]) + bias_ref[...]
        residual_ref[...] = residual
        normed_ref[...] = norm_rows(residual, gain_ref[...], shift_ref[...]).astype(bf16)

    vector = pl.BlockSpec((1, model), lambda i: (0, 0))
    placed = pl.BlockSpec((block, model), lambda i: (item * steps + i, 0))
    operands = [place, patches, weight, out_bias, norm_gain, norm_shift, heads]
    in_specs = [
        pl.BlockSpec(memory_space=pltpu.SMEM),
        pl.BlockSpec((None, block, model), lambda i: (item, i, 0)),
        pl.BlockSpec((model, model), lambda i: (0, 0)),
        vector,
        vector,
        vector,
        pl.BlockSpec((count, block, width), lambda i: (0, i, 0)),
    ]
    aliases = {}
    if before is not None:
        aliases = {len(operands) + k: k for k in range(3)}
        operands += before
        in_specs += [pl.BlockSpec(memory_space=pl.ANY)] * 3
    return pl.pallas_call(
        body,
        grid=(steps,),
        in_specs=in_specs,
        out_specs=[placed] * 3,
        out_shape=[jax.ShapeDtypeStruct((slots * rows, model), t) for t in (bf16, f32, bf16)],
        input_output_aliases=aliases,
        compiler_params=params(),
        cost_estimate=hint(2 * rows * model * model, rows * model),
        name="out_project",
    )(*operands)


def residual_back(total, residual, cotangent, scale, place, weight, norm_gain, pieces):
    slots, rows, model = cotangent.shape
    block = largest_block(rows, 256)
    steps = rows // block
    piece = model // pieces

    def body(*refs):
        place_ref, total_ref, residual_ref, cot_ref, scale_ref, weight_ref, gain_ref = refs[:7]
        grad_ref, low_ref, sum_ref, attended_ref = refs[-4:]
        residual = residual_ref[...]
        centred = residual - jnp.mean(residual, axis=-1, keepdims=True)
        rate = lax.rsqrt(jnp.mean(centred * centred, axis=-1, keepdims=True) + epsilon)
        xhat = centred * rate
        grad_normed = total_ref[...]
        scaled = grad_normed * gain_ref[...]
        inner = jnp.mean(scaled, axis=-1, keepdims=True)
        outer = jnp.mean(scaled * xhat, axis=-1, keepdims=True)
        cot = cot_ref[...].astype(f32) * scale_ref[pl.program_id(0) // steps]
        grad = cot + rate * (scaled - inner - xhat * outer)
        grad_ref[...] = grad
        low = grad.astype(bf16)
        low_ref[...] = low

        @pl.when(pl.program_id(0) == 0)
        def _():
            sum_ref[...] = jnp.zeros_like(sum_ref)

        for k, value in enumerate((grad_normed * xhat, grad_normed, grad, cot)):
            sum_ref[k : k + 1, :] += jnp.sum(value, axis=0, keepdims=True)
        attended = nt(low, weight_ref[...]).astype(bf16)
        for k in range(pieces):
            attended_ref[place_ref[0] ^ k] = attended[:, k * piece : (k + 1) * piece]

    row_spec = pl.BlockSpec((block, model), lambda i: (i, 0))
    return pl.pallas_call(
        body,
        grid=(slots * steps,),
        in_specs=[
            pl.BlockSpec(memory_space=pltpu.SMEM),
            row_spec,
            row_spec,
            pl.BlockSpec((None, block, model), lambda i: (i // steps, i % steps, 0)),
            pl.BlockSpec(memory_space=pltpu.SMEM),
            pl.BlockSpec((model, model), lambda i: (0, 0)),
            pl.BlockSpec((1, model), lambda i: (0, 0)),
        ],
        out_specs=[
            row_spec,
            row_spec,
            pl.BlockSpec((8, model), lambda i: (0, 0)),
            pl.BlockSpec((pieces, block, piece), lambda i: (0, i, 0)),
        ],
        out_shape=[
            jax.ShapeDtypeStruct((slots * rows, model), f32),
            jax.ShapeDtypeStruct((slots * rows, model), bf16),
            jax.ShapeDtypeStruct((8, model), f32),
            jax.ShapeDtypeStruct((pieces, slots * rows, piece), bf16),
        ],
        compiler_params=params(),
        cost_estimate=hint(2 * slots * rows * model * model, rows * model),
        name="residual_back",
    )(place, total, residual, cotangent, scale, weight, norm_gain)


def input_back(terms, patches, item, grad_residual, norm_gain, before):
    slots, rows, model = patches.shape
    block = largest_block(rows, 256)
    count = len(terms)

    def body(*refs):
        x_ref, grad_ref, gain_ref = refs[:3]
        out_ref = refs[-1]
        grad_normed = refs[3][...].astype(f32)
        for k in range(1, count):
            grad_normed = grad_normed + refs[3 + k][...].astype(f32)
        source = x_ref[...].astype(f32)
        centred = source - jnp.mean(source, axis=-1, keepdims=True)
        rate = lax.rsqrt(jnp.mean(centred * centred, axis=-1, keepdims=True) + epsilon)
        xhat = centred * rate
        scaled = grad_normed * gain_ref[...]
        inner = jnp.mean(scaled, axis=-1, keepdims=True)
        outer = jnp.mean(scaled * xhat, axis=-1, keepdims=True)
        out_ref[...] = (grad_ref[...] + rate * (scaled - inner - xhat * outer)).astype(bf16)

    row_spec = pl.BlockSpec((block, model), lambda i: (i, 0))
    placed = pl.BlockSpec((None, block, model), lambda i: (item, i, 0))
    operands = [patches, grad_residual, norm_gain, *terms]
    steps = rows // block
    grad_spec = pl.BlockSpec((block, model), lambda i: (item * steps + i, 0))
    in_specs = [placed, grad_spec, pl.BlockSpec((1, model), lambda i: (0, 0))] + [row_spec] * count
    aliases = {}
    if before is not None:
        aliases = {len(operands): 0}
        operands.append(before)
        in_specs.append(pl.BlockSpec(memory_space=pl.ANY))
    return pl.pallas_call(
        body,
        grid=(rows // block,),
        in_specs=in_specs,
        out_specs=placed,
        out_shape=jax.ShapeDtypeStruct((slots, rows, model), bf16),
        input_output_aliases=aliases,
        compiler_params=params(),
        cost_estimate=hint(0, rows * model),
        name="input_back",
    )(*operands)


def layer_out(total, residual, down_bias, valid, shape):
    slots, rows, model = shape
    block = largest_block(rows, 256)
    steps = rows // block

    def body(total_ref, residual_ref, bias_ref, valid_ref, out_ref):
        value = residual_ref[...] + total_ref[...] + bias_ref[...]
        out_ref[...] = (value * valid_ref[pl.program_id(0) // steps]).astype(bf16)

    row_spec = pl.BlockSpec((block, model), lambda i: (i, 0))
    return pl.pallas_call(
        body,
        grid=(slots * steps,),
        in_specs=[
            row_spec,
            row_spec,
            pl.BlockSpec((1, model), lambda i: (0, 0)),
            pl.BlockSpec(memory_space=pltpu.SMEM),
        ],
        out_specs=pl.BlockSpec((None, block, model), lambda i: (i // steps, i % steps, 0)),
        out_shape=jax.ShapeDtypeStruct(shape, bf16),
        compiler_params=params(),
        cost_estimate=hint(0, rows * model),
        name="layer_out",
    )(total, residual, down_bias, valid)


def mlp_forward(normed, cot, ups, biases, downs, total):
    rows, model = normed.shape
    count = len(ups)
    units = ups[0].shape[1]
    block = largest_block(rows, 512)
    steps = rows // block
    first = total is None

    def body(*refs):
        x_ref, cot_ref = refs[:2]
        up_refs, bias_refs, down_refs = (refs[2 + k * count : 2 + (k + 1) * count] for k in range(3))
        rest = refs[2 + 3 * count :]
        if not first:
            before_ref = rest[0]
            rest = rest[1:]
        slope_ref, sum_ref = rest[:2]
        grad_refs = rest[2 : 2 + count]
        hidden_ref, acc_ref = rest[2 + count :]
        step = pl.program_id(0)
        part = largest_block(units, 256)
        for k in range(count):
            for j in range(units // part):
                cols = slice(j * part, (j + 1) * part)
                wide = slice(k * units + j * part, k * units + (j + 1) * part)
                pre = nn(x_ref[...], up_refs[k][:, cols]) + bias_refs[k][:, cols]
                cdf = 0.5 + 0.5 * lax.erf(pre * SQRT_HALF)
                density = jnp.exp2(pre * pre * (-0.5 * LOG2E)) * INV_SQRT_2PI
                hidden_ref[:, wide] = (pre * cdf).astype(bf16)
                slope_ref[:, wide] = (cdf + pre * density).astype(bf16)
        out = None if first else before_ref[...]
        for k in range(count):
            hidden = hidden_ref[:, k * units : (k + 1) * units]
            product = nn(hidden, down_refs[k][...])
            out = product if out is None else out + product
            grad = tn(hidden, cot_ref[...])

            @pl.when(step == 0)
            def _():
                acc_ref[k] = grad

            @pl.when(step > 0)
            def _():
                acc_ref[k] += grad

        sum_ref[...] = out

        @pl.when(step == steps - 1)
        def _():
            for k in range(count):
                grad_refs[k][...] = acc_ref[k].astype(bf16)

    row_spec = pl.BlockSpec((block, model), lambda i: (i, 0))
    slope_spec = pl.BlockSpec((block, count * units), lambda i: (i, 0))
    up_spec = pl.BlockSpec((model, units), lambda i: (0, 0), pipeline_mode=pl.Buffered(1))
    down_spec = pl.BlockSpec((units, model), lambda i: (0, 0), pipeline_mode=pl.Buffered(1))
    grad_spec = pl.BlockSpec((units, model), lambda i: (0, 0))
    operands = [normed, cot, *ups, *biases, *downs]
    in_specs = [row_spec, row_spec] + [up_spec] * count
    in_specs += [pl.BlockSpec((1, units), lambda i: (0, 0))] * count + [down_spec] * count
    aliases = {}
    if not first:
        aliases = {len(operands): 1}
        operands.append(total)
        in_specs.append(row_spec)
    return pl.pallas_call(
        body,
        grid=(steps,),
        in_specs=in_specs,
        out_specs=[slope_spec, row_spec] + [grad_spec] * count,
        out_shape=[
            jax.ShapeDtypeStruct((rows, count * units), bf16),
            jax.ShapeDtypeStruct((rows, model), f32),
        ]
        + [jax.ShapeDtypeStruct((units, model), bf16)] * count,
        scratch_shapes=[pltpu.VMEM((block, count * units), bf16), pltpu.VMEM((count, units, model), f32)],
        input_output_aliases=aliases,
        compiler_params=params(),
        cost_estimate=hint(6 * rows * model * units * count, rows * units),
        name="mlp_forward",
    )(*operands)


def cot_back(cot, downs):
    rows, model = cot.shape
    count = len(downs)
    units = downs[0].shape[0]
    block = largest_block(rows, 512)

    def body(cot_ref, *refs):
        for k in range(count):
            refs[count][:, k * units : (k + 1) * units] = nt(cot_ref[...], refs[k][...]).astype(bf16)

    return pl.pallas_call(
        body,
        grid=(rows // block,),
        in_specs=[pl.BlockSpec((block, model), lambda i: (i, 0))]
        + [pl.BlockSpec((units, model), lambda i: (0, 0))] * count,
        out_specs=pl.BlockSpec((block, count * units), lambda i: (i, 0)),
        out_shape=jax.ShapeDtypeStruct((rows, count * units), bf16),
        compiler_params=params(),
        cost_estimate=hint(2 * rows * model * units * count, rows * units),
        name="cot_back",
    )(cot, *downs)


def mlp_backward(cot, slope, ups, downs, before, index, calls):
    rows, _ = cot.shape
    model = ups[0].shape[0]
    count = len(ups)
    units = ups[0].shape[1]
    block = largest_block(rows, 512)
    first = before is None

    def body(*refs):
        cot_ref, slope_ref = refs[:2]
        up_refs, down_refs = refs[2 : 2 + count], refs[2 + count : 2 + count + len(downs)]
        grad_ref, sum_ref, bias_ref = refs[-3:]

        @pl.when(pl.program_id(0) == 0)
        def _():
            bias_ref[...] = jnp.zeros_like(bias_ref)

        out = None if first else refs[3 + count + len(downs)][...]
        part = largest_block(units, 512)
        for k in range(count):
            for j in range(units // part):
                rows_of = slice(j * part, (j + 1) * part)
                wide = slice(k * units + j * part, k * units + (j + 1) * part)
                if downs:
                    product = nt(cot_ref[...], down_refs[k][rows_of, :])
                else:
                    product = cot_ref[:, wide].astype(f32)
                low = (product * slope_ref[:, wide].astype(f32)).astype(bf16)
                grad_ref[:, wide] = low
                bias_ref[:, wide] += jnp.sum(low.astype(f32), axis=0, keepdims=True)
            product = nt(grad_ref[:, k * units : (k + 1) * units], up_refs[k][...])
            out = product if out is None else out + product
        sum_ref[...] = out

    row_spec = pl.BlockSpec((block, model), lambda i: (i, 0))
    slope_spec = pl.BlockSpec((block, count * units), lambda i: (i, 0))
    up_spec = pl.BlockSpec((model, units), lambda i: (0, 0), pipeline_mode=pl.Buffered(1))
    down_spec = pl.BlockSpec((units, model), lambda i: (0, 0), pipeline_mode=pl.Buffered(1))
    operands = [cot, slope, *ups, *downs]
    in_specs = [row_spec if downs else slope_spec, slope_spec] + [up_spec] * count + [down_spec] * len(downs)
    aliases = {}
    if not first:
        aliases = {len(operands): 0, len(operands) + 1: 1}
        operands += before
        in_specs += [pl.BlockSpec(memory_space=pl.ANY), row_spec]
    return pl.pallas_call(
        body,
        grid=(rows // block,),
        in_specs=in_specs,
        out_specs=[
            pl.BlockSpec((block, count * units), lambda i: (i, index)),
            row_spec,
            pl.BlockSpec((1, count * units), lambda i: (0, 0)),
        ],
        out_shape=[
            jax.ShapeDtypeStruct((rows, calls * count * units), bf16),
            jax.ShapeDtypeStruct((rows, model), f32),
            jax.ShapeDtypeStruct((1, count * units), f32),
        ],
        input_output_aliases=aliases,
        compiler_params=params(),
        cost_estimate=hint(4 * rows * model * units * count, rows * units),
        name="mlp_backward",
    )(*operands)


def weight_back(normed, pre_grad, attended, grad_low, pieces):
    rows, model = normed.shape
    every = pre_grad.shape[1]
    units = every // pieces
    piece = model // pieces
    block = largest_block(rows, 512)
    steps = rows // block

    def body(x_ref, pre_ref, attended_ref, grad_ref, *refs):
        up_refs, out_refs = refs[:pieces], refs[pieces : 2 * pieces]
        up_acc, out_acc = refs[2 * pieces :]
        step = pl.program_id(0)

        @pl.when(step == 0)
        def _():
            up_acc[...] = jnp.zeros_like(up_acc)
            out_acc[...] = jnp.zeros_like(out_acc)

        part = largest_block(every, 512)
        for j in range(every // part):
            cols = slice(j * part, (j + 1) * part)
            up_acc[:, cols] += tn(x_ref[...], pre_ref[:, cols])
        part = largest_block(model, 512)
        for j in range(model // part):
            cols = slice(j * part, (j + 1) * part)
            out_acc[:, cols] += tn(attended_ref[...], grad_ref[:, cols])

        @pl.when(step == steps - 1)
        def _():
            for k in range(pieces):
                up_refs[k][...] = up_acc[:, k * units : (k + 1) * units].astype(bf16)
                out_refs[k][...] = out_acc[k * piece : (k + 1) * piece, :].astype(bf16)

    row_spec = pl.BlockSpec((block, model), lambda i: (i, 0))
    return pl.pallas_call(
        body,
        grid=(steps,),
        in_specs=[row_spec, pl.BlockSpec((block, every), lambda i: (i, 0)), row_spec, row_spec],
        out_specs=[pl.BlockSpec((model, units), lambda i: (0, 0))] * pieces
        + [pl.BlockSpec((piece, model), lambda i: (0, 0))] * pieces,
        out_shape=[jax.ShapeDtypeStruct((model, units), bf16)] * pieces
        + [jax.ShapeDtypeStruct((piece, model), bf16)] * pieces,
        scratch_shapes=[pltpu.VMEM((model, every), f32), pltpu.VMEM((model, model), f32)],
        compiler_params=params(),
        cost_estimate=hint(2 * rows * model * (every + model), rows * model),
        name="weight_back",
    )(normed, pre_grad, attended, grad_low)


def project_back(place, normed, dqkv, weight, before, last, pieces):
    rows, model = normed.shape
    width = weight.shape[2]
    block = rows // pieces
    steps = pieces
    first = before is None
    given = 0 if last else pieces

    def kernel(*refs):
        place_ref, normed_ref, dqkv_ref, weight_ref = refs[:4]
        rest = refs[4:]
        if not first:
            wgrad_before, column_before = rest[:2]
            rest = rest[2:]
        row_refs, rest = rest[:given], rest[given:]
        wgrad_ref, column_ref = rest[:2]
        step = pl.program_id(0)

        @pl.when(step == 0)
        def _():
            if first:
                wgrad_ref[...] = jnp.zeros_like(wgrad_ref)
                column_ref[...] = jnp.zeros_like(column_ref)
            else:
                wgrad_ref[...] = wgrad_before[...]
                column_ref[...] = column_before[...]

        if not last:
            row_grad = nt(dqkv_ref[0], weight_ref[0])
            for c in range(1, 3):
                row_grad = row_grad + nt(dqkv_ref[c], weight_ref[c])
            row_grad = row_grad.astype(bf16)
            for k in range(pieces):

                @pl.when(step == place_ref[0] ^ k)
                def _():
                    row_refs[k][...] = row_grad

        for c in range(3):
            wgrad_ref[c] += tn(normed_ref[...], dqkv_ref[c])
            column_ref[c : c + 1, :] += jnp.sum(dqkv_ref[c].astype(f32), axis=0, keepdims=True)
        if last:
            low_ref = rest[2]

            @pl.when(step == steps - 1)
            def _():
                low_ref[:, :model, :] = wgrad_ref[...].astype(bf16)
                for c in range(3):
                    row = jnp.broadcast_to(column_ref[c : c + 1, :], (16, width))
                    low_ref[c, model:, :] = row.astype(bf16)

    whole = pl.BlockSpec((3, model, width), lambda i: (0, 0, 0))
    columns = pl.BlockSpec((8, width), lambda i: (0, 0))
    row_spec = pl.BlockSpec((block, model), lambda i: (i, 0))
    operands = [place, normed, dqkv, weight]
    in_specs = [pl.BlockSpec(memory_space=pltpu.SMEM), row_spec, pl.BlockSpec((3, block, width), lambda i: (0, i, 0)), whole]
    if not first:
        operands += list(before)
        in_specs += [whole, columns]
    out_specs = [pl.BlockSpec((block, model), lambda i: (0, 0))] * given + [whole, columns]
    out_shape = [jax.ShapeDtypeStruct((block, model), bf16)] * given + [
        jax.ShapeDtypeStruct((3, model, width), f32),
        jax.ShapeDtypeStruct((8, width), f32),
    ]
    if last:
        out_specs.append(pl.BlockSpec((3, model + 16, width), lambda i: (0, 0, 0)))
        out_shape.append(jax.ShapeDtypeStruct((3, model + 16, width), bf16))
    return pl.pallas_call(
        kernel,
        grid=(steps,),
        in_specs=in_specs,
        out_specs=out_specs,
        out_shape=out_shape,
        input_output_aliases={} if first else {4: given, 5: given + 1},
        compiler_params=pltpu.CompilerParams(vmem_limit_bytes=VMEM_LIMIT),
        cost_estimate=pl.CostEstimate(
            flops=12 * rows * model * width // COST_SCALE,
            transcendentals=0,
            bytes_accessed=rows * width,
        ),
        name="project_back",
    )(*operands)


def project_rows(place, dqkv, weight, pieces):
    _, rows, width = dqkv.shape
    model = weight.shape[1]
    block = rows // pieces

    def kernel(place_ref, dqkv_ref, weight_ref, *row_refs):
        row_grad = nt(dqkv_ref[0], weight_ref[0])
        for c in range(1, 3):
            row_grad = row_grad + nt(dqkv_ref[c], weight_ref[c])
        row_grad = row_grad.astype(bf16)
        for k in range(pieces):

            @pl.when(pl.program_id(0) == place_ref[0] ^ k)
            def _():
                row_refs[k][...] = row_grad

    return pl.pallas_call(
        kernel,
        grid=(pieces,),
        in_specs=[
            pl.BlockSpec(memory_space=pltpu.SMEM),
            pl.BlockSpec((3, block, width), lambda i: (0, i, 0)),
            pl.BlockSpec((3, model, width), lambda i: (0, 0, 0)),
        ],
        out_specs=[pl.BlockSpec((block, model), lambda i: (0, 0))] * pieces,
        out_shape=[jax.ShapeDtypeStruct((block, model), bf16)] * pieces,
        compiler_params=params(),
        cost_estimate=hint(6 * rows * model * width, rows * width),
        name="project_rows",
    )(place, dqkv, weight)


def make_shards(tensor_size, group_size):
    square = tensor_size == 4

    def swap(value, bits):
        return lax.ppermute(value, "tensor", [(i, i ^ bits) for i in range(tensor_size)])

    def gather_far(own):
        return swap(own, 2) if square else lax.all_gather(own, "tensor")

    def gather_near(own, far):
        if not square:
            return [far[i] for i in range(tensor_size)]
        return [own, swap(own, 1), far, swap(far, 1)]

    def exchange(stacked):
        return lax.all_to_all(stacked, "tensor", 0, 0)

    def sum_near(blocks, anchor):
        if not square:
            return (jnp.stack(blocks),), anchor
        anchor, (near_own, near_far) = tie(anchor, (swap(blocks[1], 1), swap(blocks[3], 1)))
        far = (blocks[2].astype(f32) + near_far.astype(f32)).astype(blocks[2].dtype)
        return (blocks[0], near_own, far), anchor

    def sums_near(lists, anchor):
        if not square:
            return [sum_near(blocks, anchor)[0] for blocks in lists], anchor
        moved = [(swap(blocks[1], 1), swap(blocks[3], 1)) for blocks in lists]
        anchor, moved = tie(anchor, moved)
        return [
            (blocks[0], own, (blocks[2].astype(f32) + far.astype(f32)).astype(blocks[2].dtype))
            for blocks, (own, far) in zip(lists, moved, strict=True)
        ], anchor

    def terms_far(stage, anchor):
        if not square:
            own = lax.psum_scatter(stage[0], "tensor", scatter_dimension=0, tiled=False)
            anchor, own = tie(anchor, own)
            return [own], anchor
        own, near, far = stage
        anchor, received = tie(anchor, swap(far, 2))
        return [own, near, received], anchor

    def sum_far(stage, anchor):
        terms, anchor = terms_far(stage, anchor)
        total = terms[0].astype(f32)
        for term in terms[1:]:
            total = total + term.astype(f32)
        return total.astype(terms[0].dtype), anchor

    steps = []
    for axis, size in (("tensor", tensor_size), ("dp", group_size)):
        bit = 1
        while bit < size:
            steps.append((axis, [(i, i ^ bit) for i in range(size)]))
            bit *= 2

    def sum_step(value, step, anchor):
        anchor, received = tie(anchor, lax.ppermute(value, step[0], step[1]))
        return value + received, anchor

    def ring_plan():
        bits = [1 << k for k in range(group_size.bit_length() - 1)]
        return [(bit, True) for bit in bits] + [(bit, False) for bit in reversed(bits)]

    def ring_step(value, step, anchor):
        bit, reducing = step
        side = (lax.axis_index("dp") // bit) % 2
        pairs = [(i, i ^ bit) for i in range(group_size)]
        if reducing:
            half = value.shape[0] // 2
            sent = lax.dynamic_slice_in_dim(value, (1 - side) * half, half, axis=0)
            anchor, received = tie(anchor, lax.ppermute(sent, "dp", pairs))
            kept = lax.dynamic_slice_in_dim(value, side * half, half, axis=0)
            return (kept.astype(f32) + received.astype(f32)).astype(value.dtype), anchor
        anchor, received = tie(anchor, lax.ppermute(value, "dp", pairs))
        return in_halves(value, received, side), anchor

    def in_halves(own, other, side):
        rows = own.shape[0]
        whole = jnp.zeros((2 * rows,) + own.shape[1:], own.dtype)
        whole = lax.dynamic_update_slice_in_dim(whole, own, side * rows, axis=0)
        return lax.dynamic_update_slice_in_dim(whole, other, (1 - side) * rows, axis=0)

    def fetch_half(own):
        half = own.shape[0] // 2
        side = lax.axis_index("dp") % 2
        return swap(lax.dynamic_slice_in_dim(own, side * half, half, axis=0), 2)

    def fetch_rest(half):
        return lax.ppermute(half, "dp", [(i, i ^ 1) for i in range(group_size)])

    def in_order(stacked):
        if not square:
            return stacked
        own = lax.axis_index("tensor")
        return jnp.concatenate(
            [lax.dynamic_slice_in_dim(stacked, own ^ i, 1, axis=0) for i in range(tensor_size)], axis=0
        )

    def shards(
        patches,
        cotangent,
        empty_slots,
        dataset_id,
        dataset_weight,
        query_key_value_weight,
        qv_bias,
        output_projection_weight,
        out_bias,
        up_projection_weight,
        up_bias,
        down_projection_weight,
        down_bias,
        attn_gain,
        attn_shift,
        mlp_gain,
        mlp_shift,
    ):
        slot_count, own_rows, model = patches.shape
        width = query_key_value_weight.shape[2]
        group_slots = empty_slots.shape[0]
        slot_index = jnp.arange(group_slots * slot_count, dtype=jnp.int32) % slot_count
        filled = jnp.repeat(slot_count - empty_slots, slot_count)
        valid_all = (slot_index < filled).astype(f32)
        table_hits = dataset_id[:, None] == jnp.arange(dataset_weight.shape[0], dtype=jnp.int32)[None, :]
        numerator = jnp.sum(jnp.where(table_hits, dataset_weight[None, :], 0), axis=1).astype(f32)
        total_items = jnp.sum(valid_all)
        total_weight = jnp.sum(valid_all * numerator)
        multiplier_whole = valid_all * numerator * total_items / total_weight
        own_start = lax.axis_index("dp") * slot_count
        own_scale = lax.dynamic_slice_in_dim(multiplier_whole, own_start, slot_count)
        own_valid = lax.dynamic_slice_in_dim(valid_all, own_start, slot_count)
        all_rows = slot_count * own_rows
        row_scale = jnp.repeat(own_scale, own_rows)[:, None]
        gain_row, shift_row, mlp_gain_row, mlp_shift_row, out_bias_row = (
            value[None, :] for value in (attn_gain, attn_shift, mlp_gain, mlp_shift, out_bias)
        )
        proj_bias = jnp.stack([qv_bias[0], jnp.zeros_like(qv_bias[0]), qv_bias[1]])[:, None, :]
        bias_row = up_bias[None, :]

        dp_side = lax.axis_index("dp") % 2
        place = jnp.zeros((1,), jnp.int32)
        if square:
            place = place + lax.axis_index("tensor")
        fetch = fetch_half if square else gather_far
        weights_near = ()
        if square:
            weights_near = tuple(
                swap(value, 1) for value in (output_projection_weight, up_projection_weight, down_projection_weight)
            )

        def gather_rows(own):
            return lax.all_gather(own, "tensor", axis=0, tiled=True)

        normed = [norm_item(patches, i, gain_row, shift_row) for i in range(slot_count)]
        every = gather_rows(normed[0])
        bias_far = gather_far(bias_row)
        cot_low = (cotangent.astype(f32).reshape(all_rows, model) * row_scale).astype(bf16)
        early = None
        if square:
            early = cot_back(cot_low, [down_projection_weight, weights_near[2]])
            every, (early, normed) = tie(every, (early, normed))
        qkvs, attended, lses, heads_own, normed_every = [], [], [], [], []
        for i in range(slot_count):
            last = i == slot_count - 1
            normed_every.append(every)
            following = None
            if not last:
                every, following = tie(every, normed[i + 1])
                following = gather_rows(following)
            qkv = (
                jnp.einsum("wz,gzh->gwh", every, query_key_value_weight, preferred_element_type=f32) + proj_bias
            ).astype(bf16)
            if i == 0:
                qkv, (weights_near, bias_far) = tie(qkv, (weights_near, bias_far))
            out, lse = attend(qkv)
            if not last:
                out, following = tie(out, following)
            if i > 0:
                out, heads_own[-1] = tie(out, heads_own[-1])
            if i == min(1, slot_count - 1):
                out, (up_own, down_own, out_own) = tie(
                    out, (up_projection_weight, down_projection_weight, output_projection_weight)
                )
                out_far = gather_far(out_own)
                up_far = fetch(up_own)
                down_far = fetch(down_own)
            if last:
                out, (out_far, up_far) = tie(out, (out_far, up_far))
            heads_own.append(exchange(out.reshape(tensor_size, own_rows, width)))
            qkvs.append(qkv)
            attended.append(out)
            lses.append(lse)
            every = following
        if square:
            up_rest = fetch_rest(up_far)
            out_weight = jnp.concatenate([out_own, weights_near[0], out_far, swap(out_far, 1)], axis=0)
        else:
            out_weight = jnp.concatenate(gather_near(out_own, out_far), axis=0)
        rows_done = None
        for i in range(slot_count):
            if i == slot_count - 1:
                rows_done, (heads_own[i], down_far) = tie(rows_done, (heads_own[i], down_far))
            rows_done = out_project(
                patches, i, place, heads_own[i], out_weight, out_bias_row, mlp_gain_row, mlp_shift_row, rows_done
            )
        if square:
            down_rest = fetch_rest(down_far)
            rows_done, up_rest = tie(rows_done, up_rest)
            up_far = in_halves(up_far, up_rest, dp_side)
            up_diag = swap(up_far, 1)
        attended_rows, residual, normed_mlp = rows_done

        bias_blocks = gather_near(bias_row, bias_far)
        if square:
            up_blocks = [up_own, weights_near[1]]
            down_blocks = [down_own, weights_near[2]]
        else:
            up_blocks = gather_near(up_own, up_far)
            down_blocks = gather_near(down_own, down_far)
        calls = tensor_size // 2
        total = None
        slopes, down_grads = [], []
        for c in range(calls):
            pair = slice(2 * c, 2 * c + 2)
            if c == 1 and square:
                total, (up_diag, down_rest) = tie(total, (up_diag, down_rest))
                down_far = in_halves(down_far, down_rest, dp_side)
                up_blocks += [up_far, up_diag]
                down_blocks += [down_far, swap(down_far, 1)]
            slope, total, *grads = mlp_forward(
                normed_mlp, cot_low, up_blocks[pair], bias_blocks[pair], down_blocks[pair], total
            )
            slopes.append(slope)
            down_grads += grads
        layer_sum = total

        cot_late, down_grads = tie(cot_low, down_grads)
        before = None
        bias_grads = []
        for c in range(calls):
            pair = slice(2 * c, 2 * c + 2)
            if c == 0 and square:
                *before, bias_grad = mlp_backward(early, slopes[c], up_blocks[pair], [], before, c, calls)
            else:
                *before, bias_grad = mlp_backward(
                    cot_late, slopes[c], up_blocks[pair], down_blocks[pair], before, c, calls
                )
            bias_grads.append(bias_grad)
            if c == 0:
                down_stage, before = sum_near(down_grads, before)
        ring = ring_plan()
        pre_grad, total = before

        grad_residual, grad_low, small_rows, pieces = residual_back(
            total, residual, cotangent, own_scale, place, out_weight, mlp_gain_row, tensor_size
        )
        down_sum, pieces = sum_far(down_stage, pieces)
        grad_attended = exchange(pieces)
        weight_grads = weight_back(normed_mlp, pre_grad, attended_rows, grad_low, tensor_size)
        weight_grads = list(weight_grads)
        weight_grads[0], grad_attended = tie(weight_grads[0], grad_attended)
        up_grads, out_grads = weight_grads[:tensor_size], weight_grads[tensor_size:]

        (up_stage, out_stage), grad_attended = sums_near([up_grads, out_grads], grad_attended)
        bias_rows = in_order(jnp.concatenate(bias_grads, axis=1).reshape(tensor_size, -1))
        smalls = jnp.concatenate([small_rows[:4].reshape(-1), bias_rows.reshape(-1)]).reshape(-1, 128)
        waiting = list(steps)

        weights_wide = query_key_value_weight.astype(f32)
        sums = None
        grad_normed = []
        for i in range(slot_count):
            last = i == slot_count - 1
            dqkv = attend_back(qkvs[i], attended[i], grad_attended, i, lses[i])
            if i >= 2:
                grad_normed[i - 2], dqkv = terms_far(grad_normed[i - 2], dqkv)
            if i >= 1 and not last:
                grad_normed[i - 1], dqkv = sum_near(grad_normed[i - 1], dqkv)
            if i == 0:
                up_sum, dqkv = sum_far(up_stage, dqkv)
                out_sum, dqkv = sum_far(out_stage, dqkv)
                up_all = lax.psum((up_sum, out_sum), "dp")
            if last:
                dqkv, up_all = tie(dqkv, up_all)
            if waiting and i > 0:
                smalls, dqkv = sum_step(smalls, waiting.pop(0), dqkv)
            if ring:
                down_sum, dqkv = ring_step(down_sum, ring.pop(0), dqkv)
            results = project_back(place, normed_every[i], dqkv, query_key_value_weight, sums, last, tensor_size)
            if not last:
                partial, sums = results[:tensor_size], results[tensor_size:]
                if waiting:
                    smalls, partial = sum_step(smalls, waiting.pop(0), partial)
                if ring:
                    down_sum, partial = ring_step(down_sum, ring.pop(0), partial)
            else:
                *sums, qkv_low = results
                qkv_low, (dqkv, grad_residual, layer_sum) = tie(qkv_low, (dqkv, grad_residual, layer_sum))
                qkv_all = lax.psum(qkv_low, "dp")
                output = layer_out(layer_sum, residual, down_bias[None, :], own_valid, patches.shape)
                partial = project_rows(place, dqkv, query_key_value_weight, tensor_size)
                if i >= 1:
                    grad_normed[i - 1], partial = sum_near(grad_normed[i - 1], partial)
                raw = jnp.stack(
                    [
                        jnp.sum(sums[0] * weights_wide, axis=(0, 2)),
                        jnp.sum(sums[1][:3, None, :] * weights_wide, axis=(0, 2)),
                    ]
                )
                for step in steps:
                    raw = raw + lax.ppermute(raw, step[0], step[1])
            grad_normed.append(partial)
        grad_inputs = None
        for i in range(slot_count):
            if i == slot_count - 1:
                grad_normed[i], grad_residual = sum_near(grad_normed[i], grad_residual)
            terms = grad_normed[i]
            if i >= slot_count - 2:
                terms, grad_residual = terms_far(terms, grad_residual)
            grad_inputs = input_back(terms, patches, i, grad_residual, gain_row, grad_inputs)
        grad_inputs, qkv_all = tie(grad_inputs, qkv_all)
        for step in ring:
            down_sum = ring_step(down_sum, step, place)[0]
        for step in waiting:
            smalls = sum_step(smalls, step, place)[0]
        weight_grad = qkv_all[:, :model].astype(f32)
        columns = qkv_all[:, model].astype(f32)
        up_all, out_all = [value.astype(f32) for value in up_all]
        down_all = down_sum.astype(f32)
        inverse = 1.0 / total_items
        smalls = smalls.reshape(-1) * inverse
        small_rows = smalls[: 4 * model].reshape(4, model)
        units = up_bias.shape[0]
        bias_all = lax.dynamic_slice_in_dim(smalls[4 * model :], lax.axis_index("tensor") * units, units)
        shift_all = raw[1] * inverse
        gain_all = (raw[0] * inverse - attn_shift * shift_all) / attn_gain
        columns = columns * inverse
        return (
            output,
            grad_inputs,
            weight_grad * inverse,
            jnp.stack([columns[0], columns[2]]),
            out_all * inverse,
            small_rows[2],
            up_all * inverse,
            bias_all,
            down_all * inverse,
            small_rows[3],
            gain_all,
            shift_all,
            small_rows[0],
            small_rows[1],
        )

    return shards


def solution(mesh):
    items = P("dp", "tensor", None)
    return jax.shard_map(
        make_shards(mesh.shape["tensor"], mesh.shape["dp"]),
        mesh=mesh,
        in_specs=(
            items,
            items,
            P(),
            P(),
            P(),
            P(None, None, "tensor"),
            P(None, "tensor"),
            P("tensor", None),
            P(),
            P(None, "tensor"),
            P("tensor"),
            P("tensor", None),
            P(),
            P(),
            P(),
            P(),
            P(),
        ),
        out_specs=(
            items,
            items,
            P(None, None, "tensor"),
            P(None, "tensor"),
            P("tensor", None),
            P(),
            P(None, "tensor"),
            P("tensor"),
            P("tensor", None),
            P(),
            P(),
            P(),
            P(),
            P(),
        ),
        check_vma=False,
    )
```

```python
import jax
import jax.numpy as jnp
from jax import lax
from jax.experimental import pallas as pl
from jax.experimental.pallas import tpu as pltpu
from jax.sharding import PartitionSpec as P

HD = 64
SCORE_SCALE = HD ** (-0.5)
LOG2E = 1.4426950408889634
SQRT_HALF = 0.7071067811865476
INV_SQRT_2PI = 0.3989422804014327
epsilon = 1e-05
f32 = jnp.float32
bf16 = jnp.bfloat16
VMEM_LIMIT = 60 << 20
COST_SCALE = 64


def nn(a, b):
    return lax.dot_general(a, b, (((1,), (0,)), ((), ())), preferred_element_type=f32)


def nt(a, b):
    return lax.dot_general(a, b, (((1,), (1,)), ((), ())), preferred_element_type=f32)


def tn(a, b):
    return lax.dot_general(a, b, (((0,), (0,)), ((), ())), preferred_element_type=f32)


def tie(first, second):
    return lax.optimization_barrier((first, second))


def largest_block(extent, limit):
    block = min(extent, limit)
    while extent % block:
        block //= 2
    return block


def norm_rows(source, norm_gain, norm_shift):
    row_mean = jnp.mean(source, axis=-1, keepdims=True)
    centred = source - row_mean
    spread = jnp.mean(centred * centred, axis=-1, keepdims=True)
    return centred * lax.rsqrt(spread + epsilon) * norm_gain + norm_shift


def attend(qkv):
    _, length, width = qkv.shape
    lanes = min(128, width)
    heads = lanes // HD
    qblock = largest_block(length, 2048)
    to_log2 = SCORE_SCALE * LOG2E

    def body(q_ref, k_ref, v_ref, out_ref, lse_ref):
        queries = q_ref[...]
        keys = k_ref[...]
        values_t = v_ref[...].T
        lane = lax.broadcasted_iota(jnp.int32, (1, lanes), 1)
        outs = []
        for h in range(heads):
            own = queries
            if heads > 1:
                own = jnp.where(lane // HD == h, queries, jnp.zeros_like(queries))
            scores = nt(keys, own)
            top = jnp.max(scores, axis=0, keepdims=True)
            exp_scores = jnp.exp2((scores - top) * to_log2)
            total = jnp.sum(exp_scores, axis=0, keepdims=True)
            outs.append(nn(values_t[h * HD : (h + 1) * HD, :], exp_scores.astype(bf16)) / total)
            lse_ref[h : h + 1, :] = top * to_log2 + jnp.log2(total)
        out_ref[...] = jnp.concatenate(outs, axis=0).T.astype(bf16)

    pairs = width // lanes
    return pl.pallas_call(
        body,
        grid=(pairs, length // qblock),
        in_specs=[
            pl.BlockSpec((None, qblock, lanes), lambda h, j: (0, j, h)),
            pl.BlockSpec((None, length, lanes), lambda h, j: (1, 0, h)),
            pl.BlockSpec((None, length, lanes), lambda h, j: (2, 0, h)),
        ],
        out_specs=[
            pl.BlockSpec((qblock, lanes), lambda h, j: (j, h)),
            pl.BlockSpec((None, heads, qblock), lambda h, j: (h, 0, j)),
        ],
        out_shape=[
            jax.ShapeDtypeStruct((length, width), bf16),
            jax.ShapeDtypeStruct((pairs, heads, length), f32),
        ],
        compiler_params=pltpu.CompilerParams(vmem_limit_bytes=VMEM_LIMIT),
        cost_estimate=pl.CostEstimate(
            flops=8 * length * length * width // COST_SCALE,
            transcendentals=0,
            bytes_accessed=length * width,
        ),
        name="attend",
    )(qkv, qkv, qkv)


def attend_back(qkv, attended, grad_attended, item, lse):
    _, length, width = qkv.shape
    lanes = min(128, width)
    shards_of = grad_attended.shape[0]
    heads = lanes // HD
    kblock = largest_block(length, 1024)
    kblocks = length // kblock
    to_log2 = SCORE_SCALE * LOG2E

    def body(q_ref, k_ref, v_ref, out_ref, grad_ref, lse_ref, dqkv_ref, dq_acc, row_dot):
        kb = pl.program_id(1)
        queries = q_ref[...]
        grads = grad_ref[...].reshape(length, lanes)
        keys = k_ref[...]
        values = v_ref[...]
        keys_t = keys.T
        lane = lax.broadcasted_iota(jnp.int32, (1, lanes), 1)

        @pl.when(kb == 0)
        def _():
            product = out_ref[...].astype(f32) * grads.astype(f32)
            high = product.astype(bf16)
            rest = (product - high.astype(f32)).astype(bf16)
            pick = lax.broadcasted_iota(jnp.int32, (8, lanes), 0)
            mask = (lax.broadcasted_iota(jnp.int32, (8, lanes), 1) // HD == pick).astype(f32).astype(bf16)
            row_dot[...] = nt(mask, high) + nt(mask, rest)

        dk = None
        dv = None
        dqs = []
        for h in range(heads):
            own_q = queries
            own_g = grads
            if heads > 1:
                mine = lane // HD == h
                own_q = jnp.where(mine, queries, jnp.zeros_like(queries))
                own_g = jnp.where(mine, grads, jnp.zeros_like(grads))
            scores = nt(keys, own_q)
            weights = jnp.exp2(scores * to_log2 - lse_ref[h : h + 1, :])
            grad_weights = nt(values, own_g)
            grad_scores = (weights * (grad_weights - row_dot[h : h + 1, :])).astype(bf16)
            dv_h = nn(weights.astype(bf16), own_g)
            dk_h = nn(grad_scores, own_q)
            dv = dv_h if dv is None else dv + dv_h
            dk = dk_h if dk is None else dk + dk_h
            dqs.append(nn(keys_t[h * HD : (h + 1) * HD, :], grad_scores))
        rows = pl.ds(pl.multiple_of(kb * kblock, kblock), kblock)
        dqkv_ref[1, rows, :] = (dk * SCORE_SCALE).astype(bf16)
        dqkv_ref[2, rows, :] = dv.astype(bf16)
        dq = jnp.concatenate(dqs, axis=0)
        if kblocks == 1:
            dqkv_ref[0] = (dq * SCORE_SCALE).T.astype(bf16)
            return

        @pl.when(kb == 0)
        def _():
            dq_acc[...] = dq

        @pl.when((kb > 0) & (kb < kblocks - 1))
        def _():
            dq_acc[...] += dq

        @pl.when(kb == kblocks - 1)
        def _():
            dqkv_ref[0] = ((dq_acc[...] + dq) * SCORE_SCALE).T.astype(bf16)

    pairs = width // lanes
    return pl.pallas_call(
        body,
        grid=(pairs, kblocks),
        in_specs=[
            pl.BlockSpec((None, length, lanes), lambda h, kb: (0, 0, h)),
            pl.BlockSpec((None, kblock, lanes), lambda h, kb: (1, kb, h)),
            pl.BlockSpec((None, kblock, lanes), lambda h, kb: (2, kb, h)),
            pl.BlockSpec((length, lanes), lambda h, kb: (0, h)),
            pl.BlockSpec((shards_of, length // shards_of, lanes), lambda h, kb: (0, item, h)),
            pl.BlockSpec((None, heads, length), lambda h, kb: (h, 0, 0)),
        ],
        out_specs=pl.BlockSpec((3, length, lanes), lambda h, kb: (0, 0, h)),
        out_shape=jax.ShapeDtypeStruct((3, length, width), bf16),
        scratch_shapes=[pltpu.VMEM((lanes, length), f32), pltpu.VMEM((8, length), f32)],
        compiler_params=pltpu.CompilerParams(vmem_limit_bytes=VMEM_LIMIT),
        cost_estimate=pl.CostEstimate(
            flops=20 * length * length * width // COST_SCALE,
            transcendentals=0,
            bytes_accessed=length * width,
        ),
        name="attend_back",
    )(qkv, qkv, qkv, attended, grad_attended, lse)


def hint(flops, size):
    return pl.CostEstimate(flops=flops // COST_SCALE, transcendentals=0, bytes_accessed=size)


def params():
    return pltpu.CompilerParams(vmem_limit_bytes=VMEM_LIMIT)


def norm_item(patches, item, norm_gain, norm_shift):
    _, rows, model = patches.shape
    block = largest_block(rows, 256)

    def body(x_ref, gain_ref, shift_ref, out_ref):
        out_ref[...] = norm_rows(x_ref[...].astype(f32), gain_ref[...], shift_ref[...]).astype(bf16)

    vector = pl.BlockSpec((1, model), lambda i: (0, 0))
    return pl.pallas_call(
        body,
        grid=(rows // block,),
        in_specs=[pl.BlockSpec((None, block, model), lambda i: (item, i, 0)), vector, vector],
        out_specs=pl.BlockSpec((block, model), lambda i: (i, 0)),
        out_shape=jax.ShapeDtypeStruct((rows, model), bf16),
        compiler_params=params(),
        cost_estimate=hint(0, rows * model),
        name="norm_item",
    )(patches, norm_gain, norm_shift)


def out_project(patches, item, place, heads, weight, out_bias, norm_gain, norm_shift, before):
    slots, rows, model = patches.shape
    block = largest_block(rows, 256)
    steps = rows // block
    count, _, width = heads.shape

    def body(*refs):
        place_ref, x_ref, weight_ref, bias_ref, gain_ref, shift_ref, head_ref = refs[:7]
        attended_ref, residual_ref, normed_ref = refs[-3:]
        for k in range(count):
            attended_ref[:, k * width : (k + 1) * width] = head_ref[place_ref[0] ^ k]
        attended = attended_ref[...]
        residual = x_ref[...].astype(f32) + nn(attended, weight_ref[...]) + bias_ref[...]
        residual_ref[...] = residual
        normed_ref[...] = norm_rows(residual, gain_ref[...], shift_ref[...]).astype(bf16)

    vector = pl.BlockSpec((1, model), lambda i: (0, 0))
    placed = pl.BlockSpec((block, model), lambda i: (item * steps + i, 0))
    operands = [place, patches, weight, out_bias, norm_gain, norm_shift, heads]
    in_specs = [
        pl.BlockSpec(memory_space=pltpu.SMEM),
        pl.BlockSpec((None, block, model), lambda i: (item, i, 0)),
        pl.BlockSpec((model, model), lambda i: (0, 0)),
        vector,
        vector,
        vector,
        pl.BlockSpec((count, block, width), lambda i: (0, i, 0)),
    ]
    aliases = {}
    if before is not None:
        aliases = {len(operands) + k: k for k in range(3)}
        operands += before
        in_specs += [pl.BlockSpec(memory_space=pl.ANY)] * 3
    return pl.pallas_call(
        body,
        grid=(steps,),
        in_specs=in_specs,
        out_specs=[placed] * 3,
        out_shape=[jax.ShapeDtypeStruct((slots * rows, model), t) for t in (bf16, f32, bf16)],
        input_output_aliases=aliases,
        compiler_params=params(),
        cost_estimate=hint(2 * rows * model * model, rows * model),
        name="out_project",
    )(*operands)


def residual_back(total, residual, cotangent, scale, place, weight, norm_gain, pieces):
    slots, rows, model = cotangent.shape
    block = largest_block(rows, 256)
    steps = rows // block
    piece = model // pieces

    def body(*refs):
        place_ref, total_ref, residual_ref, cot_ref, scale_ref, weight_ref, gain_ref = refs[:7]
        grad_ref, low_ref, sum_ref, attended_ref = refs[-4:]
        residual = residual_ref[...]
        centred = residual - jnp.mean(residual, axis=-1, keepdims=True)
        rate = lax.rsqrt(jnp.mean(centred * centred, axis=-1, keepdims=True) + epsilon)
        xhat = centred * rate
        grad_normed = total_ref[...]
        scaled = grad_normed * gain_ref[...]
        inner = jnp.mean(scaled, axis=-1, keepdims=True)
        outer = jnp.mean(scaled * xhat, axis=-1, keepdims=True)
        cot = cot_ref[...].astype(f32) * scale_ref[pl.program_id(0) // steps]
        grad = cot + rate * (scaled - inner - xhat * outer)
        grad_ref[...] = grad
        low = grad.astype(bf16)
        low_ref[...] = low

        @pl.when(pl.program_id(0) == 0)
        def _():
            sum_ref[...] = jnp.zeros_like(sum_ref)

        for k, value in enumerate((grad_normed * xhat, grad_normed, grad, cot)):
            sum_ref[k : k + 1, :] += jnp.sum(value, axis=0, keepdims=True)
        attended = nt(low, weight_ref[...]).astype(bf16)
        for k in range(pieces):
            attended_ref[place_ref[0] ^ k] = attended[:, k * piece : (k + 1) * piece]

    row_spec = pl.BlockSpec((block, model), lambda i: (i, 0))
    return pl.pallas_call(
        body,
        grid=(slots * steps,),
        in_specs=[
            pl.BlockSpec(memory_space=pltpu.SMEM),
            row_spec,
            row_spec,
            pl.BlockSpec((None, block, model), lambda i: (i // steps, i % steps, 0)),
            pl.BlockSpec(memory_space=pltpu.SMEM),
            pl.BlockSpec((model, model), lambda i: (0, 0)),
            pl.BlockSpec((1, model), lambda i: (0, 0)),
        ],
        out_specs=[
            row_spec,
            row_spec,
            pl.BlockSpec((8, model), lambda i: (0, 0)),
            pl.BlockSpec((pieces, block, piece), lambda i: (0, i, 0)),
        ],
        out_shape=[
            jax.ShapeDtypeStruct((slots * rows, model), f32),
            jax.ShapeDtypeStruct((slots * rows, model), bf16),
            jax.ShapeDtypeStruct((8, model), f32),
            jax.ShapeDtypeStruct((pieces, slots * rows, piece), bf16),
        ],
        compiler_params=params(),
        cost_estimate=hint(2 * slots * rows * model * model, rows * model),
        name="residual_back",
    )(place, total, residual, cotangent, scale, weight, norm_gain)


def input_back(terms, patches, item, grad_residual, norm_gain, before):
    slots, rows, model = patches.shape
    block = largest_block(rows, 256)
    count = len(terms)

    def body(*refs):
        x_ref, grad_ref, gain_ref = refs[:3]
        out_ref = refs[-1]
        grad_normed = refs[3][...].astype(f32)
        for k in range(1, count):
            grad_normed = grad_normed + refs[3 + k][...].astype(f32)
        source = x_ref[...].astype(f32)
        centred = source - jnp.mean(source, axis=-1, keepdims=True)
        rate = lax.rsqrt(jnp.mean(centred * centred, axis=-1, keepdims=True) + epsilon)
        xhat = centred * rate
        scaled = grad_normed * gain_ref[...]
        inner = jnp.mean(scaled, axis=-1, keepdims=True)
        outer = jnp.mean(scaled * xhat, axis=-1, keepdims=True)
        out_ref[...] = (grad_ref[...] + rate * (scaled - inner - xhat * outer)).astype(bf16)

    row_spec = pl.BlockSpec((block, model), lambda i: (i, 0))
    placed = pl.BlockSpec((None, block, model), lambda i: (item, i, 0))
    operands = [patches, grad_residual, norm_gain, *terms]
    steps = rows // block
    grad_spec = pl.BlockSpec((block, model), lambda i: (item * steps + i, 0))
    in_specs = [placed, grad_spec, pl.BlockSpec((1, model), lambda i: (0, 0))] + [row_spec] * count
    aliases = {}
    if before is not None:
        aliases = {len(operands): 0}
        operands.append(before)
        in_specs.append(pl.BlockSpec(memory_space=pl.ANY))
    return pl.pallas_call(
        body,
        grid=(rows // block,),
        in_specs=in_specs,
        out_specs=placed,
        out_shape=jax.ShapeDtypeStruct((slots, rows, model), bf16),
        input_output_aliases=aliases,
        compiler_params=params(),
        cost_estimate=hint(0, rows * model),
        name="input_back",
    )(*operands)


def layer_out(total, residual, down_bias, valid, shape):
    slots, rows, model = shape
    block = largest_block(rows, 256)
    steps = rows // block

    def body(total_ref, residual_ref, bias_ref, valid_ref, out_ref):
        value = residual_ref[...] + total_ref[...] + bias_ref[...]
        out_ref[...] = (value * valid_ref[pl.program_id(0) // steps]).astype(bf16)

    row_spec = pl.BlockSpec((block, model), lambda i: (i, 0))
    return pl.pallas_call(
        body,
        grid=(slots * steps,),
        in_specs=[
            row_spec,
            row_spec,
            pl.BlockSpec((1, model), lambda i: (0, 0)),
            pl.BlockSpec(memory_space=pltpu.SMEM),
        ],
        out_specs=pl.BlockSpec((None, block, model), lambda i: (i // steps, i % steps, 0)),
        out_shape=jax.ShapeDtypeStruct(shape, bf16),
        compiler_params=params(),
        cost_estimate=hint(0, rows * model),
        name="layer_out",
    )(total, residual, down_bias, valid)


def mlp_forward(normed, cot, ups, biases, downs, total):
    rows, model = normed.shape
    count = len(ups)
    units = ups[0].shape[1]
    block = largest_block(rows, 512)
    steps = rows // block
    first = total is None

    def body(*refs):
        x_ref, cot_ref = refs[:2]
        up_refs, bias_refs, down_refs = (refs[2 + k * count : 2 + (k + 1) * count] for k in range(3))
        rest = refs[2 + 3 * count :]
        if not first:
            before_ref = rest[0]
            rest = rest[1:]
        slope_ref, sum_ref = rest[:2]
        grad_refs = rest[2 : 2 + count]
        hidden_ref, acc_ref = rest[2 + count :]
        step = pl.program_id(0)
        part = largest_block(units, 256)
        for k in range(count):
            for j in range(units // part):
                cols = slice(j * part, (j + 1) * part)
                wide = slice(k * units + j * part, k * units + (j + 1) * part)
                pre = nn(x_ref[...], up_refs[k][:, cols]) + bias_refs[k][:, cols]
                cdf = 0.5 + 0.5 * lax.erf(pre * SQRT_HALF)
                density = jnp.exp2(pre * pre * (-0.5 * LOG2E)) * INV_SQRT_2PI
                hidden_ref[:, wide] = (pre * cdf).astype(bf16)
                slope_ref[:, wide] = (cdf + pre * density).astype(bf16)
        out = None if first else before_ref[...]
        for k in range(count):
            hidden = hidden_ref[:, k * units : (k + 1) * units]
            product = nn(hidden, down_refs[k][...])
            out = product if out is None else out + product
            grad = tn(hidden, cot_ref[...])

            @pl.when(step == 0)
            def _():
                acc_ref[k] = grad

            @pl.when(step > 0)
            def _():
                acc_ref[k] += grad

        sum_ref[...] = out

        @pl.when(step == steps - 1)
        def _():
            for k in range(count):
                grad_refs[k][...] = acc_ref[k].astype(bf16)

    row_spec = pl.BlockSpec((block, model), lambda i: (i, 0))
    slope_spec = pl.BlockSpec((block, count * units), lambda i: (i, 0))
    up_spec = pl.BlockSpec((model, units), lambda i: (0, 0), pipeline_mode=pl.Buffered(1))
    down_spec = pl.BlockSpec((units, model), lambda i: (0, 0), pipeline_mode=pl.Buffered(1))
    grad_spec = pl.BlockSpec((units, model), lambda i: (0, 0))
    operands = [normed, cot, *ups, *biases, *downs]
    in_specs = [row_spec, row_spec] + [up_spec] * count
    in_specs += [pl.BlockSpec((1, units), lambda i: (0, 0))] * count + [down_spec] * count
    aliases = {}
    if not first:
        aliases = {len(operands): 1}
        operands.append(total)
        in_specs.append(row_spec)
    return pl.pallas_call(
        body,
        grid=(steps,),
        in_specs=in_specs,
        out_specs=[slope_spec, row_spec] + [grad_spec] * count,
        out_shape=[
            jax.ShapeDtypeStruct((rows, count * units), bf16),
            jax.ShapeDtypeStruct((rows, model), f32),
        ]
        + [jax.ShapeDtypeStruct((units, model), bf16)] * count,
        scratch_shapes=[pltpu.VMEM((block, count * units), bf16), pltpu.VMEM((count, units, model), f32)],
        input_output_aliases=aliases,
        compiler_params=params(),
        cost_estimate=hint(6 * rows * model * units * count, rows * units),
        name="mlp_forward",
    )(*operands)


def cot_back(cot, downs):
    rows, model = cot.shape
    count = len(downs)
    units = downs[0].shape[0]
    block = largest_block(rows, 512)

    def body(cot_ref, *refs):
        for k in range(count):
            refs[count][:, k * units : (k + 1) * units] = nt(cot_ref[...], refs[k][...]).astype(bf16)

    return pl.pallas_call(
        body,
        grid=(rows // block,),
        in_specs=[pl.BlockSpec((block, model), lambda i: (i, 0))]
        + [pl.BlockSpec((units, model), lambda i: (0, 0))] * count,
        out_specs=pl.BlockSpec((block, count * units), lambda i: (i, 0)),
        out_shape=jax.ShapeDtypeStruct((rows, count * units), bf16),
        compiler_params=params(),
        cost_estimate=hint(2 * rows * model * units * count, rows * units),
        name="cot_back",
    )(cot, *downs)


def mlp_backward(cot, slope, ups, downs, before, index, calls):
    rows, _ = cot.shape
    model = ups[0].shape[0]
    count = len(ups)
    units = ups[0].shape[1]
    block = largest_block(rows, 512)
    first = before is None

    def body(*refs):
        cot_ref, slope_ref = refs[:2]
        up_refs, down_refs = refs[2 : 2 + count], refs[2 + count : 2 + count + len(downs)]
        grad_ref, sum_ref, bias_ref = refs[-3:]

        @pl.when(pl.program_id(0) == 0)
        def _():
            bias_ref[...] = jnp.zeros_like(bias_ref)

        out = None if first else refs[3 + count + len(downs)][...]
        part = largest_block(units, 512)
        for k in range(count):
            for j in range(units // part):
                rows_of = slice(j * part, (j + 1) * part)
                wide = slice(k * units + j * part, k * units + (j + 1) * part)
                if downs:
                    product = nt(cot_ref[...], down_refs[k][rows_of, :])
                else:
                    product = cot_ref[:, wide].astype(f32)
                low = (product * slope_ref[:, wide].astype(f32)).astype(bf16)
                grad_ref[:, wide] = low
                bias_ref[:, wide] += jnp.sum(low.astype(f32), axis=0, keepdims=True)
            product = nt(grad_ref[:, k * units : (k + 1) * units], up_refs[k][...])
            out = product if out is None else out + product
        sum_ref[...] = out

    row_spec = pl.BlockSpec((block, model), lambda i: (i, 0))
    slope_spec = pl.BlockSpec((block, count * units), lambda i: (i, 0))
    up_spec = pl.BlockSpec((model, units), lambda i: (0, 0), pipeline_mode=pl.Buffered(1))
    down_spec = pl.BlockSpec((units, model), lambda i: (0, 0), pipeline_mode=pl.Buffered(1))
    operands = [cot, slope, *ups, *downs]
    in_specs = [row_spec if downs else slope_spec, slope_spec] + [up_spec] * count + [down_spec] * len(downs)
    aliases = {}
    if not first:
        aliases = {len(operands): 0, len(operands) + 1: 1}
        operands += before
        in_specs += [pl.BlockSpec(memory_space=pl.ANY), row_spec]
    return pl.pallas_call(
        body,
        grid=(rows // block,),
        in_specs=in_specs,
        out_specs=[
            pl.BlockSpec((block, count * units), lambda i: (i, index)),
            row_spec,
            pl.BlockSpec((1, count * units), lambda i: (0, 0)),
        ],
        out_shape=[
            jax.ShapeDtypeStruct((rows, calls * count * units), bf16),
            jax.ShapeDtypeStruct((rows, model), f32),
            jax.ShapeDtypeStruct((1, count * units), f32),
        ],
        input_output_aliases=aliases,
        compiler_params=params(),
        cost_estimate=hint(4 * rows * model * units * count, rows * units),
        name="mlp_backward",
    )(*operands)


def weight_back(normed, pre_grad, picks, attended, grad_low, pieces):
    rows, model = normed.shape
    units = pre_grad.shape[1] // pieces
    piece = model // pieces
    block = largest_block(rows, 512)
    steps = rows // block
    count = len(picks)
    outs = 0 if attended is None else pieces

    def body(x_ref, *refs):
        pre_refs = refs[:count]
        rest = refs[count:]
        if outs:
            attended_ref, grad_ref = rest[:2]
            rest = rest[2:]
        up_refs, out_refs = rest[:count], rest[count : count + outs]
        up_acc = rest[count + outs]
        step = pl.program_id(0)

        def add(acc, place, value):
            @pl.when(step == 0)
            def _():
                acc[place] = value

            @pl.when(step > 0)
            def _():
                acc[place] += value

        for k in range(count):
            add(up_acc, (slice(None), slice(k * units, (k + 1) * units)), tn(x_ref[...], pre_refs[k][...]))
        if outs:
            out_acc = rest[-1]
            add(out_acc, (slice(None), slice(None)), tn(attended_ref[...], grad_ref[...]))

        @pl.when(step == steps - 1)
        def _():
            for k in range(count):
                up_refs[k][...] = up_acc[:, k * units : (k + 1) * units].astype(bf16)
            for k in range(outs):
                out_refs[k][...] = out_acc[k * piece : (k + 1) * piece, :].astype(bf16)

    row_spec = pl.BlockSpec((block, model), lambda i: (i, 0))

    def columns_of(pick):
        return pl.BlockSpec((block, units), lambda i: (i, pick))

    operands = [normed] + [pre_grad] * count
    in_specs = [row_spec] + [columns_of(pick) for pick in picks]
    scratch = [pltpu.VMEM((model, count * units), f32)]
    if outs:
        operands += [attended, grad_low]
        in_specs += [row_spec, row_spec]
        scratch.append(pltpu.VMEM((model, model), f32))
    return pl.pallas_call(
        body,
        grid=(steps,),
        in_specs=in_specs,
        out_specs=[pl.BlockSpec((model, units), lambda i: (0, 0))] * count
        + [pl.BlockSpec((piece, model), lambda i: (0, 0))] * outs,
        out_shape=[jax.ShapeDtypeStruct((model, units), bf16)] * count
        + [jax.ShapeDtypeStruct((piece, model), bf16)] * outs,
        scratch_shapes=scratch,
        compiler_params=params(),
        cost_estimate=hint(2 * rows * model * units * count, rows * model),
        name="weight_back",
    )(*operands)


def project_back(place, normed, dqkv, weight, before, last, pieces):
    rows, model = normed.shape
    width = weight.shape[2]
    block = rows // pieces
    steps = pieces
    first = before is None
    given = 0 if last else pieces

    def kernel(*refs):
        place_ref, normed_ref, dqkv_ref, weight_ref = refs[:4]
        rest = refs[4:]
        if not first:
            wgrad_before, column_before = rest[:2]
            rest = rest[2:]
        row_refs, rest = rest[:given], rest[given:]
        wgrad_ref, column_ref = rest[:2]
        step = pl.program_id(0)

        @pl.when(step == 0)
        def _():
            if first:
                wgrad_ref[...] = jnp.zeros_like(wgrad_ref)
                column_ref[...] = jnp.zeros_like(column_ref)
            else:
                wgrad_ref[...] = wgrad_before[...]
                column_ref[...] = column_before[...]

        if not last:
            row_grad = nt(dqkv_ref[0], weight_ref[0])
            for c in range(1, 3):
                row_grad = row_grad + nt(dqkv_ref[c], weight_ref[c])
            row_grad = row_grad.astype(bf16)
            for k in range(pieces):

                @pl.when(step == place_ref[0] ^ k)
                def _():
                    row_refs[k][...] = row_grad

        for c in range(3):
            wgrad_ref[c] += tn(normed_ref[...], dqkv_ref[c])
            column_ref[c : c + 1, :] += jnp.sum(dqkv_ref[c].astype(f32), axis=0, keepdims=True)
        if last:
            low_ref = rest[2]

            @pl.when(step == steps - 1)
            def _():
                low_ref[:, :model, :] = wgrad_ref[...].astype(bf16)
                for c in range(3):
                    row = jnp.broadcast_to(column_ref[c : c + 1, :], (16, width))
                    low_ref[c, model:, :] = row.astype(bf16)

    whole = pl.BlockSpec((3, model, width), lambda i: (0, 0, 0))
    columns = pl.BlockSpec((8, width), lambda i: (0, 0))
    row_spec = pl.BlockSpec((block, model), lambda i: (i, 0))
    operands = [place, normed, dqkv, weight]
    in_specs = [pl.BlockSpec(memory_space=pltpu.SMEM), row_spec, pl.BlockSpec((3, block, width), lambda i: (0, i, 0)), whole]
    if not first:
        operands += list(before)
        in_specs += [whole, columns]
    out_specs = [pl.BlockSpec((block, model), lambda i: (0, 0))] * given + [whole, columns]
    out_shape = [jax.ShapeDtypeStruct((block, model), bf16)] * given + [
        jax.ShapeDtypeStruct((3, model, width), f32),
        jax.ShapeDtypeStruct((8, width), f32),
    ]
    if last:
        out_specs.append(pl.BlockSpec((3, model + 16, width), lambda i: (0, 0, 0)))
        out_shape.append(jax.ShapeDtypeStruct((3, model + 16, width), bf16))
    return pl.pallas_call(
        kernel,
        grid=(steps,),
        in_specs=in_specs,
        out_specs=out_specs,
        out_shape=out_shape,
        input_output_aliases={} if first else {4: given, 5: given + 1},
        compiler_params=pltpu.CompilerParams(vmem_limit_bytes=VMEM_LIMIT),
        cost_estimate=pl.CostEstimate(
            flops=12 * rows * model * width // COST_SCALE,
            transcendentals=0,
            bytes_accessed=rows * width,
        ),
        name="project_back",
    )(*operands)


def project_rows(place, dqkv, weight, pieces):
    _, rows, width = dqkv.shape
    model = weight.shape[1]
    block = rows // pieces

    def kernel(place_ref, dqkv_ref, weight_ref, *row_refs):
        row_grad = nt(dqkv_ref[0], weight_ref[0])
        for c in range(1, 3):
            row_grad = row_grad + nt(dqkv_ref[c], weight_ref[c])
        row_grad = row_grad.astype(bf16)
        for k in range(pieces):

            @pl.when(pl.program_id(0) == place_ref[0] ^ k)
            def _():
                row_refs[k][...] = row_grad

    return pl.pallas_call(
        kernel,
        grid=(pieces,),
        in_specs=[
            pl.BlockSpec(memory_space=pltpu.SMEM),
            pl.BlockSpec((3, block, width), lambda i: (0, i, 0)),
            pl.BlockSpec((3, model, width), lambda i: (0, 0, 0)),
        ],
        out_specs=[pl.BlockSpec((block, model), lambda i: (0, 0))] * pieces,
        out_shape=[jax.ShapeDtypeStruct((block, model), bf16)] * pieces,
        compiler_params=params(),
        cost_estimate=hint(6 * rows * model * width, rows * width),
        name="project_rows",
    )(place, dqkv, weight)


def make_shards(tensor_size, group_size):
    square = tensor_size == 4

    def swap(value, bits):
        return lax.ppermute(value, "tensor", [(i, i ^ bits) for i in range(tensor_size)])

    def gather_far(own):
        return swap(own, 2) if square else lax.all_gather(own, "tensor")

    def gather_near(own, far):
        if not square:
            return [far[i] for i in range(tensor_size)]
        return [own, swap(own, 1), far, swap(far, 1)]

    def exchange(stacked):
        return lax.all_to_all(stacked, "tensor", 0, 0)

    def sum_near(blocks, anchor):
        if not square:
            return (jnp.stack(blocks),), anchor
        anchor, (near_own, near_far) = tie(anchor, (swap(blocks[1], 1), swap(blocks[3], 1)))
        far = (blocks[2].astype(f32) + near_far.astype(f32)).astype(blocks[2].dtype)
        return (blocks[0], near_own, far), anchor

    def terms_far(stage, anchor):
        if not square:
            own = lax.psum_scatter(stage[0], "tensor", scatter_dimension=0, tiled=False)
            anchor, own = tie(anchor, own)
            return [own], anchor
        own, near, far = stage
        anchor, received = tie(anchor, swap(far, 2))
        return [own, near, received], anchor

    def sum_far(stage, anchor):
        terms, anchor = terms_far(stage, anchor)
        total = terms[0].astype(f32)
        for term in terms[1:]:
            total = total + term.astype(f32)
        return total.astype(terms[0].dtype), anchor

    steps = []
    for axis, size in (("tensor", tensor_size), ("dp", group_size)):
        bit = 1
        while bit < size:
            steps.append((axis, [(i, i ^ bit) for i in range(size)]))
            bit *= 2

    def sum_step(value, step, anchor):
        anchor, received = tie(anchor, lax.ppermute(value, step[0], step[1]))
        return value + received, anchor

    def ring_plan():
        bits = [1 << k for k in range(group_size.bit_length() - 1)]
        return [(bit, True) for bit in bits] + [(bit, False) for bit in reversed(bits)]

    def ring_step(value, step, anchor):
        bit, reducing = step
        side = (lax.axis_index("dp") // bit) % 2
        pairs = [(i, i ^ bit) for i in range(group_size)]
        if reducing:
            half = value.shape[0] // 2
            sent = lax.dynamic_slice_in_dim(value, (1 - side) * half, half, axis=0)
            anchor, received = tie(anchor, lax.ppermute(sent, "dp", pairs))
            kept = lax.dynamic_slice_in_dim(value, side * half, half, axis=0)
            return (kept.astype(f32) + received.astype(f32)).astype(value.dtype), anchor
        anchor, received = tie(anchor, lax.ppermute(value, "dp", pairs))
        return in_halves(value, received, side), anchor

    def in_halves(own, other, side):
        rows = own.shape[0]
        whole = jnp.zeros((2 * rows,) + own.shape[1:], own.dtype)
        whole = lax.dynamic_update_slice_in_dim(whole, own, side * rows, axis=0)
        return lax.dynamic_update_slice_in_dim(whole, other, (1 - side) * rows, axis=0)

    def fetch_half(own):
        half = own.shape[0] // 2
        side = lax.axis_index("dp") % 2
        return swap(lax.dynamic_slice_in_dim(own, side * half, half, axis=0), 2)

    def fetch_rest(half):
        return lax.ppermute(half, "dp", [(i, i ^ 1) for i in range(group_size)])

    def in_order(stacked):
        if not square:
            return stacked
        own = lax.axis_index("tensor")
        return jnp.concatenate(
            [lax.dynamic_slice_in_dim(stacked, own ^ i, 1, axis=0) for i in range(tensor_size)], axis=0
        )

    def shards(
        patches,
        cotangent,
        empty_slots,
        dataset_id,
        dataset_weight,
        query_key_value_weight,
        qv_bias,
        output_projection_weight,
        out_bias,
        up_projection_weight,
        up_bias,
        down_projection_weight,
        down_bias,
        attn_gain,
        attn_shift,
        mlp_gain,
        mlp_shift,
    ):
        slot_count, own_rows, model = patches.shape
        width = query_key_value_weight.shape[2]
        group_slots = empty_slots.shape[0]
        slot_index = jnp.arange(group_slots * slot_count, dtype=jnp.int32) % slot_count
        filled = jnp.repeat(slot_count - empty_slots, slot_count)
        valid_all = (slot_index < filled).astype(f32)
        table_hits = dataset_id[:, None] == jnp.arange(dataset_weight.shape[0], dtype=jnp.int32)[None, :]
        numerator = jnp.sum(jnp.where(table_hits, dataset_weight[None, :], 0), axis=1).astype(f32)
        total_items = jnp.sum(valid_all)
        total_weight = jnp.sum(valid_all * numerator)
        multiplier_whole = valid_all * numerator * total_items / total_weight
        own_start = lax.axis_index("dp") * slot_count
        own_scale = lax.dynamic_slice_in_dim(multiplier_whole, own_start, slot_count)
        own_valid = lax.dynamic_slice_in_dim(valid_all, own_start, slot_count)
        all_rows = slot_count * own_rows
        row_scale = jnp.repeat(own_scale, own_rows)[:, None]
        gain_row, shift_row, mlp_gain_row, mlp_shift_row, out_bias_row = (
            value[None, :] for value in (attn_gain, attn_shift, mlp_gain, mlp_shift, out_bias)
        )
        proj_bias = jnp.stack([qv_bias[0], jnp.zeros_like(qv_bias[0]), qv_bias[1]])[:, None, :]
        bias_row = up_bias[None, :]

        dp_side = lax.axis_index("dp") % 2
        place = jnp.zeros((1,), jnp.int32)
        if square:
            place = place + lax.axis_index("tensor")
        fetch = fetch_half if square else gather_far
        weights_near = ()
        if square:
            weights_near = tuple(
                swap(value, 1) for value in (output_projection_weight, up_projection_weight, down_projection_weight)
            )

        def gather_rows(own):
            return lax.all_gather(own, "tensor", axis=0, tiled=True)

        normed = [norm_item(patches, i, gain_row, shift_row) for i in range(slot_count)]
        every = gather_rows(normed[0])
        bias_far = gather_far(bias_row)
        cot_low = (cotangent.astype(f32).reshape(all_rows, model) * row_scale).astype(bf16)
        early = None
        if square:
            early = cot_back(cot_low, [down_projection_weight, weights_near[2]])
            every, (early, normed) = tie(every, (early, normed))
        qkvs, attended, lses, heads_own, normed_every = [], [], [], [], []
        for i in range(slot_count):
            last = i == slot_count - 1
            normed_every.append(every)
            following = None
            if not last:
                every, following = tie(every, normed[i + 1])
                following = gather_rows(following)
            qkv = (
                jnp.einsum("wz,gzh->gwh", every, query_key_value_weight, preferred_element_type=f32) + proj_bias
            ).astype(bf16)
            if i == 0:
                qkv, (weights_near, bias_far) = tie(qkv, (weights_near, bias_far))
            out, lse = attend(qkv)
            if not last:
                out, following = tie(out, following)
            if i > 0:
                out, heads_own[-1] = tie(out, heads_own[-1])
            if i == min(1, slot_count - 1):
                out, (up_own, down_own, out_own) = tie(
                    out, (up_projection_weight, down_projection_weight, output_projection_weight)
                )
                out_far = gather_far(out_own)
                up_far = fetch(up_own)
                down_far = fetch(down_own)
            if last:
                out, (out_far, up_far) = tie(out, (out_far, up_far))
            heads_own.append(exchange(out.reshape(tensor_size, own_rows, width)))
            qkvs.append(qkv)
            attended.append(out)
            lses.append(lse)
            every = following
        if square:
            up_rest = fetch_rest(up_far)
            out_weight = jnp.concatenate([out_own, weights_near[0], out_far, swap(out_far, 1)], axis=0)
        else:
            out_weight = jnp.concatenate(gather_near(out_own, out_far), axis=0)
        rows_done = None
        for i in range(slot_count):
            if i == slot_count - 1:
                rows_done, (heads_own[i], down_far) = tie(rows_done, (heads_own[i], down_far))
            rows_done = out_project(
                patches, i, place, heads_own[i], out_weight, out_bias_row, mlp_gain_row, mlp_shift_row, rows_done
            )
        if square:
            down_rest = fetch_rest(down_far)
            rows_done, up_rest = tie(rows_done, up_rest)
            up_far = in_halves(up_far, up_rest, dp_side)
            up_diag = swap(up_far, 1)
        attended_rows, residual, normed_mlp = rows_done

        bias_blocks = gather_near(bias_row, bias_far)
        if square:
            up_blocks = [up_own, weights_near[1]]
            down_blocks = [down_own, weights_near[2]]
        else:
            up_blocks = gather_near(up_own, up_far)
            down_blocks = gather_near(down_own, down_far)
        calls = tensor_size // 2
        total = None
        slopes, down_grads = [], []
        for c in range(calls):
            pair = slice(2 * c, 2 * c + 2)
            if c == 1 and square:
                total, (up_diag, down_rest) = tie(total, (up_diag, down_rest))
                down_far = in_halves(down_far, down_rest, dp_side)
                up_blocks += [up_far, up_diag]
                down_blocks += [down_far, swap(down_far, 1)]
            slope, total, *grads = mlp_forward(
                normed_mlp, cot_low, up_blocks[pair], bias_blocks[pair], down_blocks[pair], total
            )
            slopes.append(slope)
            down_grads += grads
        layer_sum = total

        cot_late, down_grads = tie(cot_low, down_grads)
        before = None
        bias_grads = []
        for c in range(calls):
            pair = slice(2 * c, 2 * c + 2)
            if c == 0 and square:
                *before, bias_grad = mlp_backward(early, slopes[c], up_blocks[pair], [], before, c, calls)
            else:
                *before, bias_grad = mlp_backward(
                    cot_late, slopes[c], up_blocks[pair], down_blocks[pair], before, c, calls
                )
            bias_grads.append(bias_grad)
            if c == 0:
                down_stage, before = sum_near(down_grads, before)
        ring = ring_plan()
        pre_grad, total = before

        if square:
            ahead = weight_back(normed_mlp, pre_grad, [1, 3], None, None, tensor_size)
            total, ahead = tie(total, ahead)
        grad_residual, grad_low, small_rows, pieces = residual_back(
            total, residual, cotangent, own_scale, place, out_weight, mlp_gain_row, tensor_size
        )
        down_sum, pieces = sum_far(down_stage, pieces)
        grad_attended = exchange(pieces)
        if square:
            up_near, up_diag_near = swap(ahead[0], 1), swap(ahead[1], 1)
            first, second, *out_grads = weight_back(
                normed_mlp, pre_grad, [2, 0], attended_rows, grad_low, tensor_size
            )
            second, (up_near, up_diag_near) = tie(second, (up_near, up_diag_near))
            up_far_sum = (first.astype(f32) + up_diag_near.astype(f32)).astype(bf16)
            out_stage, up_far_sum = sum_near(out_grads, up_far_sum)
            up_far_sum, grad_attended = tie(up_far_sum, grad_attended)
            up_stage = (second, up_near, up_far_sum)
        else:
            weight_grads = weight_back(
                normed_mlp, pre_grad, list(range(tensor_size)), attended_rows, grad_low, tensor_size
            )
            up_stage, grad_attended = sum_near(weight_grads[:tensor_size], grad_attended)
            out_stage, grad_attended = sum_near(weight_grads[tensor_size:], grad_attended)
        bias_rows = in_order(jnp.concatenate(bias_grads, axis=1).reshape(tensor_size, -1))
        smalls = jnp.concatenate([small_rows[:4].reshape(-1), bias_rows.reshape(-1)]).reshape(-1, 128)

        waiting = list(steps)
        weights_wide = query_key_value_weight.astype(f32)
        sums = None
        grad_normed = []
        for i in range(slot_count):
            last = i == slot_count - 1
            dqkv = attend_back(qkvs[i], attended[i], grad_attended, i, lses[i])
            if i >= 2:
                grad_normed[i - 2], dqkv = terms_far(grad_normed[i - 2], dqkv)
            if i >= 1 and not last:
                grad_normed[i - 1], dqkv = sum_near(grad_normed[i - 1], dqkv)
            if i == 0:
                up_sum, dqkv = sum_far(up_stage, dqkv)
                out_sum, dqkv = sum_far(out_stage, dqkv)
                up_all = lax.psum((up_sum, out_sum), "dp")
            if last:
                dqkv, up_all = tie(dqkv, up_all)
            if waiting and i > 0:
                smalls, dqkv = sum_step(smalls, waiting.pop(0), dqkv)
            if ring:
                down_sum, dqkv = ring_step(down_sum, ring.pop(0), dqkv)
            results = project_back(place, normed_every[i], dqkv, query_key_value_weight, sums, last, tensor_size)
            if not last:
                partial, sums = results[:tensor_size], results[tensor_size:]
                if waiting:
                    smalls, partial = sum_step(smalls, waiting.pop(0), partial)
                if ring:
                    down_sum, partial = ring_step(down_sum, ring.pop(0), partial)
            else:
                *sums, qkv_low = results
                qkv_low, (dqkv, grad_residual, layer_sum) = tie(qkv_low, (dqkv, grad_residual, layer_sum))
                qkv_all = lax.psum(qkv_low, "dp")
                output = layer_out(layer_sum, residual, down_bias[None, :], own_valid, patches.shape)
                partial = project_rows(place, dqkv, query_key_value_weight, tensor_size)
                if i >= 1:
                    grad_normed[i - 1], partial = sum_near(grad_normed[i - 1], partial)
                raw = jnp.stack(
                    [
                        jnp.sum(sums[0] * weights_wide, axis=(0, 2)),
                        jnp.sum(sums[1][:3, None, :] * weights_wide, axis=(0, 2)),
                    ]
                )
                for axis, pairs in steps:
                    raw = raw + lax.ppermute(raw, axis, pairs)
            grad_normed.append(partial)
        grad_inputs = None
        for i in range(slot_count):
            if i == slot_count - 1:
                grad_normed[i], grad_residual = sum_near(grad_normed[i], grad_residual)
            terms = grad_normed[i]
            if i >= slot_count - 2:
                terms, grad_residual = terms_far(terms, grad_residual)
            grad_inputs = input_back(terms, patches, i, grad_residual, gain_row, grad_inputs)
        grad_inputs, qkv_all = tie(grad_inputs, qkv_all)
        for step in ring:
            down_sum = ring_step(down_sum, step, place)[0]
        for step in waiting:
            smalls = sum_step(smalls, step, place)[0]
        weight_grad = qkv_all[:, :model].astype(f32)
        columns = qkv_all[:, model].astype(f32)
        up_all, out_all = [value.astype(f32) for value in up_all]
        down_all = down_sum.astype(f32)
        inverse = 1.0 / total_items
        smalls = smalls.reshape(-1) * inverse
        raw = raw * inverse
        small_rows = smalls[: 4 * model].reshape(4, model)
        units = up_bias.shape[0]
        bias_all = lax.dynamic_slice_in_dim(smalls[4 * model :], lax.axis_index("tensor") * units, units)
        shift_all = raw[1]
        gain_all = (raw[0] - attn_shift * shift_all) / attn_gain
        columns = columns * inverse
        return (
            output,
            grad_inputs,
            weight_grad * inverse,
            jnp.stack([columns[0], columns[2]]),
            out_all * inverse,
            small_rows[2],
            up_all * inverse,
            bias_all,
            down_all * inverse,
            small_rows[3],
            gain_all,
            shift_all,
            small_rows[0],
            small_rows[1],
        )

    return shards


def solution(mesh):
    items = P("dp", "tensor", None)
    return jax.shard_map(
        make_shards(mesh.shape["tensor"], mesh.shape["dp"]),
        mesh=mesh,
        in_specs=(
            items,
            items,
            P(),
            P(),
            P(),
            P(None, None, "tensor"),
            P(None, "tensor"),
            P("tensor", None),
            P(),
            P(None, "tensor"),
            P("tensor"),
            P("tensor", None),
            P(),
            P(),
            P(),
            P(),
            P(),
        ),
        out_specs=(
            items,
            items,
            P(None, None, "tensor"),
            P(None, "tensor"),
            P("tensor", None),
            P(),
            P(None, "tensor"),
            P("tensor"),
            P("tensor", None),
            P(),
            P(),
            P(),
            P(),
            P(),
        ),
        check_vma=False,
    )
```

```python
import jax
import jax.numpy as jnp
from jax import lax
from jax.experimental import pallas as pl
from jax.experimental.pallas import tpu as pltpu
from jax.sharding import PartitionSpec as P

HD = 64
SCORE_SCALE = HD ** (-0.5)
LOG2E = 1.4426950408889634
SQRT_HALF = 0.7071067811865476
INV_SQRT_2PI = 0.3989422804014327
epsilon = 1e-05
f32 = jnp.float32
bf16 = jnp.bfloat16
VMEM_LIMIT = 60 << 20
COST_SCALE = 64


def nn(a, b):
    return lax.dot_general(a, b, (((1,), (0,)), ((), ())), preferred_element_type=f32)


def nt(a, b):
    return lax.dot_general(a, b, (((1,), (1,)), ((), ())), preferred_element_type=f32)


def tn(a, b):
    return lax.dot_general(a, b, (((0,), (0,)), ((), ())), preferred_element_type=f32)


def tie(first, second):
    return lax.optimization_barrier((first, second))


def largest_block(extent, limit):
    block = min(extent, limit)
    while extent % block:
        block //= 2
    return block


def norm_rows(source, norm_gain, norm_shift):
    row_mean = jnp.mean(source, axis=-1, keepdims=True)
    centred = source - row_mean
    spread = jnp.mean(centred * centred, axis=-1, keepdims=True)
    return centred * lax.rsqrt(spread + epsilon) * norm_gain + norm_shift


def attend(qkv):
    _, length, width = qkv.shape
    lanes = min(128, width)
    heads = lanes // HD
    qblock = largest_block(length, 2048)
    to_log2 = SCORE_SCALE * LOG2E

    def body(q_ref, k_ref, v_ref, out_ref, lse_ref):
        queries = q_ref[...]
        keys = k_ref[...]
        values_t = v_ref[...].T
        lane = lax.broadcasted_iota(jnp.int32, (1, lanes), 1)
        outs = []
        for h in range(heads):
            own = queries
            if heads > 1:
                own = jnp.where(lane // HD == h, queries, jnp.zeros_like(queries))
            scores = nt(keys, own)
            top = jnp.max(scores, axis=0, keepdims=True)
            exp_scores = jnp.exp2((scores - top) * to_log2)
            total = jnp.sum(exp_scores, axis=0, keepdims=True)
            outs.append(nn(values_t[h * HD : (h + 1) * HD, :], exp_scores.astype(bf16)) / total)
            lse_ref[h : h + 1, :] = top * to_log2 + jnp.log2(total)
        out_ref[...] = jnp.concatenate(outs, axis=0).T.astype(bf16)

    pairs = width // lanes
    return pl.pallas_call(
        body,
        grid=(pairs, length // qblock),
        in_specs=[
            pl.BlockSpec((None, qblock, lanes), lambda h, j: (0, j, h)),
            pl.BlockSpec((None, length, lanes), lambda h, j: (1, 0, h)),
            pl.BlockSpec((None, length, lanes), lambda h, j: (2, 0, h)),
        ],
        out_specs=[
            pl.BlockSpec((qblock, lanes), lambda h, j: (j, h)),
            pl.BlockSpec((None, heads, qblock), lambda h, j: (h, 0, j)),
        ],
        out_shape=[
            jax.ShapeDtypeStruct((length, width), bf16),
            jax.ShapeDtypeStruct((pairs, heads, length), f32),
        ],
        compiler_params=pltpu.CompilerParams(vmem_limit_bytes=VMEM_LIMIT),
        cost_estimate=pl.CostEstimate(
            flops=8 * length * length * width // COST_SCALE,
            transcendentals=0,
            bytes_accessed=length * width,
        ),
        name="attend",
    )(qkv, qkv, qkv)


def attend_back(qkv, attended, grad_attended, item, lse):
    _, length, width = qkv.shape
    lanes = min(128, width)
    shards_of = grad_attended.shape[0]
    heads = lanes // HD
    kblock = largest_block(length, 1024)
    kblocks = length // kblock
    to_log2 = SCORE_SCALE * LOG2E

    def body(q_ref, k_ref, v_ref, out_ref, grad_ref, lse_ref, dqkv_ref, dq_acc, row_dot):
        kb = pl.program_id(1)
        queries = q_ref[...]
        grads = grad_ref[...].reshape(length, lanes)
        keys = k_ref[...]
        values = v_ref[...]
        keys_t = keys.T
        lane = lax.broadcasted_iota(jnp.int32, (1, lanes), 1)

        @pl.when(kb == 0)
        def _():
            product = out_ref[...].astype(f32) * grads.astype(f32)
            high = product.astype(bf16)
            rest = (product - high.astype(f32)).astype(bf16)
            pick = lax.broadcasted_iota(jnp.int32, (8, lanes), 0)
            mask = (lax.broadcasted_iota(jnp.int32, (8, lanes), 1) // HD == pick).astype(f32).astype(bf16)
            row_dot[...] = nt(mask, high) + nt(mask, rest)

        dk = None
        dv = None
        dqs = []
        for h in range(heads):
            own_q = queries
            own_g = grads
            if heads > 1:
                mine = lane // HD == h
                own_q = jnp.where(mine, queries, jnp.zeros_like(queries))
                own_g = jnp.where(mine, grads, jnp.zeros_like(grads))
            scores = nt(keys, own_q)
            weights = jnp.exp2(scores * to_log2 - lse_ref[h : h + 1, :])
            grad_weights = nt(values, own_g)
            grad_scores = (weights * (grad_weights - row_dot[h : h + 1, :])).astype(bf16)
            dv_h = nn(weights.astype(bf16), own_g)
            dk_h = nn(grad_scores, own_q)
            dv = dv_h if dv is None else dv + dv_h
            dk = dk_h if dk is None else dk + dk_h
            dqs.append(nn(keys_t[h * HD : (h + 1) * HD, :], grad_scores))
        rows = pl.ds(pl.multiple_of(kb * kblock, kblock), kblock)
        dqkv_ref[1, rows, :] = (dk * SCORE_SCALE).astype(bf16)
        dqkv_ref[2, rows, :] = dv.astype(bf16)
        dq = jnp.concatenate(dqs, axis=0)
        if kblocks == 1:
            dqkv_ref[0] = (dq * SCORE_SCALE).T.astype(bf16)
            return

        @pl.when(kb == 0)
        def _():
            dq_acc[...] = dq

        @pl.when((kb > 0) & (kb < kblocks - 1))
        def _():
            dq_acc[...] += dq

        @pl.when(kb == kblocks - 1)
        def _():
            dqkv_ref[0] = ((dq_acc[...] + dq) * SCORE_SCALE).T.astype(bf16)

    pairs = width // lanes
    return pl.pallas_call(
        body,
        grid=(pairs, kblocks),
        in_specs=[
            pl.BlockSpec((None, length, lanes), lambda h, kb: (0, 0, h)),
            pl.BlockSpec((None, kblock, lanes), lambda h, kb: (1, kb, h)),
            pl.BlockSpec((None, kblock, lanes), lambda h, kb: (2, kb, h)),
            pl.BlockSpec((length, lanes), lambda h, kb: (0, h)),
            pl.BlockSpec((shards_of, length // shards_of, lanes), lambda h, kb: (0, item, h)),
            pl.BlockSpec((None, heads, length), lambda h, kb: (h, 0, 0)),
        ],
        out_specs=pl.BlockSpec((3, length, lanes), lambda h, kb: (0, 0, h)),
        out_shape=jax.ShapeDtypeStruct((3, length, width), bf16),
        scratch_shapes=[pltpu.VMEM((lanes, length), f32), pltpu.VMEM((8, length), f32)],
        compiler_params=pltpu.CompilerParams(vmem_limit_bytes=VMEM_LIMIT),
        cost_estimate=pl.CostEstimate(
            flops=20 * length * length * width // COST_SCALE,
            transcendentals=0,
            bytes_accessed=length * width,
        ),
        name="attend_back",
    )(qkv, qkv, qkv, attended, grad_attended, lse)


def hint(flops, size):
    return pl.CostEstimate(flops=flops // COST_SCALE, transcendentals=0, bytes_accessed=size)


def params():
    return pltpu.CompilerParams(vmem_limit_bytes=VMEM_LIMIT)


def add_terms(*terms):
    rows, columns = terms[0].shape
    block = largest_block(rows, 256)

    def body(*refs):
        total = refs[0][...].astype(f32)
        for ref in refs[1:-1]:
            total = total + ref[...].astype(f32)
        refs[-1][...] = total.astype(refs[-1].dtype)

    spec = pl.BlockSpec((block, columns), lambda i: (i, 0))
    return pl.pallas_call(
        body,
        grid=(rows // block,),
        in_specs=[spec] * len(terms),
        out_specs=spec,
        out_shape=jax.ShapeDtypeStruct((rows, columns), terms[0].dtype),
        compiler_params=params(),
        cost_estimate=hint(0, rows * columns),
        name="add_terms",
    )(*terms)


def join_halves(side, own, other):
    half, columns = own.shape

    def body(side_ref, own_ref, other_ref, out_ref):
        first = pl.multiple_of(side_ref[0] * half, half)
        second = pl.multiple_of((1 - side_ref[0]) * half, half)
        out_ref[pl.ds(first, half), :] = own_ref[...]
        out_ref[pl.ds(second, half), :] = other_ref[...]

    width = largest_block(columns, 256)
    spec = pl.BlockSpec((half, width), lambda i: (0, i))
    return pl.pallas_call(
        body,
        grid=(columns // width,),
        in_specs=[pl.BlockSpec(memory_space=pltpu.SMEM), spec, spec],
        out_specs=pl.BlockSpec((2 * half, width), lambda i: (0, i)),
        out_shape=jax.ShapeDtypeStruct((2 * half, columns), own.dtype),
        compiler_params=params(),
        cost_estimate=hint(0, half * columns),
        name="join_halves",
    )(side, own, other)


def project(rows_in, weight, bias):
    rows, model = rows_in.shape
    width = weight.shape[2]
    block = largest_block(rows, 512)

    def body(x_ref, weight_ref, bias_ref, out_ref):
        for c in range(3):
            out_ref[c] = (nn(x_ref[...], weight_ref[c]) + bias_ref[c]).astype(bf16)

    return pl.pallas_call(
        body,
        grid=(rows // block,),
        in_specs=[
            pl.BlockSpec((block, model), lambda i: (i, 0)),
            pl.BlockSpec((3, model, width), lambda i: (0, 0, 0)),
            pl.BlockSpec((3, 1, width), lambda i: (0, 0, 0)),
        ],
        out_specs=pl.BlockSpec((3, block, width), lambda i: (0, i, 0)),
        out_shape=jax.ShapeDtypeStruct((3, rows, width), bf16),
        compiler_params=params(),
        cost_estimate=hint(6 * rows * model * width, rows * width),
        name="project",
    )(rows_in, weight, bias)


def norm_item(patches, item, norm_gain, norm_shift):
    _, rows, model = patches.shape
    block = largest_block(rows, 256)

    def body(x_ref, gain_ref, shift_ref, out_ref):
        out_ref[...] = norm_rows(x_ref[...].astype(f32), gain_ref[...], shift_ref[...]).astype(bf16)

    vector = pl.BlockSpec((1, model), lambda i: (0, 0))
    return pl.pallas_call(
        body,
        grid=(rows // block,),
        in_specs=[pl.BlockSpec((None, block, model), lambda i: (item, i, 0)), vector, vector],
        out_specs=pl.BlockSpec((block, model), lambda i: (i, 0)),
        out_shape=jax.ShapeDtypeStruct((rows, model), bf16),
        compiler_params=params(),
        cost_estimate=hint(0, rows * model),
        name="norm_item",
    )(patches, norm_gain, norm_shift)


def out_project(patches, item, place, heads, weight, out_bias, norm_gain, norm_shift, before):
    slots, rows, model = patches.shape
    block = largest_block(rows, 256)
    steps = rows // block
    count, _, width = heads.shape

    def body(*refs):
        place_ref, x_ref, weight_ref, bias_ref, gain_ref, shift_ref, head_ref = refs[:7]
        attended_ref, residual_ref, normed_ref = refs[-3:]
        for k in range(count):
            attended_ref[:, k * width : (k + 1) * width] = head_ref[place_ref[0] ^ k]
        attended = attended_ref[...]
        residual = x_ref[...].astype(f32) + nn(attended, weight_ref[...]) + bias_ref[...]
        residual_ref[...] = residual
        normed_ref[...] = norm_rows(residual, gain_ref[...], shift_ref[...]).astype(bf16)

    vector = pl.BlockSpec((1, model), lambda i: (0, 0))
    placed = pl.BlockSpec((block, model), lambda i: (item * steps + i, 0))
    operands = [place, patches, weight, out_bias, norm_gain, norm_shift, heads]
    in_specs = [
        pl.BlockSpec(memory_space=pltpu.SMEM),
        pl.BlockSpec((None, block, model), lambda i: (item, i, 0)),
        pl.BlockSpec((model, model), lambda i: (0, 0)),
        vector,
        vector,
        vector,
        pl.BlockSpec((count, block, width), lambda i: (0, i, 0)),
    ]
    aliases = {}
    if before is not None:
        aliases = {len(operands) + k: k for k in range(3)}
        operands += before
        in_specs += [pl.BlockSpec(memory_space=pl.ANY)] * 3
    return pl.pallas_call(
        body,
        grid=(steps,),
        in_specs=in_specs,
        out_specs=[placed] * 3,
        out_shape=[jax.ShapeDtypeStruct((slots * rows, model), t) for t in (bf16, f32, bf16)],
        input_output_aliases=aliases,
        compiler_params=params(),
        cost_estimate=hint(2 * rows * model * model, rows * model),
        name="out_project",
    )(*operands)


def residual_back(total, residual, cotangent, scale, place, weight, norm_gain, pieces):
    slots, rows, model = cotangent.shape
    block = largest_block(rows, 256)
    steps = rows // block
    piece = model // pieces

    def body(*refs):
        place_ref, total_ref, residual_ref, cot_ref, scale_ref, weight_ref, gain_ref = refs[:7]
        grad_ref, low_ref, sum_ref, attended_ref = refs[-4:]
        residual = residual_ref[...]
        centred = residual - jnp.mean(residual, axis=-1, keepdims=True)
        rate = lax.rsqrt(jnp.mean(centred * centred, axis=-1, keepdims=True) + epsilon)
        xhat = centred * rate
        grad_normed = total_ref[...]
        scaled = grad_normed * gain_ref[...]
        inner = jnp.mean(scaled, axis=-1, keepdims=True)
        outer = jnp.mean(scaled * xhat, axis=-1, keepdims=True)
        cot = cot_ref[...].astype(f32) * scale_ref[pl.program_id(0) // steps]
        grad = cot + rate * (scaled - inner - xhat * outer)
        grad_ref[...] = grad
        low = grad.astype(bf16)
        low_ref[...] = low

        @pl.when(pl.program_id(0) == 0)
        def _():
            sum_ref[...] = jnp.zeros_like(sum_ref)

        for k, value in enumerate((grad_normed * xhat, grad_normed, grad, cot)):
            sum_ref[k : k + 1, :] += jnp.sum(value, axis=0, keepdims=True)
        attended = nt(low, weight_ref[...]).astype(bf16)
        for k in range(pieces):
            attended_ref[place_ref[0] ^ k] = attended[:, k * piece : (k + 1) * piece]

    row_spec = pl.BlockSpec((block, model), lambda i: (i, 0))
    return pl.pallas_call(
        body,
        grid=(slots * steps,),
        in_specs=[
            pl.BlockSpec(memory_space=pltpu.SMEM),
            row_spec,
            row_spec,
            pl.BlockSpec((None, block, model), lambda i: (i // steps, i % steps, 0)),
            pl.BlockSpec(memory_space=pltpu.SMEM),
            pl.BlockSpec((model, model), lambda i: (0, 0)),
            pl.BlockSpec((1, model), lambda i: (0, 0)),
        ],
        out_specs=[
            row_spec,
            row_spec,
            pl.BlockSpec((8, model), lambda i: (0, 0)),
            pl.BlockSpec((pieces, block, piece), lambda i: (0, i, 0)),
        ],
        out_shape=[
            jax.ShapeDtypeStruct((slots * rows, model), f32),
            jax.ShapeDtypeStruct((slots * rows, model), bf16),
            jax.ShapeDtypeStruct((8, model), f32),
            jax.ShapeDtypeStruct((pieces, slots * rows, piece), bf16),
        ],
        compiler_params=params(),
        cost_estimate=hint(2 * slots * rows * model * model, rows * model),
        name="residual_back",
    )(place, total, residual, cotangent, scale, weight, norm_gain)


def input_back(terms, patches, item, grad_residual, norm_gain, before):
    slots, rows, model = patches.shape
    block = largest_block(rows, 256)
    count = len(terms)

    def body(*refs):
        x_ref, grad_ref, gain_ref = refs[:3]
        out_ref = refs[-1]
        grad_normed = refs[3][...].astype(f32)
        for k in range(1, count):
            grad_normed = grad_normed + refs[3 + k][...].astype(f32)
        source = x_ref[...].astype(f32)
        centred = source - jnp.mean(source, axis=-1, keepdims=True)
        rate = lax.rsqrt(jnp.mean(centred * centred, axis=-1, keepdims=True) + epsilon)
        xhat = centred * rate
        scaled = grad_normed * gain_ref[...]
        inner = jnp.mean(scaled, axis=-1, keepdims=True)
        outer = jnp.mean(scaled * xhat, axis=-1, keepdims=True)
        out_ref[...] = (grad_ref[...] + rate * (scaled - inner - xhat * outer)).astype(bf16)

    row_spec = pl.BlockSpec((block, model), lambda i: (i, 0))
    placed = pl.BlockSpec((None, block, model), lambda i: (item, i, 0))
    operands = [patches, grad_residual, norm_gain, *terms]
    steps = rows // block
    grad_spec = pl.BlockSpec((block, model), lambda i: (item * steps + i, 0))
    in_specs = [placed, grad_spec, pl.BlockSpec((1, model), lambda i: (0, 0))] + [row_spec] * count
    aliases = {}
    if before is not None:
        aliases = {len(operands): 0}
        operands.append(before)
        in_specs.append(pl.BlockSpec(memory_space=pl.ANY))
    return pl.pallas_call(
        body,
        grid=(rows // block,),
        in_specs=in_specs,
        out_specs=placed,
        out_shape=jax.ShapeDtypeStruct((slots, rows, model), bf16),
        input_output_aliases=aliases,
        compiler_params=params(),
        cost_estimate=hint(0, rows * model),
        name="input_back",
    )(*operands)


def layer_out(total, residual, down_bias, valid, shape):
    slots, rows, model = shape
    block = largest_block(rows, 256)
    steps = rows // block

    def body(total_ref, residual_ref, bias_ref, valid_ref, out_ref):
        value = residual_ref[...] + total_ref[...] + bias_ref[...]
        out_ref[...] = (value * valid_ref[pl.program_id(0) // steps]).astype(bf16)

    row_spec = pl.BlockSpec((block, model), lambda i: (i, 0))
    return pl.pallas_call(
        body,
        grid=(slots * steps,),
        in_specs=[
            row_spec,
            row_spec,
            pl.BlockSpec((1, model), lambda i: (0, 0)),
            pl.BlockSpec(memory_space=pltpu.SMEM),
        ],
        out_specs=pl.BlockSpec((None, block, model), lambda i: (i // steps, i % steps, 0)),
        out_shape=jax.ShapeDtypeStruct(shape, bf16),
        compiler_params=params(),
        cost_estimate=hint(0, rows * model),
        name="layer_out",
    )(total, residual, down_bias, valid)


def mlp_forward(normed, cot, ups, biases, downs, total):
    rows, model = normed.shape
    count = len(ups)
    units = ups[0].shape[1]
    block = largest_block(rows, 512)
    steps = rows // block
    first = total is None

    def body(*refs):
        x_ref, cot_ref = refs[:2]
        up_refs, bias_refs, down_refs = (refs[2 + k * count : 2 + (k + 1) * count] for k in range(3))
        rest = refs[2 + 3 * count :]
        if not first:
            before_ref = rest[0]
            rest = rest[1:]
        slope_ref, sum_ref = rest[:2]
        grad_refs = rest[2 : 2 + count]
        hidden_ref, acc_ref = rest[2 + count :]
        step = pl.program_id(0)
        part = largest_block(units, 256)
        for k in range(count):
            for j in range(units // part):
                cols = slice(j * part, (j + 1) * part)
                wide = slice(k * units + j * part, k * units + (j + 1) * part)
                pre = nn(x_ref[...], up_refs[k][:, cols]) + bias_refs[k][:, cols]
                cdf = 0.5 + 0.5 * lax.erf(pre * SQRT_HALF)
                density = jnp.exp2(pre * pre * (-0.5 * LOG2E)) * INV_SQRT_2PI
                hidden_ref[:, wide] = (pre * cdf).astype(bf16)
                slope_ref[:, wide] = (cdf + pre * density).astype(bf16)
        out = None if first else before_ref[...]
        for k in range(count):
            hidden = hidden_ref[:, k * units : (k + 1) * units]
            product = nn(hidden, down_refs[k][...])
            out = product if out is None else out + product
            grad = tn(hidden, cot_ref[...])

            @pl.when(step == 0)
            def _():
                acc_ref[k] = grad

            @pl.when(step > 0)
            def _():
                acc_ref[k] += grad

        sum_ref[...] = out

        @pl.when(step == steps - 1)
        def _():
            for k in range(count):
                grad_refs[k][...] = acc_ref[k].astype(bf16)

    row_spec = pl.BlockSpec((block, model), lambda i: (i, 0))
    slope_spec = pl.BlockSpec((block, count * units), lambda i: (i, 0))
    up_spec = pl.BlockSpec((model, units), lambda i: (0, 0), pipeline_mode=pl.Buffered(1))
    down_spec = pl.BlockSpec((units, model), lambda i: (0, 0), pipeline_mode=pl.Buffered(1))
    grad_spec = pl.BlockSpec((units, model), lambda i: (0, 0))
    operands = [normed, cot, *ups, *biases, *downs]
    in_specs = [row_spec, row_spec] + [up_spec] * count
    in_specs += [pl.BlockSpec((1, units), lambda i: (0, 0))] * count + [down_spec] * count
    aliases = {}
    if not first:
        aliases = {len(operands): 1}
        operands.append(total)
        in_specs.append(row_spec)
    return pl.pallas_call(
        body,
        grid=(steps,),
        in_specs=in_specs,
        out_specs=[slope_spec, row_spec] + [grad_spec] * count,
        out_shape=[
            jax.ShapeDtypeStruct((rows, count * units), bf16),
            jax.ShapeDtypeStruct((rows, model), f32),
        ]
        + [jax.ShapeDtypeStruct((units, model), bf16)] * count,
        scratch_shapes=[pltpu.VMEM((block, count * units), bf16), pltpu.VMEM((count, units, model), f32)],
        input_output_aliases=aliases,
        compiler_params=params(),
        cost_estimate=hint(6 * rows * model * units * count, rows * units),
        name="mlp_forward",
    )(*operands)


def cot_back(cot, downs):
    rows, model = cot.shape
    count = len(downs)
    units = downs[0].shape[0]
    block = largest_block(rows, 512)

    def body(cot_ref, *refs):
        for k in range(count):
            refs[count][:, k * units : (k + 1) * units] = nt(cot_ref[...], refs[k][...]).astype(bf16)

    return pl.pallas_call(
        body,
        grid=(rows // block,),
        in_specs=[pl.BlockSpec((block, model), lambda i: (i, 0))]
        + [pl.BlockSpec((units, model), lambda i: (0, 0))] * count,
        out_specs=pl.BlockSpec((block, count * units), lambda i: (i, 0)),
        out_shape=jax.ShapeDtypeStruct((rows, count * units), bf16),
        compiler_params=params(),
        cost_estimate=hint(2 * rows * model * units * count, rows * units),
        name="cot_back",
    )(cot, *downs)


def mlp_backward(cot, slope, ups, downs, before, index, calls):
    rows, _ = cot.shape
    model = ups[0].shape[0]
    count = len(ups)
    units = ups[0].shape[1]
    block = largest_block(rows, 512)
    first = before is None

    def body(*refs):
        cot_ref, slope_ref = refs[:2]
        up_refs, down_refs = refs[2 : 2 + count], refs[2 + count : 2 + count + len(downs)]
        grad_ref, sum_ref, bias_ref = refs[-3:]

        @pl.when(pl.program_id(0) == 0)
        def _():
            bias_ref[...] = jnp.zeros_like(bias_ref)

        out = None if first else refs[3 + count + len(downs)][...]
        part = largest_block(units, 512)
        for k in range(count):
            for j in range(units // part):
                rows_of = slice(j * part, (j + 1) * part)
                wide = slice(k * units + j * part, k * units + (j + 1) * part)
                if downs:
                    product = nt(cot_ref[...], down_refs[k][rows_of, :])
                else:
                    product = cot_ref[:, wide].astype(f32)
                low = (product * slope_ref[:, wide].astype(f32)).astype(bf16)
                grad_ref[:, wide] = low
                bias_ref[:, wide] += jnp.sum(low.astype(f32), axis=0, keepdims=True)
            product = nt(grad_ref[:, k * units : (k + 1) * units], up_refs[k][...])
            out = product if out is None else out + product
        sum_ref[...] = out

    row_spec = pl.BlockSpec((block, model), lambda i: (i, 0))
    slope_spec = pl.BlockSpec((block, count * units), lambda i: (i, 0))
    up_spec = pl.BlockSpec((model, units), lambda i: (0, 0), pipeline_mode=pl.Buffered(1))
    down_spec = pl.BlockSpec((units, model), lambda i: (0, 0), pipeline_mode=pl.Buffered(1))
    operands = [cot, slope, *ups, *downs]
    in_specs = [row_spec if downs else slope_spec, slope_spec] + [up_spec] * count + [down_spec] * len(downs)
    aliases = {}
    if not first:
        aliases = {len(operands): 0, len(operands) + 1: 1}
        operands += before
        in_specs += [pl.BlockSpec(memory_space=pl.ANY), row_spec]
    return pl.pallas_call(
        body,
        grid=(rows // block,),
        in_specs=in_specs,
        out_specs=[
            pl.BlockSpec((block, count * units), lambda i: (i, index)),
            row_spec,
            pl.BlockSpec((1, count * units), lambda i: (0, 0)),
        ],
        out_shape=[
            jax.ShapeDtypeStruct((rows, calls * count * units), bf16),
            jax.ShapeDtypeStruct((rows, model), f32),
            jax.ShapeDtypeStruct((1, count * units), f32),
        ],
        input_output_aliases=aliases,
        compiler_params=params(),
        cost_estimate=hint(4 * rows * model * units * count, rows * units),
        name="mlp_backward",
    )(*operands)


def weight_back(normed, pre_grad, picks, attended, grad_low, pieces):
    rows, model = normed.shape
    units = pre_grad.shape[1] // pieces
    piece = model // pieces
    block = largest_block(rows, 512)
    steps = rows // block
    count = len(picks)
    outs = 0 if attended is None else pieces

    def body(x_ref, *refs):
        pre_refs = refs[:count]
        rest = refs[count:]
        if outs:
            attended_ref, grad_ref = rest[:2]
            rest = rest[2:]
        up_refs, out_refs = rest[:count], rest[count : count + outs]
        up_acc = rest[count + outs]
        step = pl.program_id(0)

        def add(acc, place, value):
            @pl.when(step == 0)
            def _():
                acc[place] = value

            @pl.when(step > 0)
            def _():
                acc[place] += value

        for k in range(count):
            add(up_acc, (slice(None), slice(k * units, (k + 1) * units)), tn(x_ref[...], pre_refs[k][...]))
        if outs:
            out_acc = rest[-1]
            add(out_acc, (slice(None), slice(None)), tn(attended_ref[...], grad_ref[...]))

        @pl.when(step == steps - 1)
        def _():
            for k in range(count):
                up_refs[k][...] = up_acc[:, k * units : (k + 1) * units].astype(bf16)
            for k in range(outs):
                out_refs[k][...] = out_acc[k * piece : (k + 1) * piece, :].astype(bf16)

    row_spec = pl.BlockSpec((block, model), lambda i: (i, 0))

    def columns_of(pick):
        return pl.BlockSpec((block, units), lambda i: (i, pick))

    operands = [normed] + [pre_grad] * count
    in_specs = [row_spec] + [columns_of(pick) for pick in picks]
    scratch = [pltpu.VMEM((model, count * units), f32)]
    if outs:
        operands += [attended, grad_low]
        in_specs += [row_spec, row_spec]
        scratch.append(pltpu.VMEM((model, model), f32))
    return pl.pallas_call(
        body,
        grid=(steps,),
        in_specs=in_specs,
        out_specs=[pl.BlockSpec((model, units), lambda i: (0, 0))] * count
        + [pl.BlockSpec((piece, model), lambda i: (0, 0))] * outs,
        out_shape=[jax.ShapeDtypeStruct((model, units), bf16)] * count
        + [jax.ShapeDtypeStruct((piece, model), bf16)] * outs,
        scratch_shapes=scratch,
        compiler_params=params(),
        cost_estimate=hint(2 * rows * model * units * count, rows * model),
        name="weight_back",
    )(*operands)


def project_back(place, normed, dqkv, weight, before, last, pieces):
    rows, model = normed.shape
    width = weight.shape[2]
    block = rows // pieces
    steps = pieces
    first = before is None
    given = 0 if last else pieces

    def kernel(*refs):
        place_ref, normed_ref, dqkv_ref, weight_ref = refs[:4]
        rest = refs[4:]
        if not first:
            wgrad_before, column_before = rest[:2]
            rest = rest[2:]
        row_refs, rest = rest[:given], rest[given:]
        wgrad_ref, column_ref = rest[:2]
        step = pl.program_id(0)

        @pl.when(step == 0)
        def _():
            if first:
                wgrad_ref[...] = jnp.zeros_like(wgrad_ref)
                column_ref[...] = jnp.zeros_like(column_ref)
            else:
                wgrad_ref[...] = wgrad_before[...]
                column_ref[...] = column_before[...]

        if not last:
            row_grad = nt(dqkv_ref[0], weight_ref[0])
            for c in range(1, 3):
                row_grad = row_grad + nt(dqkv_ref[c], weight_ref[c])
            row_grad = row_grad.astype(bf16)
            for k in range(pieces):

                @pl.when(step == place_ref[0] ^ k)
                def _():
                    row_refs[k][...] = row_grad

        for c in range(3):
            wgrad_ref[c] += tn(normed_ref[...], dqkv_ref[c])
            column_ref[c : c + 1, :] += jnp.sum(dqkv_ref[c].astype(f32), axis=0, keepdims=True)
        if last:
            low_ref = rest[2]

            @pl.when(step == steps - 1)
            def _():
                low_ref[:, :model, :] = wgrad_ref[...].astype(bf16)
                for c in range(3):
                    row = jnp.broadcast_to(column_ref[c : c + 1, :], (16, width))
                    low_ref[c, model:, :] = row.astype(bf16)

    whole = pl.BlockSpec((3, model, width), lambda i: (0, 0, 0))
    columns = pl.BlockSpec((8, width), lambda i: (0, 0))
    row_spec = pl.BlockSpec((block, model), lambda i: (i, 0))
    operands = [place, normed, dqkv, weight]
    in_specs = [pl.BlockSpec(memory_space=pltpu.SMEM), row_spec, pl.BlockSpec((3, block, width), lambda i: (0, i, 0)), whole]
    if not first:
        operands += list(before)
        in_specs += [whole, columns]
    out_specs = [pl.BlockSpec((block, model), lambda i: (0, 0))] * given + [whole, columns]
    out_shape = [jax.ShapeDtypeStruct((block, model), bf16)] * given + [
        jax.ShapeDtypeStruct((3, model, width), f32),
        jax.ShapeDtypeStruct((8, width), f32),
    ]
    if last:
        out_specs.append(pl.BlockSpec((3, model + 16, width), lambda i: (0, 0, 0)))
        out_shape.append(jax.ShapeDtypeStruct((3, model + 16, width), bf16))
    return pl.pallas_call(
        kernel,
        grid=(steps,),
        in_specs=in_specs,
        out_specs=out_specs,
        out_shape=out_shape,
        input_output_aliases={} if first else {4: given, 5: given + 1},
        compiler_params=pltpu.CompilerParams(vmem_limit_bytes=VMEM_LIMIT),
        cost_estimate=pl.CostEstimate(
            flops=12 * rows * model * width // COST_SCALE,
            transcendentals=0,
            bytes_accessed=rows * width,
        ),
        name="project_back",
    )(*operands)


def project_rows(place, dqkv, weight, pieces):
    _, rows, width = dqkv.shape
    model = weight.shape[1]
    block = rows // pieces

    def kernel(place_ref, dqkv_ref, weight_ref, *row_refs):
        row_grad = nt(dqkv_ref[0], weight_ref[0])
        for c in range(1, 3):
            row_grad = row_grad + nt(dqkv_ref[c], weight_ref[c])
        row_grad = row_grad.astype(bf16)
        for k in range(pieces):

            @pl.when(pl.program_id(0) == place_ref[0] ^ k)
            def _():
                row_refs[k][...] = row_grad

    return pl.pallas_call(
        kernel,
        grid=(pieces,),
        in_specs=[
            pl.BlockSpec(memory_space=pltpu.SMEM),
            pl.BlockSpec((3, block, width), lambda i: (0, i, 0)),
            pl.BlockSpec((3, model, width), lambda i: (0, 0, 0)),
        ],
        out_specs=[pl.BlockSpec((block, model), lambda i: (0, 0))] * pieces,
        out_shape=[jax.ShapeDtypeStruct((block, model), bf16)] * pieces,
        compiler_params=params(),
        cost_estimate=hint(6 * rows * model * width, rows * width),
        name="project_rows",
    )(place, dqkv, weight)


def make_shards(tensor_size, group_size):
    square = tensor_size == 4

    def swap(value, bits):
        return lax.ppermute(value, "tensor", [(i, i ^ bits) for i in range(tensor_size)])

    def gather_far(own):
        return swap(own, 2) if square else lax.all_gather(own, "tensor")

    def gather_near(own, far):
        if not square:
            return [far[i] for i in range(tensor_size)]
        return [own, swap(own, 1), far, swap(far, 1)]

    def exchange(stacked):
        return lax.all_to_all(stacked, "tensor", 0, 0)

    def sum_near(blocks, anchor, plain=False):
        if not square:
            return (jnp.stack(blocks),), anchor
        anchor, (near_own, near_far) = tie(anchor, (swap(blocks[1], 1), swap(blocks[3], 1)))
        if plain:
            far = (blocks[2].astype(f32) + near_far.astype(f32)).astype(blocks[2].dtype)
        else:
            far = add_terms(blocks[2], near_far)
        return (blocks[0], near_own, far), anchor

    def terms_far(stage, anchor):
        if not square:
            own = lax.psum_scatter(stage[0], "tensor", scatter_dimension=0, tiled=False)
            anchor, own = tie(anchor, own)
            return [own], anchor
        own, near, far = stage
        anchor, received = tie(anchor, swap(far, 2))
        return [own, near, received], anchor

    def sum_far(stage, anchor):
        terms, anchor = terms_far(stage, anchor)
        return (add_terms(*terms) if len(terms) > 1 else terms[0]), anchor

    steps = []
    for axis, size in (("tensor", tensor_size), ("dp", group_size)):
        bit = 1
        while bit < size:
            steps.append((axis, [(i, i ^ bit) for i in range(size)]))
            bit *= 2

    def sum_step(value, step, anchor):
        anchor, received = tie(anchor, lax.ppermute(value, step[0], step[1]))
        return value + received, anchor

    def ring_plan():
        bits = [1 << k for k in range(group_size.bit_length() - 1)]
        return [(bit, True) for bit in bits] + [(bit, False) for bit in reversed(bits)]

    def ring_step(value, step, anchor):
        bit, reducing = step
        side = (lax.axis_index("dp") // bit) % 2
        pairs = [(i, i ^ bit) for i in range(group_size)]
        if reducing:
            half = value.shape[0] // 2
            sent = lax.dynamic_slice_in_dim(value, (1 - side) * half, half, axis=0)
            anchor, received = tie(anchor, lax.ppermute(sent, "dp", pairs))
            kept = lax.dynamic_slice_in_dim(value, side * half, half, axis=0)
            return (kept.astype(f32) + received.astype(f32)).astype(value.dtype), anchor
        anchor, received = tie(anchor, lax.ppermute(value, "dp", pairs))
        return in_halves(value, received, side), anchor

    def in_halves(own, other, side):
        return join_halves(side.reshape(1).astype(jnp.int32), own, other)

    def fetch_half(own):
        half = own.shape[0] // 2
        side = lax.axis_index("dp") % 2
        return swap(lax.dynamic_slice_in_dim(own, side * half, half, axis=0), 2)

    def fetch_rest(half):
        return lax.ppermute(half, "dp", [(i, i ^ 1) for i in range(group_size)])

    def in_order(stacked):
        if not square:
            return stacked
        own = lax.axis_index("tensor")
        return jnp.concatenate(
            [lax.dynamic_slice_in_dim(stacked, own ^ i, 1, axis=0) for i in range(tensor_size)], axis=0
        )

    def shards(
        patches,
        cotangent,
        empty_slots,
        dataset_id,
        dataset_weight,
        query_key_value_weight,
        qv_bias,
        output_projection_weight,
        out_bias,
        up_projection_weight,
        up_bias,
        down_projection_weight,
        down_bias,
        attn_gain,
        attn_shift,
        mlp_gain,
        mlp_shift,
    ):
        slot_count, own_rows, model = patches.shape
        width = query_key_value_weight.shape[2]
        group_slots = empty_slots.shape[0]
        slot_index = jnp.arange(group_slots * slot_count, dtype=jnp.int32) % slot_count
        filled = jnp.repeat(slot_count - empty_slots, slot_count)
        valid_all = (slot_index < filled).astype(f32)
        table_hits = dataset_id[:, None] == jnp.arange(dataset_weight.shape[0], dtype=jnp.int32)[None, :]
        numerator = jnp.sum(jnp.where(table_hits, dataset_weight[None, :], 0), axis=1).astype(f32)
        total_items = jnp.sum(valid_all)
        total_weight = jnp.sum(valid_all * numerator)
        multiplier_whole = valid_all * numerator * total_items / total_weight
        own_start = lax.axis_index("dp") * slot_count
        own_scale = lax.dynamic_slice_in_dim(multiplier_whole, own_start, slot_count)
        own_valid = lax.dynamic_slice_in_dim(valid_all, own_start, slot_count)
        all_rows = slot_count * own_rows
        row_scale = jnp.repeat(own_scale, own_rows)[:, None]
        gain_row, shift_row, mlp_gain_row, mlp_shift_row, out_bias_row = (
            value[None, :] for value in (attn_gain, attn_shift, mlp_gain, mlp_shift, out_bias)
        )
        proj_bias = jnp.stack([qv_bias[0], jnp.zeros_like(qv_bias[0]), qv_bias[1]])[:, None, :]
        bias_row = up_bias[None, :]

        dp_side = lax.axis_index("dp") % 2
        place = jnp.zeros((1,), jnp.int32)
        if square:
            place = place + lax.axis_index("tensor")
        fetch = fetch_half if square else gather_far
        weights_near = ()
        if square:
            weights_near = tuple(
                swap(value, 1) for value in (output_projection_weight, up_projection_weight, down_projection_weight)
            )

        def gather_rows(own):
            return lax.all_gather(own, "tensor", axis=0, tiled=True)

        normed = [norm_item(patches, i, gain_row, shift_row) for i in range(slot_count)]
        every = gather_rows(normed[0])
        bias_far = gather_far(bias_row)
        cot_low = (cotangent.astype(f32).reshape(all_rows, model) * row_scale).astype(bf16)
        early = None
        if square:
            early = cot_back(cot_low, [down_projection_weight, weights_near[2]])
            every, (early, normed) = tie(every, (early, normed))
        qkvs, attended, lses, heads_own, normed_every = [], [], [], [], []
        for i in range(slot_count):
            last = i == slot_count - 1
            normed_every.append(every)
            following = None
            if not last:
                every, following = tie(every, normed[i + 1])
                following = gather_rows(following)
            qkv = project(every, query_key_value_weight, proj_bias)
            if i == 0:
                qkv, (weights_near, bias_far) = tie(qkv, (weights_near, bias_far))
            out, lse = attend(qkv)
            if not last:
                out, following = tie(out, following)
            if i > 0:
                out, heads_own[-1] = tie(out, heads_own[-1])
            if i == min(1, slot_count - 1):
                out, (up_own, down_own, out_own) = tie(
                    out, (up_projection_weight, down_projection_weight, output_projection_weight)
                )
                out_far = gather_far(out_own)
                up_far = fetch(up_own)
                down_far = fetch(down_own)
            if last:
                out, (out_far, up_far) = tie(out, (out_far, up_far))
            heads_own.append(exchange(out.reshape(tensor_size, own_rows, width)))
            qkvs.append(qkv)
            attended.append(out)
            lses.append(lse)
            every = following
        if square:
            up_rest = fetch_rest(up_far)
            out_weight = jnp.concatenate([out_own, weights_near[0], out_far, swap(out_far, 1)], axis=0)
        else:
            out_weight = jnp.concatenate(gather_near(out_own, out_far), axis=0)
        rows_done = None
        for i in range(slot_count):
            if i == slot_count - 1:
                rows_done, (heads_own[i], down_far) = tie(rows_done, (heads_own[i], down_far))
            rows_done = out_project(
                patches, i, place, heads_own[i], out_weight, out_bias_row, mlp_gain_row, mlp_shift_row, rows_done
            )
        if square:
            down_rest = fetch_rest(down_far)
            rows_done, up_rest = tie(rows_done, up_rest)
            up_far = in_halves(up_far, up_rest, dp_side)
            up_diag = swap(up_far, 1)
        attended_rows, residual, normed_mlp = rows_done

        bias_blocks = gather_near(bias_row, bias_far)
        if square:
            up_blocks = [up_own, weights_near[1]]
            down_blocks = [down_own, weights_near[2]]
        else:
            up_blocks = gather_near(up_own, up_far)
            down_blocks = gather_near(down_own, down_far)
        calls = tensor_size // 2
        total = None
        slopes, down_grads = [], []
        for c in range(calls):
            pair = slice(2 * c, 2 * c + 2)
            if c == 1 and square:
                total, (up_diag, down_rest) = tie(total, (up_diag, down_rest))
                down_far = in_halves(down_far, down_rest, dp_side)
                up_blocks += [up_far, up_diag]
                down_blocks += [down_far, swap(down_far, 1)]
            slope, total, *grads = mlp_forward(
                normed_mlp, cot_low, up_blocks[pair], bias_blocks[pair], down_blocks[pair], total
            )
            slopes.append(slope)
            down_grads += grads
        layer_sum = total

        cot_late, down_grads = tie(cot_low, down_grads)
        before = None
        bias_grads = []
        for c in range(calls):
            pair = slice(2 * c, 2 * c + 2)
            if c == 0 and square:
                *before, bias_grad = mlp_backward(early, slopes[c], up_blocks[pair], [], before, c, calls)
            else:
                *before, bias_grad = mlp_backward(
                    cot_late, slopes[c], up_blocks[pair], down_blocks[pair], before, c, calls
                )
            bias_grads.append(bias_grad)
            if c == 0:
                down_stage, before = sum_near(down_grads, before)
        ring = ring_plan()
        pre_grad, total = before

        if square:
            ahead = weight_back(normed_mlp, pre_grad, [1, 3], None, None, tensor_size)
            total, ahead = tie(total, ahead)
        grad_residual, grad_low, small_rows, pieces = residual_back(
            total, residual, cotangent, own_scale, place, out_weight, mlp_gain_row, tensor_size
        )
        down_sum, pieces = sum_far(down_stage, pieces)
        grad_attended = exchange(pieces)
        if square:
            up_near, up_diag_near = swap(ahead[0], 1), swap(ahead[1], 1)
            first, second, *out_grads = weight_back(
                normed_mlp, pre_grad, [2, 0], attended_rows, grad_low, tensor_size
            )
            second, (up_near, up_diag_near) = tie(second, (up_near, up_diag_near))
            up_far_sum = add_terms(first, up_diag_near)
            out_stage, up_far_sum = sum_near(out_grads, up_far_sum)
            up_far_sum, grad_attended = tie(up_far_sum, grad_attended)
            up_stage = (second, up_near, up_far_sum)
        else:
            weight_grads = weight_back(
                normed_mlp, pre_grad, list(range(tensor_size)), attended_rows, grad_low, tensor_size
            )
            up_stage, grad_attended = sum_near(weight_grads[:tensor_size], grad_attended)
            out_stage, grad_attended = sum_near(weight_grads[tensor_size:], grad_attended)
        bias_rows = in_order(jnp.concatenate(bias_grads, axis=1).reshape(tensor_size, -1))
        smalls = jnp.concatenate([small_rows[:4].reshape(-1), bias_rows.reshape(-1)]).reshape(-1, 128)

        waiting = list(steps)
        weights_wide = query_key_value_weight.astype(f32)
        sums = None
        grad_normed = []
        for i in range(slot_count):
            last = i == slot_count - 1
            dqkv = attend_back(qkvs[i], attended[i], grad_attended, i, lses[i])
            if i >= 2:
                grad_normed[i - 2], dqkv = terms_far(grad_normed[i - 2], dqkv)
            if i >= 1 and not last:
                grad_normed[i - 1], dqkv = sum_near(grad_normed[i - 1], dqkv)
            if i == 0:
                up_sum, dqkv = sum_far(up_stage, dqkv)
                out_sum, dqkv = sum_far(out_stage, dqkv)
                up_all = lax.psum((up_sum, out_sum), "dp")
            if last:
                dqkv, up_all = tie(dqkv, up_all)
            if waiting and i > 0:
                smalls, dqkv = sum_step(smalls, waiting.pop(0), dqkv)
            if ring:
                down_sum, dqkv = ring_step(down_sum, ring.pop(0), dqkv)
            results = project_back(place, normed_every[i], dqkv, query_key_value_weight, sums, last, tensor_size)
            if not last:
                partial, sums = results[:tensor_size], results[tensor_size:]
                if waiting:
                    smalls, partial = sum_step(smalls, waiting.pop(0), partial)
                if ring:
                    down_sum, partial = ring_step(down_sum, ring.pop(0), partial)
            else:
                *sums, qkv_low = results
                qkv_low, (dqkv, grad_residual, layer_sum) = tie(qkv_low, (dqkv, grad_residual, layer_sum))
                qkv_all = lax.psum(qkv_low, "dp")
                output = layer_out(layer_sum, residual, down_bias[None, :], own_valid, patches.shape)
                partial = project_rows(place, dqkv, query_key_value_weight, tensor_size)
                if i >= 1:
                    grad_normed[i - 1], partial = sum_near(grad_normed[i - 1], partial, True)
                raw = jnp.stack(
                    [
                        jnp.sum(sums[0] * weights_wide, axis=(0, 2)),
                        jnp.sum(sums[1][:3, None, :] * weights_wide, axis=(0, 2)),
                    ]
                )
                for axis, pairs in steps:
                    raw = raw + lax.ppermute(raw, axis, pairs)
            grad_normed.append(partial)
        grad_inputs = None
        for i in range(slot_count):
            if i == slot_count - 1:
                grad_normed[i], grad_residual = sum_near(grad_normed[i], grad_residual, True)
            terms = grad_normed[i]
            if i >= slot_count - 2:
                terms, grad_residual = terms_far(terms, grad_residual)
            grad_inputs = input_back(terms, patches, i, grad_residual, gain_row, grad_inputs)
        grad_inputs, qkv_all = tie(grad_inputs, qkv_all)
        for step in ring:
            down_sum = ring_step(down_sum, step, place)[0]
        for step in waiting:
            smalls = sum_step(smalls, step, place)[0]
        weight_grad = qkv_all[:, :model].astype(f32)
        columns = qkv_all[:, model].astype(f32)
        up_all, out_all = [value.astype(f32) for value in up_all]
        down_all = down_sum.astype(f32)
        inverse = 1.0 / total_items
        smalls = smalls.reshape(-1) * inverse
        raw = raw * inverse
        small_rows = smalls[: 4 * model].reshape(4, model)
        units = up_bias.shape[0]
        bias_all = lax.dynamic_slice_in_dim(smalls[4 * model :], lax.axis_index("tensor") * units, units)
        shift_all = raw[1]
        gain_all = (raw[0] - attn_shift * shift_all) / attn_gain
        columns = columns * inverse
        return (
            output,
            grad_inputs,
            weight_grad * inverse,
            jnp.stack([columns[0], columns[2]]),
            out_all * inverse,
            small_rows[2],
            up_all * inverse,
            bias_all,
            down_all * inverse,
            small_rows[3],
            gain_all,
            shift_all,
            small_rows[0],
            small_rows[1],
        )

    return shards


def solution(mesh):
    items = P("dp", "tensor", None)
    return jax.shard_map(
        make_shards(mesh.shape["tensor"], mesh.shape["dp"]),
        mesh=mesh,
        in_specs=(
            items,
            items,
            P(),
            P(),
            P(),
            P(None, None, "tensor"),
            P(None, "tensor"),
            P("tensor", None),
            P(),
            P(None, "tensor"),
            P("tensor"),
            P("tensor", None),
            P(),
            P(),
            P(),
            P(),
            P(),
        ),
        out_specs=(
            items,
            items,
            P(None, None, "tensor"),
            P(None, "tensor"),
            P("tensor", None),
            P(),
            P(None, "tensor"),
            P("tensor"),
            P("tensor", None),
            P(),
            P(),
            P(),
            P(),
            P(),
        ),
        check_vma=False,
    )
```

```python
import jax
import jax.numpy as jnp
from jax import lax
from jax.experimental import pallas as pl
from jax.experimental.pallas import tpu as pltpu
from jax.sharding import PartitionSpec as P

HD = 64
SCORE_SCALE = HD ** (-0.5)
LOG2E = 1.4426950408889634
SQRT_HALF = 0.7071067811865476
INV_SQRT_2PI = 0.3989422804014327
epsilon = 1e-05
f32 = jnp.float32
bf16 = jnp.bfloat16
VMEM_LIMIT = 60 << 20
COST_SCALE = 64


def nn(a, b):
    return lax.dot_general(a, b, (((1,), (0,)), ((), ())), preferred_element_type=f32)


def nt(a, b):
    return lax.dot_general(a, b, (((1,), (1,)), ((), ())), preferred_element_type=f32)


def tn(a, b):
    return lax.dot_general(a, b, (((0,), (0,)), ((), ())), preferred_element_type=f32)


def tie(first, second):
    return lax.optimization_barrier((first, second))


def largest_block(extent, limit):
    block = min(extent, limit)
    while extent % block:
        block //= 2
    return block


def norm_rows(source, norm_gain, norm_shift):
    row_mean = jnp.mean(source, axis=-1, keepdims=True)
    centred = source - row_mean
    spread = jnp.mean(centred * centred, axis=-1, keepdims=True)
    return centred * lax.rsqrt(spread + epsilon) * norm_gain + norm_shift


def attend(qkv):
    _, length, width = qkv.shape
    lanes = min(128, width)
    heads = lanes // HD
    qblock = largest_block(length, 2048)
    to_log2 = SCORE_SCALE * LOG2E

    def body(q_ref, k_ref, v_ref, out_ref, lse_ref):
        queries = q_ref[...]
        keys = k_ref[...]
        values_t = v_ref[...].T
        lane = lax.broadcasted_iota(jnp.int32, (1, lanes), 1)
        outs = []
        for h in range(heads):
            own = queries
            if heads > 1:
                own = jnp.where(lane // HD == h, queries, jnp.zeros_like(queries))
            scores = nt(keys, own)
            top = jnp.max(scores, axis=0, keepdims=True)
            exp_scores = jnp.exp2((scores - top) * to_log2)
            total = jnp.sum(exp_scores, axis=0, keepdims=True)
            outs.append(nn(values_t[h * HD : (h + 1) * HD, :], exp_scores.astype(bf16)) / total)
            lse_ref[h : h + 1, :] = top * to_log2 + jnp.log2(total)
        out_ref[...] = jnp.concatenate(outs, axis=0).T.astype(bf16)

    pairs = width // lanes
    return pl.pallas_call(
        body,
        grid=(pairs, length // qblock),
        in_specs=[
            pl.BlockSpec((None, qblock, lanes), lambda h, j: (0, j, h)),
            pl.BlockSpec((None, length, lanes), lambda h, j: (1, 0, h)),
            pl.BlockSpec((None, length, lanes), lambda h, j: (2, 0, h)),
        ],
        out_specs=[
            pl.BlockSpec((qblock, lanes), lambda h, j: (j, h)),
            pl.BlockSpec((None, heads, qblock), lambda h, j: (h, 0, j)),
        ],
        out_shape=[
            jax.ShapeDtypeStruct((length, width), bf16),
            jax.ShapeDtypeStruct((pairs, heads, length), f32),
        ],
        compiler_params=pltpu.CompilerParams(vmem_limit_bytes=VMEM_LIMIT),
        cost_estimate=pl.CostEstimate(
            flops=8 * length * length * width // COST_SCALE,
            transcendentals=0,
            bytes_accessed=length * width,
        ),
        name="attend",
    )(qkv, qkv, qkv)


def attend_back(qkv, attended, grad_attended, item, lse):
    _, length, width = qkv.shape
    lanes = min(128, width)
    shards_of = grad_attended.shape[0]
    heads = lanes // HD
    kblock = largest_block(length, 1024)
    kblocks = length // kblock
    to_log2 = SCORE_SCALE * LOG2E

    def body(q_ref, k_ref, v_ref, out_ref, grad_ref, lse_ref, dqkv_ref, dq_acc, row_dot):
        kb = pl.program_id(1)
        queries = q_ref[...]
        grads = grad_ref[...].reshape(length, lanes)
        keys = k_ref[...]
        values = v_ref[...]
        keys_t = keys.T
        lane = lax.broadcasted_iota(jnp.int32, (1, lanes), 1)

        @pl.when(kb == 0)
        def _():
            product = out_ref[...].astype(f32) * grads.astype(f32)
            high = product.astype(bf16)
            rest = (product - high.astype(f32)).astype(bf16)
            pick = lax.broadcasted_iota(jnp.int32, (8, lanes), 0)
            mask = (lax.broadcasted_iota(jnp.int32, (8, lanes), 1) // HD == pick).astype(f32).astype(bf16)
            row_dot[...] = nt(mask, high) + nt(mask, rest)

        dk = None
        dv = None
        dqs = []
        for h in range(heads):
            own_q = queries
            own_g = grads
            if heads > 1:
                mine = lane // HD == h
                own_q = jnp.where(mine, queries, jnp.zeros_like(queries))
                own_g = jnp.where(mine, grads, jnp.zeros_like(grads))
            scores = nt(keys, own_q)
            weights = jnp.exp2(scores * to_log2 - lse_ref[h : h + 1, :])
            grad_weights = nt(values, own_g)
            grad_scores = (weights * (grad_weights - row_dot[h : h + 1, :])).astype(bf16)
            dv_h = nn(weights.astype(bf16), own_g)
            dk_h = nn(grad_scores, own_q)
            dv = dv_h if dv is None else dv + dv_h
            dk = dk_h if dk is None else dk + dk_h
            dqs.append(nn(keys_t[h * HD : (h + 1) * HD, :], grad_scores))
        rows = pl.ds(pl.multiple_of(kb * kblock, kblock), kblock)
        dqkv_ref[1, rows, :] = (dk * SCORE_SCALE).astype(bf16)
        dqkv_ref[2, rows, :] = dv.astype(bf16)
        dq = jnp.concatenate(dqs, axis=0)
        if kblocks == 1:
            dqkv_ref[0] = (dq * SCORE_SCALE).T.astype(bf16)
            return

        @pl.when(kb == 0)
        def _():
            dq_acc[...] = dq

        @pl.when((kb > 0) & (kb < kblocks - 1))
        def _():
            dq_acc[...] += dq

        @pl.when(kb == kblocks - 1)
        def _():
            dqkv_ref[0] = ((dq_acc[...] + dq) * SCORE_SCALE).T.astype(bf16)

    pairs = width // lanes
    return pl.pallas_call(
        body,
        grid=(pairs, kblocks),
        in_specs=[
            pl.BlockSpec((None, length, lanes), lambda h, kb: (0, 0, h)),
            pl.BlockSpec((None, kblock, lanes), lambda h, kb: (1, kb, h)),
            pl.BlockSpec((None, kblock, lanes), lambda h, kb: (2, kb, h)),
            pl.BlockSpec((length, lanes), lambda h, kb: (0, h)),
            pl.BlockSpec((shards_of, length // shards_of, lanes), lambda h, kb: (0, item, h)),
            pl.BlockSpec((None, heads, length), lambda h, kb: (h, 0, 0)),
        ],
        out_specs=pl.BlockSpec((3, length, lanes), lambda h, kb: (0, 0, h)),
        out_shape=jax.ShapeDtypeStruct((3, length, width), bf16),
        scratch_shapes=[pltpu.VMEM((lanes, length), f32), pltpu.VMEM((8, length), f32)],
        compiler_params=pltpu.CompilerParams(vmem_limit_bytes=VMEM_LIMIT),
        cost_estimate=pl.CostEstimate(
            flops=20 * length * length * width // COST_SCALE,
            transcendentals=0,
            bytes_accessed=length * width,
        ),
        name="attend_back",
    )(qkv, qkv, qkv, attended, grad_attended, lse)


def hint(flops, size):
    return pl.CostEstimate(flops=flops // COST_SCALE, transcendentals=0, bytes_accessed=size)


def params():
    return pltpu.CompilerParams(vmem_limit_bytes=VMEM_LIMIT)


def norm_item(patches, item, norm_gain, norm_shift):
    _, rows, model = patches.shape
    block = largest_block(rows, 256)

    def body(x_ref, gain_ref, shift_ref, out_ref):
        out_ref[...] = norm_rows(x_ref[...].astype(f32), gain_ref[...], shift_ref[...]).astype(bf16)

    vector = pl.BlockSpec((1, model), lambda i: (0, 0))
    return pl.pallas_call(
        body,
        grid=(rows // block,),
        in_specs=[pl.BlockSpec((None, block, model), lambda i: (item, i, 0)), vector, vector],
        out_specs=pl.BlockSpec((block, model), lambda i: (i, 0)),
        out_shape=jax.ShapeDtypeStruct((rows, model), bf16),
        compiler_params=params(),
        cost_estimate=hint(0, rows * model),
        name="norm_item",
    )(patches, norm_gain, norm_shift)


def out_project(patches, item, place, heads, weight, out_bias, norm_gain, norm_shift, before):
    slots, rows, model = patches.shape
    block = largest_block(rows, 256)
    steps = rows // block
    count, _, width = heads.shape

    def body(*refs):
        place_ref, x_ref, weight_ref, bias_ref, gain_ref, shift_ref, head_ref = refs[:7]
        attended_ref, residual_ref, normed_ref = refs[-3:]
        for k in range(count):
            attended_ref[:, k * width : (k + 1) * width] = head_ref[place_ref[0] ^ k]
        attended = attended_ref[...]
        residual = x_ref[...].astype(f32) + nn(attended, weight_ref[...]) + bias_ref[...]
        residual_ref[...] = residual
        normed_ref[...] = norm_rows(residual, gain_ref[...], shift_ref[...]).astype(bf16)

    vector = pl.BlockSpec((1, model), lambda i: (0, 0))
    placed = pl.BlockSpec((block, model), lambda i: (item * steps + i, 0))
    operands = [place, patches, weight, out_bias, norm_gain, norm_shift, heads]
    in_specs = [
        pl.BlockSpec(memory_space=pltpu.SMEM),
        pl.BlockSpec((None, block, model), lambda i: (item, i, 0)),
        pl.BlockSpec((model, model), lambda i: (0, 0)),
        vector,
        vector,
        vector,
        pl.BlockSpec((count, block, width), lambda i: (0, i, 0)),
    ]
    aliases = {}
    if before is not None:
        aliases = {len(operands) + k: k for k in range(3)}
        operands += before
        in_specs += [pl.BlockSpec(memory_space=pl.ANY)] * 3
    return pl.pallas_call(
        body,
        grid=(steps,),
        in_specs=in_specs,
        out_specs=[placed] * 3,
        out_shape=[jax.ShapeDtypeStruct((slots * rows, model), t) for t in (bf16, f32, bf16)],
        input_output_aliases=aliases,
        compiler_params=params(),
        cost_estimate=hint(2 * rows * model * model, rows * model),
        name="out_project",
    )(*operands)


def residual_back(total, residual, cotangent, scale, place, weight, norm_gain, pieces):
    slots, rows, model = cotangent.shape
    block = largest_block(rows, 256)
    steps = rows // block
    piece = model // pieces

    def body(*refs):
        place_ref, total_ref, residual_ref, cot_ref, scale_ref, weight_ref, gain_ref = refs[:7]
        grad_ref, low_ref, sum_ref, attended_ref = refs[-4:]
        residual = residual_ref[...]
        centred = residual - jnp.mean(residual, axis=-1, keepdims=True)
        rate = lax.rsqrt(jnp.mean(centred * centred, axis=-1, keepdims=True) + epsilon)
        xhat = centred * rate
        grad_normed = total_ref[...]
        scaled = grad_normed * gain_ref[...]
        inner = jnp.mean(scaled, axis=-1, keepdims=True)
        outer = jnp.mean(scaled * xhat, axis=-1, keepdims=True)
        cot = cot_ref[...].astype(f32) * scale_ref[pl.program_id(0) // steps]
        grad = cot + rate * (scaled - inner - xhat * outer)
        grad_ref[...] = grad
        low = grad.astype(bf16)
        low_ref[...] = low

        @pl.when(pl.program_id(0) == 0)
        def _():
            sum_ref[...] = jnp.zeros_like(sum_ref)

        for k, value in enumerate((grad_normed * xhat, grad_normed, grad, cot)):
            sum_ref[k : k + 1, :] += jnp.sum(value, axis=0, keepdims=True)
        attended = nt(low, weight_ref[...]).astype(bf16)
        for k in range(pieces):
            attended_ref[place_ref[0] ^ k] = attended[:, k * piece : (k + 1) * piece]

    row_spec = pl.BlockSpec((block, model), lambda i: (i, 0))
    return pl.pallas_call(
        body,
        grid=(slots * steps,),
        in_specs=[
            pl.BlockSpec(memory_space=pltpu.SMEM),
            row_spec,
            row_spec,
            pl.BlockSpec((None, block, model), lambda i: (i // steps, i % steps, 0)),
            pl.BlockSpec(memory_space=pltpu.SMEM),
            pl.BlockSpec((model, model), lambda i: (0, 0)),
            pl.BlockSpec((1, model), lambda i: (0, 0)),
        ],
        out_specs=[
            row_spec,
            row_spec,
            pl.BlockSpec((8, model), lambda i: (0, 0)),
            pl.BlockSpec((pieces, block, piece), lambda i: (0, i, 0)),
        ],
        out_shape=[
            jax.ShapeDtypeStruct((slots * rows, model), f32),
            jax.ShapeDtypeStruct((slots * rows, model), bf16),
            jax.ShapeDtypeStruct((8, model), f32),
            jax.ShapeDtypeStruct((pieces, slots * rows, piece), bf16),
        ],
        compiler_params=params(),
        cost_estimate=hint(2 * slots * rows * model * model, rows * model),
        name="residual_back",
    )(place, total, residual, cotangent, scale, weight, norm_gain)


def input_back(terms, patches, item, grad_residual, norm_gain, before):
    slots, rows, model = patches.shape
    block = largest_block(rows, 256)
    count = len(terms)

    def body(*refs):
        x_ref, grad_ref, gain_ref = refs[:3]
        out_ref = refs[-1]
        grad_normed = refs[3][...].astype(f32)
        for k in range(1, count):
            grad_normed = grad_normed + refs[3 + k][...].astype(f32)
        source = x_ref[...].astype(f32)
        centred = source - jnp.mean(source, axis=-1, keepdims=True)
        rate = lax.rsqrt(jnp.mean(centred * centred, axis=-1, keepdims=True) + epsilon)
        xhat = centred * rate
        scaled = grad_normed * gain_ref[...]
        inner = jnp.mean(scaled, axis=-1, keepdims=True)
        outer = jnp.mean(scaled * xhat, axis=-1, keepdims=True)
        out_ref[...] = (grad_ref[...] + rate * (scaled - inner - xhat * outer)).astype(bf16)

    row_spec = pl.BlockSpec((block, model), lambda i: (i, 0))
    placed = pl.BlockSpec((None, block, model), lambda i: (item, i, 0))
    operands = [patches, grad_residual, norm_gain, *terms]
    steps = rows // block
    grad_spec = pl.BlockSpec((block, model), lambda i: (item * steps + i, 0))
    in_specs = [placed, grad_spec, pl.BlockSpec((1, model), lambda i: (0, 0))] + [row_spec] * count
    aliases = {}
    if before is not None:
        aliases = {len(operands): 0}
        operands.append(before)
        in_specs.append(pl.BlockSpec(memory_space=pl.ANY))
    return pl.pallas_call(
        body,
        grid=(rows // block,),
        in_specs=in_specs,
        out_specs=placed,
        out_shape=jax.ShapeDtypeStruct((slots, rows, model), bf16),
        input_output_aliases=aliases,
        compiler_params=params(),
        cost_estimate=hint(0, rows * model),
        name="input_back",
    )(*operands)


def layer_out(total, residual, down_bias, valid, shape):
    slots, rows, model = shape
    block = largest_block(rows, 256)
    steps = rows // block

    def body(total_ref, residual_ref, bias_ref, valid_ref, out_ref):
        value = residual_ref[...] + total_ref[...] + bias_ref[...]
        out_ref[...] = (value * valid_ref[pl.program_id(0) // steps]).astype(bf16)

    row_spec = pl.BlockSpec((block, model), lambda i: (i, 0))
    return pl.pallas_call(
        body,
        grid=(slots * steps,),
        in_specs=[
            row_spec,
            row_spec,
            pl.BlockSpec((1, model), lambda i: (0, 0)),
            pl.BlockSpec(memory_space=pltpu.SMEM),
        ],
        out_specs=pl.BlockSpec((None, block, model), lambda i: (i // steps, i % steps, 0)),
        out_shape=jax.ShapeDtypeStruct(shape, bf16),
        compiler_params=params(),
        cost_estimate=hint(0, rows * model),
        name="layer_out",
    )(total, residual, down_bias, valid)


def mlp_forward(normed, cot, ups, biases, downs, total):
    rows, model = normed.shape
    count = len(ups)
    units = ups[0].shape[1]
    block = largest_block(rows, 512)
    steps = rows // block
    first = total is None

    def body(*refs):
        x_ref, cot_ref = refs[:2]
        up_refs, bias_refs, down_refs = (refs[2 + k * count : 2 + (k + 1) * count] for k in range(3))
        rest = refs[2 + 3 * count :]
        if not first:
            before_ref = rest[0]
            rest = rest[1:]
        slope_ref, sum_ref = rest[:2]
        grad_refs = rest[2 : 2 + count]
        hidden_ref, acc_ref = rest[2 + count :]
        step = pl.program_id(0)
        part = largest_block(units, 256)
        for k in range(count):
            for j in range(units // part):
                cols = slice(j * part, (j + 1) * part)
                wide = slice(k * units + j * part, k * units + (j + 1) * part)
                pre = nn(x_ref[...], up_refs[k][:, cols]) + bias_refs[k][:, cols]
                cdf = 0.5 + 0.5 * lax.erf(pre * SQRT_HALF)
                density = jnp.exp2(pre * pre * (-0.5 * LOG2E)) * INV_SQRT_2PI
                hidden_ref[:, wide] = (pre * cdf).astype(bf16)
                slope_ref[:, wide] = (cdf + pre * density).astype(bf16)
        out = None if first else before_ref[...]
        for k in range(count):
            hidden = hidden_ref[:, k * units : (k + 1) * units]
            product = nn(hidden, down_refs[k][...])
            out = product if out is None else out + product
            grad = tn(hidden, cot_ref[...])

            @pl.when(step == 0)
            def _():
                acc_ref[k] = grad

            @pl.when(step > 0)
            def _():
                acc_ref[k] += grad

        sum_ref[...] = out

        @pl.when(step == steps - 1)
        def _():
            for k in range(count):
                grad_refs[k][...] = acc_ref[k].astype(bf16)

    row_spec = pl.BlockSpec((block, model), lambda i: (i, 0))
    slope_spec = pl.BlockSpec((block, count * units), lambda i: (i, 0))
    up_spec = pl.BlockSpec((model, units), lambda i: (0, 0), pipeline_mode=pl.Buffered(1))
    down_spec = pl.BlockSpec((units, model), lambda i: (0, 0), pipeline_mode=pl.Buffered(1))
    grad_spec = pl.BlockSpec((units, model), lambda i: (0, 0))
    operands = [normed, cot, *ups, *biases, *downs]
    in_specs = [row_spec, row_spec] + [up_spec] * count
    in_specs += [pl.BlockSpec((1, units), lambda i: (0, 0))] * count + [down_spec] * count
    aliases = {}
    if not first:
        aliases = {len(operands): 1}
        operands.append(total)
        in_specs.append(row_spec)
    return pl.pallas_call(
        body,
        grid=(steps,),
        in_specs=in_specs,
        out_specs=[slope_spec, row_spec] + [grad_spec] * count,
        out_shape=[
            jax.ShapeDtypeStruct((rows, count * units), bf16),
            jax.ShapeDtypeStruct((rows, model), f32),
        ]
        + [jax.ShapeDtypeStruct((units, model), bf16)] * count,
        scratch_shapes=[pltpu.VMEM((block, count * units), bf16), pltpu.VMEM((count, units, model), f32)],
        input_output_aliases=aliases,
        compiler_params=params(),
        cost_estimate=hint(6 * rows * model * units * count, rows * units),
        name="mlp_forward",
    )(*operands)


def cot_back(cot, downs):
    rows, model = cot.shape
    count = len(downs)
    units = downs[0].shape[0]
    block = largest_block(rows, 512)

    def body(cot_ref, *refs):
        for k in range(count):
            refs[count][:, k * units : (k + 1) * units] = nt(cot_ref[...], refs[k][...]).astype(bf16)

    return pl.pallas_call(
        body,
        grid=(rows // block,),
        in_specs=[pl.BlockSpec((block, model), lambda i: (i, 0))]
        + [pl.BlockSpec((units, model), lambda i: (0, 0))] * count,
        out_specs=pl.BlockSpec((block, count * units), lambda i: (i, 0)),
        out_shape=jax.ShapeDtypeStruct((rows, count * units), bf16),
        compiler_params=params(),
        cost_estimate=hint(2 * rows * model * units * count, rows * units),
        name="cot_back",
    )(cot, *downs)


def mlp_backward(cot, slope, ups, downs, before, index, calls):
    rows, _ = cot.shape
    model = ups[0].shape[0]
    count = len(ups)
    units = ups[0].shape[1]
    block = largest_block(rows, 512)
    first = before is None

    def body(*refs):
        cot_ref, slope_ref = refs[:2]
        up_refs, down_refs = refs[2 : 2 + count], refs[2 + count : 2 + count + len(downs)]
        grad_ref, sum_ref, bias_ref = refs[-3:]

        @pl.when(pl.program_id(0) == 0)
        def _():
            bias_ref[...] = jnp.zeros_like(bias_ref)

        out = None if first else refs[3 + count + len(downs)][...]
        part = largest_block(units, 512)
        for k in range(count):
            for j in range(units // part):
                rows_of = slice(j * part, (j + 1) * part)
                wide = slice(k * units + j * part, k * units + (j + 1) * part)
                if downs:
                    product = nt(cot_ref[...], down_refs[k][rows_of, :])
                else:
                    product = cot_ref[:, wide].astype(f32)
                low = (product * slope_ref[:, wide].astype(f32)).astype(bf16)
                grad_ref[:, wide] = low
                bias_ref[:, wide] += jnp.sum(low.astype(f32), axis=0, keepdims=True)
            product = nt(grad_ref[:, k * units : (k + 1) * units], up_refs[k][...])
            out = product if out is None else out + product
        sum_ref[...] = out

    row_spec = pl.BlockSpec((block, model), lambda i: (i, 0))
    slope_spec = pl.BlockSpec((block, count * units), lambda i: (i, 0))
    up_spec = pl.BlockSpec((model, units), lambda i: (0, 0), pipeline_mode=pl.Buffered(1))
    down_spec = pl.BlockSpec((units, model), lambda i: (0, 0), pipeline_mode=pl.Buffered(1))
    operands = [cot, slope, *ups, *downs]
    in_specs = [row_spec if downs else slope_spec, slope_spec] + [up_spec] * count + [down_spec] * len(downs)
    aliases = {}
    if not first:
        aliases = {len(operands): 0, len(operands) + 1: 1}
        operands += before
        in_specs += [pl.BlockSpec(memory_space=pl.ANY), row_spec]
    return pl.pallas_call(
        body,
        grid=(rows // block,),
        in_specs=in_specs,
        out_specs=[
            pl.BlockSpec((block, count * units), lambda i: (i, index)),
            row_spec,
            pl.BlockSpec((1, count * units), lambda i: (0, 0)),
        ],
        out_shape=[
            jax.ShapeDtypeStruct((rows, calls * count * units), bf16),
            jax.ShapeDtypeStruct((rows, model), f32),
            jax.ShapeDtypeStruct((1, count * units), f32),
        ],
        input_output_aliases=aliases,
        compiler_params=params(),
        cost_estimate=hint(4 * rows * model * units * count, rows * units),
        name="mlp_backward",
    )(*operands)


def weight_back(normed, pre_grad, picks, attended, grad_low, pieces):
    rows, model = normed.shape
    units = pre_grad.shape[1] // pieces
    piece = model // pieces
    block = largest_block(rows, 512)
    steps = rows // block
    count = len(picks)
    outs = 0 if attended is None else pieces

    def body(x_ref, *refs):
        pre_refs = refs[:count]
        rest = refs[count:]
        if outs:
            attended_ref, grad_ref = rest[:2]
            rest = rest[2:]
        up_refs, out_refs = rest[:count], rest[count : count + outs]
        up_acc = rest[count + outs]
        step = pl.program_id(0)

        def add(acc, place, value):
            @pl.when(step == 0)
            def _():
                acc[place] = value

            @pl.when(step > 0)
            def _():
                acc[place] += value

        for k in range(count):
            add(up_acc, (slice(None), slice(k * units, (k + 1) * units)), tn(x_ref[...], pre_refs[k][...]))
        if outs:
            out_acc = rest[-1]
            add(out_acc, (slice(None), slice(None)), tn(attended_ref[...], grad_ref[...]))

        @pl.when(step == steps - 1)
        def _():
            for k in range(count):
                up_refs[k][...] = up_acc[:, k * units : (k + 1) * units].astype(bf16)
            for k in range(outs):
                out_refs[k][...] = out_acc[k * piece : (k + 1) * piece, :].astype(bf16)

    row_spec = pl.BlockSpec((block, model), lambda i: (i, 0))

    def columns_of(pick):
        return pl.BlockSpec((block, units), lambda i: (i, pick))

    operands = [normed] + [pre_grad] * count
    in_specs = [row_spec] + [columns_of(pick) for pick in picks]
    scratch = [pltpu.VMEM((model, count * units), f32)]
    if outs:
        operands += [attended, grad_low]
        in_specs += [row_spec, row_spec]
        scratch.append(pltpu.VMEM((model, model), f32))
    return pl.pallas_call(
        body,
        grid=(steps,),
        in_specs=in_specs,
        out_specs=[pl.BlockSpec((model, units), lambda i: (0, 0))] * count
        + [pl.BlockSpec((piece, model), lambda i: (0, 0))] * outs,
        out_shape=[jax.ShapeDtypeStruct((model, units), bf16)] * count
        + [jax.ShapeDtypeStruct((piece, model), bf16)] * outs,
        scratch_shapes=scratch,
        compiler_params=params(),
        cost_estimate=hint(2 * rows * model * units * count, rows * model),
        name="weight_back",
    )(*operands)


def project_back(place, normed, dqkv, weight, before, last, pieces):
    rows, model = normed.shape
    width = weight.shape[2]
    block = rows // pieces
    steps = pieces
    first = before is None
    given = 0 if last else pieces

    def kernel(*refs):
        place_ref, normed_ref, dqkv_ref, weight_ref = refs[:4]
        rest = refs[4:]
        if not first:
            wgrad_before, column_before = rest[:2]
            rest = rest[2:]
        row_refs, rest = rest[:given], rest[given:]
        wgrad_ref, column_ref = rest[:2]
        step = pl.program_id(0)

        @pl.when(step == 0)
        def _():
            if first:
                wgrad_ref[...] = jnp.zeros_like(wgrad_ref)
                column_ref[...] = jnp.zeros_like(column_ref)
            else:
                wgrad_ref[...] = wgrad_before[...]
                column_ref[...] = column_before[...]

        if not last:
            row_grad = nt(dqkv_ref[0], weight_ref[0])
            for c in range(1, 3):
                row_grad = row_grad + nt(dqkv_ref[c], weight_ref[c])
            row_grad = row_grad.astype(bf16)
            for k in range(pieces):

                @pl.when(step == place_ref[0] ^ k)
                def _():
                    row_refs[k][...] = row_grad

        for c in range(3):
            wgrad_ref[c] += tn(normed_ref[...], dqkv_ref[c])
            column_ref[c : c + 1, :] += jnp.sum(dqkv_ref[c].astype(f32), axis=0, keepdims=True)
        if last:
            low_ref = rest[2]

            @pl.when(step == steps - 1)
            def _():
                low_ref[:, :model, :] = wgrad_ref[...].astype(bf16)
                for c in range(3):
                    row = jnp.broadcast_to(column_ref[c : c + 1, :], (16, width))
                    low_ref[c, model:, :] = row.astype(bf16)

    whole = pl.BlockSpec((3, model, width), lambda i: (0, 0, 0))
    columns = pl.BlockSpec((8, width), lambda i: (0, 0))
    row_spec = pl.BlockSpec((block, model), lambda i: (i, 0))
    operands = [place, normed, dqkv, weight]
    in_specs = [pl.BlockSpec(memory_space=pltpu.SMEM), row_spec, pl.BlockSpec((3, block, width), lambda i: (0, i, 0)), whole]
    if not first:
        operands += list(before)
        in_specs += [whole, columns]
    out_specs = [pl.BlockSpec((block, model), lambda i: (0, 0))] * given + [whole, columns]
    out_shape = [jax.ShapeDtypeStruct((block, model), bf16)] * given + [
        jax.ShapeDtypeStruct((3, model, width), f32),
        jax.ShapeDtypeStruct((8, width), f32),
    ]
    if last:
        out_specs.append(pl.BlockSpec((3, model + 16, width), lambda i: (0, 0, 0)))
        out_shape.append(jax.ShapeDtypeStruct((3, model + 16, width), bf16))
    return pl.pallas_call(
        kernel,
        grid=(steps,),
        in_specs=in_specs,
        out_specs=out_specs,
        out_shape=out_shape,
        input_output_aliases={} if first else {4: given, 5: given + 1},
        compiler_params=pltpu.CompilerParams(vmem_limit_bytes=VMEM_LIMIT),
        cost_estimate=pl.CostEstimate(
            flops=12 * rows * model * width // COST_SCALE,
            transcendentals=0,
            bytes_accessed=rows * width,
        ),
        name="project_back",
    )(*operands)


def project_rows(place, dqkv, weight, pieces):
    _, rows, width = dqkv.shape
    model = weight.shape[1]
    block = rows // pieces

    def kernel(place_ref, dqkv_ref, weight_ref, *row_refs):
        row_grad = nt(dqkv_ref[0], weight_ref[0])
        for c in range(1, 3):
            row_grad = row_grad + nt(dqkv_ref[c], weight_ref[c])
        row_grad = row_grad.astype(bf16)
        for k in range(pieces):

            @pl.when(pl.program_id(0) == place_ref[0] ^ k)
            def _():
                row_refs[k][...] = row_grad

    return pl.pallas_call(
        kernel,
        grid=(pieces,),
        in_specs=[
            pl.BlockSpec(memory_space=pltpu.SMEM),
            pl.BlockSpec((3, block, width), lambda i: (0, i, 0)),
            pl.BlockSpec((3, model, width), lambda i: (0, 0, 0)),
        ],
        out_specs=[pl.BlockSpec((block, model), lambda i: (0, 0))] * pieces,
        out_shape=[jax.ShapeDtypeStruct((block, model), bf16)] * pieces,
        compiler_params=params(),
        cost_estimate=hint(6 * rows * model * width, rows * width),
        name="project_rows",
    )(place, dqkv, weight)


def make_shards(tensor_size, group_size):
    square = tensor_size == 4

    def swap(value, bits):
        return lax.ppermute(value, "tensor", [(i, i ^ bits) for i in range(tensor_size)])

    def gather_far(own):
        return swap(own, 2) if square else lax.all_gather(own, "tensor")

    def gather_near(own, far):
        if not square:
            return [far[i] for i in range(tensor_size)]
        return [own, swap(own, 1), far, swap(far, 1)]

    def exchange(stacked):
        return lax.all_to_all(stacked, "tensor", 0, 0)

    def sum_near(blocks, anchor):
        if not square:
            return (jnp.stack(blocks),), anchor
        anchor, (near_own, near_far) = tie(anchor, (swap(blocks[1], 1), swap(blocks[3], 1)))
        far = (blocks[2].astype(f32) + near_far.astype(f32)).astype(blocks[2].dtype)
        return (blocks[0], near_own, far), anchor

    def terms_far(stage, anchor):
        if not square:
            own = lax.psum_scatter(stage[0], "tensor", scatter_dimension=0, tiled=False)
            anchor, own = tie(anchor, own)
            return [own], anchor
        own, near, far = stage
        anchor, received = tie(anchor, swap(far, 2))
        return [own, near, received], anchor

    def sum_far(stage, anchor):
        terms, anchor = terms_far(stage, anchor)
        total = terms[0].astype(f32)
        for term in terms[1:]:
            total = total + term.astype(f32)
        return total.astype(terms[0].dtype), anchor

    steps = []
    for axis, size in (("tensor", tensor_size), ("dp", group_size)):
        bit = 1
        while bit < size:
            steps.append((axis, [(i, i ^ bit) for i in range(size)]))
            bit *= 2

    def sum_step(value, step, anchor):
        anchor, received = tie(anchor, lax.ppermute(value, step[0], step[1]))
        return value + received, anchor

    def ring_plan():
        bits = [1 << k for k in range(group_size.bit_length() - 1)]
        return [(bit, True) for bit in bits] + [(bit, False) for bit in reversed(bits)]

    def ring_step(value, step, anchor):
        bit, reducing = step
        side = (lax.axis_index("dp") // bit) % 2
        pairs = [(i, i ^ bit) for i in range(group_size)]
        if reducing:
            half = value.shape[0] // 2
            sent = lax.dynamic_slice_in_dim(value, (1 - side) * half, half, axis=0)
            anchor, received = tie(anchor, lax.ppermute(sent, "dp", pairs))
            kept = lax.dynamic_slice_in_dim(value, side * half, half, axis=0)
            return (kept.astype(f32) + received.astype(f32)).astype(value.dtype), anchor
        anchor, received = tie(anchor, lax.ppermute(value, "dp", pairs))
        return in_halves(value, received, side), anchor

    def in_halves(own, other, side):
        rows = own.shape[0]
        whole = jnp.zeros((2 * rows,) + own.shape[1:], own.dtype)
        whole = lax.dynamic_update_slice_in_dim(whole, own, side * rows, axis=0)
        return lax.dynamic_update_slice_in_dim(whole, other, (1 - side) * rows, axis=0)

    def fetch_half(own):
        half = own.shape[0] // 2
        side = lax.axis_index("dp") % 2
        return swap(lax.dynamic_slice_in_dim(own, side * half, half, axis=0), 2)

    def fetch_rest(half):
        return lax.ppermute(half, "dp", [(i, i ^ 1) for i in range(group_size)])

    def in_order(stacked):
        if not square:
            return stacked
        own = lax.axis_index("tensor")
        return jnp.concatenate(
            [lax.dynamic_slice_in_dim(stacked, own ^ i, 1, axis=0) for i in range(tensor_size)], axis=0
        )

    def shards(
        patches,
        cotangent,
        empty_slots,
        dataset_id,
        dataset_weight,
        query_key_value_weight,
        qv_bias,
        output_projection_weight,
        out_bias,
        up_projection_weight,
        up_bias,
        down_projection_weight,
        down_bias,
        attn_gain,
        attn_shift,
        mlp_gain,
        mlp_shift,
    ):
        slot_count, own_rows, model = patches.shape
        width = query_key_value_weight.shape[2]
        group_slots = empty_slots.shape[0]
        slot_index = jnp.arange(group_slots * slot_count, dtype=jnp.int32) % slot_count
        filled = jnp.repeat(slot_count - empty_slots, slot_count)
        valid_all = (slot_index < filled).astype(f32)
        table_hits = dataset_id[:, None] == jnp.arange(dataset_weight.shape[0], dtype=jnp.int32)[None, :]
        numerator = jnp.sum(jnp.where(table_hits, dataset_weight[None, :], 0), axis=1).astype(f32)
        total_items = jnp.sum(valid_all)
        total_weight = jnp.sum(valid_all * numerator)
        multiplier_whole = valid_all * numerator * total_items / total_weight
        own_start = lax.axis_index("dp") * slot_count
        own_scale = lax.dynamic_slice_in_dim(multiplier_whole, own_start, slot_count)
        own_valid = lax.dynamic_slice_in_dim(valid_all, own_start, slot_count)
        all_rows = slot_count * own_rows
        row_scale = jnp.repeat(own_scale, own_rows)[:, None]
        gain_row, shift_row, mlp_gain_row, mlp_shift_row, out_bias_row = (
            value[None, :] for value in (attn_gain, attn_shift, mlp_gain, mlp_shift, out_bias)
        )
        proj_bias = jnp.stack([qv_bias[0], jnp.zeros_like(qv_bias[0]), qv_bias[1]])[:, None, :]
        bias_row = up_bias[None, :]

        dp_side = lax.axis_index("dp") % 2
        place = jnp.zeros((1,), jnp.int32)
        if square:
            place = place + lax.axis_index("tensor")
        fetch = fetch_half if square else gather_far
        weights_near = ()
        if square:
            weights_near = tuple(
                swap(value, 1) for value in (output_projection_weight, up_projection_weight, down_projection_weight)
            )

        def gather_rows(own):
            return lax.all_gather(own, "tensor", axis=0, tiled=True)

        normed = [norm_item(patches, i, gain_row, shift_row) for i in range(slot_count)]
        every = gather_rows(normed[0])
        bias_far = gather_far(bias_row)
        cot_low = (cotangent.astype(f32).reshape(all_rows, model) * row_scale).astype(bf16)
        early = None
        if square:
            early = cot_back(cot_low, [down_projection_weight, weights_near[2]])
            every, (early, normed) = tie(every, (early, normed))
        qkvs, attended, lses, heads_own, normed_every = [], [], [], [], []
        for i in range(slot_count):
            last = i == slot_count - 1
            normed_every.append(every)
            following = None
            if not last:
                every, following = tie(every, normed[i + 1])
                following = gather_rows(following)
            qkv = (
                jnp.einsum("wz,gzh->gwh", every, query_key_value_weight, preferred_element_type=f32) + proj_bias
            ).astype(bf16)
            if i == 0:
                qkv, (weights_near, bias_far) = tie(qkv, (weights_near, bias_far))
            out, lse = attend(qkv)
            if not last:
                out, following = tie(out, following)
            if i > 0:
                out, heads_own[-1] = tie(out, heads_own[-1])
            if i == min(1, slot_count - 1):
                out, (up_own, out_own) = tie(out, (up_projection_weight, output_projection_weight))
                out_far = gather_far(out_own)
                up_far = fetch(up_own)
            if last:
                out, (out_far, up_far) = tie(out, (out_far, up_far))
            heads_own.append(exchange(out.reshape(tensor_size, own_rows, width)))
            qkvs.append(qkv)
            attended.append(out)
            lses.append(lse)
            every = following
        if square:
            up_rest = fetch_rest(up_far)
            out_weight = jnp.concatenate([out_own, weights_near[0], out_far, swap(out_far, 1)], axis=0)
        else:
            out_weight = jnp.concatenate(gather_near(out_own, out_far), axis=0)
        rows_done = None
        for i in range(slot_count):
            if i == slot_count - 1:
                rows_done, heads_own[i] = tie(rows_done, heads_own[i])
                heads_own[i], down_own = tie(heads_own[i], down_projection_weight)
                down_far = gather_far(down_own)
            rows_done = out_project(
                patches, i, place, heads_own[i], out_weight, out_bias_row, mlp_gain_row, mlp_shift_row, rows_done
            )
        if square:
            rows_done, up_rest = tie(rows_done, up_rest)
            up_far = in_halves(up_far, up_rest, dp_side)
            up_diag = swap(up_far, 1)
        attended_rows, residual, normed_mlp = rows_done

        bias_blocks = gather_near(bias_row, bias_far)
        if square:
            up_blocks = [up_own, weights_near[1]]
            down_blocks = [down_own, weights_near[2]]
        else:
            up_blocks = gather_near(up_own, up_far)
            down_blocks = gather_near(down_own, down_far)
        calls = tensor_size // 2
        total = None
        slopes, down_grads = [], []
        for c in range(calls):
            pair = slice(2 * c, 2 * c + 2)
            if c == 1 and square:
                total, (up_diag, down_far) = tie(total, (up_diag, down_far))
                up_blocks += [up_far, up_diag]
                down_blocks += [down_far, swap(down_far, 1)]
            slope, total, *grads = mlp_forward(
                normed_mlp, cot_low, up_blocks[pair], bias_blocks[pair], down_blocks[pair], total
            )
            slopes.append(slope)
            down_grads += grads
        layer_sum = total

        cot_late, down_grads = tie(cot_low, down_grads)
        before = None
        bias_grads = []
        for c in range(calls):
            pair = slice(2 * c, 2 * c + 2)
            if c == 0 and square:
                *before, bias_grad = mlp_backward(early, slopes[c], up_blocks[pair], [], before, c, calls)
            else:
                *before, bias_grad = mlp_backward(
                    cot_late, slopes[c], up_blocks[pair], down_blocks[pair], before, c, calls
                )
            bias_grads.append(bias_grad)
            if c == 0:
                down_stage, before = sum_near(down_grads, before)
        ring = ring_plan()
        pre_grad, total = before

        if square:
            ahead = weight_back(normed_mlp, pre_grad, [1, 3], None, None, tensor_size)
            total, ahead = tie(total, ahead)
        grad_residual, grad_low, small_rows, pieces = residual_back(
            total, residual, cotangent, own_scale, place, out_weight, mlp_gain_row, tensor_size
        )
        down_sum, pieces = sum_far(down_stage, pieces)
        grad_attended = exchange(pieces)
        if square:
            up_near, up_diag_near = swap(ahead[0], 1), swap(ahead[1], 1)
            first, second, *out_grads = weight_back(
                normed_mlp, pre_grad, [2, 0], attended_rows, grad_low, tensor_size
            )
            second, (up_near, up_diag_near) = tie(second, (up_near, up_diag_near))
            up_far_sum = (first.astype(f32) + up_diag_near.astype(f32)).astype(bf16)
            out_stage, up_far_sum = sum_near(out_grads, up_far_sum)
            up_far_sum, grad_attended = tie(up_far_sum, grad_attended)
            up_stage = (second, up_near, up_far_sum)
        else:
            weight_grads = weight_back(
                normed_mlp, pre_grad, list(range(tensor_size)), attended_rows, grad_low, tensor_size
            )
            up_stage, grad_attended = sum_near(weight_grads[:tensor_size], grad_attended)
            out_stage, grad_attended = sum_near(weight_grads[tensor_size:], grad_attended)
        bias_rows = in_order(jnp.concatenate(bias_grads, axis=1).reshape(tensor_size, -1))
        smalls = jnp.concatenate([small_rows[:4].reshape(-1), bias_rows.reshape(-1)]).reshape(-1, 128)

        waiting = list(steps)
        weights_wide = query_key_value_weight.astype(f32)
        sums = None
        grad_normed = []
        for i in range(slot_count):
            last = i == slot_count - 1
            dqkv = attend_back(qkvs[i], attended[i], grad_attended, i, lses[i])
            if i >= 2:
                grad_normed[i - 2], dqkv = terms_far(grad_normed[i - 2], dqkv)
            if i >= 1 and not last:
                grad_normed[i - 1], dqkv = sum_near(grad_normed[i - 1], dqkv)
            if i == 0:
                up_sum, dqkv = sum_far(up_stage, dqkv)
                out_sum, dqkv = sum_far(out_stage, dqkv)
                up_all = lax.psum((up_sum, out_sum), "dp")
            if last:
                dqkv, up_all = tie(dqkv, up_all)
            if waiting and i > 0:
                smalls, dqkv = sum_step(smalls, waiting.pop(0), dqkv)
            if ring:
                down_sum, dqkv = ring_step(down_sum, ring.pop(0), dqkv)
            results = project_back(place, normed_every[i], dqkv, query_key_value_weight, sums, last, tensor_size)
            if not last:
                partial, sums = results[:tensor_size], results[tensor_size:]
                if waiting:
                    smalls, partial = sum_step(smalls, waiting.pop(0), partial)
                if ring:
                    down_sum, partial = ring_step(down_sum, ring.pop(0), partial)
            else:
                *sums, qkv_low = results
                qkv_low, (dqkv, grad_residual, layer_sum) = tie(qkv_low, (dqkv, grad_residual, layer_sum))
                qkv_all = lax.psum(qkv_low, "dp")
                output = layer_out(layer_sum, residual, down_bias[None, :], own_valid, patches.shape)
                partial = project_rows(place, dqkv, query_key_value_weight, tensor_size)
                if i >= 1:
                    grad_normed[i - 1], partial = sum_near(grad_normed[i - 1], partial)
                raw = jnp.stack(
                    [
                        jnp.sum(sums[0] * weights_wide, axis=(0, 2)),
                        jnp.sum(sums[1][:3, None, :] * weights_wide, axis=(0, 2)),
                    ]
                )
                for axis, pairs in steps:
                    raw = raw + lax.ppermute(raw, axis, pairs)
            grad_normed.append(partial)
        grad_inputs = None
        for i in range(slot_count):
            if i == slot_count - 1:
                grad_normed[i], grad_residual = sum_near(grad_normed[i], grad_residual)
            terms = grad_normed[i]
            if i >= slot_count - 2:
                terms, grad_residual = terms_far(terms, grad_residual)
            grad_inputs = input_back(terms, patches, i, grad_residual, gain_row, grad_inputs)
        grad_inputs, qkv_all = tie(grad_inputs, qkv_all)
        for step in ring:
            down_sum = ring_step(down_sum, step, place)[0]
        for step in waiting:
            smalls = sum_step(smalls, step, place)[0]
        weight_grad = qkv_all[:, :model].astype(f32)
        columns = qkv_all[:, model].astype(f32)
        up_all, out_all = [value.astype(f32) for value in up_all]
        down_all = down_sum.astype(f32)
        inverse = 1.0 / total_items
        smalls = smalls.reshape(-1) * inverse
        raw = raw * inverse
        small_rows = smalls[: 4 * model].reshape(4, model)
        units = up_bias.shape[0]
        bias_all = lax.dynamic_slice_in_dim(smalls[4 * model :], lax.axis_index("tensor") * units, units)
        shift_all = raw[1]
        gain_all = (raw[0] - attn_shift * shift_all) / attn_gain
        columns = columns * inverse
        return (
            output,
            grad_inputs,
            weight_grad * inverse,
            jnp.stack([columns[0], columns[2]]),
            out_all * inverse,
            small_rows[2],
            up_all * inverse,
            bias_all,
            down_all * inverse,
            small_rows[3],
            gain_all,
            shift_all,
            small_rows[0],
            small_rows[1],
        )

    return shards


def solution(mesh):
    items = P("dp", "tensor", None)
    return jax.shard_map(
        make_shards(mesh.shape["tensor"], mesh.shape["dp"]),
        mesh=mesh,
        in_specs=(
            items,
            items,
            P(),
            P(),
            P(),
            P(None, None, "tensor"),
            P(None, "tensor"),
            P("tensor", None),
            P(),
            P(None, "tensor"),
            P("tensor"),
            P("tensor", None),
            P(),
            P(),
            P(),
            P(),
            P(),
        ),
        out_specs=(
            items,
            items,
            P(None, None, "tensor"),
            P(None, "tensor"),
            P("tensor", None),
            P(),
            P(None, "tensor"),
            P("tensor"),
            P("tensor", None),
            P(),
            P(),
            P(),
            P(),
            P(),
        ),
        check_vma=False,
    )
```

```python
import jax
import jax.numpy as jnp
from jax import lax
from jax.experimental import pallas as pl
from jax.experimental.pallas import tpu as pltpu
from jax.sharding import PartitionSpec as P

HD = 64
SCORE_SCALE = HD ** (-0.5)
LOG2E = 1.4426950408889634
SQRT_HALF = 0.7071067811865476
INV_SQRT_2PI = 0.3989422804014327
epsilon = 1e-05
f32 = jnp.float32
bf16 = jnp.bfloat16
VMEM_LIMIT = 60 << 20
COST_SCALE = 64


def nn(a, b):
    return lax.dot_general(a, b, (((1,), (0,)), ((), ())), preferred_element_type=f32)


def nt(a, b):
    return lax.dot_general(a, b, (((1,), (1,)), ((), ())), preferred_element_type=f32)


def tn(a, b):
    return lax.dot_general(a, b, (((0,), (0,)), ((), ())), preferred_element_type=f32)


def tie(first, second):
    return lax.optimization_barrier((first, second))


def largest_block(extent, limit):
    block = min(extent, limit)
    while extent % block:
        block //= 2
    return block


def norm_rows(source, norm_gain, norm_shift):
    row_mean = jnp.mean(source, axis=-1, keepdims=True)
    centred = source - row_mean
    spread = jnp.mean(centred * centred, axis=-1, keepdims=True)
    return centred * lax.rsqrt(spread + epsilon) * norm_gain + norm_shift


def attend(qkv):
    _, length, width = qkv.shape
    lanes = min(128, width)
    heads = lanes // HD
    qblock = largest_block(length, 2048)
    to_log2 = SCORE_SCALE * LOG2E

    def body(q_ref, k_ref, v_ref, out_ref, lse_ref):
        queries = q_ref[...]
        keys = k_ref[...]
        values_t = v_ref[...].T
        lane = lax.broadcasted_iota(jnp.int32, (1, lanes), 1)
        outs = []
        for h in range(heads):
            own = queries
            if heads > 1:
                own = jnp.where(lane // HD == h, queries, jnp.zeros_like(queries))
            scores = nt(keys, own)
            top = jnp.max(scores, axis=0, keepdims=True)
            exp_scores = jnp.exp2((scores - top) * to_log2)
            total = jnp.sum(exp_scores, axis=0, keepdims=True)
            outs.append(nn(values_t[h * HD : (h + 1) * HD, :], exp_scores.astype(bf16)) / total)
            lse_ref[h : h + 1, :] = top * to_log2 + jnp.log2(total)
        out_ref[...] = jnp.concatenate(outs, axis=0).T.astype(bf16)

    pairs = width // lanes
    return pl.pallas_call(
        body,
        grid=(pairs, length // qblock),
        in_specs=[
            pl.BlockSpec((None, qblock, lanes), lambda h, j: (0, j, h)),
            pl.BlockSpec((None, length, lanes), lambda h, j: (1, 0, h)),
            pl.BlockSpec((None, length, lanes), lambda h, j: (2, 0, h)),
        ],
        out_specs=[
            pl.BlockSpec((qblock, lanes), lambda h, j: (j, h)),
            pl.BlockSpec((None, heads, qblock), lambda h, j: (h, 0, j)),
        ],
        out_shape=[
            jax.ShapeDtypeStruct((length, width), bf16),
            jax.ShapeDtypeStruct((pairs, heads, length), f32),
        ],
        compiler_params=pltpu.CompilerParams(vmem_limit_bytes=VMEM_LIMIT),
        cost_estimate=pl.CostEstimate(
            flops=8 * length * length * width // COST_SCALE,
            transcendentals=0,
            bytes_accessed=length * width,
        ),
        name="attend",
    )(qkv, qkv, qkv)


def attend_back(qkv, attended, grad_attended, item, lse):
    _, length, width = qkv.shape
    lanes = min(128, width)
    shards_of = grad_attended.shape[0]
    heads = lanes // HD
    kblock = largest_block(length, 1024)
    kblocks = length // kblock
    to_log2 = SCORE_SCALE * LOG2E

    def body(q_ref, k_ref, v_ref, out_ref, grad_ref, lse_ref, dqkv_ref, dq_acc, row_dot):
        kb = pl.program_id(1)
        queries = q_ref[...]
        grads = grad_ref[...].reshape(length, lanes)
        keys = k_ref[...]
        values = v_ref[...]
        keys_t = keys.T
        lane = lax.broadcasted_iota(jnp.int32, (1, lanes), 1)

        @pl.when(kb == 0)
        def _():
            product = out_ref[...].astype(f32) * grads.astype(f32)
            high = product.astype(bf16)
            rest = (product - high.astype(f32)).astype(bf16)
            pick = lax.broadcasted_iota(jnp.int32, (8, lanes), 0)
            mask = (lax.broadcasted_iota(jnp.int32, (8, lanes), 1) // HD == pick).astype(f32).astype(bf16)
            row_dot[...] = nt(mask, high) + nt(mask, rest)

        dk = None
        dv = None
        dqs = []
        for h in range(heads):
            own_q = queries
            own_g = grads
            if heads > 1:
                mine = lane // HD == h
                own_q = jnp.where(mine, queries, jnp.zeros_like(queries))
                own_g = jnp.where(mine, grads, jnp.zeros_like(grads))
            scores = nt(keys, own_q)
            weights = jnp.exp2(scores * to_log2 - lse_ref[h : h + 1, :])
            grad_weights = nt(values, own_g)
            grad_scores = (weights * (grad_weights - row_dot[h : h + 1, :])).astype(bf16)
            dv_h = nn(weights.astype(bf16), own_g)
            dk_h = nn(grad_scores, own_q)
            dv = dv_h if dv is None else dv + dv_h
            dk = dk_h if dk is None else dk + dk_h
            dqs.append(nn(keys_t[h * HD : (h + 1) * HD, :], grad_scores))
        rows = pl.ds(pl.multiple_of(kb * kblock, kblock), kblock)
        dqkv_ref[1, rows, :] = (dk * SCORE_SCALE).astype(bf16)
        dqkv_ref[2, rows, :] = dv.astype(bf16)
        dq = jnp.concatenate(dqs, axis=0)
        if kblocks == 1:
            dqkv_ref[0] = (dq * SCORE_SCALE).T.astype(bf16)
            return

        @pl.when(kb == 0)
        def _():
            dq_acc[...] = dq

        @pl.when((kb > 0) & (kb < kblocks - 1))
        def _():
            dq_acc[...] += dq

        @pl.when(kb == kblocks - 1)
        def _():
            dqkv_ref[0] = ((dq_acc[...] + dq) * SCORE_SCALE).T.astype(bf16)

    pairs = width // lanes
    return pl.pallas_call(
        body,
        grid=(pairs, kblocks),
        in_specs=[
            pl.BlockSpec((None, length, lanes), lambda h, kb: (0, 0, h)),
            pl.BlockSpec((None, kblock, lanes), lambda h, kb: (1, kb, h)),
            pl.BlockSpec((None, kblock, lanes), lambda h, kb: (2, kb, h)),
            pl.BlockSpec((length, lanes), lambda h, kb: (0, h)),
            pl.BlockSpec((shards_of, length // shards_of, lanes), lambda h, kb: (0, item, h)),
            pl.BlockSpec((None, heads, length), lambda h, kb: (h, 0, 0)),
        ],
        out_specs=pl.BlockSpec((3, length, lanes), lambda h, kb: (0, 0, h)),
        out_shape=jax.ShapeDtypeStruct((3, length, width), bf16),
        scratch_shapes=[pltpu.VMEM((lanes, length), f32), pltpu.VMEM((8, length), f32)],
        compiler_params=pltpu.CompilerParams(vmem_limit_bytes=VMEM_LIMIT),
        cost_estimate=pl.CostEstimate(
            flops=20 * length * length * width // COST_SCALE,
            transcendentals=0,
            bytes_accessed=length * width,
        ),
        name="attend_back",
    )(qkv, qkv, qkv, attended, grad_attended, lse)


def hint(flops, size):
    return pl.CostEstimate(flops=flops // COST_SCALE, transcendentals=0, bytes_accessed=size)


def params():
    return pltpu.CompilerParams(vmem_limit_bytes=VMEM_LIMIT)


def norm_item(patches, item, norm_gain, norm_shift):
    _, rows, model = patches.shape
    block = largest_block(rows, 256)

    def body(x_ref, gain_ref, shift_ref, out_ref):
        out_ref[...] = norm_rows(x_ref[...].astype(f32), gain_ref[...], shift_ref[...]).astype(bf16)

    vector = pl.BlockSpec((1, model), lambda i: (0, 0))
    return pl.pallas_call(
        body,
        grid=(rows // block,),
        in_specs=[pl.BlockSpec((None, block, model), lambda i: (item, i, 0)), vector, vector],
        out_specs=pl.BlockSpec((block, model), lambda i: (i, 0)),
        out_shape=jax.ShapeDtypeStruct((rows, model), bf16),
        compiler_params=params(),
        cost_estimate=hint(0, rows * model),
        name="norm_item",
    )(patches, norm_gain, norm_shift)


def out_project(patches, item, place, heads, weight, out_bias, norm_gain, norm_shift, before):
    slots, rows, model = patches.shape
    block = largest_block(rows, 256)
    steps = rows // block
    count, _, width = heads.shape

    def body(*refs):
        place_ref, x_ref, weight_ref, bias_ref, gain_ref, shift_ref, head_ref = refs[:7]
        attended_ref, residual_ref, normed_ref = refs[-3:]
        for k in range(count):
            attended_ref[:, k * width : (k + 1) * width] = head_ref[place_ref[0] ^ k]
        attended = attended_ref[...]
        residual = x_ref[...].astype(f32) + nn(attended, weight_ref[...]) + bias_ref[...]
        residual_ref[...] = residual
        normed_ref[...] = norm_rows(residual, gain_ref[...], shift_ref[...]).astype(bf16)

    vector = pl.BlockSpec((1, model), lambda i: (0, 0))
    placed = pl.BlockSpec((block, model), lambda i: (item * steps + i, 0))
    operands = [place, patches, weight, out_bias, norm_gain, norm_shift, heads]
    in_specs = [
        pl.BlockSpec(memory_space=pltpu.SMEM),
        pl.BlockSpec((None, block, model), lambda i: (item, i, 0)),
        pl.BlockSpec((model, model), lambda i: (0, 0)),
        vector,
        vector,
        vector,
        pl.BlockSpec((count, block, width), lambda i: (0, i, 0)),
    ]
    aliases = {}
    if before is not None:
        aliases = {len(operands) + k: k for k in range(3)}
        operands += before
        in_specs += [pl.BlockSpec(memory_space=pl.ANY)] * 3
    return pl.pallas_call(
        body,
        grid=(steps,),
        in_specs=in_specs,
        out_specs=[placed] * 3,
        out_shape=[jax.ShapeDtypeStruct((slots * rows, model), t) for t in (bf16, f32, bf16)],
        input_output_aliases=aliases,
        compiler_params=params(),
        cost_estimate=hint(2 * rows * model * model, rows * model),
        name="out_project",
    )(*operands)


def residual_back(total, residual, cotangent, scale, place, weight, norm_gain, pieces):
    slots, rows, model = cotangent.shape
    block = largest_block(rows, 256)
    steps = rows // block
    piece = model // pieces

    def body(*refs):
        place_ref, total_ref, residual_ref, cot_ref, scale_ref, weight_ref, gain_ref = refs[:7]
        grad_ref, low_ref, sum_ref, attended_ref = refs[-4:]
        residual = residual_ref[...]
        centred = residual - jnp.mean(residual, axis=-1, keepdims=True)
        rate = lax.rsqrt(jnp.mean(centred * centred, axis=-1, keepdims=True) + epsilon)
        xhat = centred * rate
        grad_normed = total_ref[...]
        scaled = grad_normed * gain_ref[...]
        inner = jnp.mean(scaled, axis=-1, keepdims=True)
        outer = jnp.mean(scaled * xhat, axis=-1, keepdims=True)
        cot = cot_ref[...].astype(f32) * scale_ref[pl.program_id(0) // steps]
        grad = cot + rate * (scaled - inner - xhat * outer)
        grad_ref[...] = grad
        low = grad.astype(bf16)
        low_ref[...] = low

        @pl.when(pl.program_id(0) == 0)
        def _():
            sum_ref[...] = jnp.zeros_like(sum_ref)

        for k, value in enumerate((grad_normed * xhat, grad_normed, grad, cot)):
            sum_ref[k : k + 1, :] += jnp.sum(value, axis=0, keepdims=True)
        attended = nt(low, weight_ref[...]).astype(bf16)
        for k in range(pieces):
            attended_ref[place_ref[0] ^ k] = attended[:, k * piece : (k + 1) * piece]

    row_spec = pl.BlockSpec((block, model), lambda i: (i, 0))
    return pl.pallas_call(
        body,
        grid=(slots * steps,),
        in_specs=[
            pl.BlockSpec(memory_space=pltpu.SMEM),
            row_spec,
            row_spec,
            pl.BlockSpec((None, block, model), lambda i: (i // steps, i % steps, 0)),
            pl.BlockSpec(memory_space=pltpu.SMEM),
            pl.BlockSpec((model, model), lambda i: (0, 0)),
            pl.BlockSpec((1, model), lambda i: (0, 0)),
        ],
        out_specs=[
            row_spec,
            row_spec,
            pl.BlockSpec((8, model), lambda i: (0, 0)),
            pl.BlockSpec((pieces, block, piece), lambda i: (0, i, 0)),
        ],
        out_shape=[
            jax.ShapeDtypeStruct((slots * rows, model), f32),
            jax.ShapeDtypeStruct((slots * rows, model), bf16),
            jax.ShapeDtypeStruct((8, model), f32),
            jax.ShapeDtypeStruct((pieces, slots * rows, piece), bf16),
        ],
        compiler_params=params(),
        cost_estimate=hint(2 * slots * rows * model * model, rows * model),
        name="residual_back",
    )(place, total, residual, cotangent, scale, weight, norm_gain)


def input_back(terms, patches, item, grad_residual, norm_gain, before):
    slots, rows, model = patches.shape
    block = largest_block(rows, 256)
    count = len(terms)

    def body(*refs):
        x_ref, grad_ref, gain_ref = refs[:3]
        out_ref = refs[-1]
        grad_normed = refs[3][...].astype(f32)
        for k in range(1, count):
            grad_normed = grad_normed + refs[3 + k][...].astype(f32)
        source = x_ref[...].astype(f32)
        centred = source - jnp.mean(source, axis=-1, keepdims=True)
        rate = lax.rsqrt(jnp.mean(centred * centred, axis=-1, keepdims=True) + epsilon)
        xhat = centred * rate
        scaled = grad_normed * gain_ref[...]
        inner = jnp.mean(scaled, axis=-1, keepdims=True)
        outer = jnp.mean(scaled * xhat, axis=-1, keepdims=True)
        out_ref[...] = (grad_ref[...] + rate * (scaled - inner - xhat * outer)).astype(bf16)

    row_spec = pl.BlockSpec((block, model), lambda i: (i, 0))
    placed = pl.BlockSpec((None, block, model), lambda i: (item, i, 0))
    operands = [patches, grad_residual, norm_gain, *terms]
    steps = rows // block
    grad_spec = pl.BlockSpec((block, model), lambda i: (item * steps + i, 0))
    in_specs = [placed, grad_spec, pl.BlockSpec((1, model), lambda i: (0, 0))] + [row_spec] * count
    aliases = {}
    if before is not None:
        aliases = {len(operands): 0}
        operands.append(before)
        in_specs.append(pl.BlockSpec(memory_space=pl.ANY))
    return pl.pallas_call(
        body,
        grid=(rows // block,),
        in_specs=in_specs,
        out_specs=placed,
        out_shape=jax.ShapeDtypeStruct((slots, rows, model), bf16),
        input_output_aliases=aliases,
        compiler_params=params(),
        cost_estimate=hint(0, rows * model),
        name="input_back",
    )(*operands)


def layer_out(total, residual, down_bias, valid, shape):
    slots, rows, model = shape
    block = largest_block(rows, 256)
    steps = rows // block

    def body(total_ref, residual_ref, bias_ref, valid_ref, out_ref):
        value = residual_ref[...] + total_ref[...] + bias_ref[...]
        out_ref[...] = (value * valid_ref[pl.program_id(0) // steps]).astype(bf16)

    row_spec = pl.BlockSpec((block, model), lambda i: (i, 0))
    return pl.pallas_call(
        body,
        grid=(slots * steps,),
        in_specs=[
            row_spec,
            row_spec,
            pl.BlockSpec((1, model), lambda i: (0, 0)),
            pl.BlockSpec(memory_space=pltpu.SMEM),
        ],
        out_specs=pl.BlockSpec((None, block, model), lambda i: (i // steps, i % steps, 0)),
        out_shape=jax.ShapeDtypeStruct(shape, bf16),
        compiler_params=params(),
        cost_estimate=hint(0, rows * model),
        name="layer_out",
    )(total, residual, down_bias, valid)


def mlp_forward(normed, cot, ups, biases, downs, total):
    rows, model = normed.shape
    count = len(ups)
    units = ups[0].shape[1]
    block = largest_block(rows, 512)
    steps = rows // block
    first = total is None

    def body(*refs):
        x_ref, cot_ref = refs[:2]
        up_refs, bias_refs, down_refs = (refs[2 + k * count : 2 + (k + 1) * count] for k in range(3))
        rest = refs[2 + 3 * count :]
        if not first:
            before_ref = rest[0]
            rest = rest[1:]
        slope_ref, sum_ref = rest[:2]
        grad_refs = rest[2 : 2 + count]
        hidden_ref, acc_ref = rest[2 + count :]
        step = pl.program_id(0)
        part = largest_block(units, 256)
        for k in range(count):
            for j in range(units // part):
                cols = slice(j * part, (j + 1) * part)
                wide = slice(k * units + j * part, k * units + (j + 1) * part)
                pre = nn(x_ref[...], up_refs[k][:, cols]) + bias_refs[k][:, cols]
                cdf = 0.5 + 0.5 * lax.erf(pre * SQRT_HALF)
                density = jnp.exp2(pre * pre * (-0.5 * LOG2E)) * INV_SQRT_2PI
                hidden_ref[:, wide] = (pre * cdf).astype(bf16)
                slope_ref[:, wide] = (cdf + pre * density).astype(bf16)
        out = None if first else before_ref[...]
        for k in range(count):
            hidden = hidden_ref[:, k * units : (k + 1) * units]
            product = nn(hidden, down_refs[k][...])
            out = product if out is None else out + product
            grad = tn(hidden, cot_ref[...])

            @pl.when(step == 0)
            def _():
                acc_ref[k] = grad

            @pl.when(step > 0)
            def _():
                acc_ref[k] += grad

        sum_ref[...] = out

        @pl.when(step == steps - 1)
        def _():
            for k in range(count):
                grad_refs[k][...] = acc_ref[k].astype(bf16)

    row_spec = pl.BlockSpec((block, model), lambda i: (i, 0))
    slope_spec = pl.BlockSpec((block, count * units), lambda i: (i, 0))
    up_spec = pl.BlockSpec((model, units), lambda i: (0, 0), pipeline_mode=pl.Buffered(1))
    down_spec = pl.BlockSpec((units, model), lambda i: (0, 0), pipeline_mode=pl.Buffered(1))
    grad_spec = pl.BlockSpec((units, model), lambda i: (0, 0))
    operands = [normed, cot, *ups, *biases, *downs]
    in_specs = [row_spec, row_spec] + [up_spec] * count
    in_specs += [pl.BlockSpec((1, units), lambda i: (0, 0))] * count + [down_spec] * count
    aliases = {}
    if not first:
        aliases = {len(operands): 1}
        operands.append(total)
        in_specs.append(row_spec)
    return pl.pallas_call(
        body,
        grid=(steps,),
        in_specs=in_specs,
        out_specs=[slope_spec, row_spec] + [grad_spec] * count,
        out_shape=[
            jax.ShapeDtypeStruct((rows, count * units), bf16),
            jax.ShapeDtypeStruct((rows, model), f32),
        ]
        + [jax.ShapeDtypeStruct((units, model), bf16)] * count,
        scratch_shapes=[pltpu.VMEM((block, count * units), bf16), pltpu.VMEM((count, units, model), f32)],
        input_output_aliases=aliases,
        compiler_params=params(),
        cost_estimate=hint(6 * rows * model * units * count, rows * units),
        name="mlp_forward",
    )(*operands)


def cot_back(cot, downs):
    rows, model = cot.shape
    count = len(downs)
    units = downs[0].shape[0]
    block = largest_block(rows, 512)

    def body(cot_ref, *refs):
        for k in range(count):
            refs[count][:, k * units : (k + 1) * units] = nt(cot_ref[...], refs[k][...]).astype(bf16)

    return pl.pallas_call(
        body,
        grid=(rows // block,),
        in_specs=[pl.BlockSpec((block, model), lambda i: (i, 0))]
        + [pl.BlockSpec((units, model), lambda i: (0, 0))] * count,
        out_specs=pl.BlockSpec((block, count * units), lambda i: (i, 0)),
        out_shape=jax.ShapeDtypeStruct((rows, count * units), bf16),
        compiler_params=params(),
        cost_estimate=hint(2 * rows * model * units * count, rows * units),
        name="cot_back",
    )(cot, *downs)


def mlp_backward(cot, slope, ups, downs, before, index, calls):
    rows, _ = cot.shape
    model = ups[0].shape[0]
    count = len(ups)
    units = ups[0].shape[1]
    block = largest_block(rows, 512)
    first = before is None

    def body(*refs):
        cot_ref, slope_ref = refs[:2]
        up_refs, down_refs = refs[2 : 2 + count], refs[2 + count : 2 + count + len(downs)]
        grad_ref, sum_ref, bias_ref = refs[-3:]

        @pl.when(pl.program_id(0) == 0)
        def _():
            bias_ref[...] = jnp.zeros_like(bias_ref)

        out = None if first else refs[3 + count + len(downs)][...]
        part = largest_block(units, 512)
        for k in range(count):
            for j in range(units // part):
                rows_of = slice(j * part, (j + 1) * part)
                wide = slice(k * units + j * part, k * units + (j + 1) * part)
                if downs:
                    product = nt(cot_ref[...], down_refs[k][rows_of, :])
                else:
                    product = cot_ref[:, wide].astype(f32)
                low = (product * slope_ref[:, wide].astype(f32)).astype(bf16)
                grad_ref[:, wide] = low
                bias_ref[:, wide] += jnp.sum(low.astype(f32), axis=0, keepdims=True)
            product = nt(grad_ref[:, k * units : (k + 1) * units], up_refs[k][...])
            out = product if out is None else out + product
        sum_ref[...] = out

    row_spec = pl.BlockSpec((block, model), lambda i: (i, 0))
    slope_spec = pl.BlockSpec((block, count * units), lambda i: (i, 0))
    up_spec = pl.BlockSpec((model, units), lambda i: (0, 0), pipeline_mode=pl.Buffered(1))
    down_spec = pl.BlockSpec((units, model), lambda i: (0, 0), pipeline_mode=pl.Buffered(1))
    operands = [cot, slope, *ups, *downs]
    in_specs = [row_spec if downs else slope_spec, slope_spec] + [up_spec] * count + [down_spec] * len(downs)
    aliases = {}
    if not first:
        aliases = {len(operands): 0, len(operands) + 1: 1}
        operands += before
        in_specs += [pl.BlockSpec(memory_space=pl.ANY), row_spec]
    return pl.pallas_call(
        body,
        grid=(rows // block,),
        in_specs=in_specs,
        out_specs=[
            pl.BlockSpec((block, count * units), lambda i: (i, index)),
            row_spec,
            pl.BlockSpec((1, count * units), lambda i: (0, 0)),
        ],
        out_shape=[
            jax.ShapeDtypeStruct((rows, calls * count * units), bf16),
            jax.ShapeDtypeStruct((rows, model), f32),
            jax.ShapeDtypeStruct((1, count * units), f32),
        ],
        input_output_aliases=aliases,
        compiler_params=params(),
        cost_estimate=hint(4 * rows * model * units * count, rows * units),
        name="mlp_backward",
    )(*operands)


def weight_back(normed, pre_grad, picks, attended, grad_low, pieces):
    rows, model = normed.shape
    units = pre_grad.shape[1] // pieces
    piece = model // pieces
    block = largest_block(rows, 512)
    steps = rows // block
    count = len(picks)
    outs = 0 if attended is None else pieces

    def body(x_ref, *refs):
        pre_refs = refs[:count]
        rest = refs[count:]
        if outs:
            attended_ref, grad_ref = rest[:2]
            rest = rest[2:]
        up_refs, out_refs = rest[:count], rest[count : count + outs]
        up_acc = rest[count + outs]
        step = pl.program_id(0)

        def add(acc, place, value):
            @pl.when(step == 0)
            def _():
                acc[place] = value

            @pl.when(step > 0)
            def _():
                acc[place] += value

        for k in range(count):
            add(up_acc, (slice(None), slice(k * units, (k + 1) * units)), tn(x_ref[...], pre_refs[k][...]))
        if outs:
            out_acc = rest[-1]
            add(out_acc, (slice(None), slice(None)), tn(attended_ref[...], grad_ref[...]))

        @pl.when(step == steps - 1)
        def _():
            for k in range(count):
                up_refs[k][...] = up_acc[:, k * units : (k + 1) * units].astype(bf16)
            for k in range(outs):
                out_refs[k][...] = out_acc[k * piece : (k + 1) * piece, :].astype(bf16)

    row_spec = pl.BlockSpec((block, model), lambda i: (i, 0))

    def columns_of(pick):
        return pl.BlockSpec((block, units), lambda i: (i, pick))

    operands = [normed] + [pre_grad] * count
    in_specs = [row_spec] + [columns_of(pick) for pick in picks]
    scratch = [pltpu.VMEM((model, count * units), f32)]
    if outs:
        operands += [attended, grad_low]
        in_specs += [row_spec, row_spec]
        scratch.append(pltpu.VMEM((model, model), f32))
    return pl.pallas_call(
        body,
        grid=(steps,),
        in_specs=in_specs,
        out_specs=[pl.BlockSpec((model, units), lambda i: (0, 0))] * count
        + [pl.BlockSpec((piece, model), lambda i: (0, 0))] * outs,
        out_shape=[jax.ShapeDtypeStruct((model, units), bf16)] * count
        + [jax.ShapeDtypeStruct((piece, model), bf16)] * outs,
        scratch_shapes=scratch,
        compiler_params=params(),
        cost_estimate=hint(2 * rows * model * units * count, rows * model),
        name="weight_back",
    )(*operands)


def project_back(place, normed, dqkv, weight, before, last, pieces):
    rows, model = normed.shape
    width = weight.shape[2]
    block = rows // pieces
    steps = pieces
    first = before is None
    given = 0 if last else pieces

    def kernel(*refs):
        place_ref, normed_ref, dqkv_ref, weight_ref = refs[:4]
        rest = refs[4:]
        if not first:
            wgrad_before, column_before = rest[:2]
            rest = rest[2:]
        row_refs, rest = rest[:given], rest[given:]
        wgrad_ref, column_ref = rest[:2]
        step = pl.program_id(0)

        @pl.when(step == 0)
        def _():
            if first:
                wgrad_ref[...] = jnp.zeros_like(wgrad_ref)
                column_ref[...] = jnp.zeros_like(column_ref)
            else:
                wgrad_ref[...] = wgrad_before[...]
                column_ref[...] = column_before[...]

        if not last:
            row_grad = nt(dqkv_ref[0], weight_ref[0])
            for c in range(1, 3):
                row_grad = row_grad + nt(dqkv_ref[c], weight_ref[c])
            row_grad = row_grad.astype(bf16)
            for k in range(pieces):

                @pl.when(step == place_ref[0] ^ k)
                def _():
                    row_refs[k][...] = row_grad

        for c in range(3):
            wgrad_ref[c] += tn(normed_ref[...], dqkv_ref[c])
            column_ref[c : c + 1, :] += jnp.sum(dqkv_ref[c].astype(f32), axis=0, keepdims=True)
        if last:
            low_ref = rest[2]

            @pl.when(step == steps - 1)
            def _():
                low_ref[:, :model, :] = wgrad_ref[...].astype(bf16)
                for c in range(3):
                    row = jnp.broadcast_to(column_ref[c : c + 1, :], (16, width))
                    low_ref[c, model:, :] = row.astype(bf16)

    whole = pl.BlockSpec((3, model, width), lambda i: (0, 0, 0))
    columns = pl.BlockSpec((8, width), lambda i: (0, 0))
    row_spec = pl.BlockSpec((block, model), lambda i: (i, 0))
    operands = [place, normed, dqkv, weight]
    in_specs = [pl.BlockSpec(memory_space=pltpu.SMEM), row_spec, pl.BlockSpec((3, block, width), lambda i: (0, i, 0)), whole]
    if not first:
        operands += list(before)
        in_specs += [whole, columns]
    out_specs = [pl.BlockSpec((block, model), lambda i: (0, 0))] * given + [whole, columns]
    out_shape = [jax.ShapeDtypeStruct((block, model), bf16)] * given + [
        jax.ShapeDtypeStruct((3, model, width), f32),
        jax.ShapeDtypeStruct((8, width), f32),
    ]
    if last:
        out_specs.append(pl.BlockSpec((3, model + 16, width), lambda i: (0, 0, 0)))
        out_shape.append(jax.ShapeDtypeStruct((3, model + 16, width), bf16))
    return pl.pallas_call(
        kernel,
        grid=(steps,),
        in_specs=in_specs,
        out_specs=out_specs,
        out_shape=out_shape,
        input_output_aliases={} if first else {4: given, 5: given + 1},
        compiler_params=pltpu.CompilerParams(vmem_limit_bytes=VMEM_LIMIT),
        cost_estimate=pl.CostEstimate(
            flops=12 * rows * model * width // COST_SCALE,
            transcendentals=0,
            bytes_accessed=rows * width,
        ),
        name="project_back",
    )(*operands)


def project_rows(place, dqkv, weight, pieces):
    _, rows, width = dqkv.shape
    model = weight.shape[1]
    block = rows // pieces

    def kernel(place_ref, dqkv_ref, weight_ref, *row_refs):
        row_grad = nt(dqkv_ref[0], weight_ref[0])
        for c in range(1, 3):
            row_grad = row_grad + nt(dqkv_ref[c], weight_ref[c])
        row_grad = row_grad.astype(bf16)
        for k in range(pieces):

            @pl.when(pl.program_id(0) == place_ref[0] ^ k)
            def _():
                row_refs[k][...] = row_grad

    return pl.pallas_call(
        kernel,
        grid=(pieces,),
        in_specs=[
            pl.BlockSpec(memory_space=pltpu.SMEM),
            pl.BlockSpec((3, block, width), lambda i: (0, i, 0)),
            pl.BlockSpec((3, model, width), lambda i: (0, 0, 0)),
        ],
        out_specs=[pl.BlockSpec((block, model), lambda i: (0, 0))] * pieces,
        out_shape=[jax.ShapeDtypeStruct((block, model), bf16)] * pieces,
        compiler_params=params(),
        cost_estimate=hint(6 * rows * model * width, rows * width),
        name="project_rows",
    )(place, dqkv, weight)


def make_shards(tensor_size, group_size):
    square = tensor_size == 4

    def swap(value, bits):
        return lax.ppermute(value, "tensor", [(i, i ^ bits) for i in range(tensor_size)])

    def gather_far(own):
        return swap(own, 2) if square else lax.all_gather(own, "tensor")

    def gather_near(own, far):
        if not square:
            return [far[i] for i in range(tensor_size)]
        return [own, swap(own, 1), far, swap(far, 1)]

    def exchange(stacked):
        return lax.all_to_all(stacked, "tensor", 0, 0)

    def sum_near(blocks, anchor):
        if not square:
            return (jnp.stack(blocks),), anchor
        anchor, (near_own, near_far) = tie(anchor, (swap(blocks[1], 1), swap(blocks[3], 1)))
        far = (blocks[2].astype(f32) + near_far.astype(f32)).astype(blocks[2].dtype)
        return (blocks[0], near_own, far), anchor

    def terms_far(stage, anchor):
        if not square:
            own = lax.psum_scatter(stage[0], "tensor", scatter_dimension=0, tiled=False)
            anchor, own = tie(anchor, own)
            return [own], anchor
        own, near, far = stage
        anchor, received = tie(anchor, swap(far, 2))
        return [own, near, received], anchor

    def sum_far(stage, anchor):
        terms, anchor = terms_far(stage, anchor)
        total = terms[0].astype(f32)
        for term in terms[1:]:
            total = total + term.astype(f32)
        return total.astype(terms[0].dtype), anchor

    steps = []
    for axis, size in (("tensor", tensor_size), ("dp", group_size)):
        bit = 1
        while bit < size:
            steps.append((axis, [(i, i ^ bit) for i in range(size)]))
            bit *= 2

    def sum_step(value, step, anchor):
        anchor, received = tie(anchor, lax.ppermute(value, step[0], step[1]))
        return value + received, anchor

    def ring_plan():
        bits = [1 << k for k in range(group_size.bit_length() - 1)]
        return [(bit, True) for bit in bits] + [(bit, False) for bit in reversed(bits)]

    def ring_step(value, step, anchor):
        bit, reducing = step
        side = (lax.axis_index("dp") // bit) % 2
        pairs = [(i, i ^ bit) for i in range(group_size)]
        if reducing:
            half = value.shape[0] // 2
            sent = lax.dynamic_slice_in_dim(value, (1 - side) * half, half, axis=0)
            anchor, received = tie(anchor, lax.ppermute(sent, "dp", pairs))
            kept = lax.dynamic_slice_in_dim(value, side * half, half, axis=0)
            return (kept.astype(f32) + received.astype(f32)).astype(value.dtype), anchor
        anchor, received = tie(anchor, lax.ppermute(value, "dp", pairs))
        return in_halves(value, received, side), anchor

    def in_halves(own, other, side):
        rows = own.shape[0]
        whole = jnp.zeros((2 * rows,) + own.shape[1:], own.dtype)
        whole = lax.dynamic_update_slice_in_dim(whole, own, side * rows, axis=0)
        return lax.dynamic_update_slice_in_dim(whole, other, (1 - side) * rows, axis=0)

    def fetch_half(own):
        half = own.shape[0] // 2
        side = lax.axis_index("dp") % 2
        return swap(lax.dynamic_slice_in_dim(own, side * half, half, axis=0), 2)

    def fetch_rest(half):
        return lax.ppermute(half, "dp", [(i, i ^ 1) for i in range(group_size)])

    def in_order(stacked):
        if not square:
            return stacked
        own = lax.axis_index("tensor")
        return jnp.concatenate(
            [lax.dynamic_slice_in_dim(stacked, own ^ i, 1, axis=0) for i in range(tensor_size)], axis=0
        )

    def shards(
        patches,
        cotangent,
        empty_slots,
        dataset_id,
        dataset_weight,
        query_key_value_weight,
        qv_bias,
        output_projection_weight,
        out_bias,
        up_projection_weight,
        up_bias,
        down_projection_weight,
        down_bias,
        attn_gain,
        attn_shift,
        mlp_gain,
        mlp_shift,
    ):
        slot_count, own_rows, model = patches.shape
        width = query_key_value_weight.shape[2]
        group_slots = empty_slots.shape[0]
        slot_index = jnp.arange(group_slots * slot_count, dtype=jnp.int32) % slot_count
        filled = jnp.repeat(slot_count - empty_slots, slot_count)
        valid_all = (slot_index < filled).astype(f32)
        table_hits = dataset_id[:, None] == jnp.arange(dataset_weight.shape[0], dtype=jnp.int32)[None, :]
        numerator = jnp.sum(jnp.where(table_hits, dataset_weight[None, :], 0), axis=1).astype(f32)
        total_items = jnp.sum(valid_all)
        total_weight = jnp.sum(valid_all * numerator)
        multiplier_whole = valid_all * numerator * total_items / total_weight
        own_start = lax.axis_index("dp") * slot_count
        own_scale = lax.dynamic_slice_in_dim(multiplier_whole, own_start, slot_count)
        own_valid = lax.dynamic_slice_in_dim(valid_all, own_start, slot_count)
        all_rows = slot_count * own_rows
        row_scale = jnp.repeat(own_scale, own_rows)[:, None]
        gain_row, shift_row, mlp_gain_row, mlp_shift_row, out_bias_row = (
            value[None, :] for value in (attn_gain, attn_shift, mlp_gain, mlp_shift, out_bias)
        )
        proj_bias = jnp.stack([qv_bias[0], jnp.zeros_like(qv_bias[0]), qv_bias[1]])[:, None, :]
        bias_row = up_bias[None, :]

        dp_side = lax.axis_index("dp") % 2
        place = jnp.zeros((1,), jnp.int32)
        if square:
            place = place + lax.axis_index("tensor")
        fetch = fetch_half if square else gather_far
        weights_near = ()
        if square:
            weights_near = tuple(
                swap(value, 1) for value in (output_projection_weight, up_projection_weight, down_projection_weight)
            )

        def gather_rows(own):
            return lax.all_gather(own, "tensor", axis=0, tiled=True)

        normed = [norm_item(patches, i, gain_row, shift_row) for i in range(slot_count)]
        every = gather_rows(normed[0])
        bias_far = gather_far(bias_row)
        cot_low = (cotangent.astype(f32).reshape(all_rows, model) * row_scale).astype(bf16)
        early = None
        if square:
            early = cot_back(cot_low, [down_projection_weight, weights_near[2]])
            every, (early, normed) = tie(every, (early, normed))
        qkvs, attended, lses, heads_own, normed_every = [], [], [], [], []
        for i in range(slot_count):
            last = i == slot_count - 1
            normed_every.append(every)
            following = None
            if not last:
                every, following = tie(every, normed[i + 1])
                following = gather_rows(following)
            qkv = (
                jnp.einsum("wz,gzh->gwh", every, query_key_value_weight, preferred_element_type=f32) + proj_bias
            ).astype(bf16)
            if i == 0:
                qkv, (weights_near, bias_far) = tie(qkv, (weights_near, bias_far))
            out, lse = attend(qkv)
            if not last:
                out, following = tie(out, following)
            if i > 0:
                out, heads_own[-1] = tie(out, heads_own[-1])
            if i == min(1, slot_count - 1):
                out, (up_own, out_own) = tie(out, (up_projection_weight, output_projection_weight))
                out_far = gather_far(out_own)
                up_far = fetch(up_own)
            if last:
                out, out_far = tie(out, out_far)
            heads_own.append(exchange(out.reshape(tensor_size, own_rows, width)))
            qkvs.append(qkv)
            attended.append(out)
            lses.append(lse)
            every = following
        if square:
            out_weight = jnp.concatenate([out_own, weights_near[0], out_far, swap(out_far, 1)], axis=0)
        else:
            out_weight = jnp.concatenate(gather_near(out_own, out_far), axis=0)
        rows_done = None
        for i in range(slot_count):
            if i == slot_count - 1:
                rows_done, (heads_own[i], up_far) = tie(rows_done, (heads_own[i], up_far))
                heads_own[i], down_own = tie(heads_own[i], down_projection_weight)
                down_far = gather_far(down_own)
            rows_done = out_project(
                patches, i, place, heads_own[i], out_weight, out_bias_row, mlp_gain_row, mlp_shift_row, rows_done
            )
        if square:
            up_rest = fetch_rest(up_far)
        attended_rows, residual, normed_mlp = rows_done

        bias_blocks = gather_near(bias_row, bias_far)
        if square:
            up_blocks = [up_own, weights_near[1]]
            down_blocks = [down_own, weights_near[2]]
        else:
            up_blocks = gather_near(up_own, up_far)
            down_blocks = gather_near(down_own, down_far)
        calls = tensor_size // 2
        total = None
        slopes, down_grads = [], []
        for c in range(calls):
            pair = slice(2 * c, 2 * c + 2)
            if c == 1 and square:
                total, (up_rest, down_far) = tie(total, (up_rest, down_far))
                up_far = in_halves(up_far, up_rest, dp_side)
                up_blocks += [up_far, swap(up_far, 1)]
                down_blocks += [down_far, swap(down_far, 1)]
            slope, total, *grads = mlp_forward(
                normed_mlp, cot_low, up_blocks[pair], bias_blocks[pair], down_blocks[pair], total
            )
            slopes.append(slope)
            down_grads += grads
        layer_sum = total

        cot_late, down_grads = tie(cot_low, down_grads)
        before = None
        bias_grads = []
        for c in range(calls):
            pair = slice(2 * c, 2 * c + 2)
            if c == 0 and square:
                *before, bias_grad = mlp_backward(early, slopes[c], up_blocks[pair], [], before, c, calls)
            else:
                *before, bias_grad = mlp_backward(
                    cot_late, slopes[c], up_blocks[pair], down_blocks[pair], before, c, calls
                )
            bias_grads.append(bias_grad)
            if c == 0:
                down_stage, before = sum_near(down_grads, before)
        ring = ring_plan()
        pre_grad, total = before

        if square:
            ahead = weight_back(normed_mlp, pre_grad, [1, 3], None, None, tensor_size)
            total, ahead = tie(total, ahead)
        grad_residual, grad_low, small_rows, pieces = residual_back(
            total, residual, cotangent, own_scale, place, out_weight, mlp_gain_row, tensor_size
        )
        down_sum, pieces = sum_far(down_stage, pieces)
        grad_attended = exchange(pieces)
        if square:
            up_near, up_diag_near = swap(ahead[0], 1), swap(ahead[1], 1)
            first, second, *out_grads = weight_back(
                normed_mlp, pre_grad, [2, 0], attended_rows, grad_low, tensor_size
            )
            second, (up_near, up_diag_near) = tie(second, (up_near, up_diag_near))
            up_far_sum = (first.astype(f32) + up_diag_near.astype(f32)).astype(bf16)
            out_stage, up_far_sum = sum_near(out_grads, up_far_sum)
            up_far_sum, grad_attended = tie(up_far_sum, grad_attended)
            up_stage = (second, up_near, up_far_sum)
        else:
            weight_grads = weight_back(
                normed_mlp, pre_grad, list(range(tensor_size)), attended_rows, grad_low, tensor_size
            )
            up_stage, grad_attended = sum_near(weight_grads[:tensor_size], grad_attended)
            out_stage, grad_attended = sum_near(weight_grads[tensor_size:], grad_attended)
        bias_rows = in_order(jnp.concatenate(bias_grads, axis=1).reshape(tensor_size, -1))
        smalls = jnp.concatenate([small_rows[:4].reshape(-1), bias_rows.reshape(-1)]).reshape(-1, 128)

        waiting = list(steps)
        weights_wide = query_key_value_weight.astype(f32)
        sums = None
        grad_normed = []
        for i in range(slot_count):
            last = i == slot_count - 1
            dqkv = attend_back(qkvs[i], attended[i], grad_attended, i, lses[i])
            if i >= 2:
                grad_normed[i - 2], dqkv = terms_far(grad_normed[i - 2], dqkv)
            if i >= 1 and not last:
                grad_normed[i - 1], dqkv = sum_near(grad_normed[i - 1], dqkv)
            if i == 0:
                up_sum, dqkv = sum_far(up_stage, dqkv)
                out_sum, dqkv = sum_far(out_stage, dqkv)
                up_all = lax.psum((up_sum, out_sum), "dp")
            if last:
                dqkv, up_all = tie(dqkv, up_all)
            if waiting and i > 0:
                smalls, dqkv = sum_step(smalls, waiting.pop(0), dqkv)
            if ring:
                down_sum, dqkv = ring_step(down_sum, ring.pop(0), dqkv)
            results = project_back(place, normed_every[i], dqkv, query_key_value_weight, sums, last, tensor_size)
            if not last:
                partial, sums = results[:tensor_size], results[tensor_size:]
                if waiting:
                    smalls, partial = sum_step(smalls, waiting.pop(0), partial)
                if ring:
                    down_sum, partial = ring_step(down_sum, ring.pop(0), partial)
            else:
                *sums, qkv_low = results
                qkv_low, (dqkv, grad_residual, layer_sum) = tie(qkv_low, (dqkv, grad_residual, layer_sum))
                qkv_all = lax.psum(qkv_low, "dp")
                output = layer_out(layer_sum, residual, down_bias[None, :], own_valid, patches.shape)
                partial = project_rows(place, dqkv, query_key_value_weight, tensor_size)
                if i >= 1:
                    grad_normed[i - 1], partial = sum_near(grad_normed[i - 1], partial)
                raw = jnp.stack(
                    [
                        jnp.sum(sums[0] * weights_wide, axis=(0, 2)),
                        jnp.sum(sums[1][:3, None, :] * weights_wide, axis=(0, 2)),
                    ]
                )
                for axis, pairs in steps:
                    raw = raw + lax.ppermute(raw, axis, pairs)
            grad_normed.append(partial)
        grad_inputs = None
        for i in range(slot_count):
            if i == slot_count - 1:
                grad_normed[i], grad_residual = sum_near(grad_normed[i], grad_residual)
            terms = grad_normed[i]
            if i >= slot_count - 2:
                terms, grad_residual = terms_far(terms, grad_residual)
            grad_inputs = input_back(terms, patches, i, grad_residual, gain_row, grad_inputs)
        grad_inputs, qkv_all = tie(grad_inputs, qkv_all)
        for step in ring:
            down_sum = ring_step(down_sum, step, place)[0]
        for step in waiting:
            smalls = sum_step(smalls, step, place)[0]
        weight_grad = qkv_all[:, :model].astype(f32)
        columns = qkv_all[:, model].astype(f32)
        up_all, out_all = [value.astype(f32) for value in up_all]
        down_all = down_sum.astype(f32)
        inverse = 1.0 / total_items
        smalls = smalls.reshape(-1) * inverse
        raw = raw * inverse
        small_rows = smalls[: 4 * model].reshape(4, model)
        units = up_bias.shape[0]
        bias_all = lax.dynamic_slice_in_dim(smalls[4 * model :], lax.axis_index("tensor") * units, units)
        shift_all = raw[1]
        gain_all = (raw[0] - attn_shift * shift_all) / attn_gain
        columns = columns * inverse
        return (
            output,
            grad_inputs,
            weight_grad * inverse,
            jnp.stack([columns[0], columns[2]]),
            out_all * inverse,
            small_rows[2],
            up_all * inverse,
            bias_all,
            down_all * inverse,
            small_rows[3],
            gain_all,
            shift_all,
            small_rows[0],
            small_rows[1],
        )

    return shards


def solution(mesh):
    items = P("dp", "tensor", None)
    return jax.shard_map(
        make_shards(mesh.shape["tensor"], mesh.shape["dp"]),
        mesh=mesh,
        in_specs=(
            items,
            items,
            P(),
            P(),
            P(),
            P(None, None, "tensor"),
            P(None, "tensor"),
            P("tensor", None),
            P(),
            P(None, "tensor"),
            P("tensor"),
            P("tensor", None),
            P(),
            P(),
            P(),
            P(),
            P(),
        ),
        out_specs=(
            items,
            items,
            P(None, None, "tensor"),
            P(None, "tensor"),
            P("tensor", None),
            P(),
            P(None, "tensor"),
            P("tensor"),
            P("tensor", None),
            P(),
            P(),
            P(),
            P(),
            P(),
        ),
        check_vma=False,
    )
```
